32 devices in a mesh: dp: 16 (over z, x, core), tensor: 2 (over y).
Axes of the slice: x: 2, y: 2, z: 4, core: 2. Of those that a mesh axis runs over, the one named last changes fastest.
Arguments:
- layer_input: bfloat16 [16384, 768], P(('dp', 'tensor')), may hold values from -11 to 11
- grad_out: bfloat16 [16384, 768], P(('dp', 'tensor')), may hold values from -6 to 6
- segment: int32 [16384], P('dp'), may hold values from 0 to 63, never falling along the last dimension, each value on 1 to 1024 neighbouring positions
- entity: int32 [16384], P('dp'), may hold values 0 or 1
- valid_mask: int32 [16384], P('dp'), may hold values from 0 to 1, as said below
- query_weight: bfloat16 [4, 768, 768], P(None, 'dp', 'tensor'), may hold values from -0.4375 to 0.4375
- key_value_weight: bfloat16 [2, 768, 768], P(None, 'dp', 'tensor'), may hold values from -0.21875 to 0.21875
- attn_bias: bfloat16 [5, 768], P(None, 'tensor'), may hold values from -3 to 3
- out_weight: bfloat16 [768, 768], P('tensor', 'dp'), may hold values from -0.875 to 0.875
- out_bias: bfloat16 [2, 768], replicated, may hold values from -2 to 2
- ln_gain: bfloat16 [2, 768], replicated, may hold values from 0.25 to 1.75
- ln_bias: bfloat16 [2, 768], replicated, may hold values from -2 to 2
- up_weight: bfloat16 [768, 3072], P('dp', 'tensor'), may hold values from -0.21875 to 0.21875
- ffn_bias: bfloat16 [3072], P('tensor'), may hold values from -3 to 3
- down_weight: bfloat16 [3072, 768], P('tensor', 'dp'), may hold values from -0.109375 to 0.109375
Outputs:
- output: bfloat16 [16384, 768], P(('dp', 'tensor'))
- input_grad: float32 [16384, 768], P(('dp', 'tensor'))
- residual_rms: float32 [4], replicated
- query_weight_grad: float32 [4, 768, 768], P(None, 'dp', 'tensor')
- key_value_weight_grad: float32 [2, 768, 768], P(None, 'dp', 'tensor')
- attn_bias_grad: float32 [5, 768], P(None, 'tensor')
- out_weight_grad: float32 [768, 768], P('tensor', 'dp')
- out_bias_grad: float32 [2, 768], replicated
- ln_gain_grad: float32 [2, 768], replicated
- ln_bias_grad: float32 [2, 768], replicated
- up_weight_grad: float32 [768, 3072], P('dp', 'tensor')
- ffn_bias_grad: float32 [3072], P('tensor')
- down_weight_grad: float32 [3072, 768], P('tensor', 'dp')
The draws below stay inside these ranges and needn't reach their ends.
Inputs may be any that keep to these rules, and one draw needn't show every extreme that they name: segment numbers never fall along the tokens. `valid_mask`: the first token of every sequence of 1024 tokens is real.
All inputs are finite; a program needn't handle non-finite values. No bound on the sum of `entity` on one device may be relied on, other than what follows from the above.
Results may differ from the reference program's by a relative error of at most 0.017.
Values may be sent and summed in bfloat16 or wider, within the bound.
A program may use at most 128 MiB of HBM per device.

```python
import math
import jax
import jax.numpy as jnp
import numpy as np
from jax import lax

D = 768
HEADS = 12
HEAD = 64
FF = 3072
SEQ = 1024
TOKENS = 16384


def draw_layer_input(key, part):
    row_index = jnp.arange(TOKENS, dtype=jnp.float32)
    row_scale = 0.6 + 1.2 * row_index / TOKENS
    base = jnp.clip(jax.random.normal(key, (TOKENS, D), jnp.float32), -6.0, 6.0)
    return (base * row_scale[:, None]).astype(jnp.bfloat16)


def draw_valid_mask(key, part):
    draws = jax.random.randint(jax.random.fold_in(key, 7), (TOKENS,), 0, 16)
    positions = jnp.arange(TOKENS, dtype=jnp.int32)
    real = (draws < 15).astype(jnp.int32)
    return jnp.where(positions % SEQ == 0, jnp.ones_like(real), real).astype(jnp.int32)


def set_ends(values, rng, low, high):
    extent = values.shape
    spot = [jax.random.randint(jax.random.fold_in(rng, axis), (), 0, extent[axis]) for axis in range(len(extent))]
    values = values.at[tuple(spot)].set(low)
    longest = extent.index(max(extent))
    spot[longest] = (spot[longest] + 1) % extent[longest]
    return values.at[tuple(spot)].set(high)


def levels(key, dims, split, least, top_value):
    def one(dim, shards_of):
        steps = jax.random.uniform(jax.random.fold_in(jax.random.fold_in(key, 6), dim), (shards_of,), jnp.float32, least / len(split), top_value / len(split))
        return jnp.repeat(jnp.exp(steps), dims[dim] // shards_of).reshape((-1,) + (1,) * (len(dims) - dim - 1))

    level = one(*split[0])
    for cut in split[1:]:
        level = level * one(*cut)
    return level


def split_up(number_of, total, reach, lean):
    loads = [(1 << 20) // math.isqrt(grade ** lean) + 1 for grade in range(2, number_of + 1)]
    surplus, counts = total - reach - (number_of - 1), [1] * (number_of - 1)
    while surplus > 0:
        free = [i for i in range(number_of - 1) if counts[i] < reach]
        whole, remaining = sum([loads[i] for i in free]), surplus
        for i in free:
            extra = min(reach - counts[i], max(1, remaining * loads[i] // whole), surplus)
            counts[i] = counts[i] + extra
            surplus = surplus - extra
    return np.array([reach] + counts)


def ragged_sizes(own_key, count, total, bound, slope):
    if count == 2:
        one = jax.random.randint(own_key, (), max(1, total - bound), min(bound, total - 1) + 1)
        return jnp.stack([one, total - one])
    sizes = jnp.asarray(split_up(count, total, bound, slope), jnp.int32)
    couples = (count - 1) // 2
    giver, sink = sizes[1:1 + 2 * couples:2], sizes[2:2 + 2 * couples:2]
    margin = jnp.minimum(giver - 1, bound - sink)
    moved = jax.random.randint(jax.random.fold_in(own_key, 1), (couples,), 0, 1 << 20) % (margin + 1)
    sizes = sizes.at[1:1 + 2 * couples:2].set(giver - moved).at[2:2 + 2 * couples:2].set(sink + moved)
    return sizes[jax.random.permutation(jax.random.fold_in(own_key, 2), count)]


def bell_draw(stream_key, shape, deviation, bound, cuts=(), kind=jnp.bfloat16):
    entries = jax.random.normal(stream_key, shape, jnp.float32) * deviation
    if len(cuts) > 0:
        entries = levels(stream_key, shape, cuts, -0.22, 0.18) * entries
    return jnp.clip(entries, min=-bound, max=bound).astype(kind)


def setup_inputs(seed: int = 0) -> dict:
    seeds = jax.random.split(jax.random.key(seed), 16)
    return {
        "layer_input": draw_layer_input(jax.random.fold_in(seeds[15], 71), 0),
        "grad_out": bell_draw(seeds[1], (TOKENS, D), 1.0, 6.0, ((0, 32),)),
        "segment": jnp.searchsorted(jnp.cumsum(ragged_sizes(seeds[2], TOKENS // (SEQ // 4), TOKENS, SEQ, 1)), jnp.arange(TOKENS), side="right").astype(jnp.int32),
        "entity": set_ends((jax.random.randint(seeds[3], (TOKENS,), 0, 4) < 1).astype(jnp.int32), jax.random.fold_in(seeds[3], 1), 0, 1),
        "valid_mask": draw_valid_mask(jax.random.fold_in(seeds[15], 71), 0),
        "query_weight": bell_draw(seeds[5], (4, D, D), (D // 4) ** -0.5, 0.4375, ((1, 16), (2, 2))),
        "key_value_weight": bell_draw(seeds[6], (2, D, D), D ** -0.5, 0.21875, ((1, 16), (2, 2))),
        "attn_bias": bell_draw(seeds[7], (5, D), 0.5, 3.0, ((1, 2),)),
        "out_weight": bell_draw(seeds[8], (D, D), (D // 16) ** -0.5, 0.875, ((0, 2), (1, 16))),
        "out_bias": bell_draw(seeds[9], (2, D), 0.3, 2.0),
        "ln_gain": jnp.clip(1.0 + 0.15 * jax.random.normal(seeds[10], (2, D), jnp.float32), 0.25, 1.75).astype(jnp.bfloat16),
        "ln_bias": bell_draw(seeds[11], (2, D), 0.3, 2.0),
        "up_weight": bell_draw(seeds[12], (D, FF), D ** -0.5, 0.21875, ((0, 16), (1, 2))),
        "ffn_bias": bell_draw(seeds[13], (FF,), 0.5, 3.0, ((0, 2),)),
        "down_weight": bell_draw(seeds[14], (FF, D), FF ** -0.5, 0.109375, ((0, 2), (1, 16))),
    }


EPS = 1e-06
NEG = -1e+30
HIGHEST = lax.Precision.HIGHEST

@jax.custom_vjp
def low(v):
    return lax.optimization_barrier(v.astype(jnp.bfloat16)).astype(jnp.float32)

@jax.custom_vjp
def low_back(v):
    return v

def low_keep(v):
    return (low(v), None)

def low_pass(kept, grad):
    return (grad,)

def back_keep(v):
    return (v, None)

def back_low(kept, grad):
    return (low(grad),)
low.defvjp(low_keep, low_pass)
low_back.defvjp(back_keep, back_low)

def layer_norm(resid, gain, shift):
    center = resid - lax.optimization_barrier(jnp.mean(resid, -1, keepdims=True))
    spread = lax.optimization_barrier(jnp.mean(center * center, -1, keepdims=True))
    return center * lax.rsqrt(spread + EPS) * gain + shift

def layer(inputs, params, segs, ents, valids):
    query_w, kv_w, attn_b, out_w, out_b, gains, shifts, up_w, ffn_b, down_w = params
    length = inputs.shape[0]
    scale = HEAD ** (-0.5)
    query_four = jnp.einsum('ld,mde->mle', inputs, query_w, precision=HIGHEST) + attn_b[:4, None, :]
    ent_rows = (ents == 1)[:, None]
    query_word = low(low_back(jnp.where(ent_rows, query_four[2], query_four[0])))
    query_ent = low(low_back(jnp.where(ent_rows, query_four[3], query_four[1])))
    keys = low(low_back(jnp.dot(inputs, kv_w[0], precision=HIGHEST)))
    values = low(low_back(jnp.dot(inputs, kv_w[1], precision=HIGHEST) + attn_b[4]))
    shape3 = (length, HEADS, HEAD)
    score_word = jnp.einsum('qhd,khd->hqk', query_word.reshape(shape3), keys.reshape(shape3), precision=HIGHEST)
    score_ent = jnp.einsum('qhd,khd->hqk', query_ent.reshape(shape3), keys.reshape(shape3), precision=HIGHEST)
    scores = low_back(jnp.where((ents == 1)[None, None, :], score_ent, score_word) * scale)
    positions = jnp.arange(length)
    allowed = (segs[:, None] == segs[None, :]) & ((valids[None, :] == 1) | (positions[:, None] == positions[None, :]))
    masked = jnp.where(allowed[None], scores, NEG)
    row_max = lax.optimization_barrier(jnp.max(masked, -1, keepdims=True))
    expo_vals = jnp.exp(masked - row_max)
    probs = expo_vals / lax.optimization_barrier(jnp.sum(expo_vals, -1, keepdims=True))
    context = jnp.einsum('hqk,khd->qhd', low(probs), values.reshape(shape3), precision=HIGHEST)
    context = low(low_back(context.reshape(length, HEADS * HEAD)))
    attn = low_back(jnp.dot(context, out_w, precision=HIGHEST) + out_b[0])
    resid_one = inputs + attn
    hidden = layer_norm(resid_one, gains[0], shifts[0])
    pre = low_back(jnp.dot(low(hidden), up_w, precision=HIGHEST) + ffn_b)
    act = low(jax.nn.gelu(pre, approximate=False))
    ffn = low_back(jnp.dot(act, down_w, precision=HIGHEST) + out_b[1])
    resid_two = hidden + ffn
    result = layer_norm(resid_two, gains[1], shifts[1])
    weight_rows = valids.astype(jnp.float32)[:, None]
    aux = jnp.stack([jnp.sum(weight_rows * resid_one * resid_one), jnp.sum(weight_rows * attn * attn), jnp.sum(weight_rows * ffn * ffn), jnp.sum(weight_rows * resid_two * resid_two), jnp.sum(valids.astype(jnp.float32))])
    return (result, aux)

def reference(layer_input, grad_out, segment, entity, valid_mask, query_weight, key_value_weight, attn_bias, out_weight, out_bias, ln_gain, ln_bias, up_weight, ffn_bias, down_weight):
    params = tuple((param.astype(jnp.float32) for param in (query_weight, key_value_weight, attn_bias, out_weight, out_bias, ln_gain, ln_bias, up_weight, ffn_bias, down_weight)))
    number = TOKENS // SEQ
    pieces_all = (layer_input.astype(jnp.float32).reshape(number, SEQ, D), grad_out.astype(jnp.float32).reshape(number, SEQ, D), segment.reshape(number, SEQ), entity.reshape(number, SEQ), valid_mask.reshape(number, SEQ))
    zero_grads = jax.tree.map(jnp.zeros_like, params)
    zero_aux = jnp.zeros((5,), jnp.float32)

    def one_sequence(carry, pieces):
        inputs, cotangent, segs, ents, valids = pieces

        def forward(inputs_f, params_f):
            return layer(inputs_f, params_f, segs, ents, valids)
        result, pullback, aux = jax.vjp(forward, inputs, params, has_aux=True)
        input_grad, param_grads = pullback(cotangent)
        grads, totals = carry
        grads = jax.tree.map(jnp.add, grads, param_grads)
        return ((grads, totals + aux), (result.astype(jnp.bfloat16), input_grad))
    (grads, totals), (outputs, input_grads) = lax.scan(one_sequence, (zero_grads, zero_aux), pieces_all)
    rms_values = jnp.sqrt(totals[:4] / (totals[4] * D))
    return (outputs.reshape(TOKENS, D), input_grads.reshape(TOKENS, D), rms_values, grads[0], grads[1], grads[2], grads[3], grads[4], grads[5], grads[6], grads[7], grads[8], grads[9])
```

```python
import functools

import jax
import jax.numpy as jnp
from jax import lax
from jax.experimental import pallas as pl
from jax.experimental.pallas import tpu as pltpu
from jax.sharding import PartitionSpec as P

HEAD = 64
EPS = 1e-06
NEG = -1e30
GRID = 16
LANES = 128
MESH = pl.DeviceIdType.MESH
BF16 = jnp.bfloat16
F32 = jnp.float32
VMEM_LIMIT = 60 * 1024 * 1024


def layer_norm(resid, gain, shift):
    center = resid - jnp.mean(resid, -1, keepdims=True)
    spread = jnp.mean(center * center, -1, keepdims=True)
    return center * lax.rsqrt(spread + EPS) * gain + shift


def gelu_exact(values):
    return jax.nn.gelu(values, approximate=False)


class Place:
    def __init__(self, subs):
        rank = lax.axis_index("dp")
        self.subs = subs
        self.sub = rank % subs
        block = rank // subs
        self.z = block // 4
        self.x = (block // 2) % 2
        self.c = block % 2
        self.y = lax.axis_index("tensor")
        self.x1 = jnp.where(self.c == 0, 1 - self.x, self.x)
        self.y1 = jnp.where(self.c == 0, self.y, 1 - self.y)
        self.x2 = jnp.where(self.c == 0, self.x, 1 - self.x)
        self.y2 = jnp.where(self.c == 0, 1 - self.y, self.y)

    def device(self, z=None, x=None, c=None, y=None):
        z = self.z if z is None else z
        x = self.x if x is None else x
        c = self.c if c is None else c
        y = self.y if y is None else y
        return (((z * 2 + x) * 2 + c) * self.subs + self.sub, y)

    def z_peer(self, step):
        return self.device(z=(self.z + step) % 4)

    def first(self):
        return self.device(x=self.x1, y=self.y1)

    def second(self):
        return self.device(x=self.x2, y=self.y2)

    def sibling(self):
        return self.device(c=1 - self.c)

    def pieces(self):
        return (
            (self.x, self.y),
            (self.x1, self.y1),
            (self.x2, self.y2),
            (1 - self.x, 1 - self.y),
        )


def entry_barrier(place):
    barrier = pltpu.get_barrier_semaphore()
    peers = [place.z_peer(step) for step in (1, 2, 3)]
    peers += [place.device(x=1 - place.x), place.device(y=1 - place.y), place.sibling()]
    for peer in peers:
        pl.semaphore_signal(barrier, inc=1, device_id=peer, device_id_type=MESH)
    pl.semaphore_wait(barrier, len(peers))


def remote(src, dst, send, recv, peer):
    return pltpu.make_async_remote_copy(
        src_ref=src, dst_ref=dst, send_sem=send, recv_sem=recv, device_id=peer, device_id_type=MESH
    )


class Gather:
    def __init__(self, place, shard, full, send, recv, local):
        self.place, self.shard, self.full = place, shard, full
        self.send, self.recv, self.local = send, recv, local
        self.w = shard.shape[-1]
        self.started = []

    def cols(self, y):
        return pl.ds(pl.multiple_of(y * self.w, LANES), self.w)

    def piece(self, spot, c):
        x, y = spot
        return self.full.at[:, :, x, c, :, self.cols(y)]

    def copy(self, index, src, dst, peer):
        step = remote(src, dst, self.send.at[index], self.recv.at[index], peer)
        step.start()
        self.started.append(step)

    def arrive(self, index, ref):
        remote(ref, ref, self.send.at[index], self.recv.at[index], self.place.sibling()).wait_recv()

    def own(self, z):
        p = self.place
        return self.full.at[:, z, p.x, p.c, :, self.cols(p.y)]

    def stage1(self):
        p = self.place
        self.kept = pltpu.make_async_copy(self.shard, self.own(p.z), self.local)
        self.kept.start()
        for step in (1, 2, 3):
            self.copy(step - 1, self.shard, self.own(p.z), p.z_peer(step))

    def stage2(self):
        p = self.place
        self.kept.wait()
        for step in (1, 2, 3):
            self.arrive(step - 1, self.own((p.z + 4 - step) % 4))
        mine = self.piece(p.pieces()[0], p.c)
        self.copy(3, mine, mine, p.first())
        self.copy(4, mine, mine, p.second())
        self.copy(6, mine, mine, p.sibling())

    def stage3(self):
        p = self.place
        got = self.piece(p.pieces()[1], p.c)
        self.arrive(3, got)
        self.copy(5, got, got, p.second())
        self.copy(7, got, got, p.sibling())

    def stage4(self):
        p = self.place
        for index, spot in ((4, 2), (5, 3)):
            got = self.piece(p.pieces()[spot], p.c)
            self.arrive(index, got)
            self.copy(index + 4, got, got, p.sibling())

    def stage5(self):
        p = self.place
        spots = p.pieces()
        for index, spot in ((6, 0), (7, 2), (8, 1), (9, 3)):
            self.arrive(index, self.piece(spots[spot], 1 - p.c))
        for step in self.started:
            step.wait_send()

    def stages(self):
        return [self.stage1, self.stage2, self.stage3, self.stage4, self.stage5]


def wavefront(movers):
    lists = [mover.stages() for mover in movers]
    depth = max(len(stages) for stages in lists)
    order = []
    for time in range(len(lists) + depth - 1):
        for index in range(len(lists)):
            stage = time - index
            if 0 <= stage < len(lists[index]):
                order.append(lists[index][stage])
    return order


def gather_kernel(subs, count, *refs):
    shards, rows = refs[:count], refs[count]
    fulls, both = refs[count + 1 : 2 * count + 1], refs[2 * count + 1]
    send, recv, local, row_sems = refs[2 * count + 2 :]
    place = Place(subs)
    entry_barrier(place)
    kept = pltpu.make_async_copy(rows, both.at[place.y], row_sems.at[0])
    kept.start()
    across = remote(
        rows, both.at[place.y], row_sems.at[1], row_sems.at[2], place.device(y=1 - place.y)
    )
    across.start()
    movers = [
        Gather(place, shards[i], fulls[i], send.at[i], recv.at[i], local.at[i]) for i in range(count)
    ]
    for mover in movers:
        mover.stage1()
    for step in wavefront(movers):
        if step.__func__ is not Gather.stage1:
            step()
    kept.wait()
    across.wait()


def gather_weights(subs, shards, rows):
    count = len(shards)
    outs = [
        jax.ShapeDtypeStruct((s.shape[0], 4, 2, 2, s.shape[1], 2 * s.shape[2]), BF16) for s in shards
    ]
    outs.append(jax.ShapeDtypeStruct((2,) + rows.shape, BF16))
    results = pl.pallas_call(
        functools.partial(gather_kernel, subs, count),
        out_shape=outs,
        in_specs=[pl.BlockSpec(memory_space=pltpu.VMEM)] * (count + 1),
        out_specs=[pl.BlockSpec(memory_space=pl.ANY)] * (count + 1),
        scratch_shapes=[
            pltpu.SemaphoreType.DMA((count, 10)),
            pltpu.SemaphoreType.DMA((count, 10)),
            pltpu.SemaphoreType.DMA((count,)),
            pltpu.SemaphoreType.DMA((3,)),
        ],
        compiler_params=pltpu.CompilerParams(
            collective_id=0, has_side_effects=True, vmem_limit_bytes=VMEM_LIMIT
        ),
        name="gather_weights",
    )(*shards, rows)
    fulls = [r.reshape(r.shape[0], GRID * r.shape[4], r.shape[5]) for r in results[:count]]
    return fulls, results[count]


class Scatter:
    def __init__(self, place, part, total, mine, from_core, from_second, from_first, from_z, send, recv, local):
        self.place, self.part, self.total = place, part, total
        self.mine, self.from_core = mine, from_core
        self.from_second, self.from_first, self.from_z = from_second, from_first, from_z
        self.send, self.recv, self.local = send, recv, local
        self.m, self.rows, self.w = total.shape
        self.started = []

    def cols(self, y):
        return pl.ds(pl.multiple_of(y * self.w, LANES), self.w)

    def copy(self, index, src, dst, peer):
        step = remote(src, dst, self.send.at[index], self.recv.at[index], peer)
        step.start()
        self.started.append(step)

    def arrive(self, index, ref):
        remote(ref, ref, self.send.at[index], self.recv.at[index], self.place.sibling()).wait_recv()

    def add(self, target, source):
        m = self.m

        def step(index, carry):
            i, z = index // 4, index % 4
            target[i, z] = (target[i, z].astype(F32) + source[i, z].astype(F32)).astype(BF16)
            return carry

        lax.fori_loop(0, m * 4, step, 0)

    def stage1(self):
        p = self.place
        spots = p.pieces()
        self.kept = []
        for slot, (here, there) in enumerate(((3, 3), (2, 1), (1, 2), (0, 0))):
            x, y = spots[here]
            keep = pltpu.make_async_copy(
                self.part.at[:, :, x, p.c, :, self.cols(y)], self.mine.at[slot], self.local.at[slot]
            )
            keep.start()
            self.kept.append(keep)
            x, y = spots[there]
            self.copy(
                slot,
                self.part.at[:, :, x, 1 - p.c, :, self.cols(y)],
                self.from_core.at[slot],
                p.sibling(),
            )

    def joined(self, slot):
        self.kept[slot].wait()
        self.arrive(slot, self.from_core.at[slot])
        self.add(self.mine.at[slot], self.from_core.at[slot])

    def stage2(self):
        p = self.place
        for slot in (0, 1):
            self.joined(slot)
            self.copy(4 + slot, self.mine.at[slot], self.from_second.at[slot], p.second())
        for slot in (2, 3):
            self.joined(slot)

    def stage3(self):
        p = self.place
        self.arrive(4, self.from_second.at[0])
        self.add(self.mine.at[2], self.from_second.at[0])
        self.copy(6, self.mine.at[2], self.from_first, p.first())
        self.arrive(5, self.from_second.at[1])
        self.add(self.mine.at[3], self.from_second.at[1])

    def stage4(self):
        p = self.place
        self.arrive(6, self.from_first)
        self.add(self.mine.at[3], self.from_first)
        for step in (1, 2, 3):
            self.copy(
                6 + step, self.mine.at[3, :, (p.z + step) % 4], self.from_z.at[step - 1], p.z_peer(step)
            )

    def stage5(self):
        p = self.place
        for step in (1, 2, 3):
            self.arrive(6 + step, self.from_z.at[step - 1])

        def step(i, carry):
            total = self.mine[3, i, p.z].astype(F32)
            for s in range(3):
                total = total + self.from_z[s, i].astype(F32)
            self.total[i] = total
            return carry

        lax.fori_loop(0, self.m, step, 0)
        for step in self.started:
            step.wait_send()

    def stages(self):
        return [self.stage1, self.stage2, self.stage3, self.stage4, self.stage5]


class Sum:
    def __init__(self, place, source, total, box, send, recv):
        self.place, self.source, self.total = place, source, total
        self.box, self.send, self.recv = box, send, recv

    def hop(self, index):
        p = self.place
        flip = p.z + 1 - 2 * (p.z % 2)
        far = (p.z + 2) % 4
        peers = (p.sibling(), p.device(x=1 - p.x), p.device(y=1 - p.y), p.device(z=flip), p.device(z=far))
        if index < 5:
            src = self.source if index == 0 else self.total.at[index - 1]
            step = remote(src, self.box.at[index], self.send.at[index], self.recv.at[index], peers[index])
            step.start()
            self.flying = step

    def land(self, index):
        self.flying.wait()
        src = self.source if index == 0 else self.total.at[index - 1]
        self.total[index] = src[...] + self.box[index]

    def stages(self):
        def first():
            self.hop(0)

        def later(index):
            self.land(index)
            self.hop(index + 1)

        return [first] + [functools.partial(later, i) for i in range(5)]


def scatter_scratch(shape):
    m, rows, w = shape
    return [
        pltpu.VMEM((4, m, 4, rows, w), BF16),
        pltpu.VMEM((4, m, 4, rows, w), BF16),
        pltpu.VMEM((2, m, 4, rows, w), BF16),
        pltpu.VMEM((m, 4, rows, w), BF16),
        pltpu.VMEM((3, m, rows, w), BF16),
        pltpu.SemaphoreType.DMA((10,)),
        pltpu.SemaphoreType.DMA((10,)),
        pltpu.SemaphoreType.DMA((4,)),
    ]


def scatter_kernel(subs, count, *refs):
    parts, small = refs[:count], refs[count]
    totals, small_total = refs[count + 1 : 2 * count + 1], refs[2 * count + 1]
    scratch = refs[2 * count + 2 :]
    place = Place(subs)
    entry_barrier(place)
    movers = [
        Scatter(place, parts[i], totals[i], *scratch[8 * i : 8 * i + 8]) for i in range(count)
    ]
    running, box, send, recv = scratch[8 * count :]
    small_sum = Sum(place, small, running, box, send, recv)
    for mover in movers:
        mover.stage1()
    steps = [s for s in wavefront(movers) if s.__func__ is not Scatter.stage1]
    extra = small_sum.stages()
    for index, step in enumerate(steps):
        if index < len(extra):
            extra[index]()
        step()
    for step in extra[len(steps) :]:
        step()
    small_total[...] = running[4]


def scatter_gradients(subs, parts, small):
    count = len(parts)
    rows = parts[0].shape[1] // GRID
    shaped = [p.reshape(p.shape[0], 4, 2, 2, rows, p.shape[2]) for p in parts]
    shapes = [(p.shape[0], rows, p.shape[2] // 2) for p in parts]
    outs = [jax.ShapeDtypeStruct(s, F32) for s in shapes]
    outs.append(jax.ShapeDtypeStruct(small.shape, F32))
    scratch = []
    for s in shapes:
        scratch += scatter_scratch(s)
    scratch += [
        pltpu.VMEM((5,) + small.shape, F32),
        pltpu.VMEM((5,) + small.shape, F32),
        pltpu.SemaphoreType.DMA((5,)),
        pltpu.SemaphoreType.DMA((5,)),
    ]
    results = pl.pallas_call(
        functools.partial(scatter_kernel, subs, count),
        out_shape=outs,
        in_specs=[pl.BlockSpec(memory_space=pl.ANY)] * count + [pl.BlockSpec(memory_space=pltpu.VMEM)],
        out_specs=[pl.BlockSpec(memory_space=pltpu.VMEM)] * (count + 1),
        scratch_shapes=scratch,
        compiler_params=pltpu.CompilerParams(
            collective_id=1, has_side_effects=True, vmem_limit_bytes=VMEM_LIMIT
        ),
        name="scatter_gradients",
    )(*shaped, small)
    return results[:count], results[count]


def head_lanes(half):
    lane = lax.broadcasted_iota(jnp.int32, (1, LANES), 1)
    return (lane // HEAD) == half


def dot_nt(a, b):
    return lax.dot_general(a, b, (((1,), (1,)), ((), ())), preferred_element_type=F32)


def dot_nn(a, b):
    return lax.dot_general(a, b, (((1,), (0,)), ((), ())), preferred_element_type=F32)


def forward_kernel(qw, qe, keys, values, seg_col, valid_col, ent_col, seg_row, pos_row, ctx, probs, bias):
    length, rows = bias.shape

    @pl.when(pl.program_id(0) == 0)
    def _():
        spot = lax.broadcasted_iota(jnp.int32, (length, rows), 0)
        same = seg_col[...] == seg_row[...]
        seen = (valid_col[...] == 1) | (spot == pos_row[...])
        bias[...] = jnp.where(same & seen, 0.0, NEG)

    queries = jnp.concatenate([qw[...], qe[...]], axis=1)
    key = keys[...]
    ent = ent_col[...] == 1
    zero = jnp.zeros_like(key)
    turned = values[...].T
    for half in range(2):
        lanes = head_lanes(half)
        wide = jnp.concatenate(
            [jnp.where(lanes & ~ent, key, zero), jnp.where(lanes & ent, key, zero)], axis=1
        )
        scores = dot_nt(wide, queries) + bias[...]
        top = jnp.max(scores, axis=0, keepdims=True)
        expo = jnp.exp(scores - top)
        total = jnp.sum(expo, axis=0, keepdims=True)
        prob = (expo * (1.0 / total)).astype(BF16)
        probs[half] = prob
        ctx[half * HEAD : (half + 1) * HEAD, :] = dot_nn(
            turned[half * HEAD : (half + 1) * HEAD, :], prob
        ).astype(BF16)


def attention_forward(qw, qe, keys, values, seg_col, valid_col, ent_col, seg_row, pos_row):
    rows, width = qw.shape
    length = keys.shape[0]
    pairs = width // LANES
    block = lambda n: pl.BlockSpec((n, LANES), lambda i: (0, i))
    whole = lambda a: pl.BlockSpec(a.shape, lambda i: (0,) * a.ndim)
    return pl.pallas_call(
        forward_kernel,
        grid=(pairs,),
        out_shape=[
            jax.ShapeDtypeStruct((width, rows), BF16),
            jax.ShapeDtypeStruct((2 * pairs, length, rows), BF16),
        ],
        in_specs=[block(rows), block(rows), block(length), block(length)]
        + [whole(a) for a in (seg_col, valid_col, ent_col, seg_row, pos_row)],
        out_specs=[
            pl.BlockSpec((LANES, rows), lambda i: (i, 0)),
            pl.BlockSpec((2, length, rows), lambda i: (i, 0, 0)),
        ],
        scratch_shapes=[pltpu.VMEM((length, rows), F32)],
        compiler_params=pltpu.CompilerParams(vmem_limit_bytes=VMEM_LIMIT),
        name="attention_forward",
    )(qw, qe, keys, values, seg_col, valid_col, ent_col, seg_row, pos_row)


def backward_kernel(probs, qw, qe, keys, values, ctx, dctx, ent_col, ent_row, dqw, dqe, dkeys, dvalues):
    queries = jnp.concatenate([qw[...], qe[...]], axis=1)
    value = values[...]
    turned = keys[...].T
    ent = ent_col[...] == 1
    ent_lane = ent_row[...] == 1
    grad = dctx[...]
    zero = jnp.zeros_like(value)
    dk, dv = [], []
    for half in range(2):
        lanes = head_lanes(half)
        here = slice(half * HEAD, (half + 1) * HEAD)
        prob = probs[half]
        delta = jnp.sum(
            ctx[here, :].astype(F32) * grad[here, :].astype(F32), axis=0, keepdims=True
        )
        dprob = dot_nn(jnp.where(lanes, value, zero), grad)
        dscore = (prob.astype(F32) * (dprob - delta)).astype(BF16)
        key_t = turned[here, :]
        none = jnp.zeros_like(key_t)
        tall = jnp.concatenate(
            [jnp.where(ent_lane, none, key_t), jnp.where(ent_lane, key_t, none)], axis=0
        )
        dq = dot_nn(tall, dscore) * (HEAD ** (-0.5))
        dqw[here, :] = dq[:HEAD].astype(BF16)
        dqe[here, :] = dq[HEAD:].astype(BF16)
        both = dot_nn(dscore, queries)
        dk.append(jnp.where(ent, both[:, LANES:], both[:, :LANES]))
        dv.append(dot_nt(prob, grad))
    dkeys[...] = jnp.where(head_lanes(0), dk[0], dk[1]).astype(BF16)
    dvalues[...] = jnp.where(head_lanes(0), dv[0], dv[1]).astype(BF16)


def attention_backward(probs, qw, qe, keys, values, ctx, dctx, ent_col, ent_row):
    rows, width = qw.shape
    length = keys.shape[0]
    pairs = width // LANES
    block = lambda n: pl.BlockSpec((n, LANES), lambda i: (0, i))
    turned = pl.BlockSpec((LANES, rows), lambda i: (i, 0))
    whole = lambda a: pl.BlockSpec(a.shape, lambda i: (0,) * a.ndim)
    return pl.pallas_call(
        backward_kernel,
        grid=(pairs,),
        out_shape=[
            jax.ShapeDtypeStruct((width, rows), BF16),
            jax.ShapeDtypeStruct((width, rows), BF16),
            jax.ShapeDtypeStruct((length, width), BF16),
            jax.ShapeDtypeStruct((length, width), BF16),
        ],
        in_specs=[
            pl.BlockSpec((2, length, rows), lambda i: (i, 0, 0)),
            block(rows),
            block(rows),
            block(length),
            block(length),
            turned,
            turned,
            whole(ent_col),
            whole(ent_row),
        ],
        out_specs=[turned, turned, block(length), block(length)],
        compiler_params=pltpu.CompilerParams(vmem_limit_bytes=VMEM_LIMIT),
        name="attention_backward",
    )(probs, qw, qe, keys, values, ctx, dctx, ent_col, ent_row)


def body(
    layer_input,
    grad_out,
    segment,
    entity,
    valid_mask,
    query_weight,
    key_value_weight,
    attn_bias,
    out_weight,
    out_bias,
    ln_gain,
    ln_bias,
    up_weight,
    ffn_bias,
    down_weight,
):
    rows, width = layer_input.shape
    length = segment.shape[0]
    rank = lax.axis_index("tensor")
    subs = lax.axis_size("dp") // GRID
    start = rank * rows

    shards = [
        query_weight,
        key_value_weight,
        out_weight.T[None],
        up_weight[None],
        down_weight.T[None],
    ]
    groups = [[b * subs + s for s in range(subs)] for b in range(GRID)]
    if subs > 1:
        shards = [
            lax.all_gather(s, "dp", axis=1, tiled=True, axis_index_groups=groups) for s in shards
        ]
    shards = [shards[1], shards[0]] + shards[2:]
    (w_kv, w_q, w_out_t, w_up, w_down_t), both = gather_weights(subs, shards, layer_input)
    w_out_t, w_up, w_down_t = w_out_t[0], w_up[0], w_down_t[0]
    bias_full = lax.all_gather(attn_bias, "tensor", axis=1, tiled=True).astype(F32)
    ffn_bias_full = lax.all_gather(ffn_bias, "tensor", axis=0, tiled=True).astype(F32)
    tokens = both.reshape(length, width)

    ent_own = lax.dynamic_slice_in_dim(entity, start, rows)
    valid_own = lax.dynamic_slice_in_dim(valid_mask, start, rows).astype(F32)[:, None]
    ent_flag = (ent_own == 1)[:, None]
    scale = HEAD ** (-0.5)
    four = jnp.einsum("ld,mde->mle", layer_input, w_q, preferred_element_type=F32)
    four = four + bias_full[:4, None, :]
    query_word = jnp.where(ent_flag, four[2], four[0]).astype(BF16) * BF16(scale)
    query_ent = jnp.where(ent_flag, four[3], four[1]).astype(BF16) * BF16(scale)
    keys = jnp.dot(tokens, w_kv[0], preferred_element_type=F32).astype(BF16)
    values = (jnp.dot(tokens, w_kv[1], preferred_element_type=F32) + bias_full[4]).astype(BF16)

    ent_col = entity[:, None]
    ent_row = entity[None, :]
    seg_row = lax.dynamic_slice_in_dim(segment, start, rows)[None, :]
    pos_row = (start + jnp.arange(rows, dtype=jnp.int32))[None, :]
    context_t, probs = attention_forward(
        query_word, query_ent, keys, values, segment[:, None], valid_mask[:, None], ent_col, seg_row, pos_row
    )

    attn = jnp.einsum("cl,dc->ld", context_t, w_out_t, preferred_element_type=F32)
    attn = attn + out_bias[0].astype(F32)
    resid_one = layer_input.astype(F32) + attn
    hidden, ln_one_pull = jax.vjp(
        layer_norm, resid_one, ln_gain[0].astype(F32), ln_bias[0].astype(F32)
    )
    hidden_low = hidden.astype(BF16)
    pre = jnp.dot(hidden_low, w_up, preferred_element_type=F32) + ffn_bias_full
    active, gelu_pull = jax.vjp(gelu_exact, pre)
    active_low = active.astype(BF16)
    ffn = jnp.einsum("lf,df->ld", active_low, w_down_t, preferred_element_type=F32)
    ffn = ffn + out_bias[1].astype(F32)
    resid_two = hidden + ffn
    result, ln_two_pull = jax.vjp(
        layer_norm, resid_two, ln_gain[1].astype(F32), ln_bias[1].astype(F32)
    )
    output = result.astype(BF16)
    stats = jnp.stack(
        [
            jnp.sum(valid_own * resid_one * resid_one),
            jnp.sum(valid_own * attn * attn),
            jnp.sum(valid_own * ffn * ffn),
            jnp.sum(valid_own * resid_two * resid_two),
            jnp.sum(valid_own),
        ]
    )

    d_two, gain_two, shift_two = ln_two_pull(grad_out.astype(F32))
    d_ffn = d_two.astype(BF16)
    bias_two = jnp.sum(d_ffn.astype(F32), 0)
    d_active = jnp.dot(d_ffn, w_down_t, preferred_element_type=F32)
    (d_pre,) = gelu_pull(d_active)
    d_pre_low = d_pre.astype(BF16)
    down_part = jnp.einsum("ld,lf->df", d_ffn, active_low, preferred_element_type=F32).astype(BF16)
    up_part = jnp.einsum("ld,lf->df", hidden_low, d_pre_low, preferred_element_type=F32).astype(BF16)
    ffn_bias_part = jnp.sum(d_pre_low.astype(F32), 0)
    d_hidden = d_two + jnp.einsum("lf,df->ld", d_pre_low, w_up, preferred_element_type=F32)
    d_one, gain_one, shift_one = ln_one_pull(d_hidden)
    d_attn = d_one.astype(BF16)
    bias_one = jnp.sum(d_attn.astype(F32), 0)
    d_context_t = jnp.einsum("ld,dc->cl", d_attn, w_out_t, preferred_element_type=F32).astype(BF16)
    out_part = jnp.einsum("ld,cl->dc", d_attn, context_t, preferred_element_type=F32).astype(BF16)

    d_word_t, d_ent_t, d_keys_all, d_values_all = attention_backward(
        probs, query_word, query_ent, keys, values, context_t, d_context_t, ent_col, ent_row
    )
    pairs = lax.axis_size("tensor")
    stacked = jnp.stack([d_keys_all, d_values_all]).reshape(2, 2, rows, width)
    mine = lax.dynamic_index_in_dim(stacked, rank, 1, keepdims=False)
    theirs = lax.dynamic_index_in_dim(stacked, 1 - rank, 1, keepdims=False)
    swapped = lax.ppermute(theirs, "tensor", [(i, pairs - 1 - i) for i in range(pairs)])
    d_kv = (mine.astype(F32) + swapped.astype(F32)).astype(BF16)

    ent_lane = (ent_own == 1)[None, :]
    none = jnp.zeros_like(d_word_t)
    d_queries_t = jnp.stack(
        [
            jnp.where(ent_lane, none, d_word_t),
            jnp.where(ent_lane, none, d_ent_t),
            jnp.where(ent_lane, d_word_t, none),
            jnp.where(ent_lane, d_ent_t, none),
        ]
    )
    query_part = jnp.einsum(
        "ld,mel->mde", layer_input, d_queries_t, preferred_element_type=F32
    ).astype(BF16)
    kv_part = jnp.einsum("ld,mle->mde", layer_input, d_kv, preferred_element_type=F32).astype(BF16)
    attn_bias_part = jnp.concatenate(
        [jnp.sum(d_queries_t.astype(F32), 2), jnp.sum(d_kv[1].astype(F32), 0)[None]], 0
    )
    input_grad = (
        d_one
        + jnp.einsum("mel,mde->ld", d_queries_t, w_q, preferred_element_type=F32)
        + jnp.einsum("mle,mde->ld", d_kv, w_kv, preferred_element_type=F32)
    )

    pieces = [
        gain_one,
        gain_two,
        shift_one,
        shift_two,
        bias_one,
        bias_two,
        attn_bias_part.reshape(-1),
        ffn_bias_part,
        stats,
    ]
    flat = jnp.concatenate(pieces)
    padded = -(-flat.shape[0] // (8 * LANES)) * 8 * LANES
    small = jnp.pad(flat, (0, padded - flat.shape[0])).reshape(-1, LANES)
    sums, small_sum = scatter_gradients(
        subs, [down_part[None], up_part[None], out_part[None], query_part, kv_part], small
    )
    if subs > 1:
        sums = [
            lax.psum_scatter(s, "dp", scatter_dimension=1, tiled=True, axis_index_groups=groups)
            for s in sums
        ]
        small_sum = lax.psum(small_sum, "dp", axis_index_groups=groups)
    down_sum, up_sum, out_sum, query_sum, kv_sum = sums
    flat = small_sum.reshape(-1)
    gains = flat[: 2 * width].reshape(2, width)
    shifts = flat[2 * width : 4 * width].reshape(2, width)
    out_biases = flat[4 * width : 6 * width].reshape(2, width)
    attn_biases = flat[6 * width : 11 * width].reshape(5, width)
    units = ffn_bias_full.shape[0]
    ffn_biases = flat[11 * width : 11 * width + units]
    stat_sum = flat[11 * width + units : 11 * width + units + 5]
    cols = attn_bias.shape[1]
    half = ffn_bias.shape[0]
    return (
        output,
        input_grad,
        jnp.sqrt(stat_sum[:4] / (stat_sum[4] * width)),
        query_sum,
        kv_sum,
        lax.dynamic_slice_in_dim(attn_biases, rank * cols, cols, 1),
        out_sum[0].T,
        out_biases,
        gains,
        shifts,
        up_sum[0],
        lax.dynamic_slice_in_dim(ffn_biases, rank * half, half, 0),
        down_sum[0].T,
    )


def solution(mesh):
    placed = (
        P(("dp", "tensor"), None),
        P(("dp", "tensor"), None),
        P("dp"),
        P("dp"),
        P("dp"),
        P(None, "dp", "tensor"),
        P(None, "dp", "tensor"),
        P(None, "tensor"),
        P("tensor", "dp"),
        P(),
        P(),
        P(),
        P("dp", "tensor"),
        P("tensor"),
        P("tensor", "dp"),
    )
    return jax.shard_map(
        body,
        mesh=mesh,
        in_specs=placed,
        out_specs=(
            P(("dp", "tensor"), None),
            P(("dp", "tensor"), None),
            P(),
            P(None, "dp", "tensor"),
            P(None, "dp", "tensor"),
            P(None, "tensor"),
            P("tensor", "dp"),
            P(),
            P(),
            P(),
            P("dp", "tensor"),
            P("tensor"),
            P("tensor", "dp"),
        ),
        check_vma=False,
    )
```

```python
import functools

import jax
import jax.numpy as jnp
from jax import lax
from jax.experimental import pallas as pl
from jax.experimental.pallas import tpu as pltpu
from jax.sharding import PartitionSpec as P

HEAD = 64
EPS = 1e-06
NEG = -1e30
GRID = 16
LANES = 128
MESH = pl.DeviceIdType.MESH
BF16 = jnp.bfloat16
F32 = jnp.float32
VMEM_LIMIT = 60 * 1024 * 1024


def layer_norm(resid, gain, shift):
    center = resid - jnp.mean(resid, -1, keepdims=True)
    spread = jnp.mean(center * center, -1, keepdims=True)
    return center * lax.rsqrt(spread + EPS) * gain + shift


def gelu_exact(values):
    return jax.nn.gelu(values, approximate=False)


class Place:
    def __init__(self, subs):
        rank = lax.axis_index("dp")
        self.subs = subs
        self.sub = rank % subs
        block = rank // subs
        self.z = block // 4
        self.x = (block // 2) % 2
        self.c = block % 2
        self.y = lax.axis_index("tensor")
        self.moved = self.y != self.c
        self.x1 = jnp.where(self.c == 0, 1 - self.x, self.x)
        self.y1 = jnp.where(self.c == 0, self.y, 1 - self.y)
        self.x2 = jnp.where(self.c == 0, self.x, 1 - self.x)
        self.y2 = jnp.where(self.c == 0, 1 - self.y, self.y)

    def device(self, z=None, x=None, c=None, y=None):
        z = self.z if z is None else z
        x = self.x if x is None else x
        c = self.c if c is None else c
        y = self.y if y is None else y
        return (((z * 2 + x) * 2 + c) * self.subs + self.sub, y)

    def z_peer(self, step):
        return self.device(z=(self.z + step) % 4)

    def first(self):
        return self.device(x=self.x1, y=self.y1)

    def second(self):
        return self.device(x=self.x2, y=self.y2)

    def sibling(self):
        return self.device(c=1 - self.c)

    def across(self):
        return self.device(y=1 - self.y)

    def transposed(self):
        return self.device(c=1 - self.c, y=1 - self.y)

    def pieces(self):
        return (
            (self.x, self.y),
            (self.x1, self.y1),
            (self.x2, self.y2),
            (1 - self.x, 1 - self.y),
        )


def entry_barrier(place):
    barrier = pltpu.get_barrier_semaphore()
    peers = [place.z_peer(step) for step in (1, 2, 3)]
    peers += [place.device(x=1 - place.x), place.across(), place.sibling(), place.transposed()]
    for peer in peers:
        pl.semaphore_signal(barrier, inc=1, device_id=peer, device_id_type=MESH)
    pl.semaphore_wait(barrier, len(peers))


def remote(src, dst, send, recv, peer):
    return pltpu.make_async_remote_copy(
        src_ref=src, dst_ref=dst, send_sem=send, recv_sem=recv, device_id=peer, device_id_type=MESH
    )


class Gather:
    def __init__(self, place, shard, full, send, recv, local):
        self.place, self.shard, self.full = place, shard, full
        self.send, self.recv, self.local = send, recv, local
        self.w = shard.shape[-1]
        self.started = []

    def cols(self, y):
        return pl.ds(pl.multiple_of(y * self.w, LANES), self.w)

    def piece(self, spot, c):
        x, y = spot
        return self.full.at[:, :, x, c, :, self.cols(y)]

    def copy(self, index, src, dst, peer):
        step = remote(src, dst, self.send.at[index], self.recv.at[index], peer)
        step.start()
        self.started.append(step)

    def arrive(self, index, ref):
        remote(ref, ref, self.send.at[index], self.recv.at[index], self.place.sibling()).wait_recv()

    def own(self, z):
        p = self.place
        return self.full.at[:, z, p.x, p.c, :, self.cols(p.y)]

    def stage1(self):
        p = self.place
        self.kept = pltpu.make_async_copy(self.shard, self.own(p.z), self.local)
        self.kept.start()
        for step in (1, 2, 3):
            self.copy(step - 1, self.shard, self.own(p.z), p.z_peer(step))

    def stage2(self):
        p = self.place
        self.kept.wait()
        for step in (1, 2, 3):
            self.arrive(step - 1, self.own((p.z + 4 - step) % 4))
        mine = self.piece(p.pieces()[0], p.c)
        self.copy(3, mine, mine, p.first())
        self.copy(4, mine, mine, p.second())
        self.copy(6, mine, mine, p.sibling())

    def stage3(self):
        p = self.place
        got = self.piece(p.pieces()[1], p.c)
        self.arrive(3, got)
        self.copy(5, got, got, p.second())
        self.copy(7, got, got, p.sibling())

    def stage4(self):
        p = self.place
        for index, spot in ((4, 2), (5, 3)):
            got = self.piece(p.pieces()[spot], p.c)
            self.arrive(index, got)
            self.copy(index + 4, got, got, p.sibling())

    def stage5(self):
        p = self.place
        spots = p.pieces()
        for index, spot in ((6, 0), (7, 2), (8, 1), (9, 3)):
            self.arrive(index, self.piece(spots[spot], 1 - p.c))
        for step in self.started:
            step.wait_send()

    def stages(self):
        return [self.stage1, self.stage2, self.stage3, self.stage4, self.stage5]


def wavefront(movers):
    lists = [mover.stages() for mover in movers]
    depth = max(len(stages) for stages in lists)
    order = []
    for time in range(len(lists) + depth - 1):
        for index in range(len(lists)):
            stage = time - index
            if 0 <= stage < len(lists[index]):
                order.append(lists[index][stage])
    return order


class Share:
    def __init__(self, source, pair, index, peer, sems):
        self.kept = pltpu.make_async_copy(source, pair.at[index], sems.at[2])
        self.sent = remote(source, pair.at[index], sems.at[0], sems.at[1], peer)

    def start(self):
        self.kept.start()
        self.sent.start()

    def finish(self):
        self.kept.wait()
        self.sent.wait()


class Rows:
    def __init__(self, place, rows, both, sems):
        p = place
        half = both.at[p.c]
        self.moved = p.moved
        self.kept = pltpu.make_async_copy(rows, half, sems.at[4])
        self.swap = remote(rows, both.at[p.y], sems.at[0], sems.at[1], p.transposed())
        self.swapped = remote(half, half, sems.at[0], sems.at[1], p.transposed())
        self.share = remote(rows, half, sems.at[2], sems.at[3], p.sibling())
        self.relay = remote(half, half, sems.at[2], sems.at[3], p.sibling())
        other = both.at[1 - p.c]
        self.other = remote(other, other, sems.at[2], sems.at[3], p.sibling())

    def start(self):
        @pl.when(self.moved)
        def _():
            self.swap.start()

        @pl.when(jnp.logical_not(self.moved))
        def _():
            self.kept.start()
            self.share.start()

    def forward(self):
        @pl.when(self.moved)
        def _():
            self.swapped.wait_recv()
            self.relay.start()

    def finish(self):
        @pl.when(self.moved)
        def _():
            self.swap.wait_send()
            self.relay.wait_send()

        @pl.when(jnp.logical_not(self.moved))
        def _():
            self.kept.wait()
            self.share.wait_send()

        self.other.wait_recv()


def gather_kernel(subs, count, *refs):
    shards, (rows, bias, facts) = refs[:count], refs[count : count + 3]
    fulls, (both, biases, pair_facts) = refs[count + 3 : 2 * count + 3], refs[2 * count + 3 : 2 * count + 6]
    send, recv, local, row_sems, share_sems = refs[2 * count + 6 :]
    place = Place(subs)
    entry_barrier(place)
    tokens = Rows(place, rows, both, row_sems)
    shares = [
        Share(facts, pair_facts, place.c, place.sibling(), share_sems.at[0]),
        Share(bias, biases, place.y, place.across(), share_sems.at[1]),
    ]
    tokens.start()
    for share in shares:
        share.start()
    movers = [
        Gather(place, shards[i], fulls[i], send.at[i], recv.at[i], local.at[i]) for i in range(count)
    ]
    for mover in movers:
        mover.stage1()
    for index, step in enumerate(wavefront(movers)):
        if step.__func__ is not Gather.stage1:
            step()
        if index == count:
            tokens.forward()
    tokens.finish()
    for share in shares:
        share.finish()


def gather_weights(subs, shards, rows, bias, facts):
    count = len(shards)
    outs = [
        jax.ShapeDtypeStruct((s.shape[0], 4, 2, 2, s.shape[1], 2 * s.shape[2]), BF16) for s in shards
    ]
    outs += [jax.ShapeDtypeStruct((2,) + a.shape, a.dtype) for a in (rows, bias, facts)]
    results = pl.pallas_call(
        functools.partial(gather_kernel, subs, count),
        out_shape=outs,
        in_specs=[pl.BlockSpec(memory_space=pltpu.VMEM)] * (count + 3),
        out_specs=[pl.BlockSpec(memory_space=pl.ANY)] * (count + 3),
        scratch_shapes=[
            pltpu.SemaphoreType.DMA((count, 10)),
            pltpu.SemaphoreType.DMA((count, 10)),
            pltpu.SemaphoreType.DMA((count,)),
            pltpu.SemaphoreType.DMA((5,)),
            pltpu.SemaphoreType.DMA((2, 3)),
        ],
        compiler_params=pltpu.CompilerParams(
            collective_id=0, has_side_effects=True, vmem_limit_bytes=VMEM_LIMIT
        ),
        name="gather_weights",
    )(*shards, rows, bias, facts)
    fulls = [r.reshape(r.shape[0], GRID * r.shape[4], r.shape[5]) for r in results[:count]]
    return fulls, results[count:]


class Scatter:
    def __init__(self, place, part, total, mine, from_core, from_second, from_first, from_z, send, recv, local):
        self.place, self.part, self.total = place, part, total
        self.mine, self.from_core = mine, from_core
        self.from_second, self.from_first, self.from_z = from_second, from_first, from_z
        self.send, self.recv, self.local = send, recv, local
        self.m, self.rows, self.w = total.shape
        self.started = []

    def cols(self, y):
        return pl.ds(pl.multiple_of(y * self.w, LANES), self.w)

    def copy(self, index, src, dst, peer):
        step = remote(src, dst, self.send.at[index], self.recv.at[index], peer)
        step.start()
        self.started.append(step)

    def arrive(self, index, ref):
        remote(ref, ref, self.send.at[index], self.recv.at[index], self.place.sibling()).wait_recv()

    def add(self, target, source):
        m = self.m

        def step(index, carry):
            i, z = index // 4, index % 4
            target[i, z] = (target[i, z].astype(F32) + source[i, z].astype(F32)).astype(BF16)
            return carry

        lax.fori_loop(0, m * 4, step, 0)

    def stage1(self):
        p = self.place
        spots = p.pieces()
        self.kept = []
        for slot, (here, there) in enumerate(((3, 3), (2, 1), (1, 2), (0, 0))):
            x, y = spots[here]
            keep = pltpu.make_async_copy(
                self.part.at[:, :, x, p.c, :, self.cols(y)], self.mine.at[slot], self.local.at[slot]
            )
            keep.start()
            self.kept.append(keep)
            x, y = spots[there]
            self.copy(
                slot,
                self.part.at[:, :, x, 1 - p.c, :, self.cols(y)],
                self.from_core.at[slot],
                p.sibling(),
            )

    def joined(self, slot):
        self.kept[slot].wait()
        self.arrive(slot, self.from_core.at[slot])
        self.add(self.mine.at[slot], self.from_core.at[slot])

    def stage2(self):
        p = self.place
        for slot in (0, 1):
            self.joined(slot)
            self.copy(4 + slot, self.mine.at[slot], self.from_second.at[slot], p.second())
        for slot in (2, 3):
            self.joined(slot)

    def stage3(self):
        p = self.place
        self.arrive(4, self.from_second.at[0])
        self.add(self.mine.at[2], self.from_second.at[0])
        self.copy(6, self.mine.at[2], self.from_first, p.first())
        self.arrive(5, self.from_second.at[1])
        self.add(self.mine.at[3], self.from_second.at[1])

    def stage4(self):
        p = self.place
        self.arrive(6, self.from_first)
        self.add(self.mine.at[3], self.from_first)
        for step in (1, 2, 3):
            self.copy(
                6 + step, self.mine.at[3, :, (p.z + step) % 4], self.from_z.at[step - 1], p.z_peer(step)
            )

    def stage5(self):
        p = self.place
        for step in (1, 2, 3):
            self.arrive(6 + step, self.from_z.at[step - 1])

        def step(i, carry):
            total = self.mine[3, i, p.z].astype(F32)
            for s in range(3):
                total = total + self.from_z[s, i].astype(F32)
            self.total[i] = total
            return carry

        lax.fori_loop(0, self.m, step, 0)
        for step in self.started:
            step.wait_send()

    def stages(self):
        return [self.stage1, self.stage2, self.stage3, self.stage4, self.stage5]


class Sum:
    def __init__(self, place, source, total, box, send, recv):
        self.place, self.source, self.total = place, source, total
        self.box, self.send, self.recv = box, send, recv

    def hop(self, index):
        p = self.place
        flip = p.z + 1 - 2 * (p.z % 2)
        far = (p.z + 2) % 4
        peers = (p.sibling(), p.device(x=1 - p.x), p.device(y=1 - p.y), p.device(z=flip), p.device(z=far))
        if index < 5:
            src = self.source if index == 0 else self.total.at[index - 1]
            step = remote(src, self.box.at[index], self.send.at[index], self.recv.at[index], peers[index])
            step.start()
            self.flying = step

    def land(self, index):
        self.flying.wait()
        src = self.source if index == 0 else self.total.at[index - 1]
        self.total[index] = src[...] + self.box[index]

    def stages(self):
        def first():
            self.hop(0)

        def later(index):
            self.land(index)
            self.hop(index + 1)

        return [first] + [functools.partial(later, i) for i in range(5)]


def scatter_scratch(shape):
    m, rows, w = shape
    return [
        pltpu.VMEM((4, m, 4, rows, w), BF16),
        pltpu.VMEM((4, m, 4, rows, w), BF16),
        pltpu.VMEM((2, m, 4, rows, w), BF16),
        pltpu.VMEM((m, 4, rows, w), BF16),
        pltpu.VMEM((3, m, rows, w), BF16),
        pltpu.SemaphoreType.DMA((10,)),
        pltpu.SemaphoreType.DMA((10,)),
        pltpu.SemaphoreType.DMA((4,)),
    ]


def scatter_kernel(subs, count, *refs):
    parts, small = refs[:count], refs[count]
    totals, small_total = refs[count + 1 : 2 * count + 1], refs[2 * count + 1]
    scratch = refs[2 * count + 2 :]
    place = Place(subs)
    entry_barrier(place)
    movers = [
        Scatter(place, parts[i], totals[i], *scratch[8 * i : 8 * i + 8]) for i in range(count)
    ]
    running, box, send, recv = scratch[8 * count :]
    small_sum = Sum(place, small, running, box, send, recv)
    for mover in movers:
        mover.stage1()
    steps = [s for s in wavefront(movers) if s.__func__ is not Scatter.stage1]
    extra = small_sum.stages()
    for index, step in enumerate(steps):
        if index < len(extra):
            extra[index]()
        step()
    for step in extra[len(steps) :]:
        step()
    small_total[...] = running[4]


def scatter_gradients(subs, parts, small):
    count = len(parts)
    rows = parts[0].shape[1] // GRID
    shaped = [p.reshape(p.shape[0], 4, 2, 2, rows, p.shape[2]) for p in parts]
    shapes = [(p.shape[0], rows, p.shape[2] // 2) for p in parts]
    outs = [jax.ShapeDtypeStruct(s, F32) for s in shapes]
    outs.append(jax.ShapeDtypeStruct(small.shape, F32))
    scratch = []
    for s in shapes:
        scratch += scatter_scratch(s)
    scratch += [
        pltpu.VMEM((5,) + small.shape, F32),
        pltpu.VMEM((5,) + small.shape, F32),
        pltpu.SemaphoreType.DMA((5,)),
        pltpu.SemaphoreType.DMA((5,)),
    ]
    results = pl.pallas_call(
        functools.partial(scatter_kernel, subs, count),
        out_shape=outs,
        in_specs=[pl.BlockSpec(memory_space=pl.ANY)] * count + [pl.BlockSpec(memory_space=pltpu.VMEM)],
        out_specs=[pl.BlockSpec(memory_space=pltpu.VMEM)] * (count + 1),
        scratch_shapes=scratch,
        compiler_params=pltpu.CompilerParams(
            collective_id=1, has_side_effects=True, vmem_limit_bytes=VMEM_LIMIT
        ),
        name="scatter_gradients",
    )(*shaped, small)
    return results[:count], results[count]


def head_lanes(half):
    lane = lax.broadcasted_iota(jnp.int32, (1, LANES), 1)
    return (lane // HEAD) == half


def dot_nt(a, b):
    return lax.dot_general(a, b, (((1,), (1,)), ((), ())), preferred_element_type=F32)


def dot_nn(a, b):
    return lax.dot_general(a, b, (((1,), (0,)), ((), ())), preferred_element_type=F32)


def forward_kernel(qw, qe, keys, values, seg_col, valid_col, ent_col, seg_row, pos_row, ctx, probs, bias):
    length, rows = bias.shape

    @pl.when(pl.program_id(0) == 0)
    def _():
        spot = lax.broadcasted_iota(jnp.int32, (length, rows), 0)
        same = seg_col[...] == seg_row[...]
        seen = (valid_col[...] == 1) | (spot == pos_row[...])
        bias[...] = jnp.where(same & seen, 0.0, NEG)

    queries = jnp.concatenate([qw[...], qe[...]], axis=1)
    key = keys[...]
    ent = ent_col[...] == 1
    zero = jnp.zeros_like(key)
    turned = values[...].T
    for half in range(2):
        lanes = head_lanes(half)
        wide = jnp.concatenate(
            [jnp.where(lanes & ~ent, key, zero), jnp.where(lanes & ent, key, zero)], axis=1
        )
        scores = dot_nt(wide, queries) + bias[...]
        top = jnp.max(scores, axis=0, keepdims=True)
        expo = jnp.exp(scores - top)
        total = jnp.sum(expo, axis=0, keepdims=True)
        prob = (expo * (1.0 / total)).astype(BF16)
        probs[half] = prob
        ctx[half * HEAD : (half + 1) * HEAD, :] = dot_nn(
            turned[half * HEAD : (half + 1) * HEAD, :], prob
        ).astype(BF16)


def attention_forward(qw, qe, keys, values, seg_col, valid_col, ent_col, seg_row, pos_row):
    rows, width = qw.shape
    length = keys.shape[0]
    pairs = width // LANES
    block = lambda n: pl.BlockSpec((n, LANES), lambda i: (0, i))
    whole = lambda a: pl.BlockSpec(a.shape, lambda i: (0,) * a.ndim)
    return pl.pallas_call(
        forward_kernel,
        grid=(pairs,),
        out_shape=[
            jax.ShapeDtypeStruct((width, rows), BF16),
            jax.ShapeDtypeStruct((2 * pairs, length, rows), BF16),
        ],
        in_specs=[block(rows), block(rows), block(length), block(length)]
        + [whole(a) for a in (seg_col, valid_col, ent_col, seg_row, pos_row)],
        out_specs=[
            pl.BlockSpec((LANES, rows), lambda i: (i, 0)),
            pl.BlockSpec((2, length, rows), lambda i: (i, 0, 0)),
        ],
        scratch_shapes=[pltpu.VMEM((length, rows), F32)],
        compiler_params=pltpu.CompilerParams(vmem_limit_bytes=VMEM_LIMIT),
        name="attention_forward",
    )(qw, qe, keys, values, seg_col, valid_col, ent_col, seg_row, pos_row)


def backward_kernel(probs, qw, qe, keys, values, ctx, dctx, ent_col, ent_row, dqw, dqe, dkeys, dvalues):
    queries = jnp.concatenate([qw[...], qe[...]], axis=1)
    value = values[...]
    turned = keys[...].T
    ent = ent_col[...] == 1
    ent_lane = ent_row[...] == 1
    grad = dctx[...]
    zero = jnp.zeros_like(value)
    dk, dv = [], []
    for half in range(2):
        lanes = head_lanes(half)
        here = slice(half * HEAD, (half + 1) * HEAD)
        prob = probs[half]
        delta = jnp.sum(
            ctx[here, :].astype(F32) * grad[here, :].astype(F32), axis=0, keepdims=True
        )
        dprob = dot_nn(jnp.where(lanes, value, zero), grad)
        dscore = (prob.astype(F32) * (dprob - delta)).astype(BF16)
        key_t = turned[here, :]
        none = jnp.zeros_like(key_t)
        tall = jnp.concatenate(
            [jnp.where(ent_lane, none, key_t), jnp.where(ent_lane, key_t, none)], axis=0
        )
        dq = dot_nn(tall, dscore) * (HEAD ** (-0.5))
        dqw[here, :] = dq[:HEAD].astype(BF16)
        dqe[here, :] = dq[HEAD:].astype(BF16)
        both = dot_nn(dscore, queries)
        dk.append(jnp.where(ent, both[:, LANES:], both[:, :LANES]))
        dv.append(dot_nt(prob, grad))
    dkeys[...] = jnp.where(head_lanes(0), dk[0], dk[1]).astype(BF16)
    dvalues[...] = jnp.where(head_lanes(0), dv[0], dv[1]).astype(BF16)


def attention_backward(probs, qw, qe, keys, values, ctx, dctx, ent_col, ent_row):
    rows, width = qw.shape
    length = keys.shape[0]
    pairs = width // LANES
    block = lambda n: pl.BlockSpec((n, LANES), lambda i: (0, i))
    turned = pl.BlockSpec((LANES, rows), lambda i: (i, 0))
    whole = lambda a: pl.BlockSpec(a.shape, lambda i: (0,) * a.ndim)
    return pl.pallas_call(
        backward_kernel,
        grid=(pairs,),
        out_shape=[
            jax.ShapeDtypeStruct((width, rows), BF16),
            jax.ShapeDtypeStruct((width, rows), BF16),
            jax.ShapeDtypeStruct((length, width), BF16),
            jax.ShapeDtypeStruct((length, width), BF16),
        ],
        in_specs=[
            pl.BlockSpec((2, length, rows), lambda i: (i, 0, 0)),
            block(rows),
            block(rows),
            block(length),
            block(length),
            turned,
            turned,
            whole(ent_col),
            whole(ent_row),
        ],
        out_specs=[turned, turned, block(length), block(length)],
        compiler_params=pltpu.CompilerParams(vmem_limit_bytes=VMEM_LIMIT),
        name="attention_backward",
    )(probs, qw, qe, keys, values, ctx, dctx, ent_col, ent_row)


def body(
    layer_input,
    grad_out,
    segment,
    entity,
    valid_mask,
    query_weight,
    key_value_weight,
    attn_bias,
    out_weight,
    out_bias,
    ln_gain,
    ln_bias,
    up_weight,
    ffn_bias,
    down_weight,
):
    rows, width = layer_input.shape
    length = segment.shape[0]
    rank = lax.axis_index("tensor")
    subs = lax.axis_size("dp") // GRID
    core = (lax.axis_index("dp") // subs) % 2
    moved = rank != core
    start = core * rows
    pairs = lax.axis_size("tensor")
    trades = []
    for d in range(lax.axis_size("dp")):
        other = d + subs if (d // subs) % 2 == 0 else d - subs
        y = 1 - (d // subs) % 2
        trades.append((d * pairs + y, other * pairs + 1 - y))
    siblings = [
        (d, d + subs if (d // subs) % 2 == 0 else d - subs) for d in range(lax.axis_size("dp"))
    ]

    def trade(own):
        got = lax.ppermute(own, ("dp", "tensor"), trades)
        return jnp.where(moved, got, own)

    shards = [
        query_weight,
        key_value_weight,
        out_weight.T[None],
        up_weight[None],
        down_weight.T[None],
    ]
    groups = [[b * subs + s for s in range(subs)] for b in range(GRID)]
    if subs > 1:
        shards = [
            lax.all_gather(s, "dp", axis=1, tiled=True, axis_index_groups=groups) for s in shards
        ]
    shards = [shards[1], shards[0]] + shards[2:]
    units = pairs * ffn_bias.shape[0]
    cols = attn_bias.shape[1]
    bias_rows = jnp.concatenate([attn_bias, ffn_bias.reshape(-1, cols)]).astype(F32)
    used = bias_rows.shape[0]
    bias_rows = jnp.pad(bias_rows, ((0, -used % 16), (0, 0)))
    facts = jnp.pad(jnp.stack([segment, entity, valid_mask]), ((0, 5), (0, 0)))
    (w_kv, w_q, w_out_t, w_up, w_down_t), (both, biases, pair_facts) = gather_weights(
        subs, shards, layer_input, bias_rows, facts
    )
    grad_out, both = lax.optimization_barrier((grad_out, both))
    grad_out = trade(grad_out)
    w_out_t, w_up, w_down_t = w_out_t[0], w_up[0], w_down_t[0]
    bias_full = jnp.moveaxis(biases[:, :5], 0, 1).reshape(5, width)
    ffn_bias_full = biases[:, 5:used].reshape(units)
    facts = lax.dynamic_index_in_dim(pair_facts, rank, 0, keepdims=False)
    segment, entity, valid_mask = facts[0], facts[1], facts[2]
    tokens = both.reshape(length, width)
    layer_input = lax.dynamic_index_in_dim(both, core, 0, keepdims=False)

    ent_own = lax.dynamic_slice_in_dim(entity, start, rows)
    valid_own = lax.dynamic_slice_in_dim(valid_mask, start, rows).astype(F32)[:, None]
    ent_flag = (ent_own == 1)[:, None]
    scale = HEAD ** (-0.5)
    four = jnp.einsum("ld,mde->mle", layer_input, w_q, preferred_element_type=F32)
    four = four + bias_full[:4, None, :]
    query_word = jnp.where(ent_flag, four[2], four[0]).astype(BF16) * BF16(scale)
    query_ent = jnp.where(ent_flag, four[3], four[1]).astype(BF16) * BF16(scale)
    keys = jnp.dot(tokens, w_kv[0], preferred_element_type=F32).astype(BF16)
    values = (jnp.dot(tokens, w_kv[1], preferred_element_type=F32) + bias_full[4]).astype(BF16)

    ent_col = entity[:, None]
    ent_row = entity[None, :]
    seg_row = lax.dynamic_slice_in_dim(segment, start, rows)[None, :]
    pos_row = (start + jnp.arange(rows, dtype=jnp.int32))[None, :]
    context_t, probs = attention_forward(
        query_word, query_ent, keys, values, segment[:, None], valid_mask[:, None], ent_col, seg_row, pos_row
    )

    attn = jnp.einsum("cl,dc->ld", context_t, w_out_t, preferred_element_type=F32)
    attn = attn + out_bias[0].astype(F32)
    resid_one = layer_input.astype(F32) + attn
    hidden, ln_one_pull = jax.vjp(
        layer_norm, resid_one, ln_gain[0].astype(F32), ln_bias[0].astype(F32)
    )
    hidden_low = hidden.astype(BF16)
    pre = jnp.dot(hidden_low, w_up, preferred_element_type=F32) + ffn_bias_full
    active, gelu_pull = jax.vjp(gelu_exact, pre)
    active_low = active.astype(BF16)
    ffn = jnp.einsum("lf,df->ld", active_low, w_down_t, preferred_element_type=F32)
    ffn = ffn + out_bias[1].astype(F32)
    resid_two = hidden + ffn
    result, ln_two_pull = jax.vjp(
        layer_norm, resid_two, ln_gain[1].astype(F32), ln_bias[1].astype(F32)
    )
    output = trade(result.astype(BF16))
    stats = jnp.stack(
        [
            jnp.sum(valid_own * resid_one * resid_one),
            jnp.sum(valid_own * attn * attn),
            jnp.sum(valid_own * ffn * ffn),
            jnp.sum(valid_own * resid_two * resid_two),
            jnp.sum(valid_own),
        ]
    )

    d_two, gain_two, shift_two = ln_two_pull(grad_out.astype(F32))
    d_ffn = d_two.astype(BF16)
    bias_two = jnp.sum(d_ffn.astype(F32), 0)
    d_active = jnp.dot(d_ffn, w_down_t, preferred_element_type=F32)
    (d_pre,) = gelu_pull(d_active)
    d_pre_low = d_pre.astype(BF16)
    down_part = jnp.einsum("ld,lf->df", d_ffn, active_low, preferred_element_type=F32).astype(BF16)
    up_part = jnp.einsum("ld,lf->df", hidden_low, d_pre_low, preferred_element_type=F32).astype(BF16)
    ffn_bias_part = jnp.sum(d_pre_low.astype(F32), 0)
    d_hidden = d_two + jnp.einsum("lf,df->ld", d_pre_low, w_up, preferred_element_type=F32)
    d_one, gain_one, shift_one = ln_one_pull(d_hidden)
    d_attn = d_one.astype(BF16)
    bias_one = jnp.sum(d_attn.astype(F32), 0)
    d_context_t = jnp.einsum("ld,dc->cl", d_attn, w_out_t, preferred_element_type=F32).astype(BF16)
    out_part = jnp.einsum("ld,cl->dc", d_attn, context_t, preferred_element_type=F32).astype(BF16)

    d_word_t, d_ent_t, d_keys_all, d_values_all = attention_backward(
        probs, query_word, query_ent, keys, values, context_t, d_context_t, ent_col, ent_row
    )
    stacked = jnp.stack([d_keys_all, d_values_all]).reshape(2, 2, rows, width)
    mine = lax.dynamic_index_in_dim(stacked, core, 1, keepdims=False)
    theirs = lax.dynamic_index_in_dim(stacked, 1 - core, 1, keepdims=False)
    swapped = lax.ppermute(theirs, "dp", siblings)
    d_kv = (mine.astype(F32) + swapped.astype(F32)).astype(BF16)

    ent_lane = (ent_own == 1)[None, :]
    none = jnp.zeros_like(d_word_t)
    d_queries_t = jnp.stack(
        [
            jnp.where(ent_lane, none, d_word_t),
            jnp.where(ent_lane, none, d_ent_t),
            jnp.where(ent_lane, d_word_t, none),
            jnp.where(ent_lane, d_ent_t, none),
        ]
    )
    query_part = jnp.einsum(
        "ld,mel->mde", layer_input, d_queries_t, preferred_element_type=F32
    ).astype(BF16)
    kv_part = jnp.einsum("ld,mle->mde", layer_input, d_kv, preferred_element_type=F32).astype(BF16)
    attn_bias_part = jnp.concatenate(
        [jnp.sum(d_queries_t.astype(F32), 2), jnp.sum(d_kv[1].astype(F32), 0)[None]], 0
    )
    input_grad = (
        d_one
        + jnp.einsum("mel,mde->ld", d_queries_t, w_q, preferred_element_type=F32)
        + jnp.einsum("mle,mde->ld", d_kv, w_kv, preferred_element_type=F32)
    )
    returned = lax.ppermute(input_grad.astype(BF16), ("dp", "tensor"), trades)
    input_grad = jnp.where(moved, returned.astype(F32), input_grad)

    pieces = [
        gain_one,
        gain_two,
        shift_one,
        shift_two,
        bias_one,
        bias_two,
        attn_bias_part.reshape(-1),
        ffn_bias_part,
        stats,
    ]
    flat = jnp.concatenate(pieces)
    padded = -(-flat.shape[0] // (8 * LANES)) * 8 * LANES
    small = jnp.pad(flat, (0, padded - flat.shape[0])).reshape(-1, LANES)
    sums, small_sum = scatter_gradients(
        subs, [down_part[None], up_part[None], out_part[None], query_part, kv_part], small
    )
    if subs > 1:
        sums = [
            lax.psum_scatter(s, "dp", scatter_dimension=1, tiled=True, axis_index_groups=groups)
            for s in sums
        ]
        small_sum = lax.psum(small_sum, "dp", axis_index_groups=groups)
    down_sum, up_sum, out_sum, query_sum, kv_sum = sums
    flat = small_sum.reshape(-1)
    gains = flat[: 2 * width].reshape(2, width)
    shifts = flat[2 * width : 4 * width].reshape(2, width)
    out_biases = flat[4 * width : 6 * width].reshape(2, width)
    attn_biases = flat[6 * width : 11 * width].reshape(5, width)
    ffn_biases = flat[11 * width : 11 * width + units]
    stat_sum = flat[11 * width + units : 11 * width + units + 5]
    half = ffn_bias.shape[0]
    return (
        output,
        input_grad,
        jnp.sqrt(stat_sum[:4] / (stat_sum[4] * width)),
        query_sum,
        kv_sum,
        lax.dynamic_slice_in_dim(attn_biases, rank * cols, cols, 1),
        out_sum[0].T,
        out_biases,
        gains,
        shifts,
        up_sum[0],
        lax.dynamic_slice_in_dim(ffn_biases, rank * half, half, 0),
        down_sum[0].T,
    )


def solution(mesh):
    placed = (
        P(("dp", "tensor"), None),
        P(("dp", "tensor"), None),
        P("dp"),
        P("dp"),
        P("dp"),
        P(None, "dp", "tensor"),
        P(None, "dp", "tensor"),
        P(None, "tensor"),
        P("tensor", "dp"),
        P(),
        P(),
        P(),
        P("dp", "tensor"),
        P("tensor"),
        P("tensor", "dp"),
    )
    return jax.shard_map(
        body,
        mesh=mesh,
        in_specs=placed,
        out_specs=(
            P(("dp", "tensor"), None),
            P(("dp", "tensor"), None),
            P(),
            P(None, "dp", "tensor"),
            P(None, "dp", "tensor"),
            P(None, "tensor"),
            P("tensor", "dp"),
            P(),
            P(),
            P(),
            P("dp", "tensor"),
            P("tensor"),
            P("tensor", "dp"),
        ),
        check_vma=False,
    )
```

```python
import functools

import jax
import jax.numpy as jnp
from jax import lax
from jax.experimental import pallas as pl
from jax.experimental.pallas import tpu as pltpu
from jax.sharding import PartitionSpec as P

HEAD = 64
EPS = 1e-06
NEG = -1e30
GRID = 16
LANES = 128
MESH = pl.DeviceIdType.MESH
BF16 = jnp.bfloat16
F32 = jnp.float32
VMEM_LIMIT = 60 * 1024 * 1024


def layer_norm(resid, gain, shift):
    center = resid - jnp.mean(resid, -1, keepdims=True)
    spread = jnp.mean(center * center, -1, keepdims=True)
    return center * lax.rsqrt(spread + EPS) * gain + shift


def gelu_exact(values):
    return jax.nn.gelu(values, approximate=False)


class Place:
    def __init__(self, subs):
        rank = lax.axis_index("dp")
        self.subs = subs
        self.sub = rank % subs
        block = rank // subs
        self.z = block // 4
        self.x = (block // 2) % 2
        self.c = block % 2
        self.y = lax.axis_index("tensor")
        self.moved = self.y != self.c
        self.x1 = jnp.where(self.c == 0, 1 - self.x, self.x)
        self.y1 = jnp.where(self.c == 0, self.y, 1 - self.y)
        self.x2 = jnp.where(self.c == 0, self.x, 1 - self.x)
        self.y2 = jnp.where(self.c == 0, 1 - self.y, self.y)

    def device(self, z=None, x=None, c=None, y=None):
        z = self.z if z is None else z
        x = self.x if x is None else x
        c = self.c if c is None else c
        y = self.y if y is None else y
        return (((z * 2 + x) * 2 + c) * self.subs + self.sub, y)

    def z_peer(self, step):
        return self.device(z=(self.z + step) % 4)

    def first(self):
        return self.device(x=self.x1, y=self.y1)

    def second(self):
        return self.device(x=self.x2, y=self.y2)

    def sibling(self):
        return self.device(c=1 - self.c)

    def across(self):
        return self.device(y=1 - self.y)

    def transposed(self):
        return self.device(c=1 - self.c, y=1 - self.y)

    def pieces(self):
        return (
            (self.x, self.y),
            (self.x1, self.y1),
            (self.x2, self.y2),
            (1 - self.x, 1 - self.y),
        )


def entry_barrier(place):
    barrier = pltpu.get_barrier_semaphore()
    peers = [place.z_peer(step) for step in (1, 2, 3)]
    peers += [place.device(x=1 - place.x), place.across(), place.sibling(), place.transposed()]
    for peer in peers:
        pl.semaphore_signal(barrier, inc=1, device_id=peer, device_id_type=MESH)
    pl.semaphore_wait(barrier, len(peers))


def remote(src, dst, send, recv, peer):
    return pltpu.make_async_remote_copy(
        src_ref=src, dst_ref=dst, send_sem=send, recv_sem=recv, device_id=peer, device_id_type=MESH
    )


class Gather:
    def __init__(self, place, shard, full, send, recv, local=None, whole=True):
        self.place, self.shard, self.full, self.whole = place, shard, full, whole
        self.send, self.recv, self.local = send, recv, local
        self.w = full.shape[-1] // 2

    def cols(self, y):
        return pl.ds(pl.multiple_of(y * self.w, LANES), self.w)

    def piece(self, spot, c):
        x, y = spot
        return self.full.at[:, :, x, c, :, self.cols(y)]

    def copy(self, index, src, dst, peer):
        remote(src, dst, self.send.at[index], self.recv.at[index], peer).start()

    def arrive(self, index, ref):
        remote(ref, ref, self.send.at[index], self.recv.at[index], self.place.sibling()).wait_recv()

    def gone(self, index, ref):
        remote(ref, ref, self.send.at[index], self.recv.at[index], self.place.sibling()).wait_send()

    def own(self, z):
        p = self.place
        return self.full.at[:, z, p.x, p.c, :, self.cols(p.y)]

    def stage1(self):
        p = self.place
        self.kept = pltpu.make_async_copy(self.shard, self.own(p.z), self.local)
        self.kept.start()
        for step in (1, 2, 3):
            self.copy(step - 1, self.shard, self.own(p.z), p.z_peer(step))

    def land(self):
        p = self.place
        self.kept.wait()
        for step in (1, 2, 3):
            self.arrive(step - 1, self.own((p.z + 4 - step) % 4))

    def settle(self):
        self.land()
        for index in range(3):
            self.gone(index, self.shard)

    def spread(self):
        p = self.place
        mine = self.piece(p.pieces()[0], p.c)
        self.copy(3, mine, mine, p.first())
        self.copy(4, mine, mine, p.second())
        self.copy(6, mine, mine, p.sibling())

    def stage2(self):
        self.land()
        self.spread()

    def stage3(self):
        p = self.place
        got = self.piece(p.pieces()[1], p.c)
        self.arrive(3, got)
        self.copy(5, got, got, p.second())
        self.copy(7, got, got, p.sibling())

    def stage4(self):
        p = self.place
        for index, spot in ((4, 2), (5, 3)):
            got = self.piece(p.pieces()[spot], p.c)
            self.arrive(index, got)
            self.copy(index + 4, got, got, p.sibling())

    def stage5(self):
        p = self.place
        spots = p.pieces()
        for index, spot in ((6, 0), (7, 2), (8, 1), (9, 3)):
            self.arrive(index, self.piece(spots[spot], 1 - p.c))
        for index in range(3, 10):
            self.gone(index, self.piece(spots[0], p.c))

    def last(self):
        self.stage5()
        for index in range(3):
            self.gone(index, self.shard)

    def stages(self):
        if not self.whole:
            return [self.stage1, self.settle]
        return [self.stage1, self.stage2, self.stage3, self.stage4, self.last]


def wavefront(movers):
    lists = [mover.stages() for mover in movers]
    depth = max(len(stages) for stages in lists)
    order = []
    for time in range(len(lists) + depth - 1):
        for index in range(len(lists)):
            stage = time - index
            if 0 <= stage < len(lists[index]):
                order.append(lists[index][stage])
    return order


class Share:
    def __init__(self, source, pair, index, peer, sems):
        self.kept = pltpu.make_async_copy(source, pair.at[index], sems.at[2])
        self.sent = remote(source, pair.at[index], sems.at[0], sems.at[1], peer)

    def start(self):
        self.kept.start()
        self.sent.start()

    def finish(self):
        self.kept.wait()
        self.sent.wait()


class Rows:
    def __init__(self, place, rows, both, sems):
        p = place
        half = both.at[p.c]
        self.moved = p.moved
        self.kept = pltpu.make_async_copy(rows, half, sems.at[4])
        self.swap = remote(rows, both.at[p.y], sems.at[0], sems.at[1], p.transposed())
        self.swapped = remote(half, half, sems.at[0], sems.at[1], p.transposed())
        self.share = remote(rows, half, sems.at[2], sems.at[3], p.sibling())
        self.relay = remote(half, half, sems.at[2], sems.at[3], p.sibling())
        other = both.at[1 - p.c]
        self.other = remote(other, other, sems.at[2], sems.at[3], p.sibling())

    def start(self):
        @pl.when(self.moved)
        def _():
            self.swap.start()

        @pl.when(jnp.logical_not(self.moved))
        def _():
            self.kept.start()
            self.share.start()

    def forward(self):
        @pl.when(self.moved)
        def _():
            self.swapped.wait_recv()
            self.relay.start()

    def finish(self):
        @pl.when(self.moved)
        def _():
            self.swap.wait_send()
            self.relay.wait_send()

        @pl.when(jnp.logical_not(self.moved))
        def _():
            self.kept.wait()
            self.share.wait_send()

        self.other.wait_recv()


def gather_kernel(subs, count, wholes, *refs):
    shards, (rows, bias, facts) = refs[:count], refs[count : count + 3]
    fulls, (both, biases, pair_facts) = refs[count + 3 : 2 * count + 3], refs[2 * count + 3 : 2 * count + 6]
    send, recv, local, row_sems, share_sems = refs[2 * count + 6 :]
    place = Place(subs)
    entry_barrier(place)
    tokens = Rows(place, rows, both, row_sems)
    shares = [
        Share(facts, pair_facts, place.c, place.sibling(), share_sems.at[0]),
        Share(bias, biases, place.y, place.across(), share_sems.at[1]),
    ]
    tokens.start()
    for share in shares:
        share.start()
    movers = [
        Gather(place, shards[i], fulls[i], send.at[i], recv.at[i], local.at[i], i < wholes)
        for i in range(count)
    ]
    for mover in movers:
        mover.stage1()
    for index, step in enumerate(wavefront(movers)):
        if step.__func__ is not Gather.stage1:
            step()
        if index == count:
            tokens.forward()
    tokens.finish()
    for share in shares:
        share.finish()


def gather_weights(subs, shards, wholes, rows, bias, facts):
    count = len(shards)
    outs = [
        jax.ShapeDtypeStruct((s.shape[0], 4, 2, 2, s.shape[1], 2 * s.shape[2]), BF16) for s in shards
    ]
    outs += [jax.ShapeDtypeStruct((2,) + a.shape, a.dtype) for a in (rows, bias, facts)]
    results = pl.pallas_call(
        functools.partial(gather_kernel, subs, count, wholes),
        out_shape=outs,
        in_specs=[pl.BlockSpec(memory_space=pltpu.VMEM)] * (count + 3),
        out_specs=[pl.BlockSpec(memory_space=pl.ANY)] * (count + 3),
        scratch_shapes=[
            pltpu.SemaphoreType.DMA((count, 10)),
            pltpu.SemaphoreType.DMA((count, 10)),
            pltpu.SemaphoreType.DMA((count,)),
            pltpu.SemaphoreType.DMA((5,)),
            pltpu.SemaphoreType.DMA((2, 3)),
        ],
        compiler_params=pltpu.CompilerParams(
            collective_id=0, has_side_effects=True, vmem_limit_bytes=VMEM_LIMIT
        ),
        name="gather_weights",
    )(*shards, rows, bias, facts)
    return results[:count], results[count:]


def as_matrix(full):
    return full.reshape(full.shape[0], GRID * full.shape[4], full.shape[5])


class Scatter:
    def __init__(self, place, part, total, mine, from_core, from_second, from_first, from_z, send, recv, local):
        self.place, self.part, self.total = place, part, total
        self.mine, self.from_core = mine, from_core
        self.from_second, self.from_first, self.from_z = from_second, from_first, from_z
        self.send, self.recv, self.local = send, recv, local
        self.m, self.rows, self.w = total.shape
        self.started = []

    def cols(self, y):
        return pl.ds(pl.multiple_of(y * self.w, LANES), self.w)

    def copy(self, index, src, dst, peer):
        step = remote(src, dst, self.send.at[index], self.recv.at[index], peer)
        step.start()
        self.started.append(step)

    def arrive(self, index, ref):
        remote(ref, ref, self.send.at[index], self.recv.at[index], self.place.sibling()).wait_recv()

    def add(self, target, source):
        m = self.m

        def step(index, carry):
            i, z = index // 4, index % 4
            target[i, z] = (target[i, z].astype(F32) + source[i, z].astype(F32)).astype(BF16)
            return carry

        lax.fori_loop(0, m * 4, step, 0)

    def stage1(self):
        p = self.place
        spots = p.pieces()
        self.kept = []
        for slot, (here, there) in enumerate(((3, 3), (2, 1), (1, 2), (0, 0))):
            x, y = spots[here]
            keep = pltpu.make_async_copy(
                self.part.at[:, :, x, p.c, :, self.cols(y)], self.mine.at[slot], self.local.at[slot]
            )
            keep.start()
            self.kept.append(keep)
            x, y = spots[there]
            self.copy(
                slot,
                self.part.at[:, :, x, 1 - p.c, :, self.cols(y)],
                self.from_core.at[slot],
                p.sibling(),
            )

    def joined(self, slot):
        self.kept[slot].wait()
        self.arrive(slot, self.from_core.at[slot])
        self.add(self.mine.at[slot], self.from_core.at[slot])

    def stage2(self):
        p = self.place
        for slot in (0, 1):
            self.joined(slot)
            self.copy(4 + slot, self.mine.at[slot], self.from_second.at[slot], p.second())
        for slot in (2, 3):
            self.joined(slot)

    def stage3(self):
        p = self.place
        self.arrive(4, self.from_second.at[0])
        self.add(self.mine.at[2], self.from_second.at[0])
        self.copy(6, self.mine.at[2], self.from_first, p.first())
        self.arrive(5, self.from_second.at[1])
        self.add(self.mine.at[3], self.from_second.at[1])

    def stage4(self):
        p = self.place
        self.arrive(6, self.from_first)
        self.add(self.mine.at[3], self.from_first)
        for step in (1, 2, 3):
            self.copy(
                6 + step, self.mine.at[3, :, (p.z + step) % 4], self.from_z.at[step - 1], p.z_peer(step)
            )

    def stage5(self):
        p = self.place
        for step in (1, 2, 3):
            self.arrive(6 + step, self.from_z.at[step - 1])

        def step(i, carry):
            total = self.mine[3, i, p.z].astype(F32)
            for s in range(3):
                total = total + self.from_z[s, i].astype(F32)
            self.total[i] = total
            return carry

        lax.fori_loop(0, self.m, step, 0)
        for step in self.started:
            step.wait_send()

    def stages(self):
        return [self.stage1, self.stage2, self.stage3, self.stage4, self.stage5]


class Sum:
    def __init__(self, place, source, total, box, send, recv):
        self.place, self.source, self.total = place, source, total
        self.box, self.send, self.recv = box, send, recv

    def hop(self, index):
        p = self.place
        flip = p.z + 1 - 2 * (p.z % 2)
        far = (p.z + 2) % 4
        peers = (p.sibling(), p.device(x=1 - p.x), p.device(y=1 - p.y), p.device(z=flip), p.device(z=far))
        if index < 5:
            src = self.source if index == 0 else self.total.at[index - 1]
            step = remote(src, self.box.at[index], self.send.at[index], self.recv.at[index], peers[index])
            step.start()
            self.flying = step

    def land(self, index):
        self.flying.wait()
        src = self.source if index == 0 else self.total.at[index - 1]
        self.total[index] = src[...] + self.box[index]

    def stages(self):
        def first():
            self.hop(0)

        def later(index):
            self.land(index)
            self.hop(index + 1)

        return [first] + [functools.partial(later, i) for i in range(5)]


def scatter_scratch(shape):
    m, rows, w = shape
    return [
        pltpu.VMEM((4, m, 4, rows, w), BF16),
        pltpu.VMEM((4, m, 4, rows, w), BF16),
        pltpu.VMEM((2, m, 4, rows, w), BF16),
        pltpu.VMEM((m, 4, rows, w), BF16),
        pltpu.VMEM((3, m, rows, w), BF16),
        pltpu.SemaphoreType.DMA((10,)),
        pltpu.SemaphoreType.DMA((10,)),
        pltpu.SemaphoreType.DMA((4,)),
    ]


def scatter_kernel(subs, count, *refs):
    parts, small = refs[:count], refs[count]
    totals, small_total = refs[count + 1 : 2 * count + 1], refs[2 * count + 1]
    scratch = refs[2 * count + 2 :]
    place = Place(subs)
    entry_barrier(place)
    movers = [
        Scatter(place, parts[i], totals[i], *scratch[8 * i : 8 * i + 8]) for i in range(count)
    ]
    running, box, send, recv = scratch[8 * count :]
    small_sum = Sum(place, small, running, box, send, recv)
    for mover in movers:
        mover.stage1()
    steps = [s for s in wavefront(movers) if s.__func__ is not Scatter.stage1]
    extra = small_sum.stages()
    for index, step in enumerate(steps):
        if index < len(extra):
            extra[index]()
        step()
    for step in extra[len(steps) :]:
        step()
    small_total[...] = running[4]


def scatter_gradients(subs, parts, small):
    count = len(parts)
    rows = parts[0].shape[1] // GRID
    shaped = [p.reshape(p.shape[0], 4, 2, 2, rows, p.shape[2]) for p in parts]
    shapes = [(p.shape[0], rows, p.shape[2] // 2) for p in parts]
    outs = [jax.ShapeDtypeStruct(s, F32) for s in shapes]
    outs.append(jax.ShapeDtypeStruct(small.shape, F32))
    scratch = []
    for s in shapes:
        scratch += scatter_scratch(s)
    scratch += [
        pltpu.VMEM((5,) + small.shape, F32),
        pltpu.VMEM((5,) + small.shape, F32),
        pltpu.SemaphoreType.DMA((5,)),
        pltpu.SemaphoreType.DMA((5,)),
    ]
    results = pl.pallas_call(
        functools.partial(scatter_kernel, subs, count),
        out_shape=outs,
        in_specs=[pl.BlockSpec(memory_space=pl.ANY)] * count + [pl.BlockSpec(memory_space=pltpu.VMEM)],
        out_specs=[pl.BlockSpec(memory_space=pltpu.VMEM)] * (count + 1),
        scratch_shapes=scratch,
        compiler_params=pltpu.CompilerParams(
            collective_id=1, has_side_effects=True, vmem_limit_bytes=VMEM_LIMIT
        ),
        name="scatter_gradients",
    )(*shaped, small)
    return results[:count], results[count]


def head_lanes(half):
    lane = lax.broadcasted_iota(jnp.int32, (1, LANES), 1)
    return (lane // HEAD) == half


def dot_nt(a, b):
    return lax.dot_general(a, b, (((1,), (1,)), ((), ())), preferred_element_type=F32)


def dot_nn(a, b):
    return lax.dot_general(a, b, (((1,), (0,)), ((), ())), preferred_element_type=F32)


def forward_kernel(
    subs, both, wq, wkv, biases, facts, up_in, down_in,
    ctx, probs, word, entity, keys, values, up, down, mask, column, send, recv,
):
    place = Place(subs)
    step = pl.program_id(0)
    length, rows = mask.shape
    movers = [Gather(place, None, full, send.at[i], recv.at[i]) for i, full in enumerate((up, down))]
    own = pl.ds(pl.multiple_of(place.c * rows, LANES), rows)

    @pl.when(step == 0)
    def _():
        entry_barrier(place)
        for mover in movers:
            mover.spread()
        column[...] = facts[place.y].T
        spot = lax.broadcasted_iota(jnp.int32, (length, rows), 0)
        here = lax.broadcasted_iota(jnp.int32, (length, rows), 1) + place.c * rows
        same = column[:, 0:1] == facts[place.y, 0:1, own]
        seen = (column[:, 2:3] == 1) | (spot == here)
        mask[...] = jnp.where(same & seen, 0.0, NEG)

    @pl.when(step == 3)
    def _():
        movers[0].stage3()

    @pl.when(step == 5)
    def _():
        movers[1].stage3()

    tokens = both[...].reshape(length, both.shape[2])
    mine = both[place.c]
    bias = biases[0]
    row_ent = column[own, 1:2] == 1
    to_word = dot_nn(mine, jnp.concatenate([wq[0], wq[2]], axis=1))
    to_ent = dot_nn(mine, jnp.concatenate([wq[1], wq[3]], axis=1))
    scale = HEAD ** (-0.5)
    query_word = jnp.where(row_ent, to_word[:, LANES:] + bias[2:3], to_word[:, :LANES] + bias[0:1])
    query_ent = jnp.where(row_ent, to_ent[:, LANES:] + bias[3:4], to_ent[:, :LANES] + bias[1:2])
    word[...] = query_word.astype(BF16) * BF16(scale)
    entity[...] = query_ent.astype(BF16) * BF16(scale)
    pair = dot_nn(tokens, jnp.concatenate([wkv[0], wkv[1]], axis=1))
    key = pair[:, :LANES].astype(BF16)
    value = (pair[:, LANES:] + bias[4:5]).astype(BF16)
    keys[...] = key
    values[...] = value

    queries = jnp.concatenate([word[...], entity[...]], axis=1)
    ent = column[:, 1:2] == 1
    zero = jnp.zeros_like(key)
    turned = value.T
    for half in range(2):
        lanes = head_lanes(half)
        wide = jnp.concatenate(
            [jnp.where(lanes & ~ent, key, zero), jnp.where(lanes & ent, key, zero)], axis=1
        )
        scores = dot_nt(wide, queries) + mask[...]
        top = jnp.max(scores, axis=0, keepdims=True)
        expo = jnp.exp(scores - top)
        total = jnp.sum(expo, axis=0, keepdims=True)
        prob = (expo * (1.0 / total)).astype(BF16)
        probs[half] = prob
        ctx[half * HEAD : (half + 1) * HEAD, :] = dot_nn(
            turned[half * HEAD : (half + 1) * HEAD, :], prob
        ).astype(BF16)

    @pl.when(step == pl.num_programs(0) - 1)
    def _():
        for mover in movers:
            mover.stage4()
        for mover in movers:
            mover.stage5()


def attention_forward(subs, both, wq, wkv, biases, facts, up, down):
    _, rows, width = both.shape
    length = 2 * rows
    pairs = width // LANES
    span = biases.shape[2] // LANES
    block = lambda n: pl.BlockSpec((n, LANES), lambda i: (0, i))
    whole = lambda a: pl.BlockSpec(a.shape, lambda i: (0,) * a.ndim, pipeline_mode=pl.Buffered(1))
    cols = lambda a: pl.BlockSpec(a.shape[:2] + (LANES,), lambda i: (0, 0, i))
    anywhere = pl.BlockSpec(memory_space=pl.ANY)
    return pl.pallas_call(
        functools.partial(forward_kernel, subs),
        grid=(pairs,),
        out_shape=[
            jax.ShapeDtypeStruct((width, rows), BF16),
            jax.ShapeDtypeStruct((2 * pairs, length, rows), BF16),
            jax.ShapeDtypeStruct((rows, width), BF16),
            jax.ShapeDtypeStruct((rows, width), BF16),
            jax.ShapeDtypeStruct((length, width), BF16),
            jax.ShapeDtypeStruct((length, width), BF16),
            jax.ShapeDtypeStruct(up.shape, BF16),
            jax.ShapeDtypeStruct(down.shape, BF16),
        ],
        in_specs=[
            whole(both),
            cols(wq),
            cols(wkv),
            pl.BlockSpec((1, biases.shape[1], LANES), lambda i: (i // span, 0, i % span)),
            whole(facts),
            anywhere,
            anywhere,
        ],
        out_specs=[
            pl.BlockSpec((LANES, rows), lambda i: (i, 0)),
            pl.BlockSpec((2, length, rows), lambda i: (i, 0, 0)),
            block(rows),
            block(rows),
            block(length),
            block(length),
            anywhere,
            anywhere,
        ],
        scratch_shapes=[
            pltpu.VMEM((length, rows), F32),
            pltpu.VMEM((length, facts.shape[1]), jnp.int32),
            pltpu.SemaphoreType.DMA((2, 10)),
            pltpu.SemaphoreType.DMA((2, 10)),
        ],
        input_output_aliases={5: 6, 6: 7},
        compiler_params=pltpu.CompilerParams(
            collective_id=2, has_side_effects=True, vmem_limit_bytes=VMEM_LIMIT
        ),
        name="attention_forward",
    )(both, wq, wkv, biases, facts, up, down)


def backward_kernel(probs, qw, qe, keys, values, ctx, dctx, ent_col, ent_row, dqw, dqe, dkeys, dvalues):
    queries = jnp.concatenate([qw[...], qe[...]], axis=1)
    value = values[...]
    turned = keys[...].T
    ent = ent_col[...] == 1
    ent_lane = ent_row[...] == 1
    grad = dctx[...]
    zero = jnp.zeros_like(value)
    dk, dv = [], []
    for half in range(2):
        lanes = head_lanes(half)
        here = slice(half * HEAD, (half + 1) * HEAD)
        prob = probs[half]
        delta = jnp.sum(
            ctx[here, :].astype(F32) * grad[here, :].astype(F32), axis=0, keepdims=True
        )
        dprob = dot_nn(jnp.where(lanes, value, zero), grad)
        dscore = (prob.astype(F32) * (dprob - delta)).astype(BF16)
        key_t = turned[here, :]
        none = jnp.zeros_like(key_t)
        tall = jnp.concatenate(
            [jnp.where(ent_lane, none, key_t), jnp.where(ent_lane, key_t, none)], axis=0
        )
        dq = dot_nn(tall, dscore) * (HEAD ** (-0.5))
        dqw[here, :] = dq[:HEAD].astype(BF16)
        dqe[here, :] = dq[HEAD:].astype(BF16)
        both = dot_nn(dscore, queries)
        dk.append(jnp.where(ent, both[:, LANES:], both[:, :LANES]))
        dv.append(dot_nt(prob, grad))
    dkeys[...] = jnp.where(head_lanes(0), dk[0], dk[1]).astype(BF16)
    dvalues[...] = jnp.where(head_lanes(0), dv[0], dv[1]).astype(BF16)


def attention_backward(probs, qw, qe, keys, values, ctx, dctx, ent_col, ent_row):
    rows, width = qw.shape
    length = keys.shape[0]
    pairs = width // LANES
    block = lambda n: pl.BlockSpec((n, LANES), lambda i: (0, i))
    turned = pl.BlockSpec((LANES, rows), lambda i: (i, 0))
    whole = lambda a: pl.BlockSpec(a.shape, lambda i: (0,) * a.ndim)
    return pl.pallas_call(
        backward_kernel,
        grid=(pairs,),
        out_shape=[
            jax.ShapeDtypeStruct((width, rows), BF16),
            jax.ShapeDtypeStruct((width, rows), BF16),
            jax.ShapeDtypeStruct((length, width), BF16),
            jax.ShapeDtypeStruct((length, width), BF16),
        ],
        in_specs=[
            pl.BlockSpec((2, length, rows), lambda i: (i, 0, 0)),
            block(rows),
            block(rows),
            block(length),
            block(length),
            turned,
            turned,
            whole(ent_col),
            whole(ent_row),
        ],
        out_specs=[turned, turned, block(length), block(length)],
        compiler_params=pltpu.CompilerParams(vmem_limit_bytes=VMEM_LIMIT),
        name="attention_backward",
    )(probs, qw, qe, keys, values, ctx, dctx, ent_col, ent_row)


def body(
    layer_input,
    grad_out,
    segment,
    entity,
    valid_mask,
    query_weight,
    key_value_weight,
    attn_bias,
    out_weight,
    out_bias,
    ln_gain,
    ln_bias,
    up_weight,
    ffn_bias,
    down_weight,
):
    rows, width = layer_input.shape
    length = segment.shape[0]
    rank = lax.axis_index("tensor")
    subs = lax.axis_size("dp") // GRID
    core = (lax.axis_index("dp") // subs) % 2
    moved = rank != core
    start = core * rows
    pairs = lax.axis_size("tensor")
    trades = []
    for d in range(lax.axis_size("dp")):
        other = d + subs if (d // subs) % 2 == 0 else d - subs
        y = 1 - (d // subs) % 2
        trades.append((d * pairs + y, other * pairs + 1 - y))
    siblings = [
        (d, d + subs if (d // subs) % 2 == 0 else d - subs) for d in range(lax.axis_size("dp"))
    ]

    def trade(own):
        got = lax.ppermute(own, ("dp", "tensor"), trades)
        return jnp.where(moved, got, own)

    shards = [
        query_weight,
        key_value_weight,
        out_weight.T[None],
        up_weight[None],
        down_weight.T[None],
    ]
    groups = [[b * subs + s for s in range(subs)] for b in range(GRID)]
    if subs > 1:
        shards = [
            lax.all_gather(s, "dp", axis=1, tiled=True, axis_index_groups=groups) for s in shards
        ]
    shards = [shards[1], shards[0]] + shards[2:]
    units = pairs * ffn_bias.shape[0]
    cols = attn_bias.shape[1]
    bias_rows = jnp.concatenate([attn_bias, ffn_bias.reshape(-1, cols)]).astype(F32)
    used = bias_rows.shape[0]
    bias_rows = jnp.pad(bias_rows, ((0, -used % 16), (0, 0)))
    facts = jnp.pad(jnp.stack([segment, entity, valid_mask]), ((0, 5), (0, 0)))
    (w_kv, w_q, w_out_t, w_up, w_down_t), (both, biases, pair_facts) = gather_weights(
        subs, shards, 3, layer_input, bias_rows, facts
    )
    w_kv, w_q, w_out_t = as_matrix(w_kv), as_matrix(w_q), as_matrix(w_out_t)[0]
    grad_out, both = lax.optimization_barrier((grad_out, both))
    grad_out = trade(grad_out)
    context_t, probs, query_word, query_ent, keys, values, w_up, w_down_t = attention_forward(
        subs, both, w_q, w_kv, biases, pair_facts, w_up, w_down_t
    )
    w_up, w_down_t = as_matrix(w_up)[0], as_matrix(w_down_t)[0]
    ffn_bias_full = biases[:, 5:used].reshape(units)
    facts = lax.dynamic_index_in_dim(pair_facts, rank, 0, keepdims=False)
    segment, entity, valid_mask = facts[0], facts[1], facts[2]
    layer_input = lax.dynamic_index_in_dim(both, core, 0, keepdims=False)

    ent_own = lax.dynamic_slice_in_dim(entity, start, rows)
    valid_own = lax.dynamic_slice_in_dim(valid_mask, start, rows).astype(F32)[:, None]
    ent_col = entity[:, None]
    ent_row = entity[None, :]

    attn = jnp.einsum("cl,dc->ld", context_t, w_out_t, preferred_element_type=F32)
    attn = attn + out_bias[0].astype(F32)
    resid_one = layer_input.astype(F32) + attn
    hidden, ln_one_pull = jax.vjp(
        layer_norm, resid_one, ln_gain[0].astype(F32), ln_bias[0].astype(F32)
    )
    hidden_low = hidden.astype(BF16)
    pre = jnp.dot(hidden_low, w_up, preferred_element_type=F32) + ffn_bias_full
    active, gelu_pull = jax.vjp(gelu_exact, pre)
    active_low = active.astype(BF16)
    ffn = jnp.einsum("lf,df->ld", active_low, w_down_t, preferred_element_type=F32)
    ffn = ffn + out_bias[1].astype(F32)
    resid_two = hidden + ffn
    result, ln_two_pull = jax.vjp(
        layer_norm, resid_two, ln_gain[1].astype(F32), ln_bias[1].astype(F32)
    )
    output = trade(result.astype(BF16))
    stats = jnp.stack(
        [
            jnp.sum(valid_own * resid_one * resid_one),
            jnp.sum(valid_own * attn * attn),
            jnp.sum(valid_own * ffn * ffn),
            jnp.sum(valid_own * resid_two * resid_two),
            jnp.sum(valid_own),
        ]
    )

    d_two, gain_two, shift_two = ln_two_pull(grad_out.astype(F32))
    d_ffn = d_two.astype(BF16)
    bias_two = jnp.sum(d_ffn.astype(F32), 0)
    d_active = jnp.dot(d_ffn, w_down_t, preferred_element_type=F32)
    (d_pre,) = gelu_pull(d_active)
    d_pre_low = d_pre.astype(BF16)
    down_part = jnp.einsum("ld,lf->df", d_ffn, active_low, preferred_element_type=F32).astype(BF16)
    up_part = jnp.einsum("ld,lf->df", hidden_low, d_pre_low, preferred_element_type=F32).astype(BF16)
    ffn_bias_part = jnp.sum(d_pre_low.astype(F32), 0)
    d_hidden = d_two + jnp.einsum("lf,df->ld", d_pre_low, w_up, preferred_element_type=F32)
    d_one, gain_one, shift_one = ln_one_pull(d_hidden)
    d_attn = d_one.astype(BF16)
    bias_one = jnp.sum(d_attn.astype(F32), 0)
    d_context_t = jnp.einsum("ld,dc->cl", d_attn, w_out_t, preferred_element_type=F32).astype(BF16)
    out_part = jnp.einsum("ld,cl->dc", d_attn, context_t, preferred_element_type=F32).astype(BF16)

    d_word_t, d_ent_t, d_keys_all, d_values_all = attention_backward(
        probs, query_word, query_ent, keys, values, context_t, d_context_t, ent_col, ent_row
    )
    stacked = jnp.stack([d_keys_all, d_values_all]).reshape(2, 2, rows, width)
    mine = lax.dynamic_index_in_dim(stacked, core, 1, keepdims=False)
    theirs = lax.dynamic_index_in_dim(stacked, 1 - core, 1, keepdims=False)
    swapped = lax.ppermute(theirs, "dp", siblings)
    d_kv = (mine.astype(F32) + swapped.astype(F32)).astype(BF16)

    ent_lane = (ent_own == 1)[None, :]
    none = jnp.zeros_like(d_word_t)
    d_queries_t = jnp.stack(
        [
            jnp.where(ent_lane, none, d_word_t),
            jnp.where(ent_lane, none, d_ent_t),
            jnp.where(ent_lane, d_word_t, none),
            jnp.where(ent_lane, d_ent_t, none),
        ]
    )
    query_part = jnp.einsum(
        "ld,mel->mde", layer_input, d_queries_t, preferred_element_type=F32
    ).astype(BF16)
    kv_part = jnp.einsum("ld,mle->mde", layer_input, d_kv, preferred_element_type=F32).astype(BF16)
    attn_bias_part = jnp.concatenate(
        [jnp.sum(d_queries_t.astype(F32), 2), jnp.sum(d_kv[1].astype(F32), 0)[None]], 0
    )
    input_grad = (
        d_one
        + jnp.einsum("mel,mde->ld", d_queries_t, w_q, preferred_element_type=F32)
        + jnp.einsum("mle,mde->ld", d_kv, w_kv, preferred_element_type=F32)
    )
    returned = lax.ppermute(input_grad.astype(BF16), ("dp", "tensor"), trades)
    input_grad = jnp.where(moved, returned.astype(F32), input_grad)

    pieces = [
        gain_one,
        gain_two,
        shift_one,
        shift_two,
        bias_one,
        bias_two,
        attn_bias_part.reshape(-1),
        ffn_bias_part,
        stats,
    ]
    flat = jnp.concatenate(pieces)
    padded = -(-flat.shape[0] // (8 * LANES)) * 8 * LANES
    small = jnp.pad(flat, (0, padded - flat.shape[0])).reshape(-1, LANES)
    sums, small_sum = scatter_gradients(
        subs, [down_part[None], up_part[None], out_part[None], query_part, kv_part], small
    )
    if subs > 1:
        sums = [
            lax.psum_scatter(s, "dp", scatter_dimension=1, tiled=True, axis_index_groups=groups)
            for s in sums
        ]
        small_sum = lax.psum(small_sum, "dp", axis_index_groups=groups)
    down_sum, up_sum, out_sum, query_sum, kv_sum = sums
    flat = small_sum.reshape(-1)
    gains = flat[: 2 * width].reshape(2, width)
    shifts = flat[2 * width : 4 * width].reshape(2, width)
    out_biases = flat[4 * width : 6 * width].reshape(2, width)
    attn_biases = flat[6 * width : 11 * width].reshape(5, width)
    ffn_biases = flat[11 * width : 11 * width + units]
    stat_sum = flat[11 * width + units : 11 * width + units + 5]
    half = ffn_bias.shape[0]
    return (
        output,
        input_grad,
        jnp.sqrt(stat_sum[:4] / (stat_sum[4] * width)),
        query_sum,
        kv_sum,
        lax.dynamic_slice_in_dim(attn_biases, rank * cols, cols, 1),
        out_sum[0].T,
        out_biases,
        gains,
        shifts,
        up_sum[0],
        lax.dynamic_slice_in_dim(ffn_biases, rank * half, half, 0),
        down_sum[0].T,
    )


def solution(mesh):
    placed = (
        P(("dp", "tensor"), None),
        P(("dp", "tensor"), None),
        P("dp"),
        P("dp"),
        P("dp"),
        P(None, "dp", "tensor"),
        P(None, "dp", "tensor"),
        P(None, "tensor"),
        P("tensor", "dp"),
        P(),
        P(),
        P(),
        P("dp", "tensor"),
        P("tensor"),
        P("tensor", "dp"),
    )
    return jax.shard_map(
        body,
        mesh=mesh,
        in_specs=placed,
        out_specs=(
            P(("dp", "tensor"), None),
            P(("dp", "tensor"), None),
            P(),
            P(None, "dp", "tensor"),
            P(None, "dp", "tensor"),
            P(None, "tensor"),
            P("tensor", "dp"),
            P(),
            P(),
            P(),
            P("dp", "tensor"),
            P("tensor"),
            P("tensor", "dp"),
        ),
        check_vma=False,
    )
```

```python
import functools

import jax
import jax.numpy as jnp
from jax import lax
from jax.experimental import pallas as pl
from jax.experimental.pallas import tpu as pltpu
from jax.sharding import PartitionSpec as P

HEAD = 64
EPS = 1e-06
NEG = -1e30
GRID = 16
LANES = 128
MESH = pl.DeviceIdType.MESH
BF16 = jnp.bfloat16
F32 = jnp.float32
VMEM_LIMIT = 60 * 1024 * 1024


BLOCK = 512
TAIL = 0.34
TAIL_Q = (
    0.1918165616711201,
    0.1920366827922902,
    0.17827181747742213,
    0.1748548010854969,
    0.05944614604180367,
    0.27541659722682194,
    -0.27820700083503797,
    0.4016320911891782,
    -0.24597742961536673,
    0.050709736470982834,
)


def gelu_pair(v):
    size = jnp.abs(v)
    t = 1.0 / (1.0 + (TAIL * 0.5**0.5) * size)
    q = jnp.full_like(v, TAIL_Q[-1])
    for coefficient in TAIL_Q[-2::-1]:
        q = q * t + coefficient
    bell = jnp.exp(-0.5 * (v * v))
    tail = 0.5 * (bell * (t * q))
    cdf = jnp.where(v < 0, tail, 1.0 - tail)
    return v * cdf, cdf + v * (bell * 0.3989422804014327)


def normalize(resid):
    center = resid - jnp.mean(resid, -1, keepdims=True)
    inverse = lax.rsqrt(jnp.mean(center * center, -1, keepdims=True) + EPS)
    return center * inverse, inverse


def norm_backward(grad, normal, inverse, gain):
    scaled = grad * gain
    return inverse * (
        scaled
        - jnp.mean(scaled, -1, keepdims=True)
        - normal * jnp.mean(scaled * normal, -1, keepdims=True)
    )


def column_sum(a):
    return jnp.sum(a, 0, keepdims=True)


class Place:
    def __init__(self, subs):
        rank = lax.axis_index("dp")
        self.subs = subs
        self.sub = rank % subs
        block = rank // subs
        self.z = block // 4
        self.x = (block // 2) % 2
        self.c = block % 2
        self.y = lax.axis_index("tensor")
        self.moved = self.y != self.c
        self.x1 = jnp.where(self.c == 0, 1 - self.x, self.x)
        self.y1 = jnp.where(self.c == 0, self.y, 1 - self.y)
        self.x2 = jnp.where(self.c == 0, self.x, 1 - self.x)
        self.y2 = jnp.where(self.c == 0, 1 - self.y, self.y)

    def device(self, z=None, x=None, c=None, y=None):
        z = self.z if z is None else z
        x = self.x if x is None else x
        c = self.c if c is None else c
        y = self.y if y is None else y
        return (((z * 2 + x) * 2 + c) * self.subs + self.sub, y)

    def z_peer(self, step):
        return self.device(z=(self.z + step) % 4)

    def first(self):
        return self.device(x=self.x1, y=self.y1)

    def second(self):
        return self.device(x=self.x2, y=self.y2)

    def sibling(self):
        return self.device(c=1 - self.c)

    def across(self):
        return self.device(y=1 - self.y)

    def transposed(self):
        return self.device(c=1 - self.c, y=1 - self.y)

    def pieces(self):
        return (
            (self.x, self.y),
            (self.x1, self.y1),
            (self.x2, self.y2),
            (1 - self.x, 1 - self.y),
        )


def entry_barrier(place):
    barrier = pltpu.get_barrier_semaphore()
    peers = [place.z_peer(step) for step in (1, 2, 3)]
    peers += [place.device(x=1 - place.x), place.across(), place.sibling(), place.transposed()]
    for peer in peers:
        pl.semaphore_signal(barrier, inc=1, device_id=peer, device_id_type=MESH)
    pl.semaphore_wait(barrier, len(peers))


def remote(src, dst, send, recv, peer):
    return pltpu.make_async_remote_copy(
        src_ref=src, dst_ref=dst, send_sem=send, recv_sem=recv, device_id=peer, device_id_type=MESH
    )


class Gather:
    def __init__(self, place, shard, full, send, recv, local=None, whole=True):
        self.place, self.shard, self.full, self.whole = place, shard, full, whole
        self.send, self.recv, self.local = send, recv, local
        self.w = full.shape[-1] // 2

    def cols(self, y):
        return pl.ds(pl.multiple_of(y * self.w, LANES), self.w)

    def piece(self, spot, c):
        x, y = spot
        return self.full.at[:, :, x, c, :, self.cols(y)]

    def copy(self, index, src, dst, peer):
        remote(src, dst, self.send.at[index], self.recv.at[index], peer).start()

    def arrive(self, index, ref):
        remote(ref, ref, self.send.at[index], self.recv.at[index], self.place.sibling()).wait_recv()

    def gone(self, index, ref):
        remote(ref, ref, self.send.at[index], self.recv.at[index], self.place.sibling()).wait_send()

    def own(self, z):
        p = self.place
        return self.full.at[:, z, p.x, p.c, :, self.cols(p.y)]

    def stage1(self):
        p = self.place
        self.kept = pltpu.make_async_copy(self.shard, self.own(p.z), self.local)
        self.kept.start()
        for step in (1, 2, 3):
            self.copy(step - 1, self.shard, self.own(p.z), p.z_peer(step))

    def land(self):
        p = self.place
        self.kept.wait()
        for step in (1, 2, 3):
            self.arrive(step - 1, self.own((p.z + 4 - step) % 4))

    def settle(self):
        self.land()
        for index in range(3):
            self.gone(index, self.shard)

    def spread(self):
        p = self.place
        mine = self.piece(p.pieces()[0], p.c)
        self.copy(3, mine, mine, p.first())
        self.copy(4, mine, mine, p.second())
        self.copy(6, mine, mine, p.sibling())

    def stage2(self):
        self.land()
        self.spread()

    def stage3(self):
        p = self.place
        got = self.piece(p.pieces()[1], p.c)
        self.arrive(3, got)
        self.copy(5, got, got, p.second())
        self.copy(7, got, got, p.sibling())

    def stage4(self):
        p = self.place
        for index, spot in ((4, 2), (5, 3)):
            got = self.piece(p.pieces()[spot], p.c)
            self.arrive(index, got)
            self.copy(index + 4, got, got, p.sibling())

    def stage5(self):
        p = self.place
        spots = p.pieces()
        for index, spot in ((6, 0), (7, 2), (8, 1), (9, 3)):
            self.arrive(index, self.piece(spots[spot], 1 - p.c))
        for index in range(3, 10):
            self.gone(index, self.piece(spots[0], p.c))

    def last(self):
        self.stage5()
        for index in range(3):
            self.gone(index, self.shard)

    def stages(self):
        if not self.whole:
            return [self.stage1, self.settle]
        return [self.stage1, self.stage2, self.stage3, self.stage4, self.last]


def wavefront(movers):
    lists = [mover.stages() for mover in movers]
    depth = max(len(stages) for stages in lists)
    order = []
    for time in range(len(lists) + depth - 1):
        for index in range(len(lists)):
            stage = time - index
            if 0 <= stage < len(lists[index]):
                order.append(lists[index][stage])
    return order


class Share:
    def __init__(self, source, pair, index, peer, sems):
        self.kept = pltpu.make_async_copy(source, pair.at[index], sems.at[2])
        self.sent = remote(source, pair.at[index], sems.at[0], sems.at[1], peer)

    def start(self):
        self.kept.start()
        self.sent.start()

    def finish(self):
        self.kept.wait()
        self.sent.wait()


class Rows:
    def __init__(self, place, rows, both, sems):
        p = place
        half = both.at[p.c]
        self.moved = p.moved
        self.kept = pltpu.make_async_copy(rows, half, sems.at[4])
        self.swap = remote(rows, both.at[p.y], sems.at[0], sems.at[1], p.transposed())
        self.swapped = remote(half, half, sems.at[0], sems.at[1], p.transposed())
        self.share = remote(rows, half, sems.at[2], sems.at[3], p.sibling())
        self.relay = remote(half, half, sems.at[2], sems.at[3], p.sibling())
        other = both.at[1 - p.c]
        self.other = remote(other, other, sems.at[2], sems.at[3], p.sibling())

    def start(self):
        @pl.when(self.moved)
        def _():
            self.swap.start()

        @pl.when(jnp.logical_not(self.moved))
        def _():
            self.kept.start()
            self.share.start()

    def forward(self):
        @pl.when(self.moved)
        def _():
            self.swapped.wait_recv()
            self.relay.start()

    def finish(self):
        @pl.when(self.moved)
        def _():
            self.swap.wait_send()
            self.relay.wait_send()

        @pl.when(jnp.logical_not(self.moved))
        def _():
            self.kept.wait()
            self.share.wait_send()

        self.other.wait_recv()


def gather_kernel(subs, count, wholes, *refs):
    shards, (rows, bias, facts) = refs[:count], refs[count : count + 3]
    fulls, (both, biases, pair_facts) = refs[count + 3 : 2 * count + 3], refs[2 * count + 3 : 2 * count + 6]
    send, recv, local, row_sems, share_sems = refs[2 * count + 6 :]
    place = Place(subs)
    entry_barrier(place)
    tokens = Rows(place, rows, both, row_sems)
    shares = [
        Share(facts, pair_facts, place.c, place.sibling(), share_sems.at[0]),
        Share(bias, biases, place.y, place.across(), share_sems.at[1]),
    ]
    tokens.start()
    for share in shares:
        share.start()
    movers = [
        Gather(place, shards[i], fulls[i], send.at[i], recv.at[i], local.at[i], i < wholes)
        for i in range(count)
    ]
    for mover in movers:
        mover.stage1()
    for index, step in enumerate(wavefront(movers)):
        if step.__func__ is not Gather.stage1:
            step()
        if index == count:
            tokens.forward()
    tokens.finish()
    for share in shares:
        share.finish()


def gather_weights(subs, shards, wholes, rows, bias, facts):
    count = len(shards)
    outs = [
        jax.ShapeDtypeStruct((s.shape[0], 4, 2, 2, s.shape[1], 2 * s.shape[2]), BF16) for s in shards
    ]
    outs += [jax.ShapeDtypeStruct((2,) + a.shape, a.dtype) for a in (rows, bias, facts)]
    results = pl.pallas_call(
        functools.partial(gather_kernel, subs, count, wholes),
        out_shape=outs,
        in_specs=[pl.BlockSpec(memory_space=pltpu.VMEM)] * (count + 3),
        out_specs=[pl.BlockSpec(memory_space=pl.ANY)] * (count + 3),
        scratch_shapes=[
            pltpu.SemaphoreType.DMA((count, 10)),
            pltpu.SemaphoreType.DMA((count, 10)),
            pltpu.SemaphoreType.DMA((count,)),
            pltpu.SemaphoreType.DMA((5,)),
            pltpu.SemaphoreType.DMA((2, 3)),
        ],
        compiler_params=pltpu.CompilerParams(
            collective_id=0, has_side_effects=True, vmem_limit_bytes=VMEM_LIMIT
        ),
        name="gather_weights",
    )(*shards, rows, bias, facts)
    return results[:count], results[count:]


def as_matrix(full):
    return full.reshape(full.shape[0], GRID * full.shape[4], full.shape[5])


class Scatter:
    def __init__(self, place, part, total, mine, from_core, from_second, from_first, from_z, send, recv, local):
        self.place, self.part, self.total = place, part, total
        self.mine, self.from_core = mine, from_core
        self.from_second, self.from_first, self.from_z = from_second, from_first, from_z
        self.send, self.recv, self.local = send, recv, local
        self.m, self.rows, self.w = total.shape
        self.started = []

    def cols(self, y):
        return pl.ds(pl.multiple_of(y * self.w, LANES), self.w)

    def copy(self, index, src, dst, peer):
        step = remote(src, dst, self.send.at[index], self.recv.at[index], peer)
        step.start()
        self.started.append(step)

    def arrive(self, index, ref):
        remote(ref, ref, self.send.at[index], self.recv.at[index], self.place.sibling()).wait_recv()

    def add(self, target, source):
        m = self.m

        def step(index, carry):
            i, z = index // 4, index % 4
            target[i, z] = (target[i, z].astype(F32) + source[i, z].astype(F32)).astype(BF16)
            return carry

        lax.fori_loop(0, m * 4, step, 0)

    def stage1(self):
        p = self.place
        spots = p.pieces()
        self.kept = []
        for slot, (here, there) in enumerate(((3, 3), (2, 1), (1, 2), (0, 0))):
            x, y = spots[here]
            keep = pltpu.make_async_copy(
                self.part.at[:, :, x, p.c, :, self.cols(y)], self.mine.at[slot], self.local.at[slot]
            )
            keep.start()
            self.kept.append(keep)
            x, y = spots[there]
            self.copy(
                slot,
                self.part.at[:, :, x, 1 - p.c, :, self.cols(y)],
                self.from_core.at[slot],
                p.sibling(),
            )

    def joined(self, slot):
        self.kept[slot].wait()
        self.arrive(slot, self.from_core.at[slot])
        self.add(self.mine.at[slot], self.from_core.at[slot])

    def stage2(self):
        p = self.place
        for slot in (0, 1):
            self.joined(slot)
            self.copy(4 + slot, self.mine.at[slot], self.from_second.at[slot], p.second())
        for slot in (2, 3):
            self.joined(slot)

    def stage3(self):
        p = self.place
        self.arrive(4, self.from_second.at[0])
        self.add(self.mine.at[2], self.from_second.at[0])
        self.copy(6, self.mine.at[2], self.from_first, p.first())
        self.arrive(5, self.from_second.at[1])
        self.add(self.mine.at[3], self.from_second.at[1])

    def stage4(self):
        p = self.place
        self.arrive(6, self.from_first)
        self.add(self.mine.at[3], self.from_first)
        for step in (1, 2, 3):
            self.copy(
                6 + step, self.mine.at[3, :, (p.z + step) % 4], self.from_z.at[step - 1], p.z_peer(step)
            )

    def stage5(self):
        p = self.place
        for step in (1, 2, 3):
            self.arrive(6 + step, self.from_z.at[step - 1])

        def step(i, carry):
            total = self.mine[3, i, p.z].astype(F32)
            for s in range(3):
                total = total + self.from_z[s, i].astype(F32)
            self.total[i] = total
            return carry

        lax.fori_loop(0, self.m, step, 0)
        for step in self.started:
            step.wait_send()

    def stages(self):
        return [self.stage1, self.stage2, self.stage3, self.stage4, self.stage5]


class Sum:
    def __init__(self, place, source, total, box, send, recv):
        self.place, self.source, self.total = place, source, total
        self.box, self.send, self.recv = box, send, recv

    def hop(self, index):
        p = self.place
        flip = p.z + 1 - 2 * (p.z % 2)
        far = (p.z + 2) % 4
        peers = (p.sibling(), p.device(x=1 - p.x), p.device(y=1 - p.y), p.device(z=flip), p.device(z=far))
        if index < 5:
            src = self.source if index == 0 else self.total.at[index - 1]
            step = remote(src, self.box.at[index], self.send.at[index], self.recv.at[index], peers[index])
            step.start()
            self.flying = step

    def land(self, index):
        self.flying.wait()
        src = self.source if index == 0 else self.total.at[index - 1]
        self.total[index] = src[...] + self.box[index]

    def stages(self):
        def first():
            self.hop(0)

        def later(index):
            self.land(index)
            self.hop(index + 1)

        return [first] + [functools.partial(later, i) for i in range(5)]


def scatter_scratch(shape):
    m, rows, w = shape
    return [
        pltpu.VMEM((4, m, 4, rows, w), BF16),
        pltpu.VMEM((4, m, 4, rows, w), BF16),
        pltpu.VMEM((2, m, 4, rows, w), BF16),
        pltpu.VMEM((m, 4, rows, w), BF16),
        pltpu.VMEM((3, m, rows, w), BF16),
        pltpu.SemaphoreType.DMA((10,)),
        pltpu.SemaphoreType.DMA((10,)),
        pltpu.SemaphoreType.DMA((4,)),
    ]


def scatter_kernel(subs, count, *refs):
    parts, small = refs[:count], refs[count]
    totals, small_total = refs[count + 1 : 2 * count + 1], refs[2 * count + 1]
    scratch = refs[2 * count + 2 :]
    place = Place(subs)
    entry_barrier(place)
    movers = [
        Scatter(place, parts[i], totals[i], *scratch[8 * i : 8 * i + 8]) for i in range(count)
    ]
    running, box, send, recv = scratch[8 * count :]
    small_sum = Sum(place, small, running, box, send, recv)
    for mover in movers:
        mover.stage1()
    steps = [s for s in wavefront(movers) if s.__func__ is not Scatter.stage1]
    extra = small_sum.stages()
    for index, step in enumerate(steps):
        if index < len(extra):
            extra[index]()
        step()
    for step in extra[len(steps) :]:
        step()
    small_total[...] = running[4]


def scatter_gradients(subs, parts, small):
    count = len(parts)
    rows = parts[0].shape[1] // GRID
    shaped = [p.reshape(p.shape[0], 4, 2, 2, rows, p.shape[2]) for p in parts]
    shapes = [(p.shape[0], rows, p.shape[2] // 2) for p in parts]
    outs = [jax.ShapeDtypeStruct(s, F32) for s in shapes]
    outs.append(jax.ShapeDtypeStruct(small.shape, F32))
    scratch = []
    for s in shapes:
        scratch += scatter_scratch(s)
    scratch += [
        pltpu.VMEM((5,) + small.shape, F32),
        pltpu.VMEM((5,) + small.shape, F32),
        pltpu.SemaphoreType.DMA((5,)),
        pltpu.SemaphoreType.DMA((5,)),
    ]
    results = pl.pallas_call(
        functools.partial(scatter_kernel, subs, count),
        out_shape=outs,
        in_specs=[pl.BlockSpec(memory_space=pl.ANY)] * count + [pl.BlockSpec(memory_space=pltpu.VMEM)],
        out_specs=[pl.BlockSpec(memory_space=pltpu.VMEM)] * (count + 1),
        scratch_shapes=scratch,
        compiler_params=pltpu.CompilerParams(
            collective_id=1, has_side_effects=True, vmem_limit_bytes=VMEM_LIMIT
        ),
        name="scatter_gradients",
    )(*shaped, small)
    return results[:count], results[count]


def head_lanes(half):
    lane = lax.broadcasted_iota(jnp.int32, (1, LANES), 1)
    return (lane // HEAD) == half


def dot_nt(a, b):
    return lax.dot_general(a, b, (((1,), (1,)), ((), ())), preferred_element_type=F32)


def dot_nn(a, b):
    return lax.dot_general(a, b, (((1,), (0,)), ((), ())), preferred_element_type=F32)


def forward_kernel(
    subs, both, wq, wkv, biases, facts, up_in, down_in,
    ctx, probs, word, entity, keys, values, up, down, mask, column, send, recv,
):
    place = Place(subs)
    step = pl.program_id(0)
    length, rows = mask.shape
    movers = [Gather(place, None, full, send.at[i], recv.at[i]) for i, full in enumerate((up, down))]
    own = pl.ds(pl.multiple_of(place.c * rows, LANES), rows)

    @pl.when(step == 0)
    def _():
        entry_barrier(place)
        for mover in movers:
            mover.spread()
        column[...] = facts[place.y].T
        spot = lax.broadcasted_iota(jnp.int32, (length, rows), 0)
        here = lax.broadcasted_iota(jnp.int32, (length, rows), 1) + place.c * rows
        same = column[:, 0:1] == facts[place.y, 0:1, own]
        seen = (column[:, 2:3] == 1) | (spot == here)
        mask[...] = jnp.where(same & seen, 0.0, NEG)

    @pl.when(step == 3)
    def _():
        movers[0].stage3()

    @pl.when(step == 5)
    def _():
        movers[1].stage3()

    tokens = both[...].reshape(length, both.shape[2])
    mine = both[place.c]
    bias = biases[0]
    row_ent = column[own, 1:2] == 1
    to_word = dot_nn(mine, jnp.concatenate([wq[0], wq[2]], axis=1))
    to_ent = dot_nn(mine, jnp.concatenate([wq[1], wq[3]], axis=1))
    scale = HEAD ** (-0.5)
    query_word = jnp.where(row_ent, to_word[:, LANES:] + bias[2:3], to_word[:, :LANES] + bias[0:1])
    query_ent = jnp.where(row_ent, to_ent[:, LANES:] + bias[3:4], to_ent[:, :LANES] + bias[1:2])
    word[...] = query_word.astype(BF16) * BF16(scale)
    entity[...] = query_ent.astype(BF16) * BF16(scale)
    pair = dot_nn(tokens, jnp.concatenate([wkv[0], wkv[1]], axis=1))
    key = pair[:, :LANES].astype(BF16)
    value = (pair[:, LANES:] + bias[4:5]).astype(BF16)
    keys[...] = key
    values[...] = value

    queries = jnp.concatenate([word[...], entity[...]], axis=1)
    ent = column[:, 1:2] == 1
    zero = jnp.zeros_like(key)
    turned = value.T
    for half in range(2):
        lanes = head_lanes(half)
        wide = jnp.concatenate(
            [jnp.where(lanes & ~ent, key, zero), jnp.where(lanes & ent, key, zero)], axis=1
        )
        scores = dot_nt(wide, queries) + mask[...]
        top = jnp.max(scores, axis=0, keepdims=True)
        expo = jnp.exp(scores - top)
        total = jnp.sum(expo, axis=0, keepdims=True)
        prob = (expo * (1.0 / total)).astype(BF16)
        probs[half] = prob
        ctx[half * HEAD : (half + 1) * HEAD, :] = dot_nn(
            turned[half * HEAD : (half + 1) * HEAD, :], prob
        ).astype(BF16)

    @pl.when(step == pl.num_programs(0) - 1)
    def _():
        for mover in movers:
            mover.stage4()
        for mover in movers:
            mover.stage5()


def attention_forward(subs, both, wq, wkv, biases, facts, up, down):
    _, rows, width = both.shape
    length = 2 * rows
    pairs = width // LANES
    span = biases.shape[2] // LANES
    block = lambda n: pl.BlockSpec((n, LANES), lambda i: (0, i))
    whole = lambda a: pl.BlockSpec(a.shape, lambda i: (0,) * a.ndim, pipeline_mode=pl.Buffered(1))
    cols = lambda a: pl.BlockSpec(a.shape[:2] + (LANES,), lambda i: (0, 0, i))
    anywhere = pl.BlockSpec(memory_space=pl.ANY)
    return pl.pallas_call(
        functools.partial(forward_kernel, subs),
        grid=(pairs,),
        out_shape=[
            jax.ShapeDtypeStruct((width, rows), BF16),
            jax.ShapeDtypeStruct((2 * pairs, length, rows), BF16),
            jax.ShapeDtypeStruct((rows, width), BF16),
            jax.ShapeDtypeStruct((rows, width), BF16),
            jax.ShapeDtypeStruct((length, width), BF16),
            jax.ShapeDtypeStruct((length, width), BF16),
            jax.ShapeDtypeStruct(up.shape, BF16),
            jax.ShapeDtypeStruct(down.shape, BF16),
        ],
        in_specs=[
            whole(both),
            cols(wq),
            cols(wkv),
            pl.BlockSpec((1, biases.shape[1], LANES), lambda i: (i // span, 0, i % span)),
            whole(facts),
            anywhere,
            anywhere,
        ],
        out_specs=[
            pl.BlockSpec((LANES, rows), lambda i: (i, 0)),
            pl.BlockSpec((2, length, rows), lambda i: (i, 0, 0)),
            block(rows),
            block(rows),
            block(length),
            block(length),
            anywhere,
            anywhere,
        ],
        scratch_shapes=[
            pltpu.VMEM((length, rows), F32),
            pltpu.VMEM((length, facts.shape[1]), jnp.int32),
            pltpu.SemaphoreType.DMA((2, 10)),
            pltpu.SemaphoreType.DMA((2, 10)),
        ],
        input_output_aliases={5: 6, 6: 7},
        compiler_params=pltpu.CompilerParams(
            collective_id=2, has_side_effects=True, vmem_limit_bytes=VMEM_LIMIT
        ),
        name="attention_forward",
    )(both, wq, wkv, biases, facts, up, down)


def backward_kernel(probs, qw, qe, keys, values, ctx, dctx, ent_col, ent_row, dqw, dqe, dkeys, dvalues):
    queries = jnp.concatenate([qw[...], qe[...]], axis=1)
    value = values[...]
    turned = keys[...].T
    ent = ent_col[...] == 1
    ent_lane = ent_row[...] == 1
    grad = dctx[...]
    zero = jnp.zeros_like(value)
    dk, dv = [], []
    for half in range(2):
        lanes = head_lanes(half)
        here = slice(half * HEAD, (half + 1) * HEAD)
        prob = probs[half]
        delta = jnp.sum(
            ctx[here, :].astype(F32) * grad[here, :].astype(F32), axis=0, keepdims=True
        )
        dprob = dot_nn(jnp.where(lanes, value, zero), grad)
        dscore = (prob.astype(F32) * (dprob - delta)).astype(BF16)
        key_t = turned[here, :]
        none = jnp.zeros_like(key_t)
        tall = jnp.concatenate(
            [jnp.where(ent_lane, none, key_t), jnp.where(ent_lane, key_t, none)], axis=0
        )
        dq = dot_nn(tall, dscore) * (HEAD ** (-0.5))
        dqw[here, :] = dq[:HEAD].astype(BF16)
        dqe[here, :] = dq[HEAD:].astype(BF16)
        both = dot_nn(dscore, queries)
        dk.append(jnp.where(ent, both[:, LANES:], both[:, :LANES]))
        dv.append(dot_nt(prob, grad))
    dkeys[...] = jnp.where(head_lanes(0), dk[0], dk[1]).astype(BF16)
    dvalues[...] = jnp.where(head_lanes(0), dv[0], dv[1]).astype(BF16)


def attention_backward(probs, qw, qe, keys, values, ctx, dctx, ent_col, ent_row):
    rows, width = qw.shape
    length = keys.shape[0]
    pairs = width // LANES
    block = lambda n: pl.BlockSpec((n, LANES), lambda i: (0, i))
    turned = pl.BlockSpec((LANES, rows), lambda i: (i, 0))
    whole = lambda a: pl.BlockSpec(a.shape, lambda i: (0,) * a.ndim)
    return pl.pallas_call(
        backward_kernel,
        grid=(pairs,),
        out_shape=[
            jax.ShapeDtypeStruct((width, rows), BF16),
            jax.ShapeDtypeStruct((width, rows), BF16),
            jax.ShapeDtypeStruct((length, width), BF16),
            jax.ShapeDtypeStruct((length, width), BF16),
        ],
        in_specs=[
            pl.BlockSpec((2, length, rows), lambda i: (i, 0, 0)),
            block(rows),
            block(rows),
            block(length),
            block(length),
            turned,
            turned,
            whole(ent_col),
            whole(ent_row),
        ],
        out_specs=[turned, turned, block(length), block(length)],
        compiler_params=pltpu.CompilerParams(vmem_limit_bytes=VMEM_LIMIT),
        name="attention_backward",
    )(probs, qw, qe, keys, values, ctx, dctx, ent_col, ent_row)


def ffn_forward_kernel(
    subs, both, ctx, w_out, up, down, unit_bias, out_bias, gain, shift, valid, grad_out,
    active, slope, hidden_low, normal_one, inverse_one, output, d_two, sums, hidden, total,
):
    step = pl.program_id(0)
    place = Place(subs)

    @pl.when(step == 0)
    def _():
        attn = dot_nt(ctx[...].T, w_out[...]) + out_bias[0:1].astype(F32)
        resid = both[place.c].astype(F32) + attn
        normal, inverse = normalize(resid)
        out = normal * gain[0:1].astype(F32) + shift[0:1].astype(F32)
        hidden[...] = out
        hidden_low[...] = out.astype(BF16)
        normal_one[...] = normal
        inverse_one[...] = inverse
        total[...] = jnp.zeros_like(total)
        seen = valid[...]
        sums[0:1] = column_sum(seen * resid * resid)
        sums[1:2] = column_sum(seen * attn * attn)

    pre = dot_nn(hidden_low[...], up[...]) + unit_bias[...]
    act, rise = gelu_pair(pre)
    act = act.astype(BF16)
    active[...] = act
    slope[...] = rise.astype(BF16)
    total[...] += dot_nt(act, down[...])

    @pl.when(step == pl.num_programs(0) - 1)
    def _():
        ffn = total[...] + out_bias[1:2].astype(F32)
        resid = hidden[...] + ffn
        normal, inverse = normalize(resid)
        output[...] = (normal * gain[1:2].astype(F32) + shift[1:2].astype(F32)).astype(BF16)
        seen = valid[...]
        grad = grad_out[...].astype(F32)
        back = norm_backward(grad, normal, inverse, gain[1:2].astype(F32))
        d_two[...] = back
        sums[2:3] = column_sum(seen * ffn * ffn)
        sums[3:4] = column_sum(seen * resid * resid)
        sums[4:5] = column_sum(grad * normal)
        sums[5:6] = column_sum(grad)
        sums[6:7] = column_sum(back.astype(BF16).astype(F32))
        sums[7:8] = jnp.zeros_like(sums[7:8]) + jnp.sum(seen) * (1.0 / seen.shape[0])


def ffn_forward(subs, both, ctx, w_out, up, down, unit_bias, out_bias, gain, shift, valid, grad_out):
    _, rows, width = both.shape
    units = up.shape[1]
    whole = lambda a: pl.BlockSpec(a.shape, lambda i: (0,) * a.ndim, pipeline_mode=pl.Buffered(1))
    fixed = lambda r, w: pl.BlockSpec((r, w), lambda i: (0, 0), pipeline_mode=pl.Buffered(1))
    wide = lambda r: pl.BlockSpec((r, BLOCK), lambda i: (0, i))
    return pl.pallas_call(
        functools.partial(ffn_forward_kernel, subs),
        grid=(units // BLOCK,),
        out_shape=[
            jax.ShapeDtypeStruct((rows, units), BF16),
            jax.ShapeDtypeStruct((rows, units), BF16),
            jax.ShapeDtypeStruct((rows, width), BF16),
            jax.ShapeDtypeStruct((rows, width), F32),
            jax.ShapeDtypeStruct((rows, 1), F32),
            jax.ShapeDtypeStruct((rows, width), BF16),
            jax.ShapeDtypeStruct((rows, width), F32),
            jax.ShapeDtypeStruct((8, width), F32),
        ],
        in_specs=[whole(both), whole(ctx), whole(w_out), wide(width), wide(width), wide(1)]
        + [whole(a) for a in (out_bias, gain, shift, valid, grad_out)],
        out_specs=[
            wide(rows),
            wide(rows),
            fixed(rows, width),
            fixed(rows, width),
            fixed(rows, 1),
            fixed(rows, width),
            fixed(rows, width),
            fixed(8, width),
        ],
        scratch_shapes=[pltpu.VMEM((rows, width), F32), pltpu.VMEM((rows, width), F32)],
        compiler_params=pltpu.CompilerParams(vmem_limit_bytes=VMEM_LIMIT),
        cost_estimate=pl.CostEstimate(
            flops=2 * rows * width * (width + 2 * units),
            bytes_accessed=2 * width * (width + 2 * units) + 4 * rows * units,
            transcendentals=rows * units,
        ),
        name="ffn_forward",
    )(both, ctx, w_out, up, down, unit_bias, out_bias, gain, shift, valid, grad_out)


def ffn_backward_kernel(
    d_two, hidden_low, active, slope, up, down, ctx, w_out, gain, normal_one, inverse_one,
    up_part, down_part, bias_part, d_one, d_ctx, out_part, sums, d_low, d_turned, hidden_turned, total,
):
    step = pl.program_id(0)

    @pl.when(step == 0)
    def _():
        low = d_two[...].astype(BF16)
        d_low[...] = low
        d_turned[...] = low.T
        hidden_turned[...] = hidden_low[...].T
        total[...] = d_two[...]

    d_pre = (dot_nn(d_low[...], down[...]) * slope[...].astype(F32)).astype(BF16)
    bias_part[...] = column_sum(d_pre.astype(F32))
    up_part[...] = dot_nn(hidden_turned[...], d_pre).astype(BF16)
    down_part[...] = dot_nn(d_turned[...], active[...]).astype(BF16)
    total[...] += dot_nt(d_pre, up[...])

    @pl.when(step == pl.num_programs(0) - 1)
    def _():
        grad = total[...]
        normal = normal_one[...]
        back = norm_backward(grad, normal, inverse_one[...], gain[0:1].astype(F32))
        d_one[...] = back
        low = back.astype(BF16)
        d_ctx[...] = dot_nt(w_out[...].T, low).astype(BF16)
        out_part[...] = dot_nt(low.T, ctx[...]).astype(BF16)
        sums[...] = jnp.zeros_like(sums)
        sums[0:1] = column_sum(grad * normal)
        sums[1:2] = column_sum(grad)
        sums[2:3] = column_sum(low.astype(F32))


def ffn_backward(d_two, hidden_low, active, slope, up, down, ctx, w_out, gain, normal_one, inverse_one):
    rows, width = d_two.shape
    units = up.shape[1]
    whole = lambda a: pl.BlockSpec(a.shape, lambda i: (0,) * a.ndim, pipeline_mode=pl.Buffered(1))
    fixed = lambda r, w: pl.BlockSpec((r, w), lambda i: (0, 0), pipeline_mode=pl.Buffered(1))
    wide = lambda r: pl.BlockSpec((r, BLOCK), lambda i: (0, i))
    return pl.pallas_call(
        ffn_backward_kernel,
        grid=(units // BLOCK,),
        out_shape=[
            jax.ShapeDtypeStruct((width, units), BF16),
            jax.ShapeDtypeStruct((width, units), BF16),
            jax.ShapeDtypeStruct((1, units), F32),
            jax.ShapeDtypeStruct((rows, width), F32),
            jax.ShapeDtypeStruct((width, rows), BF16),
            jax.ShapeDtypeStruct((width, width), BF16),
            jax.ShapeDtypeStruct((8, width), F32),
        ],
        in_specs=[whole(d_two), whole(hidden_low), wide(rows), wide(rows), wide(width), wide(width)]
        + [whole(a) for a in (ctx, w_out, gain, normal_one, inverse_one)],
        out_specs=[
            wide(width),
            wide(width),
            wide(1),
            fixed(rows, width),
            fixed(width, rows),
            fixed(width, width),
            fixed(8, width),
        ],
        scratch_shapes=[
            pltpu.VMEM((rows, width), BF16),
            pltpu.VMEM((width, rows), BF16),
            pltpu.VMEM((width, rows), BF16),
            pltpu.VMEM((rows, width), F32),
        ],
        compiler_params=pltpu.CompilerParams(vmem_limit_bytes=VMEM_LIMIT),
        cost_estimate=pl.CostEstimate(
            flops=4 * rows * width * (width + 2 * units),
            bytes_accessed=2 * width * (3 * width + 4 * units) + 4 * rows * units,
            transcendentals=0,
        ),
        name="ffn_backward",
    )(d_two, hidden_low, active, slope, up, down, ctx, w_out, gain, normal_one, inverse_one)


def body(
    layer_input,
    grad_out,
    segment,
    entity,
    valid_mask,
    query_weight,
    key_value_weight,
    attn_bias,
    out_weight,
    out_bias,
    ln_gain,
    ln_bias,
    up_weight,
    ffn_bias,
    down_weight,
):
    rows, width = layer_input.shape
    length = segment.shape[0]
    rank = lax.axis_index("tensor")
    subs = lax.axis_size("dp") // GRID
    core = (lax.axis_index("dp") // subs) % 2
    moved = rank != core
    start = core * rows
    pairs = lax.axis_size("tensor")
    trades = []
    for d in range(lax.axis_size("dp")):
        other = d + subs if (d // subs) % 2 == 0 else d - subs
        y = 1 - (d // subs) % 2
        trades.append((d * pairs + y, other * pairs + 1 - y))
    siblings = [
        (d, d + subs if (d // subs) % 2 == 0 else d - subs) for d in range(lax.axis_size("dp"))
    ]

    def trade(own):
        got = lax.ppermute(own, ("dp", "tensor"), trades)
        return jnp.where(moved, got, own)

    shards = [
        query_weight,
        key_value_weight,
        out_weight.T[None],
        up_weight[None],
        down_weight.T[None],
    ]
    groups = [[b * subs + s for s in range(subs)] for b in range(GRID)]
    if subs > 1:
        shards = [
            lax.all_gather(s, "dp", axis=1, tiled=True, axis_index_groups=groups) for s in shards
        ]
    shards = [shards[1], shards[0]] + shards[2:]
    units = pairs * ffn_bias.shape[0]
    cols = attn_bias.shape[1]
    bias_rows = jnp.concatenate([attn_bias, ffn_bias.reshape(-1, cols)]).astype(F32)
    used = bias_rows.shape[0]
    bias_rows = jnp.pad(bias_rows, ((0, -used % 16), (0, 0)))
    facts = jnp.pad(jnp.stack([segment, entity, valid_mask]), ((0, 5), (0, 0)))
    (w_kv, w_q, w_out_t, w_up, w_down_t), (both, biases, pair_facts) = gather_weights(
        subs, shards, 3, layer_input, bias_rows, facts
    )
    w_kv, w_q, w_out_t = as_matrix(w_kv), as_matrix(w_q), as_matrix(w_out_t)[0]
    context_t, probs, query_word, query_ent, keys, values, w_up, w_down_t = attention_forward(
        subs, both, w_q, w_kv, biases, pair_facts, w_up, w_down_t
    )
    w_up, w_down_t = as_matrix(w_up)[0], as_matrix(w_down_t)[0]
    ffn_bias_full = biases[:, 5:used].reshape(units)
    facts = lax.dynamic_index_in_dim(pair_facts, rank, 0, keepdims=False)
    segment, entity, valid_mask = facts[0], facts[1], facts[2]
    layer_input = lax.dynamic_index_in_dim(both, core, 0, keepdims=False)

    ent_own = lax.dynamic_slice_in_dim(entity, start, rows)
    valid_own = lax.dynamic_slice_in_dim(valid_mask, start, rows).astype(F32)[:, None]
    ent_col = entity[:, None]
    ent_row = entity[None, :]

    grad_out, context_t = lax.optimization_barrier((grad_out, context_t))
    active, slope, hidden_low, normal_one, inverse_one, result, d_two, sums_two = ffn_forward(
        subs, both, context_t, w_out_t, w_up, w_down_t, ffn_bias_full[None], out_bias, ln_gain, ln_bias, valid_own,
        trade(grad_out),
    )
    output = trade(result)
    up_part, down_part, ffn_bias_part, d_one, d_context_t, out_part, sums_one = ffn_backward(
        d_two, hidden_low, active, slope, w_up, w_down_t, context_t, w_out_t, ln_gain, normal_one, inverse_one
    )

    d_word_t, d_ent_t, d_keys_all, d_values_all = attention_backward(
        probs, query_word, query_ent, keys, values, context_t, d_context_t, ent_col, ent_row
    )
    stacked = jnp.stack([d_keys_all, d_values_all]).reshape(2, 2, rows, width)
    mine = lax.dynamic_index_in_dim(stacked, core, 1, keepdims=False)
    theirs = lax.dynamic_index_in_dim(stacked, 1 - core, 1, keepdims=False)
    swapped = lax.ppermute(theirs, "dp", siblings)
    d_kv = (mine.astype(F32) + swapped.astype(F32)).astype(BF16)

    ent_lane = (ent_own == 1)[None, :]
    none = jnp.zeros_like(d_word_t)
    d_queries_t = jnp.stack(
        [
            jnp.where(ent_lane, none, d_word_t),
            jnp.where(ent_lane, none, d_ent_t),
            jnp.where(ent_lane, d_word_t, none),
            jnp.where(ent_lane, d_ent_t, none),
        ]
    )
    query_part = jnp.einsum(
        "ld,mel->mde", layer_input, d_queries_t, preferred_element_type=F32
    ).astype(BF16)
    kv_part = jnp.einsum("ld,mle->mde", layer_input, d_kv, preferred_element_type=F32).astype(BF16)
    attn_bias_part = jnp.concatenate(
        [jnp.sum(d_queries_t.astype(F32), 2), jnp.sum(d_kv[1].astype(F32), 0)[None]], 0
    )
    input_grad = (
        d_one
        + jnp.einsum("mel,mde->ld", d_queries_t, w_q, preferred_element_type=F32)
        + jnp.einsum("mle,mde->ld", d_kv, w_kv, preferred_element_type=F32)
    )
    returned = lax.ppermute(input_grad.astype(BF16), ("dp", "tensor"), trades)
    input_grad = jnp.where(moved, returned.astype(F32), input_grad)

    small = jnp.concatenate([sums_one.reshape(-1), sums_two.reshape(-1), attn_bias_part.reshape(-1), ffn_bias_part[0]])
    padded = -(-small.shape[0] // (8 * LANES)) * 8 * LANES
    small = jnp.pad(small, (0, padded - small.shape[0])).reshape(-1, LANES)
    sums, small_sum = scatter_gradients(
        subs, [down_part[None], up_part[None], out_part[None], query_part, kv_part], small
    )
    if subs > 1:
        sums = [
            lax.psum_scatter(s, "dp", scatter_dimension=1, tiled=True, axis_index_groups=groups)
            for s in sums
        ]
        small_sum = lax.psum(small_sum, "dp", axis_index_groups=groups)
    down_sum, up_sum, out_sum, query_sum, kv_sum = sums
    flat = small_sum.reshape(-1)
    norms = flat[: 16 * width].reshape(16, width)
    gains, shifts, out_biases = (jnp.stack([norms[i], norms[12 + i]]) for i in range(3))
    attn_biases = flat[16 * width : 21 * width].reshape(5, width)
    ffn_biases = flat[21 * width : 21 * width + units]
    squares = jnp.sum(norms[8:12], 1)
    real = norms[15, 0] * rows
    half = ffn_bias.shape[0]
    return (
        output,
        input_grad,
        jnp.sqrt(squares / (real * width)),
        query_sum,
        kv_sum,
        lax.dynamic_slice_in_dim(attn_biases, rank * cols, cols, 1),
        out_sum[0].T,
        out_biases,
        gains,
        shifts,
        up_sum[0],
        lax.dynamic_slice_in_dim(ffn_biases, rank * half, half, 0),
        down_sum[0].T,
    )


def solution(mesh):
    placed = (
        P(("dp", "tensor"), None),
        P(("dp", "tensor"), None),
        P("dp"),
        P("dp"),
        P("dp"),
        P(None, "dp", "tensor"),
        P(None, "dp", "tensor"),
        P(None, "tensor"),
        P("tensor", "dp"),
        P(),
        P(),
        P(),
        P("dp", "tensor"),
        P("tensor"),
        P("tensor", "dp"),
    )
    return jax.shard_map(
        body,
        mesh=mesh,
        in_specs=placed,
        out_specs=(
            P(("dp", "tensor"), None),
            P(("dp", "tensor"), None),
            P(),
            P(None, "dp", "tensor"),
            P(None, "dp", "tensor"),
            P(None, "tensor"),
            P("tensor", "dp"),
            P(),
            P(),
            P(),
            P("dp", "tensor"),
            P("tensor"),
            P("tensor", "dp"),
        ),
        check_vma=False,
    )
```

```python
import functools

import jax
import jax.numpy as jnp
from jax import lax
from jax.experimental import pallas as pl
from jax.experimental.pallas import tpu as pltpu
from jax.sharding import PartitionSpec as P

HEAD = 64
EPS = 1e-06
NEG = -1e30
GRID = 16
LANES = 128
MESH = pl.DeviceIdType.MESH
BF16 = jnp.bfloat16
F32 = jnp.float32
VMEM_LIMIT = 60 * 1024 * 1024


BLOCK = 512
TAIL = 0.34
TAIL_Q = (
    0.1918165616711201,
    0.1920366827922902,
    0.17827181747742213,
    0.1748548010854969,
    0.05944614604180367,
    0.27541659722682194,
    -0.27820700083503797,
    0.4016320911891782,
    -0.24597742961536673,
    0.050709736470982834,
)


def gelu_pair(v):
    size = jnp.abs(v)
    t = 1.0 / (1.0 + (TAIL * 0.5**0.5) * size)
    q = jnp.full_like(v, TAIL_Q[-1])
    for coefficient in TAIL_Q[-2::-1]:
        q = q * t + coefficient
    bell = jnp.exp(-0.5 * (v * v))
    tail = 0.5 * (bell * (t * q))
    cdf = jnp.where(v < 0, tail, 1.0 - tail)
    return v * cdf, cdf + v * (bell * 0.3989422804014327)


def normalize(resid):
    center = resid - jnp.mean(resid, -1, keepdims=True)
    inverse = lax.rsqrt(jnp.mean(center * center, -1, keepdims=True) + EPS)
    return center * inverse, inverse


def norm_backward(grad, normal, inverse, gain):
    scaled = grad * gain
    return inverse * (
        scaled
        - jnp.mean(scaled, -1, keepdims=True)
        - normal * jnp.mean(scaled * normal, -1, keepdims=True)
    )


def column_sum(a):
    return jnp.sum(a, 0, keepdims=True)


class Place:
    def __init__(self, subs):
        rank = lax.axis_index("dp")
        self.subs = subs
        self.sub = rank % subs
        block = rank // subs
        self.z = block // 4
        self.turns = [(self.z + step) % 4 for step in range(4)]
        self.x = (block // 2) % 2
        self.c = block % 2
        self.y = lax.axis_index("tensor")
        self.moved = self.y != self.c
        self.x1 = jnp.where(self.c == 0, 1 - self.x, self.x)
        self.y1 = jnp.where(self.c == 0, self.y, 1 - self.y)
        self.x2 = jnp.where(self.c == 0, self.x, 1 - self.x)
        self.y2 = jnp.where(self.c == 0, 1 - self.y, self.y)

    def device(self, z=None, x=None, c=None, y=None):
        z = self.z if z is None else z
        x = self.x if x is None else x
        c = self.c if c is None else c
        y = self.y if y is None else y
        return (((z * 2 + x) * 2 + c) * self.subs + self.sub, y)

    def z_peer(self, step):
        return self.device(z=(self.z + step) % 4)

    def first(self):
        return self.device(x=self.x1, y=self.y1)

    def second(self):
        return self.device(x=self.x2, y=self.y2)

    def sibling(self):
        return self.device(c=1 - self.c)

    def across(self):
        return self.device(y=1 - self.y)

    def transposed(self):
        return self.device(c=1 - self.c, y=1 - self.y)

    def pieces(self):
        return (
            (self.x, self.y),
            (self.x1, self.y1),
            (self.x2, self.y2),
            (1 - self.x, 1 - self.y),
        )


def entry_barrier(place):
    barrier = pltpu.get_barrier_semaphore()
    peers = [place.z_peer(step) for step in (1, 2, 3)]
    peers += [place.device(x=1 - place.x), place.across(), place.sibling(), place.transposed()]
    for peer in peers:
        pl.semaphore_signal(barrier, inc=1, device_id=peer, device_id_type=MESH)
    pl.semaphore_wait(barrier, len(peers))


def remote(src, dst, send, recv, peer):
    return pltpu.make_async_remote_copy(
        src_ref=src, dst_ref=dst, send_sem=send, recv_sem=recv, device_id=peer, device_id_type=MESH
    )


class Gather:
    def __init__(self, place, shard, full, send, recv, local=None, whole=True):
        self.place, self.shard, self.full, self.whole = place, shard, full, whole
        self.send, self.recv, self.local = send, recv, local
        self.w = full.shape[-1] // 2

    def cols(self, y):
        return pl.ds(pl.multiple_of(y * self.w, LANES), self.w)

    def piece(self, spot, c):
        x, y = spot
        return self.full.at[:, :, x, c, :, self.cols(y)]

    def copy(self, index, src, dst, peer):
        remote(src, dst, self.send.at[index], self.recv.at[index], peer).start()

    def arrive(self, index, ref):
        remote(ref, ref, self.send.at[index], self.recv.at[index], self.place.sibling()).wait_recv()

    def gone(self, index, ref):
        remote(ref, ref, self.send.at[index], self.recv.at[index], self.place.sibling()).wait_send()

    def own(self, z):
        p = self.place
        return self.full.at[:, z, p.x, p.c, :, self.cols(p.y)]

    def stage1(self):
        p = self.place
        self.kept = pltpu.make_async_copy(self.shard, self.own(p.z), self.local)
        self.kept.start()
        for step in (1, 2, 3):
            self.copy(step - 1, self.shard, self.own(p.z), p.z_peer(step))

    def land(self):
        p = self.place
        self.kept.wait()
        for step in (1, 2, 3):
            self.arrive(step - 1, self.own((p.z + 4 - step) % 4))

    def settle(self):
        self.land()
        for index in range(3):
            self.gone(index, self.shard)

    def spread(self):
        p = self.place
        mine = self.piece(p.pieces()[0], p.c)
        self.copy(3, mine, mine, p.first())
        self.copy(4, mine, mine, p.second())
        self.copy(6, mine, mine, p.sibling())

    def stage2(self):
        self.land()
        self.spread()

    def stage3(self):
        p = self.place
        got = self.piece(p.pieces()[1], p.c)
        self.arrive(3, got)
        self.copy(5, got, got, p.second())
        self.copy(7, got, got, p.sibling())

    def stage4(self):
        p = self.place
        for index, spot in ((4, 2), (5, 3)):
            got = self.piece(p.pieces()[spot], p.c)
            self.arrive(index, got)
            self.copy(index + 4, got, got, p.sibling())

    def stage5(self):
        p = self.place
        spots = p.pieces()
        for index, spot in ((6, 0), (7, 2), (8, 1), (9, 3)):
            self.arrive(index, self.piece(spots[spot], 1 - p.c))
        for index in range(3, 10):
            self.gone(index, self.piece(spots[0], p.c))

    def last(self):
        self.stage5()
        for index in range(3):
            self.gone(index, self.shard)

    def stages(self):
        if not self.whole:
            return [self.stage1, self.settle]
        return [self.stage1, self.stage2, self.stage3, self.stage4, self.last]


def wavefront(movers):
    lists = [mover.stages() for mover in movers]
    depth = max(len(stages) for stages in lists)
    order = []
    for time in range(len(lists) + depth - 1):
        for index in range(len(lists)):
            stage = time - index
            if 0 <= stage < len(lists[index]):
                order.append(lists[index][stage])
    return order


class Share:
    def __init__(self, source, pair, index, peer, sems):
        self.kept = pltpu.make_async_copy(source, pair.at[index], sems.at[2])
        self.sent = remote(source, pair.at[index], sems.at[0], sems.at[1], peer)

    def start(self):
        self.kept.start()
        self.sent.start()

    def finish(self):
        self.kept.wait()
        self.sent.wait()


class Rows:
    def __init__(self, place, rows, both, sems):
        p = place
        half = both.at[p.c]
        self.moved = p.moved
        self.kept = pltpu.make_async_copy(rows, half, sems.at[4])
        self.swap = remote(rows, both.at[p.y], sems.at[0], sems.at[1], p.transposed())
        self.swapped = remote(half, half, sems.at[0], sems.at[1], p.transposed())
        self.share = remote(rows, half, sems.at[2], sems.at[3], p.sibling())
        self.relay = remote(half, half, sems.at[2], sems.at[3], p.sibling())
        other = both.at[1 - p.c]
        self.other = remote(other, other, sems.at[2], sems.at[3], p.sibling())

    def start(self):
        @pl.when(self.moved)
        def _():
            self.swap.start()

        @pl.when(jnp.logical_not(self.moved))
        def _():
            self.kept.start()
            self.share.start()

    def forward(self):
        @pl.when(self.moved)
        def _():
            self.swapped.wait_recv()
            self.relay.start()

    def finish(self):
        @pl.when(self.moved)
        def _():
            self.swap.wait_send()
            self.relay.wait_send()

        @pl.when(jnp.logical_not(self.moved))
        def _():
            self.kept.wait()
            self.share.wait_send()

        self.other.wait_recv()


def gather_kernel(subs, count, wholes, *refs):
    shards, (rows, bias, facts) = refs[:count], refs[count : count + 3]
    fulls, (both, biases, pair_facts) = refs[count + 3 : 2 * count + 3], refs[2 * count + 3 : 2 * count + 6]
    send, recv, local, row_sems, share_sems = refs[2 * count + 6 :]
    place = Place(subs)
    entry_barrier(place)
    tokens = Rows(place, rows, both, row_sems)
    shares = [
        Share(facts, pair_facts, place.c, place.sibling(), share_sems.at[0]),
        Share(bias, biases, place.y, place.across(), share_sems.at[1]),
    ]
    tokens.start()
    for share in shares:
        share.start()
    movers = [
        Gather(place, shards[i], fulls[i], send.at[i], recv.at[i], local.at[i], i < wholes)
        for i in range(count)
    ]
    for mover in movers:
        mover.stage1()
    for index, step in enumerate(wavefront(movers)):
        if step.__func__ is not Gather.stage1:
            step()
        if index == count:
            tokens.forward()
    tokens.finish()
    for share in shares:
        share.finish()


def gather_weights(subs, shards, wholes, rows, bias, facts):
    count = len(shards)
    outs = [
        jax.ShapeDtypeStruct((s.shape[0], 4, 2, 2, s.shape[1], 2 * s.shape[2]), BF16) for s in shards
    ]
    outs += [jax.ShapeDtypeStruct((2,) + a.shape, a.dtype) for a in (rows, bias, facts)]
    results = pl.pallas_call(
        functools.partial(gather_kernel, subs, count, wholes),
        out_shape=outs,
        in_specs=[pl.BlockSpec(memory_space=pltpu.VMEM)] * (count + 3),
        out_specs=[pl.BlockSpec(memory_space=pl.ANY)] * (count + 3),
        scratch_shapes=[
            pltpu.SemaphoreType.DMA((count, 10)),
            pltpu.SemaphoreType.DMA((count, 10)),
            pltpu.SemaphoreType.DMA((count,)),
            pltpu.SemaphoreType.DMA((5,)),
            pltpu.SemaphoreType.DMA((2, 3)),
        ],
        compiler_params=pltpu.CompilerParams(
            collective_id=0, has_side_effects=True, vmem_limit_bytes=VMEM_LIMIT
        ),
        name="gather_weights",
    )(*shards, rows, bias, facts)
    return results[:count], results[count:]


def as_matrix(full):
    return full.reshape(full.shape[0], GRID * full.shape[4], full.shape[5])


class Last:
    def __init__(self, place, piece, total, from_z, send, recv):
        self.place, self.piece, self.total, self.from_z = place, piece, total, from_z
        self.send, self.recv = send, recv

    def start(self):
        p = self.place
        for step in (1, 2, 3):
            remote(
                self.piece.at[:, p.turns[step]],
                self.from_z.at[step - 1],
                self.send.at[step - 1],
                self.recv.at[step - 1],
                p.z_peer(step),
            ).start()

    def finish(self):
        p = self.place
        for step in (0, 1, 2):
            slot = self.from_z.at[step]
            remote(slot, slot, self.send.at[step], self.recv.at[step], p.sibling()).wait()

        def step(i, carry):
            total = self.piece[i, p.z].astype(F32)
            for s in range(3):
                total = total + self.from_z[s, i].astype(F32)
            self.total[i] = total
            return carry

        lax.fori_loop(0, self.total.shape[0], step, 0)


class Scatter:
    def __init__(self, place, part, mine, from_core, from_second, from_first, send, recv, local):
        self.place, self.part = place, part
        self.mine, self.from_core = mine, from_core
        self.from_second, self.from_first = from_second, from_first
        self.send, self.recv, self.local = send, recv, local
        self.m, _, self.rows, self.w = from_first.shape

    def cols(self, y):
        return pl.ds(pl.multiple_of(y * self.w, LANES), self.w)

    def copy(self, index, src, dst, peer):
        remote(src, dst, self.send.at[index], self.recv.at[index], peer).start()

    def arrive(self, index, ref):
        remote(ref, ref, self.send.at[index], self.recv.at[index], self.place.sibling()).wait_recv()

    def drain(self):
        for index in range(7):
            remote(
                self.from_first, self.from_first, self.send.at[index], self.recv.at[index], self.place.sibling()
            ).wait_send()

    def add(self, target, source):
        m = self.m

        def step(index, carry):
            i, z = index // 4, index % 4
            target[i, z] = (target[i, z].astype(F32) + source[i, z].astype(F32)).astype(BF16)
            return carry

        lax.fori_loop(0, m * 4, step, 0)

    def keep(self, slot, spot):
        x, y = self.place.pieces()[spot]
        source = self.part.at[:, :, x, self.place.c, :, self.cols(y)]
        return pltpu.make_async_copy(source, self.mine.at[slot], self.local.at[slot])

    def stage1(self):
        p = self.place
        spots = p.pieces()
        for slot, (here, there) in enumerate(((3, 3), (2, 1), (1, 2), (0, 0))):
            self.keep(slot, here).start()
            x, y = spots[there]
            self.copy(
                slot,
                self.part.at[:, :, x, 1 - p.c, :, self.cols(y)],
                self.from_core.at[slot],
                p.sibling(),
            )

    def joined(self, slot):
        self.keep(slot, 3 - slot).wait()
        self.arrive(slot, self.from_core.at[slot])
        self.add(self.mine.at[slot], self.from_core.at[slot])

    def stage2(self):
        p = self.place
        for slot in (0, 1):
            self.joined(slot)
            self.copy(4 + slot, self.mine.at[slot], self.from_second.at[slot], p.second())
        for slot in (2, 3):
            self.joined(slot)

    def stage3(self):
        p = self.place
        self.arrive(4, self.from_second.at[0])
        self.add(self.mine.at[2], self.from_second.at[0])
        self.copy(6, self.mine.at[2], self.from_first, p.first())
        self.arrive(5, self.from_second.at[1])
        self.add(self.mine.at[3], self.from_second.at[1])

    def stage4(self):
        self.arrive(6, self.from_first)
        self.add(self.mine.at[3], self.from_first)


class Sum:
    def __init__(self, place, source, total, box, send, recv):
        self.place, self.source, self.total = place, source, total
        self.box, self.send, self.recv = box, send, recv

    def hop(self, index):
        p = self.place
        flip = p.z + 1 - 2 * (p.z % 2)
        far = (p.z + 2) % 4
        peers = (p.sibling(), p.device(x=1 - p.x), p.device(y=1 - p.y), p.device(z=flip), p.device(z=far))
        if index < 5:
            src = self.source if index == 0 else self.total.at[index - 1]
            step = remote(src, self.box.at[index], self.send.at[index], self.recv.at[index], peers[index])
            step.start()
            self.flying = step

    def land(self, index):
        self.flying.wait()
        src = self.source if index == 0 else self.total.at[index - 1]
        self.total[index] = src[...] + self.box[index]

    def stages(self):
        def first():
            self.hop(0)

        def later(index):
            self.land(index)
            self.hop(index + 1)

        return [first] + [functools.partial(later, i) for i in range(5)]


def scatter_scratch(shape):
    m, rows, w = shape
    return [
        pltpu.VMEM((4, m, 4, rows, w), BF16),
        pltpu.VMEM((4, m, 4, rows, w), BF16),
        pltpu.VMEM((2, m, 4, rows, w), BF16),
        pltpu.VMEM((m, 4, rows, w), BF16),
        pltpu.SemaphoreType.DMA((7,)),
        pltpu.SemaphoreType.DMA((7,)),
        pltpu.SemaphoreType.DMA((4,)),
    ]


def last_scratch(shape):
    return [
        pltpu.VMEM((3,) + shape, BF16),
        pltpu.SemaphoreType.DMA((3,)),
        pltpu.SemaphoreType.DMA((3,)),
    ]


def as_shards(part):
    m, rows, w = part.shape
    return part.reshape(m, 4, 2, 2, rows // GRID, w)


def scatter_kernel(subs, early, count, *refs):
    pieces, parts, small = refs[:early], refs[early : early + count], refs[early + count]
    refs = refs[early + count + 1 :]
    totals, small_total = refs[: early + count], refs[early + count]
    refs = refs[early + count + 1 :]
    lasts, refs = refs[: 3 * (early + count)], refs[3 * (early + count) :]
    place = Place(subs)
    entry_barrier(place)
    movers = [Scatter(place, parts[i], *refs[7 * i : 7 * i + 7]) for i in range(count)]
    sources = list(pieces) + [mover.mine.at[3] for mover in movers]
    ends = [Last(place, sources[i], totals[i], *lasts[3 * i : 3 * i + 3]) for i in range(early + count)]
    running, box, send, recv = refs[7 * count :]
    small_sum = Sum(place, small, running, box, send, recv)
    for mover in movers:
        mover.stage1()
    for end in ends[:early]:
        end.start()
    extra = small_sum.stages()
    steps = []
    for time in range(count + 4):
        for index in range(count):
            stage = time - index
            if 0 <= stage < 5:
                mover, end = movers[index], ends[early + index]
                steps.append((mover.stage2, mover.stage3, mover.stage4, end.start, end.finish)[stage])
    for index, step in enumerate(steps):
        if index < len(extra):
            extra[index]()
        step()
    for step in extra[len(steps) :]:
        step()
    for end in ends[:early]:
        end.finish()
    for mover in movers:
        mover.drain()
    small_total[...] = running[4]


def scatter_gradients(subs, pieces, parts, small):
    early, count = len(pieces), len(parts)
    shaped = [as_shards(p) for p in parts]
    shapes = [(p.shape[0],) + p.shape[2:] for p in pieces]
    whole = [(p.shape[0], p.shape[4], p.shape[5] // 2) for p in shaped]
    outs = [jax.ShapeDtypeStruct(s, F32) for s in shapes + whole]
    outs.append(jax.ShapeDtypeStruct(small.shape, F32))
    scratch = []
    for s in shapes + whole:
        scratch += last_scratch(s)
    for s in whole:
        scratch += scatter_scratch(s)
    scratch += [
        pltpu.VMEM((5,) + small.shape, F32),
        pltpu.VMEM((5,) + small.shape, F32),
        pltpu.SemaphoreType.DMA((5,)),
        pltpu.SemaphoreType.DMA((5,)),
    ]
    local = pl.BlockSpec(memory_space=pltpu.VMEM)
    results = pl.pallas_call(
        functools.partial(scatter_kernel, subs, early, count),
        out_shape=outs,
        in_specs=[local] * early + [pl.BlockSpec(memory_space=pl.ANY)] * count + [local],
        out_specs=[local] * (early + count + 1),
        scratch_shapes=scratch,
        compiler_params=pltpu.CompilerParams(
            collective_id=1, has_side_effects=True, vmem_limit_bytes=VMEM_LIMIT
        ),
        name="scatter_gradients",
    )(*pieces, *shaped, small)
    return results[:-1], results[-1]


def head_lanes(half):
    lane = lax.broadcasted_iota(jnp.int32, (1, LANES), 1)
    return (lane // HEAD) == half


def dot_nt(a, b):
    return lax.dot_general(a, b, (((1,), (1,)), ((), ())), preferred_element_type=F32)


def dot_nn(a, b):
    return lax.dot_general(a, b, (((1,), (0,)), ((), ())), preferred_element_type=F32)


def forward_kernel(
    subs, both, wq, wkv, biases, facts, up_in, down_in,
    ctx, probs, word, entity, keys, values, up, down, mask, column, send, recv,
):
    place = Place(subs)
    step = pl.program_id(0)
    length, rows = mask.shape
    movers = [Gather(place, None, full, send.at[i], recv.at[i]) for i, full in enumerate((up, down))]
    own = pl.ds(pl.multiple_of(place.c * rows, LANES), rows)

    @pl.when(step == 0)
    def _():
        entry_barrier(place)
        for mover in movers:
            mover.spread()
        column[...] = facts[place.y].T
        spot = lax.broadcasted_iota(jnp.int32, (length, rows), 0)
        here = lax.broadcasted_iota(jnp.int32, (length, rows), 1) + place.c * rows
        same = column[:, 0:1] == facts[place.y, 0:1, own]
        seen = (column[:, 2:3] == 1) | (spot == here)
        mask[...] = jnp.where(same & seen, 0.0, NEG)

    @pl.when(step == 3)
    def _():
        movers[0].stage3()

    @pl.when(step == 5)
    def _():
        movers[1].stage3()

    tokens = both[...].reshape(length, both.shape[2])
    mine = both[place.c]
    bias = biases[0]
    row_ent = column[own, 1:2] == 1
    to_word = dot_nn(mine, jnp.concatenate([wq[0], wq[2]], axis=1))
    to_ent = dot_nn(mine, jnp.concatenate([wq[1], wq[3]], axis=1))
    scale = HEAD ** (-0.5)
    query_word = jnp.where(row_ent, to_word[:, LANES:] + bias[2:3], to_word[:, :LANES] + bias[0:1])
    query_ent = jnp.where(row_ent, to_ent[:, LANES:] + bias[3:4], to_ent[:, :LANES] + bias[1:2])
    word[...] = query_word.astype(BF16) * BF16(scale)
    entity[...] = query_ent.astype(BF16) * BF16(scale)
    pair = dot_nn(tokens, jnp.concatenate([wkv[0], wkv[1]], axis=1))
    key = pair[:, :LANES].astype(BF16)
    value = (pair[:, LANES:] + bias[4:5]).astype(BF16)
    keys[...] = key
    values[...] = value

    queries = jnp.concatenate([word[...], entity[...]], axis=1)
    ent = column[:, 1:2] == 1
    zero = jnp.zeros_like(key)
    turned = value.T
    for half in range(2):
        lanes = head_lanes(half)
        wide = jnp.concatenate(
            [jnp.where(lanes & ~ent, key, zero), jnp.where(lanes & ent, key, zero)], axis=1
        )
        scores = dot_nt(wide, queries) + mask[...]
        top = jnp.max(scores, axis=0, keepdims=True)
        expo = jnp.exp(scores - top)
        total = jnp.sum(expo, axis=0, keepdims=True)
        prob = (expo * (1.0 / total)).astype(BF16)
        probs[half] = prob
        ctx[half * HEAD : (half + 1) * HEAD, :] = dot_nn(
            turned[half * HEAD : (half + 1) * HEAD, :], prob
        ).astype(BF16)

    @pl.when(step == pl.num_programs(0) - 1)
    def _():
        for mover in movers:
            mover.stage4()
        for mover in movers:
            mover.stage5()


def attention_forward(subs, both, wq, wkv, biases, facts, up, down):
    _, rows, width = both.shape
    length = 2 * rows
    pairs = width // LANES
    span = biases.shape[2] // LANES
    block = lambda n: pl.BlockSpec((n, LANES), lambda i: (0, i))
    whole = lambda a: pl.BlockSpec(a.shape, lambda i: (0,) * a.ndim, pipeline_mode=pl.Buffered(1))
    cols = lambda a: pl.BlockSpec(a.shape[:2] + (LANES,), lambda i: (0, 0, i))
    anywhere = pl.BlockSpec(memory_space=pl.ANY)
    return pl.pallas_call(
        functools.partial(forward_kernel, subs),
        grid=(pairs,),
        out_shape=[
            jax.ShapeDtypeStruct((width, rows), BF16),
            jax.ShapeDtypeStruct((2 * pairs, length, rows), BF16),
            jax.ShapeDtypeStruct((rows, width), BF16),
            jax.ShapeDtypeStruct((rows, width), BF16),
            jax.ShapeDtypeStruct((length, width), BF16),
            jax.ShapeDtypeStruct((length, width), BF16),
            jax.ShapeDtypeStruct(up.shape, BF16),
            jax.ShapeDtypeStruct(down.shape, BF16),
        ],
        in_specs=[
            whole(both),
            cols(wq),
            cols(wkv),
            pl.BlockSpec((1, biases.shape[1], LANES), lambda i: (i // span, 0, i % span)),
            whole(facts),
            anywhere,
            anywhere,
        ],
        out_specs=[
            pl.BlockSpec((LANES, rows), lambda i: (i, 0)),
            pl.BlockSpec((2, length, rows), lambda i: (i, 0, 0)),
            block(rows),
            block(rows),
            block(length),
            block(length),
            anywhere,
            anywhere,
        ],
        scratch_shapes=[
            pltpu.VMEM((length, rows), F32),
            pltpu.VMEM((length, facts.shape[1]), jnp.int32),
            pltpu.SemaphoreType.DMA((2, 10)),
            pltpu.SemaphoreType.DMA((2, 10)),
        ],
        input_output_aliases={5: 6, 6: 7},
        compiler_params=pltpu.CompilerParams(
            collective_id=2, has_side_effects=True, vmem_limit_bytes=VMEM_LIMIT
        ),
        name="attention_forward",
    )(both, wq, wkv, biases, facts, up, down)


def backward_kernel(
    subs, both, facts, probs, word, entity, keys, values, ctx, dctx, wq, wkv, d_one, down_part, up_part,
    q_part, kv_part, input_grad, q_bias, v_bias, down_piece, up_piece,
    column, turned_rows, pair_grad, pair_got, pair_send, pair_recv, *scratch,
):
    place = Place(subs)
    step = pl.program_id(0)
    pairs = pl.num_programs(0) - 1
    rows = word.shape[0]
    movers = [Scatter(place, down_part, *scratch[:7]), Scatter(place, up_part, *scratch[7:])]
    own = pl.ds(pl.multiple_of(place.c * rows, LANES), rows)
    other = pl.ds(pl.multiple_of((1 - place.c) * rows, LANES), rows)

    @pl.when(step == 0)
    def _():
        entry_barrier(place)
        for mover in movers:
            mover.stage1()
        column[...] = facts[place.y].T
        turned_rows[...] = both[place.c].T
        input_grad[...] = d_one[...]

    @pl.when(step == 1)
    def _():
        movers[0].stage2()

    @pl.when(step == 2)
    def _():
        movers[1].stage2()

    @pl.when(step == 5)
    def _():
        movers[0].stage3()

    @pl.when(step < pairs)
    def _():
        queries = jnp.concatenate([word[...], entity[...]], axis=1)
        value = values[...]
        turned = keys[...].T
        ent = column[:, 1:2] == 1
        ent_lane = facts[place.y, 1:2, :] == 1
        own_ent = facts[place.y, 1:2, own] == 1
        grad = dctx[...]
        zero = jnp.zeros_like(value)
        dk, dv, dw, de = [], [], [], []
        for half in range(2):
            lanes = head_lanes(half)
            here = slice(half * HEAD, (half + 1) * HEAD)
            prob = probs[half]
            delta = jnp.sum(
                ctx[here, :].astype(F32) * grad[here, :].astype(F32), axis=0, keepdims=True
            )
            dprob = dot_nn(jnp.where(lanes, value, zero), grad)
            dscore = (prob.astype(F32) * (dprob - delta)).astype(BF16)
            key_t = turned[here, :]
            none = jnp.zeros_like(key_t)
            tall = jnp.concatenate(
                [jnp.where(ent_lane, none, key_t), jnp.where(ent_lane, key_t, none)], axis=0
            )
            dq = dot_nn(tall, dscore) * (HEAD ** (-0.5))
            dw.append(dq[:HEAD])
            de.append(dq[HEAD:])
            pair = dot_nn(dscore, queries)
            dk.append(jnp.where(ent, pair[:, LANES:], pair[:, :LANES]))
            dv.append(dot_nt(prob, grad))
        first = head_lanes(0)
        pair_grad[step, :, :LANES] = jnp.where(first, dk[0], dk[1]).astype(BF16)
        pair_grad[step, :, LANES:] = jnp.where(first, dv[0], dv[1]).astype(BF16)
        remote(
            pair_grad.at[step, other], pair_got.at[step], pair_send.at[step], pair_recv.at[step], place.sibling()
        ).start()
        d_word, d_ent = jnp.concatenate(dw, axis=0), jnp.concatenate(de, axis=0)
        empty = jnp.zeros_like(d_word)
        turned_grad = jnp.concatenate(
            [
                jnp.where(own_ent, empty, d_word),
                jnp.where(own_ent, empty, d_ent),
                jnp.where(own_ent, d_word, empty),
                jnp.where(own_ent, d_ent, empty),
            ],
            axis=0,
        ).astype(BF16)
        query_grad = turned_grad.T
        weights = jnp.concatenate([wq[m] for m in range(4)], axis=1)
        input_grad[...] += dot_nt(query_grad, weights)
        part = dot_nn(turned_rows[...], query_grad).astype(BF16)
        sums = column_sum(query_grad.astype(F32))
        for m in range(4):
            span = slice(m * LANES, (m + 1) * LANES)
            q_part[m] = part[:, span]
            q_bias[m : m + 1] = sums[:, span]

    @pl.when(step > 0)
    def _():
        before = step - 1
        remote(
            pair_got.at[before], pair_got.at[before], pair_send.at[before], pair_recv.at[before], place.sibling()
        ).wait()
        grad = (pair_grad[before, own].astype(F32) + pair_got[before].astype(F32)).astype(BF16)
        weights = jnp.concatenate([wkv[0], wkv[1]], axis=1)
        input_grad[...] += dot_nt(grad, weights)
        part = dot_nn(turned_rows[...], grad).astype(BF16)
        kv_part[0] = part[:, :LANES]
        kv_part[1] = part[:, LANES:]
        v_bias[0:1] = column_sum(grad[:, LANES:].astype(F32))

    @pl.when(step == pairs)
    def _():
        movers[1].stage3()
        for mover in movers:
            mover.stage4()
            mover.drain()
        down_piece[...] = movers[0].mine[3]
        up_piece[...] = movers[1].mine[3]


def attention_backward(subs, both, facts, probs, word, entity, keys, values, ctx, dctx, wq, wkv, d_one, down_part, up_part):
    _, rows, width = both.shape
    length = 2 * rows
    pairs = width // LANES
    block = lambda n: pl.BlockSpec((n, LANES), lambda i: (0, jnp.minimum(i, pairs - 1)))
    behind = lambda n: pl.BlockSpec((n, LANES), lambda i: (0, jnp.maximum(i - 1, 0)))
    turned = pl.BlockSpec((LANES, rows), lambda i: (jnp.minimum(i, pairs - 1), 0))
    whole = lambda a: pl.BlockSpec(a.shape, lambda i: (0,) * a.ndim, pipeline_mode=pl.Buffered(1))
    q_cols = pl.BlockSpec((4, width, LANES), lambda i: (0, 0, jnp.minimum(i, pairs - 1)))
    kv_cols = pl.BlockSpec((2, width, LANES), lambda i: (0, 0, jnp.maximum(i - 1, 0)))
    anywhere = pl.BlockSpec(memory_space=pl.ANY)
    local = pl.BlockSpec(memory_space=pltpu.VMEM)
    shape = (1, down_part.shape[1] // GRID, down_part.shape[2] // 2)
    piece = jax.ShapeDtypeStruct((1, 4) + shape[1:], BF16)
    return pl.pallas_call(
        functools.partial(backward_kernel, subs),
        grid=(pairs + 1,),
        out_shape=[
            jax.ShapeDtypeStruct(wq.shape, BF16),
            jax.ShapeDtypeStruct(wkv.shape, BF16),
            jax.ShapeDtypeStruct((rows, width), F32),
            jax.ShapeDtypeStruct((8, width), F32),
            jax.ShapeDtypeStruct((8, width), F32),
            piece,
            piece,
        ],
        in_specs=[
            whole(both),
            whole(facts),
            pl.BlockSpec((2, length, rows), lambda i: (jnp.minimum(i, pairs - 1), 0, 0)),
            block(rows),
            block(rows),
            block(length),
            block(length),
            turned,
            turned,
            q_cols,
            kv_cols,
            whole(d_one),
            anywhere,
            anywhere,
        ],
        out_specs=[
            q_cols,
            kv_cols,
            pl.BlockSpec((rows, width), lambda i: (0, 0), pipeline_mode=pl.Buffered(1)),
            block(8),
            behind(8),
            local,
            local,
        ],
        scratch_shapes=[
            pltpu.VMEM((length, facts.shape[1]), jnp.int32),
            pltpu.VMEM((width, rows), BF16),
            pltpu.VMEM((pairs, length, 2 * LANES), BF16),
            pltpu.VMEM((pairs, rows, 2 * LANES), BF16),
            pltpu.SemaphoreType.DMA((pairs,)),
            pltpu.SemaphoreType.DMA((pairs,)),
        ]
        + scatter_scratch(shape)
        + scatter_scratch(shape),
        compiler_params=pltpu.CompilerParams(
            collective_id=3, has_side_effects=True, vmem_limit_bytes=VMEM_LIMIT
        ),
        name="attention_backward",
    )(both, facts, probs, word, entity, keys, values, ctx, dctx, wq, wkv, d_one, as_shards(down_part), as_shards(up_part))


def ffn_forward_kernel(
    subs, both, ctx, w_out, up, down, unit_bias, out_bias, gain, shift, valid, grad_out,
    active, slope, hidden_low, normal_one, inverse_one, output, d_two, sums, hidden, total,
):
    step = pl.program_id(0)
    place = Place(subs)

    @pl.when(step == 0)
    def _():
        attn = dot_nt(ctx[...].T, w_out[...]) + out_bias[0:1].astype(F32)
        resid = both[place.c].astype(F32) + attn
        normal, inverse = normalize(resid)
        out = normal * gain[0:1].astype(F32) + shift[0:1].astype(F32)
        hidden[...] = out
        hidden_low[...] = out.astype(BF16)
        normal_one[...] = normal
        inverse_one[...] = inverse
        total[...] = jnp.zeros_like(total)
        seen = valid[...]
        sums[0:1] = column_sum(seen * resid * resid)
        sums[1:2] = column_sum(seen * attn * attn)

    pre = dot_nn(hidden_low[...], up[...]) + unit_bias[...]
    act, rise = gelu_pair(pre)
    act = act.astype(BF16)
    active[...] = act
    slope[...] = rise.astype(BF16)
    total[...] += dot_nt(act, down[...])

    @pl.when(step == pl.num_programs(0) - 1)
    def _():
        ffn = total[...] + out_bias[1:2].astype(F32)
        resid = hidden[...] + ffn
        normal, inverse = normalize(resid)
        output[...] = (normal * gain[1:2].astype(F32) + shift[1:2].astype(F32)).astype(BF16)
        seen = valid[...]
        grad = grad_out[...].astype(F32)
        back = norm_backward(grad, normal, inverse, gain[1:2].astype(F32))
        d_two[...] = back
        sums[2:3] = column_sum(seen * ffn * ffn)
        sums[3:4] = column_sum(seen * resid * resid)
        sums[4:5] = column_sum(grad * normal)
        sums[5:6] = column_sum(grad)
        sums[6:7] = column_sum(back.astype(BF16).astype(F32))
        sums[7:8] = jnp.zeros_like(sums[7:8]) + jnp.sum(seen) * (1.0 / seen.shape[0])


def ffn_forward(subs, both, ctx, w_out, up, down, unit_bias, out_bias, gain, shift, valid, grad_out):
    _, rows, width = both.shape
    units = up.shape[1]
    whole = lambda a: pl.BlockSpec(a.shape, lambda i: (0,) * a.ndim, pipeline_mode=pl.Buffered(1))
    fixed = lambda r, w: pl.BlockSpec((r, w), lambda i: (0, 0), pipeline_mode=pl.Buffered(1))
    wide = lambda r: pl.BlockSpec((r, BLOCK), lambda i: (0, i))
    return pl.pallas_call(
        functools.partial(ffn_forward_kernel, subs),
        grid=(units // BLOCK,),
        out_shape=[
            jax.ShapeDtypeStruct((rows, units), BF16),
            jax.ShapeDtypeStruct((rows, units), BF16),
            jax.ShapeDtypeStruct((rows, width), BF16),
            jax.ShapeDtypeStruct((rows, width), F32),
            jax.ShapeDtypeStruct((rows, 1), F32),
            jax.ShapeDtypeStruct((rows, width), BF16),
            jax.ShapeDtypeStruct((rows, width), F32),
            jax.ShapeDtypeStruct((8, width), F32),
        ],
        in_specs=[whole(both), whole(ctx), whole(w_out), wide(width), wide(width), wide(1)]
        + [whole(a) for a in (out_bias, gain, shift, valid, grad_out)],
        out_specs=[
            wide(rows),
            wide(rows),
            fixed(rows, width),
            fixed(rows, width),
            fixed(rows, 1),
            fixed(rows, width),
            fixed(rows, width),
            fixed(8, width),
        ],
        scratch_shapes=[pltpu.VMEM((rows, width), F32), pltpu.VMEM((rows, width), F32)],
        compiler_params=pltpu.CompilerParams(vmem_limit_bytes=VMEM_LIMIT),
        cost_estimate=pl.CostEstimate(
            flops=2 * rows * width * (width + 2 * units),
            bytes_accessed=2 * width * (width + 2 * units) + 4 * rows * units,
            transcendentals=rows * units,
        ),
        name="ffn_forward",
    )(both, ctx, w_out, up, down, unit_bias, out_bias, gain, shift, valid, grad_out)


def ffn_backward_kernel(
    d_two, hidden_low, active, slope, up, down, ctx, w_out, gain, normal_one, inverse_one,
    up_part, down_part, bias_part, d_one, d_ctx, out_part, sums, d_low, d_turned, hidden_turned, total,
):
    step = pl.program_id(0)

    @pl.when(step == 0)
    def _():
        low = d_two[...].astype(BF16)
        d_low[...] = low
        d_turned[...] = low.T
        hidden_turned[...] = hidden_low[...].T
        total[...] = d_two[...]

    d_pre = (dot_nn(d_low[...], down[...]) * slope[...].astype(F32)).astype(BF16)
    bias_part[...] = column_sum(d_pre.astype(F32))
    up_part[...] = dot_nn(hidden_turned[...], d_pre).astype(BF16)
    down_part[...] = dot_nn(d_turned[...], active[...]).astype(BF16)
    total[...] += dot_nt(d_pre, up[...])

    @pl.when(step == pl.num_programs(0) - 1)
    def _():
        grad = total[...]
        normal = normal_one[...]
        back = norm_backward(grad, normal, inverse_one[...], gain[0:1].astype(F32))
        d_one[...] = back
        low = back.astype(BF16)
        d_ctx[...] = dot_nt(w_out[...].T, low).astype(BF16)
        out_part[...] = dot_nt(low.T, ctx[...]).astype(BF16)
        sums[...] = jnp.zeros_like(sums)
        sums[0:1] = column_sum(grad * normal)
        sums[1:2] = column_sum(grad)
        sums[2:3] = column_sum(low.astype(F32))


def ffn_backward(d_two, hidden_low, active, slope, up, down, ctx, w_out, gain, normal_one, inverse_one):
    rows, width = d_two.shape
    units = up.shape[1]
    whole = lambda a: pl.BlockSpec(a.shape, lambda i: (0,) * a.ndim, pipeline_mode=pl.Buffered(1))
    fixed = lambda r, w: pl.BlockSpec((r, w), lambda i: (0, 0), pipeline_mode=pl.Buffered(1))
    wide = lambda r: pl.BlockSpec((r, BLOCK), lambda i: (0, i))
    return pl.pallas_call(
        ffn_backward_kernel,
        grid=(units // BLOCK,),
        out_shape=[
            jax.ShapeDtypeStruct((width, units), BF16),
            jax.ShapeDtypeStruct((width, units), BF16),
            jax.ShapeDtypeStruct((1, units), F32),
            jax.ShapeDtypeStruct((rows, width), F32),
            jax.ShapeDtypeStruct((width, rows), BF16),
            jax.ShapeDtypeStruct((width, width), BF16),
            jax.ShapeDtypeStruct((8, width), F32),
        ],
        in_specs=[whole(d_two), whole(hidden_low), wide(rows), wide(rows), wide(width), wide(width)]
        + [whole(a) for a in (ctx, w_out, gain, normal_one, inverse_one)],
        out_specs=[
            wide(width),
            wide(width),
            wide(1),
            fixed(rows, width),
            fixed(width, rows),
            fixed(width, width),
            fixed(8, width),
        ],
        scratch_shapes=[
            pltpu.VMEM((rows, width), BF16),
            pltpu.VMEM((width, rows), BF16),
            pltpu.VMEM((width, rows), BF16),
            pltpu.VMEM((rows, width), F32),
        ],
        compiler_params=pltpu.CompilerParams(vmem_limit_bytes=VMEM_LIMIT),
        cost_estimate=pl.CostEstimate(
            flops=4 * rows * width * (width + 2 * units),
            bytes_accessed=2 * width * (3 * width + 4 * units) + 4 * rows * units,
            transcendentals=0,
        ),
        name="ffn_backward",
    )(d_two, hidden_low, active, slope, up, down, ctx, w_out, gain, normal_one, inverse_one)


def body(
    layer_input,
    grad_out,
    segment,
    entity,
    valid_mask,
    query_weight,
    key_value_weight,
    attn_bias,
    out_weight,
    out_bias,
    ln_gain,
    ln_bias,
    up_weight,
    ffn_bias,
    down_weight,
):
    rows, width = layer_input.shape
    length = segment.shape[0]
    rank = lax.axis_index("tensor")
    subs = lax.axis_size("dp") // GRID
    core = (lax.axis_index("dp") // subs) % 2
    moved = rank != core
    start = core * rows
    pairs = lax.axis_size("tensor")
    trades = []
    for d in range(lax.axis_size("dp")):
        other = d + subs if (d // subs) % 2 == 0 else d - subs
        y = 1 - (d // subs) % 2
        trades.append((d * pairs + y, other * pairs + 1 - y))
    def trade(own):
        got = lax.ppermute(own, ("dp", "tensor"), trades)
        return jnp.where(moved, got, own)

    shards = [
        query_weight,
        key_value_weight,
        out_weight.T[None],
        up_weight[None],
        down_weight.T[None],
    ]
    groups = [[b * subs + s for s in range(subs)] for b in range(GRID)]
    if subs > 1:
        shards = [
            lax.all_gather(s, "dp", axis=1, tiled=True, axis_index_groups=groups) for s in shards
        ]
    shards = [shards[1], shards[0]] + shards[2:]
    units = pairs * ffn_bias.shape[0]
    cols = attn_bias.shape[1]
    bias_rows = jnp.concatenate([attn_bias, ffn_bias.reshape(-1, cols)]).astype(F32)
    used = bias_rows.shape[0]
    bias_rows = jnp.pad(bias_rows, ((0, -used % 16), (0, 0)))
    facts = jnp.pad(jnp.stack([segment, entity, valid_mask]), ((0, 5), (0, 0)))
    (w_kv, w_q, w_out_t, w_up, w_down_t), (both, biases, pair_facts) = gather_weights(
        subs, shards, 3, layer_input, bias_rows, facts
    )
    w_kv, w_q, w_out_t = as_matrix(w_kv), as_matrix(w_q), as_matrix(w_out_t)[0]
    context_t, probs, query_word, query_ent, keys, values, w_up, w_down_t = attention_forward(
        subs, both, w_q, w_kv, biases, pair_facts, w_up, w_down_t
    )
    w_up, w_down_t = as_matrix(w_up)[0], as_matrix(w_down_t)[0]
    ffn_bias_full = biases[:, 5:used].reshape(units)
    facts = lax.dynamic_index_in_dim(pair_facts, rank, 0, keepdims=False)

    valid_own = lax.dynamic_slice_in_dim(facts[2], start, rows).astype(F32)[:, None]
    grad_out, context_t = lax.optimization_barrier((grad_out, context_t))
    active, slope, hidden_low, normal_one, inverse_one, result, d_two, sums_two = ffn_forward(
        subs, both, context_t, w_out_t, w_up, w_down_t, ffn_bias_full[None], out_bias, ln_gain, ln_bias, valid_own,
        trade(grad_out),
    )
    output = trade(result)
    up_part, down_part, ffn_bias_part, d_one, d_context_t, out_part, sums_one = ffn_backward(
        d_two, hidden_low, active, slope, w_up, w_down_t, context_t, w_out_t, ln_gain, normal_one, inverse_one
    )

    query_part, kv_part, input_grad, q_bias, v_bias, down_piece, up_piece = attention_backward(
        subs, both, pair_facts, probs, query_word, query_ent, keys, values, context_t, d_context_t, w_q, w_kv, d_one,
        down_part[None], up_part[None],
    )
    returned = lax.ppermute(input_grad.astype(BF16), ("dp", "tensor"), trades)
    input_grad = jnp.where(moved, returned.astype(F32), input_grad)

    small = jnp.concatenate([sums_one.reshape(-1), sums_two.reshape(-1), q_bias[:4].reshape(-1), v_bias[0], ffn_bias_part[0]])
    padded = -(-small.shape[0] // (8 * LANES)) * 8 * LANES
    small = jnp.pad(small, (0, padded - small.shape[0])).reshape(-1, LANES)
    sums, small_sum = scatter_gradients(
        subs, [down_piece, up_piece], [out_part[None], query_part, kv_part], small
    )
    if subs > 1:
        sums = [
            lax.psum_scatter(s, "dp", scatter_dimension=1, tiled=True, axis_index_groups=groups)
            for s in sums
        ]
        small_sum = lax.psum(small_sum, "dp", axis_index_groups=groups)
    down_sum, up_sum, out_sum, query_sum, kv_sum = sums
    flat = small_sum.reshape(-1)
    norms = flat[: 16 * width].reshape(16, width)
    gains, shifts, out_biases = (jnp.stack([norms[i], norms[12 + i]]) for i in range(3))
    attn_biases = flat[16 * width : 21 * width].reshape(5, width)
    ffn_biases = flat[21 * width : 21 * width + units]
    squares = jnp.sum(norms[8:12], 1)
    real = norms[15, 0] * rows
    half = ffn_bias.shape[0]
    return (
        output,
        input_grad,
        jnp.sqrt(squares / (real * width)),
        query_sum,
        kv_sum,
        lax.dynamic_slice_in_dim(attn_biases, rank * cols, cols, 1),
        out_sum[0].T,
        out_biases,
        gains,
        shifts,
        up_sum[0],
        lax.dynamic_slice_in_dim(ffn_biases, rank * half, half, 0),
        down_sum[0].T,
    )


def solution(mesh):
    placed = (
        P(("dp", "tensor"), None),
        P(("dp", "tensor"), None),
        P("dp"),
        P("dp"),
        P("dp"),
        P(None, "dp", "tensor"),
        P(None, "dp", "tensor"),
        P(None, "tensor"),
        P("tensor", "dp"),
        P(),
        P(),
        P(),
        P("dp", "tensor"),
        P("tensor"),
        P("tensor", "dp"),
    )
    return jax.shard_map(
        body,
        mesh=mesh,
        in_specs=placed,
        out_specs=(
            P(("dp", "tensor"), None),
            P(("dp", "tensor"), None),
            P(),
            P(None, "dp", "tensor"),
            P(None, "dp", "tensor"),
            P(None, "tensor"),
            P("tensor", "dp"),
            P(),
            P(),
            P(),
            P("dp", "tensor"),
            P("tensor"),
            P("tensor", "dp"),
        ),
        check_vma=False,
    )
```

```python
import functools

import jax
import jax.numpy as jnp
from jax import lax
from jax.experimental import pallas as pl
from jax.experimental.pallas import tpu as pltpu
from jax.sharding import PartitionSpec as P

HEAD = 64
EPS = 1e-06
NEG = -1e30
GRID = 16
LANES = 128
MESH = pl.DeviceIdType.MESH
BF16 = jnp.bfloat16
F32 = jnp.float32
VMEM_LIMIT = 60 * 1024 * 1024


BLOCK = 512
TAIL = 0.34
TAIL_Q = (
    0.1918165616711201,
    0.1920366827922902,
    0.17827181747742213,
    0.1748548010854969,
    0.05944614604180367,
    0.27541659722682194,
    -0.27820700083503797,
    0.4016320911891782,
    -0.24597742961536673,
    0.050709736470982834,
)


def gelu_pair(v):
    size = jnp.abs(v)
    t = 1.0 / (1.0 + (TAIL * 0.5**0.5) * size)
    q = jnp.full_like(v, TAIL_Q[-1])
    for coefficient in TAIL_Q[-2::-1]:
        q = q * t + coefficient
    bell = jnp.exp(-0.5 * (v * v))
    tail = 0.5 * (bell * (t * q))
    cdf = jnp.where(v < 0, tail, 1.0 - tail)
    return v * cdf, cdf + v * (bell * 0.3989422804014327)


def normalize(resid):
    center = resid - jnp.mean(resid, -1, keepdims=True)
    inverse = lax.rsqrt(jnp.mean(center * center, -1, keepdims=True) + EPS)
    return center * inverse, inverse


def norm_backward(grad, normal, inverse, gain):
    scaled = grad * gain
    return inverse * (
        scaled
        - jnp.mean(scaled, -1, keepdims=True)
        - normal * jnp.mean(scaled * normal, -1, keepdims=True)
    )


def column_sum(a):
    return jnp.sum(a, 0, keepdims=True)


class Place:
    def __init__(self, subs):
        rank = lax.axis_index("dp")
        self.subs = subs
        self.sub = rank % subs
        block = rank // subs
        self.z = block // 4
        self.turns = [(self.z + step) % 4 for step in range(4)]
        self.x = (block // 2) % 2
        self.c = block % 2
        self.y = lax.axis_index("tensor")
        self.moved = self.y != self.c
        self.x1 = jnp.where(self.c == 0, 1 - self.x, self.x)
        self.y1 = jnp.where(self.c == 0, self.y, 1 - self.y)
        self.x2 = jnp.where(self.c == 0, self.x, 1 - self.x)
        self.y2 = jnp.where(self.c == 0, 1 - self.y, self.y)

    def device(self, z=None, x=None, c=None, y=None):
        z = self.z if z is None else z
        x = self.x if x is None else x
        c = self.c if c is None else c
        y = self.y if y is None else y
        return (((z * 2 + x) * 2 + c) * self.subs + self.sub, y)

    def z_peer(self, step):
        return self.device(z=(self.z + step) % 4)

    def first(self):
        return self.device(x=self.x1, y=self.y1)

    def second(self):
        return self.device(x=self.x2, y=self.y2)

    def sibling(self):
        return self.device(c=1 - self.c)

    def across(self):
        return self.device(y=1 - self.y)

    def transposed(self):
        return self.device(c=1 - self.c, y=1 - self.y)

    def pieces(self):
        return (
            (self.x, self.y),
            (self.x1, self.y1),
            (self.x2, self.y2),
            (1 - self.x, 1 - self.y),
        )


def entry_barrier(place):
    barrier = pltpu.get_barrier_semaphore()
    peers = [place.z_peer(step) for step in (1, 2, 3)]
    peers += [place.device(x=1 - place.x), place.across(), place.sibling(), place.transposed()]
    for peer in peers:
        pl.semaphore_signal(barrier, inc=1, device_id=peer, device_id_type=MESH)
    pl.semaphore_wait(barrier, len(peers))


def remote(src, dst, send, recv, peer):
    return pltpu.make_async_remote_copy(
        src_ref=src, dst_ref=dst, send_sem=send, recv_sem=recv, device_id=peer, device_id_type=MESH
    )


class Trade:
    def __init__(self, place, own, got, sems):
        self.moved = place.moved
        self.kept = pltpu.make_async_copy(own, got, sems.at[2])
        self.swap = remote(own, got, sems.at[0], sems.at[1], place.transposed())

    def start(self):
        @pl.when(self.moved)
        def _():
            self.swap.start()

        @pl.when(jnp.logical_not(self.moved))
        def _():
            self.kept.start()

    def finish(self):
        @pl.when(self.moved)
        def _():
            self.swap.wait()

        @pl.when(jnp.logical_not(self.moved))
        def _():
            self.kept.wait()


class Gather:
    def __init__(self, place, shard, full, send, recv, local=None, whole=True):
        self.place, self.shard, self.full, self.whole = place, shard, full, whole
        self.send, self.recv, self.local = send, recv, local
        self.w = full.shape[-1] // 2

    def cols(self, y):
        return pl.ds(pl.multiple_of(y * self.w, LANES), self.w)

    def piece(self, spot, c):
        x, y = spot
        return self.full.at[:, :, x, c, :, self.cols(y)]

    def copy(self, index, src, dst, peer):
        remote(src, dst, self.send.at[index], self.recv.at[index], peer).start()

    def arrive(self, index, ref):
        remote(ref, ref, self.send.at[index], self.recv.at[index], self.place.sibling()).wait_recv()

    def gone(self, index, ref):
        remote(ref, ref, self.send.at[index], self.recv.at[index], self.place.sibling()).wait_send()

    def own(self, z):
        p = self.place
        return self.full.at[:, z, p.x, p.c, :, self.cols(p.y)]

    def stage1(self):
        p = self.place
        self.kept = pltpu.make_async_copy(self.shard, self.own(p.z), self.local)
        self.kept.start()
        for step in (1, 2, 3):
            self.copy(step - 1, self.shard, self.own(p.z), p.z_peer(step))

    def land(self):
        p = self.place
        self.kept.wait()
        for step in (1, 2, 3):
            self.arrive(step - 1, self.own((p.z + 4 - step) % 4))

    def settle(self):
        self.land()
        for index in range(3):
            self.gone(index, self.shard)

    def spread(self):
        p = self.place
        mine = self.piece(p.pieces()[0], p.c)
        self.copy(3, mine, mine, p.first())
        self.copy(4, mine, mine, p.second())
        self.copy(6, mine, mine, p.sibling())

    def stage2(self):
        self.land()
        self.spread()

    def stage3(self):
        p = self.place
        got = self.piece(p.pieces()[1], p.c)
        self.arrive(3, got)
        self.copy(5, got, got, p.second())
        self.copy(7, got, got, p.sibling())

    def stage4(self):
        p = self.place
        for index, spot in ((4, 2), (5, 3)):
            got = self.piece(p.pieces()[spot], p.c)
            self.arrive(index, got)
            self.copy(index + 4, got, got, p.sibling())

    def stage5(self):
        p = self.place
        spots = p.pieces()
        for index, spot in ((6, 0), (7, 2), (8, 1), (9, 3)):
            self.arrive(index, self.piece(spots[spot], 1 - p.c))
        for index in range(3, 10):
            self.gone(index, self.piece(spots[0], p.c))

    def last(self):
        self.stage5()
        for index in range(3):
            self.gone(index, self.shard)

    def stages(self):
        if not self.whole:
            return [self.stage1, self.settle]
        return [self.stage1, self.stage2, self.stage3, self.stage4, self.last]


def wavefront(movers):
    lists = [mover.stages() for mover in movers]
    depth = max(len(stages) for stages in lists)
    order = []
    for time in range(len(lists) + depth - 1):
        for index in range(len(lists)):
            stage = time - index
            if 0 <= stage < len(lists[index]):
                order.append(lists[index][stage])
    return order


class Share:
    def __init__(self, source, pair, index, peer, sems):
        self.kept = pltpu.make_async_copy(source, pair.at[index], sems.at[2])
        self.sent = remote(source, pair.at[index], sems.at[0], sems.at[1], peer)

    def start(self):
        self.kept.start()
        self.sent.start()

    def finish(self):
        self.kept.wait()
        self.sent.wait()


class Rows:
    def __init__(self, place, rows, both, sems):
        p = place
        half = both.at[p.c]
        self.moved = p.moved
        self.kept = pltpu.make_async_copy(rows, half, sems.at[4])
        self.swap = remote(rows, both.at[p.y], sems.at[0], sems.at[1], p.transposed())
        self.swapped = remote(half, half, sems.at[0], sems.at[1], p.transposed())
        self.share = remote(rows, half, sems.at[2], sems.at[3], p.sibling())
        self.relay = remote(half, half, sems.at[2], sems.at[3], p.sibling())
        other = both.at[1 - p.c]
        self.other = remote(other, other, sems.at[2], sems.at[3], p.sibling())

    def start(self):
        @pl.when(self.moved)
        def _():
            self.swap.start()

        @pl.when(jnp.logical_not(self.moved))
        def _():
            self.kept.start()
            self.share.start()

    def forward(self):
        @pl.when(self.moved)
        def _():
            self.swapped.wait_recv()
            self.relay.start()

    def finish(self):
        @pl.when(self.moved)
        def _():
            self.swap.wait_send()
            self.relay.wait_send()

        @pl.when(jnp.logical_not(self.moved))
        def _():
            self.kept.wait()
            self.share.wait_send()

        self.other.wait_recv()


def gather_kernel(subs, count, wholes, *refs):
    shards, (rows, bias, facts) = refs[:count], refs[count : count + 3]
    fulls, (both, biases, pair_facts) = refs[count + 3 : 2 * count + 3], refs[2 * count + 3 : 2 * count + 6]
    send, recv, local, row_sems, share_sems = refs[2 * count + 6 :]
    place = Place(subs)
    entry_barrier(place)
    tokens = Rows(place, rows, both, row_sems)
    shares = [
        Share(facts, pair_facts, place.c, place.sibling(), share_sems.at[0]),
        Share(bias, biases, place.y, place.across(), share_sems.at[1]),
    ]
    tokens.start()
    for share in shares:
        share.start()
    movers = [
        Gather(place, shards[i], fulls[i], send.at[i], recv.at[i], local.at[i], i < wholes)
        for i in range(count)
    ]
    for mover in movers[:2]:
        mover.stage1()
    steps = [s for s in wavefront(movers) if s.__func__ is not Gather.stage1]
    late = [s for s in steps if s.__func__ is Gather.settle]
    landed = 0
    for index, step in enumerate([s for s in steps if s not in late] + late):
        step()
        if index == 1:
            tokens.forward()
        if step.__func__ in (Gather.stage2, Gather.settle):
            landed += 1
            if landed + 1 < count:
                movers[landed + 1].stage1()
    tokens.finish()
    for share in shares:
        share.finish()


def gather_weights(subs, shards, wholes, rows, bias, facts):
    count = len(shards)
    outs = [
        jax.ShapeDtypeStruct((s.shape[0], 4, 2, 2, s.shape[1], 2 * s.shape[2]), BF16) for s in shards
    ]
    outs += [jax.ShapeDtypeStruct((2,) + a.shape, a.dtype) for a in (rows, bias, facts)]
    results = pl.pallas_call(
        functools.partial(gather_kernel, subs, count, wholes),
        out_shape=outs,
        in_specs=[pl.BlockSpec(memory_space=pltpu.VMEM)] * (count + 3),
        out_specs=[pl.BlockSpec(memory_space=pl.ANY)] * (count + 3),
        scratch_shapes=[
            pltpu.SemaphoreType.DMA((count, 10)),
            pltpu.SemaphoreType.DMA((count, 10)),
            pltpu.SemaphoreType.DMA((count,)),
            pltpu.SemaphoreType.DMA((5,)),
            pltpu.SemaphoreType.DMA((2, 3)),
        ],
        compiler_params=pltpu.CompilerParams(
            collective_id=0, has_side_effects=True, vmem_limit_bytes=VMEM_LIMIT
        ),
        name="gather_weights",
    )(*shards, rows, bias, facts)
    return results[:count], results[count:]


def as_matrix(full):
    return full.reshape(full.shape[0], GRID * full.shape[4], full.shape[5])


class Last:
    def __init__(self, place, piece, total, from_z, send, recv):
        self.place, self.piece, self.total, self.from_z = place, piece, total, from_z
        self.send, self.recv = send, recv

    def start(self):
        p = self.place
        for step in (1, 2, 3):
            remote(
                self.piece.at[:, p.turns[step]],
                self.from_z.at[step - 1],
                self.send.at[step - 1],
                self.recv.at[step - 1],
                p.z_peer(step),
            ).start()

    def finish(self):
        p = self.place
        for step in (0, 1, 2):
            slot = self.from_z.at[step]
            remote(slot, slot, self.send.at[step], self.recv.at[step], p.sibling()).wait()

        def step(i, carry):
            total = self.piece[i, p.z].astype(F32)
            for s in range(3):
                total = total + self.from_z[s, i].astype(F32)
            self.total[i] = total
            return carry

        lax.fori_loop(0, self.total.shape[0], step, 0)


class Scatter:
    def __init__(self, place, part, mine, from_core, from_second, from_first, send, recv, local):
        self.place, self.part = place, part
        self.mine, self.from_core = mine, from_core
        self.from_second, self.from_first = from_second, from_first
        self.send, self.recv, self.local = send, recv, local
        self.m, _, self.rows, self.w = from_first.shape

    def cols(self, y):
        return pl.ds(pl.multiple_of(y * self.w, LANES), self.w)

    def copy(self, index, src, dst, peer):
        remote(src, dst, self.send.at[index], self.recv.at[index], peer).start()

    def arrive(self, index, ref):
        remote(ref, ref, self.send.at[index], self.recv.at[index], self.place.sibling()).wait_recv()

    def drain(self):
        for index in range(7):
            remote(
                self.from_first, self.from_first, self.send.at[index], self.recv.at[index], self.place.sibling()
            ).wait_send()

    def add(self, target, source):
        m = self.m

        def step(index, carry):
            i, z = index // 4, index % 4
            target[i, z] = (target[i, z].astype(F32) + source[i, z].astype(F32)).astype(BF16)
            return carry

        lax.fori_loop(0, m * 4, step, 0)

    def keep(self, slot, spot):
        x, y = self.place.pieces()[spot]
        source = self.part.at[:, :, x, self.place.c, :, self.cols(y)]
        return pltpu.make_async_copy(source, self.mine.at[slot], self.local.at[slot])

    def stage1(self):
        p = self.place
        spots = p.pieces()
        for slot, (here, there) in enumerate(((3, 3), (2, 1), (1, 2), (0, 0))):
            self.keep(slot, here).start()
            x, y = spots[there]
            self.copy(
                slot,
                self.part.at[:, :, x, 1 - p.c, :, self.cols(y)],
                self.from_core.at[slot],
                p.sibling(),
            )

    def joined(self, slot):
        self.keep(slot, 3 - slot).wait()
        self.arrive(slot, self.from_core.at[slot])
        self.add(self.mine.at[slot], self.from_core.at[slot])

    def stage2(self):
        p = self.place
        for slot in (0, 1):
            self.joined(slot)
            self.copy(4 + slot, self.mine.at[slot], self.from_second.at[slot], p.second())
        for slot in (2, 3):
            self.joined(slot)

    def stage3(self):
        p = self.place
        self.arrive(4, self.from_second.at[0])
        self.add(self.mine.at[2], self.from_second.at[0])
        self.copy(6, self.mine.at[2], self.from_first, p.first())
        self.arrive(5, self.from_second.at[1])
        self.add(self.mine.at[3], self.from_second.at[1])

    def stage4(self):
        self.arrive(6, self.from_first)
        self.add(self.mine.at[3], self.from_first)


class Sum:
    def __init__(self, place, source, total, box, send, recv):
        self.place, self.source, self.total = place, source, total
        self.box, self.send, self.recv = box, send, recv

    def hop(self, index):
        p = self.place
        flip = p.z + 1 - 2 * (p.z % 2)
        far = (p.z + 2) % 4
        peers = (p.sibling(), p.device(x=1 - p.x), p.device(y=1 - p.y), p.device(z=flip), p.device(z=far))
        if index < 5:
            src = self.source if index == 0 else self.total.at[index - 1]
            step = remote(src, self.box.at[index], self.send.at[index], self.recv.at[index], peers[index])
            step.start()
            self.flying = step

    def land(self, index):
        self.flying.wait()
        src = self.source if index == 0 else self.total.at[index - 1]
        self.total[index] = src[...] + self.box[index]

    def stages(self):
        def first():
            self.hop(0)

        def later(index):
            self.land(index)
            self.hop(index + 1)

        return [first] + [functools.partial(later, i) for i in range(5)]


def scatter_scratch(shape):
    m, rows, w = shape
    return [
        pltpu.VMEM((4, m, 4, rows, w), BF16),
        pltpu.VMEM((4, m, 4, rows, w), BF16),
        pltpu.VMEM((2, m, 4, rows, w), BF16),
        pltpu.VMEM((m, 4, rows, w), BF16),
        pltpu.SemaphoreType.DMA((7,)),
        pltpu.SemaphoreType.DMA((7,)),
        pltpu.SemaphoreType.DMA((4,)),
    ]


def last_scratch(shape):
    return [
        pltpu.VMEM((3,) + shape, BF16),
        pltpu.SemaphoreType.DMA((3,)),
        pltpu.SemaphoreType.DMA((3,)),
    ]


def as_shards(part):
    m, rows, w = part.shape
    return part.reshape(m, 4, 2, 2, rows // GRID, w)


def scatter_kernel(subs, early, count, *refs):
    pieces, parts, (small, input_grad, input_low) = refs[:early], refs[early : early + count], refs[early + count :][:3]
    refs = refs[early + count + 3 :]
    totals, (small_total, result, traded, trade_sems) = refs[: early + count], refs[early + count :][:4]
    refs = refs[early + count + 4 :]
    lasts, refs = refs[: 3 * (early + count)], refs[3 * (early + count) :]
    place = Place(subs)
    entry_barrier(place)
    movers = [Scatter(place, parts[i], *refs[7 * i : 7 * i + 7]) for i in range(count)]
    sources = list(pieces) + [mover.mine.at[3] for mover in movers]
    ends = [Last(place, sources[i], totals[i], *lasts[3 * i : 3 * i + 3]) for i in range(early + count)]
    running, box, send, recv = refs[7 * count :]
    small_sum = Sum(place, small, running, box, send, recv)
    trade = Trade(place, input_low, traded, trade_sems)
    for mover in movers:
        mover.stage1()
    for end in ends[:early]:
        end.start()
    trade.start()
    extra = small_sum.stages()
    steps = []
    for time in range(count + 4):
        for index in range(count):
            stage = time - index
            if 0 <= stage < 5:
                mover, end = movers[index], ends[early + index]
                steps.append((mover.stage2, mover.stage3, mover.stage4, end.start, end.finish)[stage])
    for index, step in enumerate(steps):
        if index < len(extra):
            extra[index]()
        step()
    for step in extra[len(steps) :]:
        step()
    for end in ends[:early]:
        end.finish()
    for mover in movers:
        mover.drain()
    small_total[...] = running[4]
    trade.finish()
    result[...] = jnp.where(place.moved, traded[...].astype(F32), input_grad[...])


def scatter_gradients(subs, pieces, parts, small, input_grad, input_low):
    early, count = len(pieces), len(parts)
    shaped = [as_shards(p) for p in parts]
    shapes = [(p.shape[0],) + p.shape[2:] for p in pieces]
    whole = [(p.shape[0], p.shape[4], p.shape[5] // 2) for p in shaped]
    outs = [jax.ShapeDtypeStruct(s, F32) for s in shapes + whole]
    outs += [jax.ShapeDtypeStruct(small.shape, F32), jax.ShapeDtypeStruct(input_grad.shape, F32)]
    scratch = [pltpu.VMEM(input_low.shape, BF16), pltpu.SemaphoreType.DMA((3,))]
    for s in shapes + whole:
        scratch += last_scratch(s)
    for s in whole:
        scratch += scatter_scratch(s)
    scratch += [
        pltpu.VMEM((5,) + small.shape, F32),
        pltpu.VMEM((5,) + small.shape, F32),
        pltpu.SemaphoreType.DMA((5,)),
        pltpu.SemaphoreType.DMA((5,)),
    ]
    local = pl.BlockSpec(memory_space=pltpu.VMEM)
    results = pl.pallas_call(
        functools.partial(scatter_kernel, subs, early, count),
        out_shape=outs,
        in_specs=[local] * early + [pl.BlockSpec(memory_space=pl.ANY)] * count + [local] * 3,
        out_specs=[local] * (early + count + 2),
        scratch_shapes=scratch,
        compiler_params=pltpu.CompilerParams(
            collective_id=1, has_side_effects=True, vmem_limit_bytes=VMEM_LIMIT
        ),
        name="scatter_gradients",
    )(*pieces, *shaped, small, input_grad, input_low)
    return results[:-2], results[-2], results[-1]


def head_lanes(half):
    lane = lax.broadcasted_iota(jnp.int32, (1, LANES), 1)
    return (lane // HEAD) == half


def dot_nt(a, b):
    return lax.dot_general(a, b, (((1,), (1,)), ((), ())), preferred_element_type=F32)


def dot_nn(a, b):
    return lax.dot_general(a, b, (((1,), (0,)), ((), ())), preferred_element_type=F32)


def forward_kernel(
    subs, both, wq, wkv, biases, facts, up_in, down_in,
    ctx, probs, word, entity, keys, values, up, down, mask, column, send, recv,
):
    place = Place(subs)
    step = pl.program_id(0)
    length, rows = mask.shape
    movers = [Gather(place, None, full, send.at[i], recv.at[i]) for i, full in enumerate((up, down))]
    own = pl.ds(pl.multiple_of(place.c * rows, LANES), rows)

    @pl.when(step == 0)
    def _():
        entry_barrier(place)
        for mover in movers:
            mover.spread()
        column[...] = facts[place.y].T
        spot = lax.broadcasted_iota(jnp.int32, (length, rows), 0)
        here = lax.broadcasted_iota(jnp.int32, (length, rows), 1) + place.c * rows
        same = column[:, 0:1] == facts[place.y, 0:1, own]
        seen = (column[:, 2:3] == 1) | (spot == here)
        mask[...] = jnp.where(same & seen, 0.0, NEG)

    @pl.when(step == 3)
    def _():
        movers[0].stage3()

    @pl.when(step == 5)
    def _():
        movers[1].stage3()

    tokens = both[...].reshape(length, both.shape[2])
    mine = both[place.c]
    bias = biases[0]
    row_ent = column[own, 1:2] == 1
    to_word = dot_nn(mine, jnp.concatenate([wq[0], wq[2]], axis=1))
    to_ent = dot_nn(mine, jnp.concatenate([wq[1], wq[3]], axis=1))
    scale = HEAD ** (-0.5)
    query_word = jnp.where(row_ent, to_word[:, LANES:] + bias[2:3], to_word[:, :LANES] + bias[0:1])
    query_ent = jnp.where(row_ent, to_ent[:, LANES:] + bias[3:4], to_ent[:, :LANES] + bias[1:2])
    word[...] = query_word.astype(BF16) * BF16(scale)
    entity[...] = query_ent.astype(BF16) * BF16(scale)
    pair = dot_nn(tokens, jnp.concatenate([wkv[0], wkv[1]], axis=1))
    key = pair[:, :LANES].astype(BF16)
    value = (pair[:, LANES:] + bias[4:5]).astype(BF16)
    keys[...] = key
    values[...] = value

    queries = jnp.concatenate([word[...], entity[...]], axis=1)
    ent = column[:, 1:2] == 1
    zero = jnp.zeros_like(key)
    turned = value.T
    for half in range(2):
        lanes = head_lanes(half)
        wide = jnp.concatenate(
            [jnp.where(lanes & ~ent, key, zero), jnp.where(lanes & ent, key, zero)], axis=1
        )
        scores = dot_nt(wide, queries) + mask[...]
        top = jnp.max(scores, axis=0, keepdims=True)
        expo = jnp.exp(scores - top)
        total = jnp.sum(expo, axis=0, keepdims=True)
        prob = (expo * (1.0 / total)).astype(BF16)
        probs[half] = prob
        ctx[half * HEAD : (half + 1) * HEAD, :] = dot_nn(
            turned[half * HEAD : (half + 1) * HEAD, :], prob
        ).astype(BF16)

    @pl.when(step == pl.num_programs(0) - 1)
    def _():
        for mover in movers:
            mover.stage4()
        for mover in movers:
            mover.stage5()


def attention_forward(subs, both, wq, wkv, biases, facts, up, down):
    _, rows, width = both.shape
    length = 2 * rows
    pairs = width // LANES
    span = biases.shape[2] // LANES
    block = lambda n: pl.BlockSpec((n, LANES), lambda i: (0, i))
    whole = lambda a: pl.BlockSpec(a.shape, lambda i: (0,) * a.ndim, pipeline_mode=pl.Buffered(1))
    cols = lambda a: pl.BlockSpec(a.shape[:2] + (LANES,), lambda i: (0, 0, i))
    anywhere = pl.BlockSpec(memory_space=pl.ANY)
    return pl.pallas_call(
        functools.partial(forward_kernel, subs),
        grid=(pairs,),
        out_shape=[
            jax.ShapeDtypeStruct((width, rows), BF16),
            jax.ShapeDtypeStruct((2 * pairs, length, rows), BF16),
            jax.ShapeDtypeStruct((rows, width), BF16),
            jax.ShapeDtypeStruct((rows, width), BF16),
            jax.ShapeDtypeStruct((length, width), BF16),
            jax.ShapeDtypeStruct((length, width), BF16),
            jax.ShapeDtypeStruct(up.shape, BF16),
            jax.ShapeDtypeStruct(down.shape, BF16),
        ],
        in_specs=[
            whole(both),
            cols(wq),
            cols(wkv),
            pl.BlockSpec((1, biases.shape[1], LANES), lambda i: (i // span, 0, i % span)),
            whole(facts),
            anywhere,
            anywhere,
        ],
        out_specs=[
            pl.BlockSpec((LANES, rows), lambda i: (i, 0)),
            pl.BlockSpec((2, length, rows), lambda i: (i, 0, 0)),
            block(rows),
            block(rows),
            block(length),
            block(length),
            anywhere,
            anywhere,
        ],
        scratch_shapes=[
            pltpu.VMEM((length, rows), F32),
            pltpu.VMEM((length, facts.shape[1]), jnp.int32),
            pltpu.SemaphoreType.DMA((2, 10)),
            pltpu.SemaphoreType.DMA((2, 10)),
        ],
        input_output_aliases={5: 6, 6: 7},
        compiler_params=pltpu.CompilerParams(
            collective_id=2, has_side_effects=True, vmem_limit_bytes=VMEM_LIMIT
        ),
        name="attention_forward",
    )(both, wq, wkv, biases, facts, up, down)


def backward_kernel(
    subs, both, facts, probs, word, entity, keys, values, ctx, dctx, wq, wkv, d_one, down_part, up_part,
    q_part, kv_part, input_grad, q_bias, v_bias, down_piece, up_piece, input_low,
    column, turned_rows, pair_grad, pair_got, pair_send, pair_recv, *scratch,
):
    place = Place(subs)
    step = pl.program_id(0)
    pairs = pl.num_programs(0) - 1
    rows = word.shape[0]
    movers = [Scatter(place, down_part, *scratch[:7]), Scatter(place, up_part, *scratch[7:])]
    own = pl.ds(pl.multiple_of(place.c * rows, LANES), rows)
    other = pl.ds(pl.multiple_of((1 - place.c) * rows, LANES), rows)

    @pl.when(step == 0)
    def _():
        entry_barrier(place)
        for mover in movers:
            mover.stage1()
        column[...] = facts[place.y].T
        turned_rows[...] = both[place.c].T
        input_grad[...] = d_one[...]

    @pl.when(step == 1)
    def _():
        movers[0].stage2()

    @pl.when(step == 2)
    def _():
        movers[1].stage2()

    @pl.when(step == 5)
    def _():
        movers[0].stage3()

    @pl.when(step < pairs)
    def _():
        queries = jnp.concatenate([word[...], entity[...]], axis=1)
        value = values[...]
        turned = keys[...].T
        ent = column[:, 1:2] == 1
        ent_lane = facts[place.y, 1:2, :] == 1
        own_ent = facts[place.y, 1:2, own] == 1
        grad = dctx[...]
        zero = jnp.zeros_like(value)
        dk, dv, dw, de = [], [], [], []
        for half in range(2):
            lanes = head_lanes(half)
            here = slice(half * HEAD, (half + 1) * HEAD)
            prob = probs[half]
            delta = jnp.sum(
                ctx[here, :].astype(F32) * grad[here, :].astype(F32), axis=0, keepdims=True
            )
            dprob = dot_nn(jnp.where(lanes, value, zero), grad)
            dscore = (prob.astype(F32) * (dprob - delta)).astype(BF16)
            key_t = turned[here, :]
            none = jnp.zeros_like(key_t)
            tall = jnp.concatenate(
                [jnp.where(ent_lane, none, key_t), jnp.where(ent_lane, key_t, none)], axis=0
            )
            dq = dot_nn(tall, dscore) * (HEAD ** (-0.5))
            dw.append(dq[:HEAD])
            de.append(dq[HEAD:])
            pair = dot_nn(dscore, queries)
            dk.append(jnp.where(ent, pair[:, LANES:], pair[:, :LANES]))
            dv.append(dot_nt(prob, grad))
        first = head_lanes(0)
        pair_grad[step, :, :LANES] = jnp.where(first, dk[0], dk[1]).astype(BF16)
        pair_grad[step, :, LANES:] = jnp.where(first, dv[0], dv[1]).astype(BF16)
        remote(
            pair_grad.at[step, other], pair_got.at[step], pair_send.at[step], pair_recv.at[step], place.sibling()
        ).start()
        d_word, d_ent = jnp.concatenate(dw, axis=0), jnp.concatenate(de, axis=0)
        empty = jnp.zeros_like(d_word)
        turned_grad = jnp.concatenate(
            [
                jnp.where(own_ent, empty, d_word),
                jnp.where(own_ent, empty, d_ent),
                jnp.where(own_ent, d_word, empty),
                jnp.where(own_ent, d_ent, empty),
            ],
            axis=0,
        ).astype(BF16)
        query_grad = turned_grad.T
        weights = jnp.concatenate([wq[m] for m in range(4)], axis=1)
        input_grad[...] += dot_nt(query_grad, weights)
        part = dot_nn(turned_rows[...], query_grad).astype(BF16)
        sums = column_sum(query_grad.astype(F32))
        for m in range(4):
            span = slice(m * LANES, (m + 1) * LANES)
            q_part[m] = part[:, span]
            q_bias[m : m + 1] = sums[:, span]

    @pl.when(step > 0)
    def _():
        before = step - 1
        remote(
            pair_got.at[before], pair_got.at[before], pair_send.at[before], pair_recv.at[before], place.sibling()
        ).wait()
        grad = (pair_grad[before, own].astype(F32) + pair_got[before].astype(F32)).astype(BF16)
        weights = jnp.concatenate([wkv[0], wkv[1]], axis=1)
        input_grad[...] += dot_nt(grad, weights)
        part = dot_nn(turned_rows[...], grad).astype(BF16)
        kv_part[0] = part[:, :LANES]
        kv_part[1] = part[:, LANES:]
        v_bias[0:1] = column_sum(grad[:, LANES:].astype(F32))

    @pl.when(step == pairs)
    def _():
        movers[1].stage3()
        for mover in movers:
            mover.stage4()
            mover.drain()
        down_piece[...] = movers[0].mine[3]
        up_piece[...] = movers[1].mine[3]
        input_low[...] = input_grad[...].astype(BF16)


def attention_backward(subs, both, facts, probs, word, entity, keys, values, ctx, dctx, wq, wkv, d_one, down_part, up_part):
    _, rows, width = both.shape
    length = 2 * rows
    pairs = width // LANES
    block = lambda n: pl.BlockSpec((n, LANES), lambda i: (0, jnp.minimum(i, pairs - 1)))
    behind = lambda n: pl.BlockSpec((n, LANES), lambda i: (0, jnp.maximum(i - 1, 0)))
    turned = pl.BlockSpec((LANES, rows), lambda i: (jnp.minimum(i, pairs - 1), 0))
    whole = lambda a: pl.BlockSpec(a.shape, lambda i: (0,) * a.ndim, pipeline_mode=pl.Buffered(1))
    q_cols = pl.BlockSpec((4, width, LANES), lambda i: (0, 0, jnp.minimum(i, pairs - 1)))
    kv_cols = pl.BlockSpec((2, width, LANES), lambda i: (0, 0, jnp.maximum(i - 1, 0)))
    anywhere = pl.BlockSpec(memory_space=pl.ANY)
    local = pl.BlockSpec(memory_space=pltpu.VMEM)
    shape = (1, down_part.shape[1] // GRID, down_part.shape[2] // 2)
    piece = jax.ShapeDtypeStruct((1, 4) + shape[1:], BF16)
    return pl.pallas_call(
        functools.partial(backward_kernel, subs),
        grid=(pairs + 1,),
        out_shape=[
            jax.ShapeDtypeStruct(wq.shape, BF16),
            jax.ShapeDtypeStruct(wkv.shape, BF16),
            jax.ShapeDtypeStruct((rows, width), F32),
            jax.ShapeDtypeStruct((8, width), F32),
            jax.ShapeDtypeStruct((8, width), F32),
            piece,
            piece,
            jax.ShapeDtypeStruct((rows, width), BF16),
        ],
        in_specs=[
            whole(both),
            whole(facts),
            pl.BlockSpec((2, length, rows), lambda i: (jnp.minimum(i, pairs - 1), 0, 0)),
            block(rows),
            block(rows),
            block(length),
            block(length),
            turned,
            turned,
            q_cols,
            kv_cols,
            whole(d_one),
            anywhere,
            anywhere,
        ],
        out_specs=[
            q_cols,
            kv_cols,
            pl.BlockSpec((rows, width), lambda i: (0, 0), pipeline_mode=pl.Buffered(1)),
            block(8),
            behind(8),
            local,
            local,
            local,
        ],
        scratch_shapes=[
            pltpu.VMEM((length, facts.shape[1]), jnp.int32),
            pltpu.VMEM((width, rows), BF16),
            pltpu.VMEM((pairs, length, 2 * LANES), BF16),
            pltpu.VMEM((pairs, rows, 2 * LANES), BF16),
            pltpu.SemaphoreType.DMA((pairs,)),
            pltpu.SemaphoreType.DMA((pairs,)),
        ]
        + scatter_scratch(shape)
        + scatter_scratch(shape),
        compiler_params=pltpu.CompilerParams(
            collective_id=3, has_side_effects=True, vmem_limit_bytes=VMEM_LIMIT
        ),
        name="attention_backward",
    )(both, facts, probs, word, entity, keys, values, ctx, dctx, wq, wkv, d_one, as_shards(down_part), as_shards(up_part))


def ffn_forward_kernel(
    subs, both, ctx, w_out, up, down, unit_bias, out_bias, gain, shift, valid, grad_out,
    active, slope, hidden_low, normal_one, inverse_one, output, d_two, sums, hidden, total, traded, sems,
):
    step = pl.program_id(0)
    place = Place(subs)
    trade = Trade(place, grad_out, traded, sems)

    @pl.when(step == 0)
    def _():
        entry_barrier(place)
        trade.start()
        attn = dot_nt(ctx[...].T, w_out[...]) + out_bias[0:1].astype(F32)
        resid = both[place.c].astype(F32) + attn
        normal, inverse = normalize(resid)
        out = normal * gain[0:1].astype(F32) + shift[0:1].astype(F32)
        hidden[...] = out
        hidden_low[...] = out.astype(BF16)
        normal_one[...] = normal
        inverse_one[...] = inverse
        total[...] = jnp.zeros_like(total)
        seen = valid[...]
        sums[0:1] = column_sum(seen * resid * resid)
        sums[1:2] = column_sum(seen * attn * attn)

    pre = dot_nn(hidden_low[...], up[...]) + unit_bias[...]
    act, rise = gelu_pair(pre)
    act = act.astype(BF16)
    active[...] = act
    slope[...] = rise.astype(BF16)
    total[...] += dot_nt(act, down[...])

    @pl.when(step == pl.num_programs(0) - 1)
    def _():
        ffn = total[...] + out_bias[1:2].astype(F32)
        resid = hidden[...] + ffn
        normal, inverse = normalize(resid)
        output[...] = (normal * gain[1:2].astype(F32) + shift[1:2].astype(F32)).astype(BF16)
        seen = valid[...]
        trade.finish()
        grad = traded[...].astype(F32)
        back = norm_backward(grad, normal, inverse, gain[1:2].astype(F32))
        d_two[...] = back
        sums[2:3] = column_sum(seen * ffn * ffn)
        sums[3:4] = column_sum(seen * resid * resid)
        sums[4:5] = column_sum(grad * normal)
        sums[5:6] = column_sum(grad)
        sums[6:7] = column_sum(back.astype(BF16).astype(F32))
        sums[7:8] = jnp.zeros_like(sums[7:8]) + jnp.sum(seen) * (1.0 / seen.shape[0])


def ffn_forward(subs, both, ctx, w_out, up, down, unit_bias, out_bias, gain, shift, valid, grad_out):
    _, rows, width = both.shape
    units = up.shape[1]
    whole = lambda a: pl.BlockSpec(a.shape, lambda i: (0,) * a.ndim, pipeline_mode=pl.Buffered(1))
    fixed = lambda r, w: pl.BlockSpec((r, w), lambda i: (0, 0), pipeline_mode=pl.Buffered(1))
    wide = lambda r: pl.BlockSpec((r, BLOCK), lambda i: (0, i))
    return pl.pallas_call(
        functools.partial(ffn_forward_kernel, subs),
        grid=(units // BLOCK,),
        out_shape=[
            jax.ShapeDtypeStruct((rows, units), BF16),
            jax.ShapeDtypeStruct((rows, units), BF16),
            jax.ShapeDtypeStruct((rows, width), BF16),
            jax.ShapeDtypeStruct((rows, width), F32),
            jax.ShapeDtypeStruct((rows, 1), F32),
            jax.ShapeDtypeStruct((rows, width), BF16),
            jax.ShapeDtypeStruct((rows, width), F32),
            jax.ShapeDtypeStruct((8, width), F32),
        ],
        in_specs=[whole(both), whole(ctx), whole(w_out), wide(width), wide(width), wide(1)]
        + [whole(a) for a in (out_bias, gain, shift, valid)]
        + [pl.BlockSpec(memory_space=pltpu.VMEM)],
        out_specs=[
            wide(rows),
            wide(rows),
            fixed(rows, width),
            fixed(rows, width),
            fixed(rows, 1),
            fixed(rows, width),
            fixed(rows, width),
            fixed(8, width),
        ],
        scratch_shapes=[
            pltpu.VMEM((rows, width), F32),
            pltpu.VMEM((rows, width), F32),
            pltpu.VMEM((rows, width), BF16),
            pltpu.SemaphoreType.DMA((3,)),
        ],
        compiler_params=pltpu.CompilerParams(
            collective_id=4, has_side_effects=True, vmem_limit_bytes=VMEM_LIMIT
        ),
        cost_estimate=pl.CostEstimate(
            flops=2 * rows * width * (width + 2 * units),
            bytes_accessed=2 * width * (width + 2 * units) + 4 * rows * units,
            transcendentals=rows * units,
        ),
        name="ffn_forward",
    )(both, ctx, w_out, up, down, unit_bias, out_bias, gain, shift, valid, grad_out)


def ffn_backward_kernel(
    subs, result, d_two, hidden_low, active, slope, up, down, ctx, w_out, gain, normal_one, inverse_one,
    up_part, down_part, bias_part, d_one, d_ctx, out_part, sums, output, d_low, d_turned, hidden_turned, total, sems,
):
    step = pl.program_id(0)
    place = Place(subs)
    trade = Trade(place, result, output, sems)

    @pl.when(step == 0)
    def _():
        entry_barrier(place)
        trade.start()
        low = d_two[...].astype(BF16)
        d_low[...] = low
        d_turned[...] = low.T
        hidden_turned[...] = hidden_low[...].T
        total[...] = d_two[...]

    d_pre = (dot_nn(d_low[...], down[...]) * slope[...].astype(F32)).astype(BF16)
    bias_part[...] = column_sum(d_pre.astype(F32))
    up_part[...] = dot_nn(hidden_turned[...], d_pre).astype(BF16)
    down_part[...] = dot_nn(d_turned[...], active[...]).astype(BF16)
    total[...] += dot_nt(d_pre, up[...])

    @pl.when(step == pl.num_programs(0) - 1)
    def _():
        grad = total[...]
        normal = normal_one[...]
        back = norm_backward(grad, normal, inverse_one[...], gain[0:1].astype(F32))
        d_one[...] = back
        low = back.astype(BF16)
        d_ctx[...] = dot_nt(w_out[...].T, low).astype(BF16)
        out_part[...] = dot_nt(low.T, ctx[...]).astype(BF16)
        sums[...] = jnp.zeros_like(sums)
        sums[0:1] = column_sum(grad * normal)
        sums[1:2] = column_sum(grad)
        sums[2:3] = column_sum(low.astype(F32))
        trade.finish()


def ffn_backward(subs, result, d_two, hidden_low, active, slope, up, down, ctx, w_out, gain, normal_one, inverse_one):
    rows, width = d_two.shape
    units = up.shape[1]
    whole = lambda a: pl.BlockSpec(a.shape, lambda i: (0,) * a.ndim, pipeline_mode=pl.Buffered(1))
    fixed = lambda r, w: pl.BlockSpec((r, w), lambda i: (0, 0), pipeline_mode=pl.Buffered(1))
    wide = lambda r: pl.BlockSpec((r, BLOCK), lambda i: (0, i))
    return pl.pallas_call(
        functools.partial(ffn_backward_kernel, subs),
        grid=(units // BLOCK,),
        out_shape=[
            jax.ShapeDtypeStruct((width, units), BF16),
            jax.ShapeDtypeStruct((width, units), BF16),
            jax.ShapeDtypeStruct((1, units), F32),
            jax.ShapeDtypeStruct((rows, width), F32),
            jax.ShapeDtypeStruct((width, rows), BF16),
            jax.ShapeDtypeStruct((width, width), BF16),
            jax.ShapeDtypeStruct((8, width), F32),
            jax.ShapeDtypeStruct((rows, width), BF16),
        ],
        in_specs=[pl.BlockSpec(memory_space=pltpu.VMEM), whole(d_two), whole(hidden_low), wide(rows), wide(rows), wide(width), wide(width)]
        + [whole(a) for a in (ctx, w_out, gain, normal_one, inverse_one)],
        out_specs=[
            wide(width),
            wide(width),
            wide(1),
            fixed(rows, width),
            fixed(width, rows),
            fixed(width, width),
            fixed(8, width),
            pl.BlockSpec(memory_space=pl.ANY),
        ],
        scratch_shapes=[
            pltpu.VMEM((rows, width), BF16),
            pltpu.VMEM((width, rows), BF16),
            pltpu.VMEM((width, rows), BF16),
            pltpu.VMEM((rows, width), F32),
            pltpu.SemaphoreType.DMA((3,)),
        ],
        compiler_params=pltpu.CompilerParams(
            collective_id=5, has_side_effects=True, vmem_limit_bytes=VMEM_LIMIT
        ),
        cost_estimate=pl.CostEstimate(
            flops=4 * rows * width * (width + 2 * units),
            bytes_accessed=2 * width * (3 * width + 4 * units) + 4 * rows * units,
            transcendentals=0,
        ),
        name="ffn_backward",
    )(result, d_two, hidden_low, active, slope, up, down, ctx, w_out, gain, normal_one, inverse_one)


def body(
    layer_input,
    grad_out,
    segment,
    entity,
    valid_mask,
    query_weight,
    key_value_weight,
    attn_bias,
    out_weight,
    out_bias,
    ln_gain,
    ln_bias,
    up_weight,
    ffn_bias,
    down_weight,
):
    rows, width = layer_input.shape
    length = segment.shape[0]
    rank = lax.axis_index("tensor")
    subs = lax.axis_size("dp") // GRID
    core = (lax.axis_index("dp") // subs) % 2
    start = core * rows
    pairs = lax.axis_size("tensor")
    shards = [
        query_weight,
        key_value_weight,
        out_weight.T[None],
        up_weight[None],
        down_weight.T[None],
    ]
    groups = [[b * subs + s for s in range(subs)] for b in range(GRID)]
    if subs > 1:
        shards = [
            lax.all_gather(s, "dp", axis=1, tiled=True, axis_index_groups=groups) for s in shards
        ]
    shards = [shards[1], shards[0]] + shards[2:]
    units = pairs * ffn_bias.shape[0]
    cols = attn_bias.shape[1]
    bias_rows = jnp.concatenate([attn_bias, ffn_bias.reshape(-1, cols)]).astype(F32)
    used = bias_rows.shape[0]
    bias_rows = jnp.pad(bias_rows, ((0, -used % 16), (0, 0)))
    facts = jnp.pad(jnp.stack([segment, entity, valid_mask]), ((0, 5), (0, 0)))
    (w_kv, w_q, w_out_t, w_up, w_down_t), (both, biases, pair_facts) = gather_weights(
        subs, shards, 3, layer_input, bias_rows, facts
    )
    w_kv, w_q, w_out_t = as_matrix(w_kv), as_matrix(w_q), as_matrix(w_out_t)[0]
    context_t, probs, query_word, query_ent, keys, values, w_up, w_down_t = attention_forward(
        subs, both, w_q, w_kv, biases, pair_facts, w_up, w_down_t
    )
    w_up, w_down_t = as_matrix(w_up)[0], as_matrix(w_down_t)[0]
    ffn_bias_full = biases[:, 5:used].reshape(units)
    facts = lax.dynamic_index_in_dim(pair_facts, rank, 0, keepdims=False)

    valid_own = lax.dynamic_slice_in_dim(facts[2], start, rows).astype(F32)[:, None]
    active, slope, hidden_low, normal_one, inverse_one, result, d_two, sums_two = ffn_forward(
        subs, both, context_t, w_out_t, w_up, w_down_t, ffn_bias_full[None], out_bias, ln_gain, ln_bias, valid_own,
        grad_out,
    )
    up_part, down_part, ffn_bias_part, d_one, d_context_t, out_part, sums_one, output = ffn_backward(
        subs, result, d_two, hidden_low, active, slope, w_up, w_down_t, context_t, w_out_t, ln_gain, normal_one, inverse_one
    )

    query_part, kv_part, input_grad, q_bias, v_bias, down_piece, up_piece, input_low = attention_backward(
        subs, both, pair_facts, probs, query_word, query_ent, keys, values, context_t, d_context_t, w_q, w_kv, d_one,
        down_part[None], up_part[None],
    )
    small = jnp.concatenate([sums_one.reshape(-1), sums_two.reshape(-1), q_bias[:4].reshape(-1), v_bias[0], ffn_bias_part[0]])
    padded = -(-small.shape[0] // (8 * LANES)) * 8 * LANES
    small = jnp.pad(small, (0, padded - small.shape[0])).reshape(-1, LANES)
    sums, small_sum, input_grad = scatter_gradients(
        subs, [down_piece, up_piece], [out_part[None], query_part, kv_part], small, input_grad, input_low
    )
    if subs > 1:
        sums = [
            lax.psum_scatter(s, "dp", scatter_dimension=1, tiled=True, axis_index_groups=groups)
            for s in sums
        ]
        small_sum = lax.psum(small_sum, "dp", axis_index_groups=groups)
    down_sum, up_sum, out_sum, query_sum, kv_sum = sums
    flat = small_sum.reshape(-1)
    norms = flat[: 16 * width].reshape(16, width)
    gains, shifts, out_biases = (jnp.stack([norms[i], norms[12 + i]]) for i in range(3))
    attn_biases = flat[16 * width : 21 * width].reshape(5, width)
    ffn_biases = flat[21 * width : 21 * width + units]
    squares = jnp.sum(norms[8:12], 1)
    real = norms[15, 0] * rows
    half = ffn_bias.shape[0]
    return (
        output,
        input_grad,
        jnp.sqrt(squares / (real * width)),
        query_sum,
        kv_sum,
        lax.dynamic_slice_in_dim(attn_biases, rank * cols, cols, 1),
        out_sum[0].T,
        out_biases,
        gains,
        shifts,
        up_sum[0],
        lax.dynamic_slice_in_dim(ffn_biases, rank * half, half, 0),
        down_sum[0].T,
    )


def solution(mesh):
    placed = (
        P(("dp", "tensor"), None),
        P(("dp", "tensor"), None),
        P("dp"),
        P("dp"),
        P("dp"),
        P(None, "dp", "tensor"),
        P(None, "dp", "tensor"),
        P(None, "tensor"),
        P("tensor", "dp"),
        P(),
        P(),
        P(),
        P("dp", "tensor"),
        P("tensor"),
        P("tensor", "dp"),
    )
    return jax.shard_map(
        body,
        mesh=mesh,
        in_specs=placed,
        out_specs=(
            P(("dp", "tensor"), None),
            P(("dp", "tensor"), None),
            P(),
            P(None, "dp", "tensor"),
            P(None, "dp", "tensor"),
            P(None, "tensor"),
            P("tensor", "dp"),
            P(),
            P(),
            P(),
            P("dp", "tensor"),
            P("tensor"),
            P("tensor", "dp"),
        ),
        check_vma=False,
    )
```

```python
import functools

import jax
import jax.numpy as jnp
from jax import lax
from jax.experimental import pallas as pl
from jax.experimental.pallas import tpu as pltpu
from jax.sharding import PartitionSpec as P

HEAD = 64
EPS = 1e-06
NEG = -1e30
GRID = 16
LANES = 128
MESH = pl.DeviceIdType.MESH
BF16 = jnp.bfloat16
F32 = jnp.float32
VMEM_LIMIT = 60 * 1024 * 1024


BLOCK = 768
TAIL = 0.34
TAIL_Q = (
    0.1918165616711201,
    0.1920366827922902,
    0.17827181747742213,
    0.1748548010854969,
    0.05944614604180367,
    0.27541659722682194,
    -0.27820700083503797,
    0.4016320911891782,
    -0.24597742961536673,
    0.050709736470982834,
)


def gelu_pair(v):
    size = jnp.abs(v)
    t = 1.0 / (1.0 + (TAIL * 0.5**0.5) * size)
    q = jnp.full_like(v, TAIL_Q[-1])
    for coefficient in TAIL_Q[-2::-1]:
        q = q * t + coefficient
    bell = jnp.exp(-0.5 * (v * v))
    tail = 0.5 * (bell * (t * q))
    cdf = jnp.where(v < 0, tail, 1.0 - tail)
    return v * cdf, cdf + v * (bell * 0.3989422804014327)


def normalize(resid):
    center = resid - jnp.mean(resid, -1, keepdims=True)
    inverse = lax.rsqrt(jnp.mean(center * center, -1, keepdims=True) + EPS)
    return center * inverse, inverse


def norm_backward(grad, normal, inverse, gain):
    scaled = grad * gain
    return inverse * (
        scaled
        - jnp.mean(scaled, -1, keepdims=True)
        - normal * jnp.mean(scaled * normal, -1, keepdims=True)
    )


def column_sum(a):
    return jnp.sum(a, 0, keepdims=True)


class Place:
    def __init__(self, subs):
        rank = lax.axis_index("dp")
        self.subs = subs
        self.sub = rank % subs
        block = rank // subs
        self.z = block // 4
        self.turns = [(self.z + step) % 4 for step in range(4)]
        self.x = (block // 2) % 2
        self.c = block % 2
        self.y = lax.axis_index("tensor")
        self.moved = self.y != self.c
        self.x1 = jnp.where(self.c == 0, 1 - self.x, self.x)
        self.y1 = jnp.where(self.c == 0, self.y, 1 - self.y)
        self.x2 = jnp.where(self.c == 0, self.x, 1 - self.x)
        self.y2 = jnp.where(self.c == 0, 1 - self.y, self.y)

    def device(self, z=None, x=None, c=None, y=None):
        z = self.z if z is None else z
        x = self.x if x is None else x
        c = self.c if c is None else c
        y = self.y if y is None else y
        return (((z * 2 + x) * 2 + c) * self.subs + self.sub, y)

    def z_peer(self, step):
        return self.device(z=(self.z + step) % 4)

    def first(self):
        return self.device(x=self.x1, y=self.y1)

    def second(self):
        return self.device(x=self.x2, y=self.y2)

    def sibling(self):
        return self.device(c=1 - self.c)

    def plane(self):
        x, y, c = (self.x, 1 - self.x), (self.y, 1 - self.y), (self.c, 1 - self.c)
        return [self.device(x=x[k // 4], y=y[k // 2 % 2], c=c[k % 2]) for k in range(1, 8)]

    def across(self):
        return self.device(y=1 - self.y)

    def transposed(self):
        return self.device(c=1 - self.c, y=1 - self.y)

    def pieces(self):
        return (
            (self.x, self.y),
            (self.x1, self.y1),
            (self.x2, self.y2),
            (1 - self.x, 1 - self.y),
        )


def entry_barrier(place):
    barrier = pltpu.get_barrier_semaphore()
    peers = [place.z_peer(step) for step in (1, 2, 3)]
    peers += place.plane()
    for peer in peers:
        pl.semaphore_signal(barrier, inc=1, device_id=peer, device_id_type=MESH)
    pl.semaphore_wait(barrier, len(peers))


def remote(src, dst, send, recv, peer):
    return pltpu.make_async_remote_copy(
        src_ref=src, dst_ref=dst, send_sem=send, recv_sem=recv, device_id=peer, device_id_type=MESH
    )


class Trade:
    def __init__(self, place, own, got, sems):
        self.moved = place.moved
        self.kept = pltpu.make_async_copy(own, got, sems.at[2])
        self.swap = remote(own, got, sems.at[0], sems.at[1], place.transposed())

    def start(self):
        @pl.when(self.moved)
        def _():
            self.swap.start()

        @pl.when(jnp.logical_not(self.moved))
        def _():
            self.kept.start()

    def finish(self):
        @pl.when(self.moved)
        def _():
            self.swap.wait()

        @pl.when(jnp.logical_not(self.moved))
        def _():
            self.kept.wait()


class Gather:
    def __init__(self, place, shard, full, send, recv, local=None, whole=True):
        self.place, self.shard, self.full, self.whole = place, shard, full, whole
        self.send, self.recv, self.local = send, recv, local
        self.w = full.shape[-1] // 2

    def cols(self, y):
        return pl.ds(pl.multiple_of(y * self.w, LANES), self.w)

    def piece(self, spot, c):
        x, y = spot
        return self.full.at[:, :, x, c, :, self.cols(y)]

    def copy(self, index, src, dst, peer):
        remote(src, dst, self.send.at[index], self.recv.at[index], peer).start()

    def arrive(self, index, ref):
        remote(ref, ref, self.send.at[index], self.recv.at[index], self.place.sibling()).wait_recv()

    def gone(self, index, ref):
        remote(ref, ref, self.send.at[index], self.recv.at[index], self.place.sibling()).wait_send()

    def own(self, z):
        p = self.place
        return self.full.at[:, z, p.x, p.c, :, self.cols(p.y)]

    def stage1(self):
        p = self.place
        self.kept = pltpu.make_async_copy(self.shard, self.own(p.z), self.local)
        self.kept.start()
        for step in (1, 2, 3):
            self.copy(step - 1, self.shard, self.own(p.z), p.z_peer(step))

    def land(self):
        p = self.place
        self.kept.wait()
        for step in (1, 2, 3):
            self.arrive(step - 1, self.own((p.z + 4 - step) % 4))

    def settle(self):
        self.land()
        for index in range(3):
            self.gone(index, self.shard)

    def spread(self):
        p = self.place
        mine = self.piece(p.pieces()[0], p.c)
        self.copy(3, mine, mine, p.first())
        self.copy(4, mine, mine, p.second())
        self.copy(6, mine, mine, p.sibling())

    def stage2(self):
        self.land()
        self.spread()

    def stage3(self):
        p = self.place
        got = self.piece(p.pieces()[1], p.c)
        self.arrive(3, got)
        self.copy(5, got, got, p.second())
        self.copy(7, got, got, p.sibling())

    def stage4(self):
        p = self.place
        for index, spot in ((4, 2), (5, 3)):
            got = self.piece(p.pieces()[spot], p.c)
            self.arrive(index, got)
            self.copy(index + 4, got, got, p.sibling())

    def stage5(self):
        p = self.place
        spots = p.pieces()
        for index, spot in ((6, 0), (7, 2), (8, 1), (9, 3)):
            self.arrive(index, self.piece(spots[spot], 1 - p.c))
        for index in range(3, 10):
            self.gone(index, self.piece(spots[0], p.c))

    def last(self):
        self.stage5()
        for index in range(3):
            self.gone(index, self.shard)

    def stages(self):
        if not self.whole:
            return [self.stage1, self.settle]
        return [self.stage1, self.stage2, self.stage3, self.stage4, self.last]


def wavefront(movers):
    lists = [mover.stages() for mover in movers]
    depth = max(len(stages) for stages in lists)
    order = []
    for time in range(len(lists) + depth - 1):
        for index in range(len(lists)):
            stage = time - index
            if 0 <= stage < len(lists[index]):
                order.append(lists[index][stage])
    return order


class Share:
    def __init__(self, source, pair, index, peer, sems):
        self.kept = pltpu.make_async_copy(source, pair.at[index], sems.at[2])
        self.sent = remote(source, pair.at[index], sems.at[0], sems.at[1], peer)

    def start(self):
        self.kept.start()
        self.sent.start()

    def finish(self):
        self.kept.wait()
        self.sent.wait()


class Rows:
    def __init__(self, place, rows, both, sems):
        p = place
        half = both.at[p.c]
        self.moved = p.moved
        self.kept = pltpu.make_async_copy(rows, half, sems.at[4])
        self.swap = remote(rows, both.at[p.y], sems.at[0], sems.at[1], p.transposed())
        self.swapped = remote(half, half, sems.at[0], sems.at[1], p.transposed())
        self.share = remote(rows, half, sems.at[2], sems.at[3], p.sibling())
        self.relay = remote(half, half, sems.at[2], sems.at[3], p.sibling())
        other = both.at[1 - p.c]
        self.other = remote(other, other, sems.at[2], sems.at[3], p.sibling())

    def start(self):
        @pl.when(self.moved)
        def _():
            self.swap.start()

        @pl.when(jnp.logical_not(self.moved))
        def _():
            self.kept.start()
            self.share.start()

    def forward(self):
        @pl.when(self.moved)
        def _():
            self.swapped.wait_recv()
            self.relay.start()

    def finish(self):
        @pl.when(self.moved)
        def _():
            self.swap.wait_send()
            self.relay.wait_send()

        @pl.when(jnp.logical_not(self.moved))
        def _():
            self.kept.wait()
            self.share.wait_send()

        self.other.wait_recv()


def gather_kernel(subs, count, wholes, *refs):
    shards, (rows, bias, facts) = refs[:count], refs[count : count + 3]
    fulls, (both, biases, pair_facts) = refs[count + 3 : 2 * count + 3], refs[2 * count + 3 : 2 * count + 6]
    send, recv, local, row_sems, share_sems = refs[2 * count + 6 :]
    place = Place(subs)
    entry_barrier(place)
    tokens = Rows(place, rows, both, row_sems)
    shares = [
        Share(facts, pair_facts, place.c, place.sibling(), share_sems.at[0]),
        Share(bias, biases, place.y, place.across(), share_sems.at[1]),
    ]
    tokens.start()
    for share in shares:
        share.start()
    movers = [
        Gather(place, shards[i], fulls[i], send.at[i], recv.at[i], local.at[i], i < wholes)
        for i in range(count)
    ]
    for mover in movers[:2]:
        mover.stage1()
    steps = [s for s in wavefront(movers) if s.__func__ is not Gather.stage1]
    late = [s for s in steps if s.__func__ is Gather.settle]
    landed = 0
    for index, step in enumerate([s for s in steps if s not in late] + late):
        step()
        if index == 1:
            tokens.forward()
        if step.__func__ in (Gather.stage2, Gather.settle):
            landed += 1
            if landed + 1 < count:
                movers[landed + 1].stage1()
    tokens.finish()
    for share in shares:
        share.finish()


def gather_weights(subs, shards, wholes, rows, bias, facts):
    count = len(shards)
    outs = [
        jax.ShapeDtypeStruct((s.shape[0], 4, 2, 2, s.shape[1], 2 * s.shape[2]), BF16) for s in shards
    ]
    outs += [jax.ShapeDtypeStruct((2,) + a.shape, a.dtype) for a in (rows, bias, facts)]
    results = pl.pallas_call(
        functools.partial(gather_kernel, subs, count, wholes),
        out_shape=outs,
        in_specs=[pl.BlockSpec(memory_space=pltpu.VMEM)] * (count + 3),
        out_specs=[pl.BlockSpec(memory_space=pl.ANY)] * (count + 3),
        scratch_shapes=[
            pltpu.SemaphoreType.DMA((count, 10)),
            pltpu.SemaphoreType.DMA((count, 10)),
            pltpu.SemaphoreType.DMA((count,)),
            pltpu.SemaphoreType.DMA((5,)),
            pltpu.SemaphoreType.DMA((2, 3)),
        ],
        compiler_params=pltpu.CompilerParams(
            collective_id=0, has_side_effects=True, vmem_limit_bytes=VMEM_LIMIT
        ),
        name="gather_weights",
    )(*shards, rows, bias, facts)
    return results[:count], results[count:]


def as_matrix(full):
    return full.reshape(full.shape[0], GRID * full.shape[4], full.shape[5])


class Last:
    def __init__(self, place, piece, total, from_z, send, recv):
        self.place, self.piece, self.total, self.from_z = place, piece, total, from_z
        self.send, self.recv = send, recv

    def start(self):
        p = self.place
        for step in (1, 2, 3):
            remote(
                self.piece.at[:, p.turns[step]],
                self.from_z.at[step - 1],
                self.send.at[step - 1],
                self.recv.at[step - 1],
                p.z_peer(step),
            ).start()

    def finish(self):
        p = self.place
        for step in (0, 1, 2):
            slot = self.from_z.at[step]
            remote(slot, slot, self.send.at[step], self.recv.at[step], p.sibling()).wait()

        def step(i, carry):
            total = self.piece[i, p.z].astype(F32)
            for s in range(3):
                total = total + self.from_z[s, i].astype(F32)
            self.total[i] = total
            return carry

        lax.fori_loop(0, self.total.shape[0], step, 0)


class Scatter:
    def __init__(self, place, part, mine, from_core, from_second, from_first, send, recv, local):
        self.place, self.part = place, part
        self.mine, self.from_core = mine, from_core
        self.from_second, self.from_first = from_second, from_first
        self.send, self.recv, self.local = send, recv, local
        self.m, _, self.rows, self.w = from_first.shape

    def cols(self, y):
        return pl.ds(pl.multiple_of(y * self.w, LANES), self.w)

    def copy(self, index, src, dst, peer):
        remote(src, dst, self.send.at[index], self.recv.at[index], peer).start()

    def arrive(self, index, ref):
        remote(ref, ref, self.send.at[index], self.recv.at[index], self.place.sibling()).wait_recv()

    def drain(self):
        for index in range(7):
            remote(
                self.from_first, self.from_first, self.send.at[index], self.recv.at[index], self.place.sibling()
            ).wait_send()

    def add(self, target, source):
        m = self.m

        def step(index, carry):
            i, z = index // 4, index % 4
            target[i, z] = (target[i, z].astype(F32) + source[i, z].astype(F32)).astype(BF16)
            return carry

        lax.fori_loop(0, m * 4, step, 0)

    def keep(self, slot, spot):
        x, y = self.place.pieces()[spot]
        source = self.part.at[:, :, x, self.place.c, :, self.cols(y)]
        return pltpu.make_async_copy(source, self.mine.at[slot], self.local.at[slot])

    def stage1(self):
        p = self.place
        spots = p.pieces()
        for slot, (here, there) in enumerate(((3, 3), (2, 1), (1, 2), (0, 0))):
            self.keep(slot, here).start()
            x, y = spots[there]
            self.copy(
                slot,
                self.part.at[:, :, x, 1 - p.c, :, self.cols(y)],
                self.from_core.at[slot],
                p.sibling(),
            )

    def joined(self, slot):
        self.keep(slot, 3 - slot).wait()
        self.arrive(slot, self.from_core.at[slot])
        self.add(self.mine.at[slot], self.from_core.at[slot])

    def stage2(self):
        p = self.place
        for slot in (0, 1):
            self.joined(slot)
            self.copy(4 + slot, self.mine.at[slot], self.from_second.at[slot], p.second())
        for slot in (2, 3):
            self.joined(slot)

    def stage3(self):
        p = self.place
        self.arrive(4, self.from_second.at[0])
        self.add(self.mine.at[2], self.from_second.at[0])
        self.copy(6, self.mine.at[2], self.from_first, p.first())
        self.arrive(5, self.from_second.at[1])
        self.add(self.mine.at[3], self.from_second.at[1])

    def stage4(self):
        self.arrive(6, self.from_first)
        self.add(self.mine.at[3], self.from_first)


class Sum:
    def __init__(self, place, source, total, box, send, recv):
        self.place, self.source, self.total = place, source, total
        self.box, self.send, self.recv = box, send, recv
        p = place
        flip = p.z + 1 - 2 * (p.z % 2)
        self.peers = (p.device(x=1 - p.x), p.across(), p.device(z=flip), p.device(z=p.turns[2]), p.sibling())

    def term(self, index):
        return self.source if index == 0 else self.total.at[index - 1]

    def exchange(self, index):
        return remote(
            self.term(index), self.box.at[index], self.send.at[index], self.recv.at[index], self.peers[index]
        )

    def hop(self, index):
        self.exchange(index).start()

    def land(self, index):
        self.exchange(index).wait()
        self.total[index] = self.term(index)[...] + self.box[index]


class PlaneSum:
    def __init__(self, place, source, middle, plane, line, send, recv):
        self.place, self.source, self.middle = place, source, middle
        self.plane, self.line, self.send, self.recv = plane, line, send, recv
        p = place
        spot = (p.x * 2 + p.y) * 2 + p.c
        self.first = [
            remote(source, plane.at[spot], send.at[k], recv.at[k], peer) for k, peer in enumerate(p.plane())
        ]
        self.second = [
            remote(middle, line.at[p.z], send.at[6 + k], recv.at[6 + k], p.z_peer(k)) for k in (1, 2, 3)
        ]
        self.spot = spot

    def start(self):
        for step in self.first:
            step.start()
        self.plane[self.spot] = self.source[...]

    def turn(self):
        for step in self.first:
            step.wait()
        total = self.plane[0]
        for k in range(1, 8):
            total = total + self.plane[k]
        self.middle[...] = total
        for step in self.second:
            step.start()
        self.line[self.place.z] = total

    def finish(self):
        for step in self.second:
            step.wait()
        total = self.line[0]
        for k in range(1, 4):
            total = total + self.line[k]
        return total


def scatter_scratch(shape):
    m, rows, w = shape
    return [
        pltpu.VMEM((4, m, 4, rows, w), BF16),
        pltpu.VMEM((4, m, 4, rows, w), BF16),
        pltpu.VMEM((2, m, 4, rows, w), BF16),
        pltpu.VMEM((m, 4, rows, w), BF16),
        pltpu.SemaphoreType.DMA((7,)),
        pltpu.SemaphoreType.DMA((7,)),
        pltpu.SemaphoreType.DMA((4,)),
    ]


def last_scratch(shape):
    return [
        pltpu.VMEM((3,) + shape, BF16),
        pltpu.SemaphoreType.DMA((3,)),
        pltpu.SemaphoreType.DMA((3,)),
    ]


def as_shards(part):
    m, rows, w = part.shape
    return part.reshape(m, 4, 2, 2, rows // GRID, w)


def scatter_kernel(subs, early, count, *refs):
    pieces, parts, smalls = refs[:early], refs[early : early + count], refs[early + count :][:2]
    input_grad, input_low = refs[early + count + 2 :][:2]
    refs = refs[early + count + 4 :]
    totals, (small_total, result, traded, trade_sems) = refs[: early + count], refs[early + count :][:4]
    refs = refs[early + count + 4 :]
    lasts, refs = refs[: 3 * (early + count)], refs[3 * (early + count) :]
    place = Place(subs)
    entry_barrier(place)
    movers = [Scatter(place, parts[i], *refs[7 * i : 7 * i + 7]) for i in range(count)]
    sources = list(pieces) + [mover.mine.at[3] for mover in movers]
    ends = [Last(place, sources[i], totals[i], *lasts[3 * i : 3 * i + 3]) for i in range(early + count)]
    small, *boxes = refs[7 * count :]
    small[...] = smalls[0][...]
    small[4:5] = smalls[1][0:1]
    small_sum = PlaneSum(place, small, *boxes)
    trade = Trade(place, input_low, traded, trade_sems)
    small_sum.start()
    for mover in movers:
        mover.stage1()
    small_sum.turn()
    for end in ends[:early]:
        end.start()
    for time in range(count + 2):
        for index in range(count):
            stage = time - index
            if 0 <= stage < 3:
                mover = movers[index]
                (mover.stage2, mover.stage3, mover.stage4)[stage]()
                if stage == 1 and index == count - 1:
                    trade.start()
                if stage == 2:
                    ends[early + index].start()
    small_total[...] = small_sum.finish()
    for end in ends[early:]:
        end.finish()
    for end in ends[:early]:
        end.finish()
    for mover in movers:
        mover.drain()
    trade.finish()
    result[...] = jnp.where(place.moved, traded[...].astype(F32), input_grad[...])


def scatter_gradients(subs, pieces, parts, smalls, input_grad, input_low):
    early, count = len(pieces), len(parts)
    shaped = [as_shards(p) for p in parts]
    shapes = [(p.shape[0],) + p.shape[2:] for p in pieces]
    whole = [(p.shape[0], p.shape[4], p.shape[5] // 2) for p in shaped]
    outs = [jax.ShapeDtypeStruct(s, F32) for s in shapes + whole]
    stack = smalls[0].shape
    outs += [jax.ShapeDtypeStruct(stack, F32), jax.ShapeDtypeStruct(input_grad.shape, F32)]
    scratch = [pltpu.VMEM(input_low.shape, BF16), pltpu.SemaphoreType.DMA((3,))]
    for s in shapes + whole:
        scratch += last_scratch(s)
    for s in whole:
        scratch += scatter_scratch(s)
    scratch += [
        pltpu.VMEM(stack, F32),
        pltpu.VMEM(stack, F32),
        pltpu.VMEM((8,) + stack, F32),
        pltpu.VMEM((4,) + stack, F32),
        pltpu.SemaphoreType.DMA((10,)),
        pltpu.SemaphoreType.DMA((10,)),
    ]
    local = pl.BlockSpec(memory_space=pltpu.VMEM)
    results = pl.pallas_call(
        functools.partial(scatter_kernel, subs, early, count),
        out_shape=outs,
        in_specs=[local] * early + [pl.BlockSpec(memory_space=pl.ANY)] * count + [local] * 4,
        out_specs=[local] * (early + count + 2),
        scratch_shapes=scratch,
        compiler_params=pltpu.CompilerParams(
            collective_id=1, has_side_effects=True, vmem_limit_bytes=VMEM_LIMIT
        ),
        name="scatter_gradients",
    )(*pieces, *shaped, *smalls, input_grad, input_low)
    return results[:-2], results[-2], results[-1]


def finish_kernel(place_of, stack, biases, query, kv, up, grad, out, gains, shifts, out_bias, attn_bias, *results):
    place = place_of()
    for i, ref in enumerate((gains, shifts, out_bias)):
        ref[0:1] = stack[i : i + 1]
        ref[1:2] = stack[12 + i : 13 + i]
    cols = attn_bias.shape[1]
    mine = pl.ds(pl.multiple_of(place.y * cols, LANES), cols)
    attn_bias[...] = biases[0:5, mine]
    for source, target in zip((query, kv, up, grad, out), results):
        target[...] = source[...]


def finish(subs, stack, biases, cols, arrays):
    width = stack.shape[1]
    shapes = [(2, width)] * 3 + [(5, cols)]
    outs = [jax.ShapeDtypeStruct(s, F32) for s in shapes] + [jax.ShapeDtypeStruct(a.shape, a.dtype) for a in arrays]
    return pl.pallas_call(
        functools.partial(finish_kernel, functools.partial(Place, subs)),
        out_shape=outs,
        compiler_params=pltpu.CompilerParams(vmem_limit_bytes=VMEM_LIMIT),
        name="finish",
    )(stack, biases, *arrays)


def head_lanes(half):
    lane = lax.broadcasted_iota(jnp.int32, (1, LANES), 1)
    return (lane // HEAD) == half


def dot_nt(a, b):
    return lax.dot_general(a, b, (((1,), (1,)), ((), ())), preferred_element_type=F32)


def dot_nn(a, b):
    return lax.dot_general(a, b, (((1,), (0,)), ((), ())), preferred_element_type=F32)


def forward_kernel(
    subs, both, wq, wkv, biases, facts, up_in, down_in,
    ctx, probs, word, entity, keys, values, up, down, mask, column, send, recv,
):
    place = Place(subs)
    step = pl.program_id(0)
    length, rows = mask.shape
    movers = [Gather(place, None, full, send.at[i], recv.at[i]) for i, full in enumerate((up, down))]
    own = pl.ds(pl.multiple_of(place.c * rows, LANES), rows)

    @pl.when(step == 0)
    def _():
        entry_barrier(place)
        for mover in movers:
            mover.spread()
        column[...] = facts[place.y].T
        spot = lax.broadcasted_iota(jnp.int32, (length, rows), 0)
        here = lax.broadcasted_iota(jnp.int32, (length, rows), 1) + place.c * rows
        same = column[:, 0:1] == facts[place.y, 0:1, own]
        seen = (column[:, 2:3] == 1) | (spot == here)
        mask[...] = jnp.where(same & seen, 0.0, NEG)

    @pl.when(step == 3)
    def _():
        movers[0].stage3()

    @pl.when(step == 5)
    def _():
        movers[1].stage3()

    tokens = both[...].reshape(length, both.shape[2])
    mine = both[place.c]
    bias = biases[0]
    row_ent = column[own, 1:2] == 1
    to_word = dot_nn(mine, jnp.concatenate([wq[0], wq[2]], axis=1))
    to_ent = dot_nn(mine, jnp.concatenate([wq[1], wq[3]], axis=1))
    scale = HEAD ** (-0.5)
    query_word = jnp.where(row_ent, to_word[:, LANES:] + bias[2:3], to_word[:, :LANES] + bias[0:1])
    query_ent = jnp.where(row_ent, to_ent[:, LANES:] + bias[3:4], to_ent[:, :LANES] + bias[1:2])
    word[...] = query_word.astype(BF16) * BF16(scale)
    entity[...] = query_ent.astype(BF16) * BF16(scale)
    pair = dot_nn(tokens, jnp.concatenate([wkv[0], wkv[1]], axis=1))
    key = pair[:, :LANES].astype(BF16)
    value = (pair[:, LANES:] + bias[4:5]).astype(BF16)
    keys[...] = key
    values[...] = value

    queries = jnp.concatenate([word[...], entity[...]], axis=1)
    ent = column[:, 1:2] == 1
    zero = jnp.zeros_like(key)
    turned = value.T
    for half in range(2):
        lanes = head_lanes(half)
        wide = jnp.concatenate(
            [jnp.where(lanes & ~ent, key, zero), jnp.where(lanes & ent, key, zero)], axis=1
        )
        scores = dot_nt(wide, queries) + mask[...]
        top = jnp.max(scores, axis=0, keepdims=True)
        expo = jnp.exp(scores - top)
        total = jnp.sum(expo, axis=0, keepdims=True)
        prob = (expo * (1.0 / total)).astype(BF16)
        probs[half] = prob
        ctx[half * HEAD : (half + 1) * HEAD, :] = dot_nn(
            turned[half * HEAD : (half + 1) * HEAD, :], prob
        ).astype(BF16)

    @pl.when(step == pl.num_programs(0) - 1)
    def _():
        for mover in movers:
            mover.stage4()
        for mover in movers:
            mover.stage5()


def attention_forward(subs, both, wq, wkv, biases, facts, up, down):
    _, rows, width = both.shape
    length = 2 * rows
    pairs = width // LANES
    span = biases.shape[2] // LANES
    block = lambda n: pl.BlockSpec((n, LANES), lambda i: (0, i))
    whole = lambda a: pl.BlockSpec(a.shape, lambda i: (0,) * a.ndim, pipeline_mode=pl.Buffered(1))
    cols = lambda a: pl.BlockSpec(a.shape[:2] + (LANES,), lambda i: (0, 0, i))
    anywhere = pl.BlockSpec(memory_space=pl.ANY)
    return pl.pallas_call(
        functools.partial(forward_kernel, subs),
        grid=(pairs,),
        out_shape=[
            jax.ShapeDtypeStruct((width, rows), BF16),
            jax.ShapeDtypeStruct((2 * pairs, length, rows), BF16),
            jax.ShapeDtypeStruct((rows, width), BF16),
            jax.ShapeDtypeStruct((rows, width), BF16),
            jax.ShapeDtypeStruct((length, width), BF16),
            jax.ShapeDtypeStruct((length, width), BF16),
            jax.ShapeDtypeStruct(up.shape, BF16),
            jax.ShapeDtypeStruct(down.shape, BF16),
        ],
        in_specs=[
            whole(both),
            cols(wq),
            cols(wkv),
            pl.BlockSpec((1, biases.shape[1], LANES), lambda i: (i // span, 0, i % span)),
            whole(facts),
            anywhere,
            anywhere,
        ],
        out_specs=[
            pl.BlockSpec((LANES, rows), lambda i: (i, 0)),
            pl.BlockSpec((2, length, rows), lambda i: (i, 0, 0)),
            block(rows),
            block(rows),
            block(length),
            block(length),
            anywhere,
            anywhere,
        ],
        scratch_shapes=[
            pltpu.VMEM((length, rows), F32),
            pltpu.VMEM((length, facts.shape[1]), jnp.int32),
            pltpu.SemaphoreType.DMA((2, 10)),
            pltpu.SemaphoreType.DMA((2, 10)),
        ],
        input_output_aliases={5: 6, 6: 7},
        compiler_params=pltpu.CompilerParams(
            collective_id=2, has_side_effects=True, vmem_limit_bytes=VMEM_LIMIT
        ),
        name="attention_forward",
    )(both, wq, wkv, biases, facts, up, down)


def backward_kernel(
    subs, both, facts, probs, word, entity, keys, values, ctx, dctx, wq, wkv, d_one, sums_one, sums_two, unit_sums,
    down_part, up_part, q_part, kv_part, input_grad, q_bias, v_bias, down_piece, up_piece, input_low, sums,
    column, turned_rows, pair_grad, pair_got, pair_send, pair_recv, small, running, box, sum_send, sum_recv, *scratch,
):
    place = Place(subs)
    step = pl.program_id(0)
    pairs = pl.num_programs(0) - 1
    rows = word.shape[0]
    movers = [Scatter(place, down_part, *scratch[:7]), Scatter(place, up_part, *scratch[7:])]
    small_sum = Sum(place, small, running, box, sum_send, sum_recv)
    own = pl.ds(pl.multiple_of(place.c * rows, LANES), rows)
    other = pl.ds(pl.multiple_of((1 - place.c) * rows, LANES), rows)

    @pl.when(step == 0)
    def _():
        entry_barrier(place)
        wide = small.shape[1]
        small[0:8] = sums_one[...]
        small[8:16] = sums_two[...]
        small[16:24] = jnp.zeros_like(small[16:24])
        for i in range(unit_sums.shape[1] // wide):
            small[16 + i : 17 + i] = unit_sums[:, i * wide : (i + 1) * wide]
        small_sum.hop(0)
        for mover in movers:
            mover.stage1()
        column[...] = facts[place.y].T
        turned_rows[...] = both[place.c].T
        input_grad[...] = d_one[...]

    @pl.when(step == 1)
    def _():
        small_sum.land(0)
        small_sum.hop(1)
        movers[0].stage2()

    @pl.when(step == 2)
    def _():
        small_sum.land(1)
        small_sum.hop(2)
        movers[1].stage2()

    @pl.when(step == 3)
    def _():
        small_sum.land(2)
        small_sum.hop(3)

    @pl.when(step == 4)
    def _():
        small_sum.land(3)
        small_sum.hop(4)

    @pl.when(step == 5)
    def _():
        small_sum.land(4)
        sums[...] = running[4]
        movers[0].stage3()

    @pl.when(step < pairs)
    def _():
        queries = jnp.concatenate([word[...], entity[...]], axis=1)
        value = values[...]
        turned = keys[...].T
        ent = column[:, 1:2] == 1
        ent_lane = facts[place.y, 1:2, :] == 1
        own_ent = facts[place.y, 1:2, own] == 1
        grad = dctx[...]
        zero = jnp.zeros_like(value)
        dk, dv, dw, de = [], [], [], []
        for half in range(2):
            lanes = head_lanes(half)
            here = slice(half * HEAD, (half + 1) * HEAD)
            prob = probs[half]
            delta = jnp.sum(
                ctx[here, :].astype(F32) * grad[here, :].astype(F32), axis=0, keepdims=True
            )
            dprob = dot_nn(jnp.where(lanes, value, zero), grad)
            dscore = (prob.astype(F32) * (dprob - delta)).astype(BF16)
            key_t = turned[here, :]
            none = jnp.zeros_like(key_t)
            tall = jnp.concatenate(
                [jnp.where(ent_lane, none, key_t), jnp.where(ent_lane, key_t, none)], axis=0
            )
            dq = dot_nn(tall, dscore) * (HEAD ** (-0.5))
            dw.append(dq[:HEAD])
            de.append(dq[HEAD:])
            pair = dot_nn(dscore, queries)
            dk.append(jnp.where(ent, pair[:, LANES:], pair[:, :LANES]))
            dv.append(dot_nt(prob, grad))
        first = head_lanes(0)
        pair_grad[step, :, :LANES] = jnp.where(first, dk[0], dk[1]).astype(BF16)
        pair_grad[step, :, LANES:] = jnp.where(first, dv[0], dv[1]).astype(BF16)
        remote(
            pair_grad.at[step, other], pair_got.at[step], pair_send.at[step], pair_recv.at[step], place.sibling()
        ).start()
        d_word, d_ent = jnp.concatenate(dw, axis=0), jnp.concatenate(de, axis=0)
        empty = jnp.zeros_like(d_word)
        turned_grad = jnp.concatenate(
            [
                jnp.where(own_ent, empty, d_word),
                jnp.where(own_ent, empty, d_ent),
                jnp.where(own_ent, d_word, empty),
                jnp.where(own_ent, d_ent, empty),
            ],
            axis=0,
        ).astype(BF16)
        query_grad = turned_grad.T
        weights = jnp.concatenate([wq[m] for m in range(4)], axis=1)
        input_grad[...] += dot_nt(query_grad, weights)
        part = dot_nn(turned_rows[...], query_grad).astype(BF16)
        sums = column_sum(query_grad.astype(F32))
        q_bias[...] = jnp.zeros_like(q_bias)
        for m in range(4):
            span = slice(m * LANES, (m + 1) * LANES)
            q_part[m] = part[:, span]
            q_bias[m : m + 1] = sums[:, span]

    @pl.when(step > 0)
    def _():
        before = step - 1
        remote(
            pair_got.at[before], pair_got.at[before], pair_send.at[before], pair_recv.at[before], place.sibling()
        ).wait()
        grad = (pair_grad[before, own].astype(F32) + pair_got[before].astype(F32)).astype(BF16)
        weights = jnp.concatenate([wkv[0], wkv[1]], axis=1)
        input_grad[...] += dot_nt(grad, weights)
        part = dot_nn(turned_rows[...], grad).astype(BF16)
        kv_part[0] = part[:, :LANES]
        kv_part[1] = part[:, LANES:]
        v_bias[...] = jnp.zeros_like(v_bias)
        v_bias[0:1] = column_sum(grad[:, LANES:].astype(F32))

    @pl.when(step == pairs)
    def _():
        movers[1].stage3()
        for mover in movers:
            mover.stage4()
            mover.drain()
        down_piece[...] = movers[0].mine[3]
        up_piece[...] = movers[1].mine[3]
        input_low[...] = input_grad[...].astype(BF16)


def attention_backward(
    subs, both, facts, probs, word, entity, keys, values, ctx, dctx, wq, wkv, d_one, smalls, down_part, up_part
):
    _, rows, width = both.shape
    length = 2 * rows
    pairs = width // LANES
    block = lambda n: pl.BlockSpec((n, LANES), lambda i: (0, jnp.minimum(i, pairs - 1)))
    behind = lambda n: pl.BlockSpec((n, LANES), lambda i: (0, jnp.maximum(i - 1, 0)))
    turned = pl.BlockSpec((LANES, rows), lambda i: (jnp.minimum(i, pairs - 1), 0))
    whole = lambda a: pl.BlockSpec(a.shape, lambda i: (0,) * a.ndim, pipeline_mode=pl.Buffered(1))
    q_cols = pl.BlockSpec((4, width, LANES), lambda i: (0, 0, jnp.minimum(i, pairs - 1)))
    kv_cols = pl.BlockSpec((2, width, LANES), lambda i: (0, 0, jnp.maximum(i - 1, 0)))
    anywhere = pl.BlockSpec(memory_space=pl.ANY)
    local = pl.BlockSpec(memory_space=pltpu.VMEM)
    shape = (1, down_part.shape[1] // GRID, down_part.shape[2] // 2)
    piece = jax.ShapeDtypeStruct((1, 4) + shape[1:], BF16)
    return pl.pallas_call(
        functools.partial(backward_kernel, subs),
        grid=(pairs + 1,),
        out_shape=[
            jax.ShapeDtypeStruct(wq.shape, BF16),
            jax.ShapeDtypeStruct(wkv.shape, BF16),
            jax.ShapeDtypeStruct((rows, width), F32),
            jax.ShapeDtypeStruct((8, width), F32),
            jax.ShapeDtypeStruct((8, width), F32),
            piece,
            piece,
            jax.ShapeDtypeStruct((rows, width), BF16),
            jax.ShapeDtypeStruct((24, width), F32),
        ],
        in_specs=[
            whole(both),
            whole(facts),
            pl.BlockSpec((2, length, rows), lambda i: (jnp.minimum(i, pairs - 1), 0, 0)),
            block(rows),
            block(rows),
            block(length),
            block(length),
            turned,
            turned,
            q_cols,
            kv_cols,
            whole(d_one),
        ]
        + [whole(a) for a in smalls]
        + [anywhere, anywhere],
        out_specs=[
            q_cols,
            kv_cols,
            pl.BlockSpec((rows, width), lambda i: (0, 0), pipeline_mode=pl.Buffered(1)),
            block(8),
            behind(8),
            local,
            local,
            local,
            local,
        ],
        scratch_shapes=[
            pltpu.VMEM((length, facts.shape[1]), jnp.int32),
            pltpu.VMEM((width, rows), BF16),
            pltpu.VMEM((pairs, length, 2 * LANES), BF16),
            pltpu.VMEM((pairs, rows, 2 * LANES), BF16),
            pltpu.SemaphoreType.DMA((pairs,)),
            pltpu.SemaphoreType.DMA((pairs,)),
            pltpu.VMEM((24, width), F32),
            pltpu.VMEM((5, 24, width), F32),
            pltpu.VMEM((5, 24, width), F32),
            pltpu.SemaphoreType.DMA((5,)),
            pltpu.SemaphoreType.DMA((5,)),
        ]
        + scatter_scratch(shape)
        + scatter_scratch(shape),
        compiler_params=pltpu.CompilerParams(
            collective_id=3, has_side_effects=True, vmem_limit_bytes=VMEM_LIMIT
        ),
        name="attention_backward",
    )(
        both, facts, probs, word, entity, keys, values, ctx, dctx, wq, wkv, d_one, *smalls,
        as_shards(down_part), as_shards(up_part),
    )


def ffn_forward_kernel(
    subs, both, facts, ctx, w_out, up, down, biases, out_bias, gain, shift, grad_out,
    active, slope, hidden_low, normal_one, inverse_one, output, d_two, sums, hidden, total, traded, valid, sems,
):
    step = pl.program_id(0)
    place = Place(subs)
    rows = both.shape[1]
    trade = Trade(place, grad_out, traded, sems)

    @pl.when(step == 0)
    def _():
        entry_barrier(place)
        trade.start()
        attn = dot_nt(ctx[...].T, w_out[...]) + out_bias[0:1].astype(F32)
        resid = both[place.c].astype(F32) + attn
        normal, inverse = normalize(resid)
        out = normal * gain[0:1].astype(F32) + shift[0:1].astype(F32)
        hidden[...] = out
        hidden_low[...] = out.astype(BF16)
        normal_one[...] = normal
        inverse_one[...] = inverse
        total[...] = jnp.zeros_like(total)
        own = pl.ds(pl.multiple_of(place.c * rows, LANES), rows)
        seen = facts[place.y, :, own].T[:, 2:3].astype(F32)
        valid[...] = seen
        sums[0:1] = column_sum(seen * resid * resid)
        sums[1:2] = column_sum(seen * attn * attn)

    span = biases.shape[2]
    across = pl.num_programs(0) // 2
    lines = BLOCK // span
    half = step // across
    line = 5 + lines * (step % across)
    bias = jnp.concatenate([biases[half, pl.ds(line + i, 1), :] for i in range(lines)], axis=1)
    pre = dot_nn(hidden_low[...], up[...]) + bias
    act, rise = gelu_pair(pre)
    act = act.astype(BF16)
    active[...] = act
    slope[...] = rise.astype(BF16)
    total[...] += dot_nt(act, down[...])

    @pl.when(step == pl.num_programs(0) - 1)
    def _():
        ffn = total[...] + out_bias[1:2].astype(F32)
        resid = hidden[...] + ffn
        normal, inverse = normalize(resid)
        output[...] = (normal * gain[1:2].astype(F32) + shift[1:2].astype(F32)).astype(BF16)
        seen = valid[...]
        trade.finish()
        grad = traded[...].astype(F32)
        back = norm_backward(grad, normal, inverse, gain[1:2].astype(F32))
        d_two[...] = back
        sums[2:3] = column_sum(seen * ffn * ffn)
        sums[3:4] = column_sum(seen * resid * resid)
        sums[4:5] = column_sum(grad * normal)
        sums[5:6] = column_sum(grad)
        sums[6:7] = column_sum(back.astype(BF16).astype(F32))
        sums[7:8] = jnp.zeros_like(sums[7:8]) + jnp.sum(seen) * (1.0 / seen.shape[0])


def ffn_forward(subs, both, facts, ctx, w_out, up, down, biases, out_bias, gain, shift, grad_out):
    _, rows, width = both.shape
    units = up.shape[1]
    whole = lambda a: pl.BlockSpec(a.shape, lambda i: (0,) * a.ndim, pipeline_mode=pl.Buffered(1))
    fixed = lambda r, w: pl.BlockSpec((r, w), lambda i: (0, 0), pipeline_mode=pl.Buffered(1))
    wide = lambda r: pl.BlockSpec((r, BLOCK), lambda i: (0, i))
    return pl.pallas_call(
        functools.partial(ffn_forward_kernel, subs),
        grid=(units // BLOCK,),
        out_shape=[
            jax.ShapeDtypeStruct((rows, units), BF16),
            jax.ShapeDtypeStruct((rows, units), BF16),
            jax.ShapeDtypeStruct((rows, width), BF16),
            jax.ShapeDtypeStruct((rows, width), F32),
            jax.ShapeDtypeStruct((rows, 1), F32),
            jax.ShapeDtypeStruct((rows, width), BF16),
            jax.ShapeDtypeStruct((rows, width), F32),
            jax.ShapeDtypeStruct((8, width), F32),
        ],
        in_specs=[whole(both), whole(facts), whole(ctx), whole(w_out), wide(width), wide(width)]
        + [whole(a) for a in (biases, out_bias, gain, shift)]
        + [pl.BlockSpec(memory_space=pltpu.VMEM)],
        out_specs=[
            wide(rows),
            wide(rows),
            fixed(rows, width),
            fixed(rows, width),
            fixed(rows, 1),
            fixed(rows, width),
            fixed(rows, width),
            fixed(8, width),
        ],
        scratch_shapes=[
            pltpu.VMEM((rows, width), F32),
            pltpu.VMEM((rows, width), F32),
            pltpu.VMEM((rows, width), BF16),
            pltpu.VMEM((rows, 1), F32),
            pltpu.SemaphoreType.DMA((3,)),
        ],
        compiler_params=pltpu.CompilerParams(
            collective_id=4, has_side_effects=True, vmem_limit_bytes=VMEM_LIMIT
        ),
        cost_estimate=pl.CostEstimate(
            flops=2 * rows * width * (width + 2 * units),
            bytes_accessed=2 * width * (width + 2 * units) + 4 * rows * units,
            transcendentals=rows * units,
        ),
        name="ffn_forward",
    )(both, facts, ctx, w_out, up, down, biases, out_bias, gain, shift, grad_out)


def ffn_backward_kernel(
    subs, result, d_two, hidden_low, active, slope, up, down, ctx, w_out, gain, normal_one, inverse_one,
    up_part, down_part, bias_part, d_one, d_ctx, out_part, sums, output, d_low, d_turned, hidden_turned, total, sems,
):
    step = pl.program_id(0)
    place = Place(subs)
    trade = Trade(place, result, output, sems)

    @pl.when(step == 0)
    def _():
        entry_barrier(place)
        trade.start()
        low = d_two[...].astype(BF16)
        d_low[...] = low
        d_turned[...] = low.T
        hidden_turned[...] = hidden_low[...].T
        total[...] = d_two[...]

    d_pre = (dot_nn(d_low[...], down[...]) * slope[...].astype(F32)).astype(BF16)
    bias_part[...] = column_sum(d_pre.astype(F32))
    up_part[...] = dot_nn(hidden_turned[...], d_pre).astype(BF16)
    down_part[...] = dot_nn(d_turned[...], active[...]).astype(BF16)
    total[...] += dot_nt(d_pre, up[...])

    @pl.when(step == pl.num_programs(0) - 1)
    def _():
        grad = total[...]
        normal = normal_one[...]
        back = norm_backward(grad, normal, inverse_one[...], gain[0:1].astype(F32))
        d_one[...] = back
        low = back.astype(BF16)
        d_ctx[...] = dot_nt(w_out[...].T, low).astype(BF16)
        out_part[...] = dot_nt(low.T, ctx[...]).astype(BF16)
        sums[...] = jnp.zeros_like(sums)
        sums[0:1] = column_sum(grad * normal)
        sums[1:2] = column_sum(grad)
        sums[2:3] = column_sum(low.astype(F32))
        trade.finish()


def ffn_backward(subs, result, d_two, hidden_low, active, slope, up, down, ctx, w_out, gain, normal_one, inverse_one):
    rows, width = d_two.shape
    units = up.shape[1]
    whole = lambda a: pl.BlockSpec(a.shape, lambda i: (0,) * a.ndim, pipeline_mode=pl.Buffered(1))
    fixed = lambda r, w: pl.BlockSpec((r, w), lambda i: (0, 0), pipeline_mode=pl.Buffered(1))
    wide = lambda r: pl.BlockSpec((r, BLOCK), lambda i: (0, i))
    return pl.pallas_call(
        functools.partial(ffn_backward_kernel, subs),
        grid=(units // BLOCK,),
        out_shape=[
            jax.ShapeDtypeStruct((width, units), BF16),
            jax.ShapeDtypeStruct((width, units), BF16),
            jax.ShapeDtypeStruct((1, units), F32),
            jax.ShapeDtypeStruct((rows, width), F32),
            jax.ShapeDtypeStruct((width, rows), BF16),
            jax.ShapeDtypeStruct((width, width), BF16),
            jax.ShapeDtypeStruct((8, width), F32),
            jax.ShapeDtypeStruct((rows, width), BF16),
        ],
        in_specs=[pl.BlockSpec(memory_space=pltpu.VMEM), whole(d_two), whole(hidden_low), wide(rows), wide(rows), wide(width), wide(width)]
        + [whole(a) for a in (ctx, w_out, gain, normal_one, inverse_one)],
        out_specs=[
            wide(width),
            wide(width),
            wide(1),
            fixed(rows, width),
            fixed(width, rows),
            fixed(width, width),
            fixed(8, width),
            pl.BlockSpec(memory_space=pl.ANY),
        ],
        scratch_shapes=[
            pltpu.VMEM((rows, width), BF16),
            pltpu.VMEM((width, rows), BF16),
            pltpu.VMEM((width, rows), BF16),
            pltpu.VMEM((rows, width), F32),
            pltpu.SemaphoreType.DMA((3,)),
        ],
        compiler_params=pltpu.CompilerParams(
            collective_id=5, has_side_effects=True, vmem_limit_bytes=VMEM_LIMIT
        ),
        cost_estimate=pl.CostEstimate(
            flops=4 * rows * width * (width + 2 * units),
            bytes_accessed=2 * width * (3 * width + 4 * units) + 4 * rows * units,
            transcendentals=0,
        ),
        name="ffn_backward",
    )(result, d_two, hidden_low, active, slope, up, down, ctx, w_out, gain, normal_one, inverse_one)


def body(
    layer_input,
    grad_out,
    segment,
    entity,
    valid_mask,
    query_weight,
    key_value_weight,
    attn_bias,
    out_weight,
    out_bias,
    ln_gain,
    ln_bias,
    up_weight,
    ffn_bias,
    down_weight,
):
    rows, width = layer_input.shape
    length = segment.shape[0]
    rank = lax.axis_index("tensor")
    subs = lax.axis_size("dp") // GRID
    shards = [
        query_weight,
        key_value_weight,
        out_weight.T[None],
        up_weight[None],
        down_weight.T[None],
    ]
    groups = [[b * subs + s for s in range(subs)] for b in range(GRID)]
    if subs > 1:
        shards = [
            lax.all_gather(s, "dp", axis=1, tiled=True, axis_index_groups=groups) for s in shards
        ]
    shards = [shards[1], shards[0]] + shards[2:]
    cols = attn_bias.shape[1]
    bias_rows = jnp.concatenate([attn_bias, ffn_bias.reshape(-1, cols)]).astype(F32)
    used = bias_rows.shape[0]
    bias_rows = jnp.pad(bias_rows, ((0, -used % 16), (0, 0)))
    facts = jnp.pad(jnp.stack([segment, entity, valid_mask]), ((0, 5), (0, 0)))
    (w_kv, w_q, w_out_t, w_up, w_down_t), (both, biases, pair_facts) = gather_weights(
        subs, shards, 3, layer_input, bias_rows, facts
    )
    w_kv, w_q, w_out_t = as_matrix(w_kv), as_matrix(w_q), as_matrix(w_out_t)[0]
    context_t, probs, query_word, query_ent, keys, values, w_up, w_down_t = attention_forward(
        subs, both, w_q, w_kv, biases, pair_facts, w_up, w_down_t
    )
    w_up, w_down_t = as_matrix(w_up)[0], as_matrix(w_down_t)[0]
    active, slope, hidden_low, normal_one, inverse_one, result, d_two, sums_two = ffn_forward(
        subs, both, pair_facts, context_t, w_out_t, w_up, w_down_t, biases, out_bias, ln_gain, ln_bias, grad_out,
    )
    up_part, down_part, ffn_bias_part, d_one, d_context_t, out_part, sums_one, output = ffn_backward(
        subs, result, d_two, hidden_low, active, slope, w_up, w_down_t, context_t, w_out_t, ln_gain, normal_one, inverse_one
    )

    query_part, kv_part, input_grad, q_bias, v_bias, down_piece, up_piece, input_low, stack = attention_backward(
        subs, both, pair_facts, probs, query_word, query_ent, keys, values, context_t, d_context_t, w_q, w_kv, d_one,
        [sums_one, sums_two, ffn_bias_part], down_part[None], up_part[None],
    )
    sums, bias_sum, input_grad = scatter_gradients(
        subs,
        [down_piece, up_piece],
        [query_part, kv_part, out_part[None]],
        [q_bias, v_bias],
        input_grad,
        input_low,
    )
    if subs > 1:
        sums = [
            lax.psum_scatter(s, "dp", scatter_dimension=1, tiled=True, axis_index_groups=groups)
            for s in sums
        ]
        stack = lax.psum(stack, "dp", axis_index_groups=groups)
        bias_sum = lax.psum(bias_sum, "dp", axis_index_groups=groups)
    down_sum, up_sum, query_sum, kv_sum, out_sum = sums
    half = ffn_bias.shape[0]
    gains, shifts, out_biases, attn_biases, query_sum, kv_sum, up_sum, input_grad, output = finish(
        subs, stack, bias_sum, cols, [query_sum, kv_sum, up_sum, input_grad, output]
    )
    squares = jnp.sum(stack[8:12], 1)
    real = stack[15, 0] * rows
    lines = half // width
    return (
        output,
        input_grad,
        jnp.sqrt(squares / (real * width)),
        query_sum,
        kv_sum,
        attn_biases,
        out_sum[0].T,
        out_biases,
        gains,
        shifts,
        up_sum[0],
        lax.dynamic_slice_in_dim(stack, 16 + rank * lines, lines, 0).reshape(half),
        down_sum[0].T,
    )


def solution(mesh):
    placed = (
        P(("dp", "tensor"), None),
        P(("dp", "tensor"), None),
        P("dp"),
        P("dp"),
        P("dp"),
        P(None, "dp", "tensor"),
        P(None, "dp", "tensor"),
        P(None, "tensor"),
        P("tensor", "dp"),
        P(),
        P(),
        P(),
        P("dp", "tensor"),
        P("tensor"),
        P("tensor", "dp"),
    )
    return jax.shard_map(
        body,
        mesh=mesh,
        in_specs=placed,
        out_specs=(
            P(("dp", "tensor"), None),
            P(("dp", "tensor"), None),
            P(),
            P(None, "dp", "tensor"),
            P(None, "dp", "tensor"),
            P(None, "tensor"),
            P("tensor", "dp"),
            P(),
            P(),
            P(),
            P("dp", "tensor"),
            P("tensor"),
            P("tensor", "dp"),
        ),
        check_vma=False,
    )
```

```python
import functools

import jax
import jax.numpy as jnp
from jax import lax
from jax.experimental import pallas as pl
from jax.experimental.pallas import tpu as pltpu
from jax.sharding import PartitionSpec as P

HEAD = 64
EPS = 1e-06
NEG = -1e30
GRID = 16
LANES = 128
MESH = pl.DeviceIdType.MESH
BF16 = jnp.bfloat16
F32 = jnp.float32
VMEM_LIMIT = 60 * 1024 * 1024


BLOCK = 768
TAIL = 0.34
TAIL_Q = (
    0.1918165616711201,
    0.1920366827922902,
    0.17827181747742213,
    0.1748548010854969,
    0.05944614604180367,
    0.27541659722682194,
    -0.27820700083503797,
    0.4016320911891782,
    -0.24597742961536673,
    0.050709736470982834,
)


def gelu_pair(v):
    size = jnp.abs(v)
    t = 1.0 / (1.0 + (TAIL * 0.5**0.5) * size)
    q = jnp.full_like(v, TAIL_Q[-1])
    for coefficient in TAIL_Q[-2::-1]:
        q = q * t + coefficient
    bell = jnp.exp(-0.5 * (v * v))
    tail = 0.5 * (bell * (t * q))
    cdf = jnp.where(v < 0, tail, 1.0 - tail)
    return v * cdf, cdf + v * (bell * 0.3989422804014327)


def normalize(resid):
    center = resid - jnp.mean(resid, -1, keepdims=True)
    inverse = lax.rsqrt(jnp.mean(center * center, -1, keepdims=True) + EPS)
    return center * inverse, inverse


def norm_backward(grad, normal, inverse, gain):
    scaled = grad * gain
    return inverse * (
        scaled
        - jnp.mean(scaled, -1, keepdims=True)
        - normal * jnp.mean(scaled * normal, -1, keepdims=True)
    )


def column_sum(a):
    return jnp.sum(a, 0, keepdims=True)


class Place:
    def __init__(self, subs):
        rank = lax.axis_index("dp")
        self.subs = subs
        self.sub = rank % subs
        block = rank // subs
        self.z = block // 4
        self.turns = [(self.z + step) % 4 for step in range(4)]
        self.x = (block // 2) % 2
        self.c = block % 2
        self.y = lax.axis_index("tensor")
        self.moved = self.y != self.c
        self.x1 = jnp.where(self.c == 0, 1 - self.x, self.x)
        self.y1 = jnp.where(self.c == 0, self.y, 1 - self.y)
        self.x2 = jnp.where(self.c == 0, self.x, 1 - self.x)
        self.y2 = jnp.where(self.c == 0, 1 - self.y, self.y)

    def device(self, z=None, x=None, c=None, y=None):
        z = self.z if z is None else z
        x = self.x if x is None else x
        c = self.c if c is None else c
        y = self.y if y is None else y
        return (((z * 2 + x) * 2 + c) * self.subs + self.sub, y)

    def z_peer(self, step):
        return self.device(z=(self.z + step) % 4)

    def first(self, flat=False):
        return self.across() if flat else self.device(x=self.x1, y=self.y1)

    def second(self, flat=False):
        return self.device(x=1 - self.x) if flat else self.device(x=self.x2, y=self.y2)

    def sibling(self):
        return self.device(c=1 - self.c)

    def plane(self):
        x, y, c = (self.x, 1 - self.x), (self.y, 1 - self.y), (self.c, 1 - self.c)
        return [self.device(x=x[k // 4], y=y[k // 2 % 2], c=c[k % 2]) for k in range(1, 8)]

    def across(self):
        return self.device(y=1 - self.y)

    def transposed(self):
        return self.device(c=1 - self.c, y=1 - self.y)

    def pieces(self, flat=False):
        if flat:
            return ((self.x, self.y), (self.x, 1 - self.y), (1 - self.x, self.y), (1 - self.x, 1 - self.y))
        return (
            (self.x, self.y),
            (self.x1, self.y1),
            (self.x2, self.y2),
            (1 - self.x, 1 - self.y),
        )


def entry_barrier(place):
    barrier = pltpu.get_barrier_semaphore()
    peers = [place.z_peer(step) for step in (1, 2, 3)]
    peers += place.plane()
    for peer in peers:
        pl.semaphore_signal(barrier, inc=1, device_id=peer, device_id_type=MESH)
    pl.semaphore_wait(barrier, len(peers))


def remote(src, dst, send, recv, peer):
    return pltpu.make_async_remote_copy(
        src_ref=src, dst_ref=dst, send_sem=send, recv_sem=recv, device_id=peer, device_id_type=MESH
    )


class Trade:
    def __init__(self, place, own, got, sems):
        self.moved = place.moved
        self.kept = pltpu.make_async_copy(own, got, sems.at[2])
        self.swap = remote(own, got, sems.at[0], sems.at[1], place.transposed())

    def start(self):
        @pl.when(self.moved)
        def _():
            self.swap.start()

        @pl.when(jnp.logical_not(self.moved))
        def _():
            self.kept.start()

    def finish(self):
        @pl.when(self.moved)
        def _():
            self.swap.wait()

        @pl.when(jnp.logical_not(self.moved))
        def _():
            self.kept.wait()


class Gather:
    def __init__(self, place, shard, full, send, recv, local=None, whole=True, flat=False):
        self.flat = flat
        self.place, self.shard, self.full, self.whole = place, shard, full, whole
        self.send, self.recv, self.local = send, recv, local
        self.w = full.shape[-1] // 2

    def cols(self, y):
        return pl.ds(pl.multiple_of(y * self.w, LANES), self.w)

    def piece(self, spot, c):
        x, y = spot
        return self.full.at[:, :, x, c, :, self.cols(y)]

    def copy(self, index, src, dst, peer):
        remote(src, dst, self.send.at[index], self.recv.at[index], peer).start()

    def arrive(self, index, ref):
        remote(ref, ref, self.send.at[index], self.recv.at[index], self.place.sibling()).wait_recv()

    def gone(self, index, ref):
        remote(ref, ref, self.send.at[index], self.recv.at[index], self.place.sibling()).wait_send()

    def own(self, z):
        p = self.place
        return self.full.at[:, z, p.x, p.c, :, self.cols(p.y)]

    def stage1(self):
        p = self.place
        self.kept = pltpu.make_async_copy(self.shard, self.own(p.z), self.local)
        self.kept.start()
        for step in (1, 2, 3):
            self.copy(step - 1, self.shard, self.own(p.z), p.z_peer(step))

    def land(self):
        p = self.place
        self.kept.wait()
        for step in (1, 2, 3):
            self.arrive(step - 1, self.own((p.z + 4 - step) % 4))

    def settle(self):
        self.land()
        for index in range(3):
            self.gone(index, self.shard)

    def spread(self):
        p = self.place
        mine = self.piece(p.pieces(self.flat)[0], p.c)
        self.copy(3, mine, mine, p.first(self.flat))
        self.copy(4, mine, mine, p.second(self.flat))
        self.copy(6, mine, mine, p.sibling())

    def stage2(self):
        self.land()
        self.spread()

    def stage3(self):
        p = self.place
        got = self.piece(p.pieces(self.flat)[1], p.c)
        self.arrive(3, got)
        self.copy(5, got, got, p.second(self.flat))
        self.copy(7, got, got, p.sibling())

    def stage4(self):
        p = self.place
        for index, spot in ((4, 2), (5, 3)):
            got = self.piece(p.pieces(self.flat)[spot], p.c)
            self.arrive(index, got)
            self.copy(index + 4, got, got, p.sibling())

    def stage5(self):
        p = self.place
        spots = p.pieces(self.flat)
        for index, spot in ((6, 0), (7, 1 if self.flat else 2), (8, 2 if self.flat else 1), (9, 3)):
            self.arrive(index, self.piece(spots[spot], 1 - p.c))
        for index in range(3, 10):
            self.gone(index, self.piece(spots[0], p.c))

    def last(self):
        self.stage5()
        for index in range(3):
            self.gone(index, self.shard)

    def stages(self):
        if not self.whole:
            return [self.stage1, self.settle]
        return [self.stage1, self.stage2, self.stage3, self.stage4, self.last]


def wavefront(movers):
    lists = [mover.stages() for mover in movers]
    depth = max(len(stages) for stages in lists)
    order = []
    for time in range(len(lists) + depth - 1):
        for index in range(len(lists)):
            stage = time - index
            if 0 <= stage < len(lists[index]):
                order.append(lists[index][stage])
    return order


class Share:
    def __init__(self, source, pair, index, peer, sems):
        self.kept = pltpu.make_async_copy(source, pair.at[index], sems.at[2])
        self.sent = remote(source, pair.at[index], sems.at[0], sems.at[1], peer)

    def start(self):
        self.kept.start()
        self.sent.start()

    def finish(self):
        self.kept.wait()
        self.sent.wait()


class Rows:
    def __init__(self, place, rows, both, sems):
        p = place
        half = both.at[p.c]
        self.moved = p.moved
        self.kept = pltpu.make_async_copy(rows, half, sems.at[4])
        self.swap = remote(rows, both.at[p.y], sems.at[0], sems.at[1], p.transposed())
        self.swapped = remote(half, half, sems.at[0], sems.at[1], p.transposed())
        self.share = remote(rows, half, sems.at[2], sems.at[3], p.sibling())
        self.relay = remote(half, half, sems.at[2], sems.at[3], p.sibling())
        other = both.at[1 - p.c]
        self.other = remote(other, other, sems.at[2], sems.at[3], p.sibling())

    def start(self):
        @pl.when(self.moved)
        def _():
            self.swap.start()

        @pl.when(jnp.logical_not(self.moved))
        def _():
            self.kept.start()
            self.share.start()

    def forward(self):
        @pl.when(self.moved)
        def _():
            self.swapped.wait_recv()
            self.relay.start()

    def finish(self):
        @pl.when(self.moved)
        def _():
            self.swap.wait_send()
            self.relay.wait_send()

        @pl.when(jnp.logical_not(self.moved))
        def _():
            self.kept.wait()
            self.share.wait_send()

        self.other.wait_recv()


def gather_kernel(subs, count, wholes, *refs):
    shards, (rows, bias_rows, unit_bias), columns = refs[:count], refs[count : count + 3], refs[count + 3 : count + 6]
    fulls, (both, biases, pair_facts) = refs[count + 6 : 2 * count + 6], refs[2 * count + 6 : 2 * count + 9]
    send, recv, local, row_sems, share_sems, bias, facts = refs[2 * count + 9 :]
    place = Place(subs)
    entry_barrier(place)
    tokens = Rows(place, rows, both, row_sems)
    bias[...] = jnp.zeros_like(bias)
    many, span = bias_rows.shape
    bias[0:many] = bias_rows[...].astype(F32)
    for i in range(unit_bias.shape[1] // span):
        bias[many + i : many + i + 1] = unit_bias[:, i * span : (i + 1) * span].astype(F32)
    facts[...] = jnp.zeros_like(facts)
    for i in range(3):
        facts[i : i + 1] = columns[i][...]
    shares = [
        Share(facts, pair_facts, place.c, place.sibling(), share_sems.at[0]),
        Share(bias, biases, place.y, place.across(), share_sems.at[1]),
    ]
    tokens.start()
    for share in shares:
        share.start()
    movers = [
        Gather(place, shards[i], fulls[i], send.at[i], recv.at[i], local.at[i], i < wholes)
        for i in range(count)
    ]
    for mover in movers[:2]:
        mover.stage1()
    steps = [s for s in wavefront(movers) if s.__func__ is not Gather.stage1]
    late = [s for s in steps if s.__func__ is Gather.settle]
    landed = 0
    for index, step in enumerate([s for s in steps if s not in late] + late):
        step()
        if index == 1:
            tokens.forward()
        if step.__func__ in (Gather.stage2, Gather.settle):
            landed += 1
            if landed + 1 < count:
                movers[landed + 1].stage1()
    tokens.finish()
    for share in shares:
        share.finish()


def gather_weights(subs, shards, wholes, rows, bias_rows, unit_bias, columns):
    count = len(shards)
    outs = [
        jax.ShapeDtypeStruct((s.shape[0], 4, 2, 2, s.shape[1], 2 * s.shape[2]), BF16) for s in shards
    ]
    bias, facts = (16, bias_rows.shape[1]), (8, columns[0].shape[1])
    outs += [
        jax.ShapeDtypeStruct((2,) + rows.shape, rows.dtype),
        jax.ShapeDtypeStruct((2,) + bias, F32),
        jax.ShapeDtypeStruct((2,) + facts, jnp.int32),
    ]
    results = pl.pallas_call(
        functools.partial(gather_kernel, subs, count, wholes),
        out_shape=outs,
        in_specs=[pl.BlockSpec(memory_space=pltpu.VMEM)] * (count + 6),
        out_specs=[pl.BlockSpec(memory_space=pl.ANY)] * (count + 3),
        scratch_shapes=[
            pltpu.SemaphoreType.DMA((count, 10)),
            pltpu.SemaphoreType.DMA((count, 10)),
            pltpu.SemaphoreType.DMA((count,)),
            pltpu.SemaphoreType.DMA((5,)),
            pltpu.SemaphoreType.DMA((2, 3)),
            pltpu.VMEM(bias, F32),
            pltpu.VMEM(facts, jnp.int32),
        ],
        compiler_params=pltpu.CompilerParams(
            collective_id=0, has_side_effects=True, vmem_limit_bytes=VMEM_LIMIT
        ),
        name="gather_weights",
    )(*shards, rows, bias_rows, unit_bias, *columns)
    return results[:count], results[count:]


def as_matrix(full):
    return full.reshape(full.shape[0], GRID * full.shape[4], full.shape[5])


class Last:
    def __init__(self, place, piece, total, from_z, send, recv):
        self.place, self.piece, self.total, self.from_z = place, piece, total, from_z
        self.send, self.recv = send, recv

    def start(self):
        p = self.place
        for step in (1, 2, 3):
            remote(
                self.piece.at[:, p.turns[step]],
                self.from_z.at[step - 1],
                self.send.at[step - 1],
                self.recv.at[step - 1],
                p.z_peer(step),
            ).start()

    def finish(self):
        p = self.place
        for step in (0, 1, 2):
            slot = self.from_z.at[step]
            remote(slot, slot, self.send.at[step], self.recv.at[step], p.sibling()).wait()

        def step(i, carry):
            total = self.piece[i, p.z].astype(F32)
            for s in range(3):
                total = total + self.from_z[s, i].astype(F32)
            self.total[i] = total
            return carry

        lax.fori_loop(0, self.total.shape[0], step, 0)


class Scatter:
    def __init__(self, place, part, mine, from_core, from_second, from_first, send, recv, local):
        self.place, self.part = place, part
        self.mine, self.from_core = mine, from_core
        self.from_second, self.from_first = from_second, from_first
        self.send, self.recv, self.local = send, recv, local
        self.m, _, self.rows, self.w = from_first.shape

    def cols(self, y):
        return pl.ds(pl.multiple_of(y * self.w, LANES), self.w)

    def copy(self, index, src, dst, peer):
        remote(src, dst, self.send.at[index], self.recv.at[index], peer).start()

    def arrive(self, index, ref):
        remote(ref, ref, self.send.at[index], self.recv.at[index], self.place.sibling()).wait_recv()

    def drain(self):
        for index in range(7):
            remote(
                self.from_first, self.from_first, self.send.at[index], self.recv.at[index], self.place.sibling()
            ).wait_send()

    def add(self, target, source):
        m = self.m

        def step(index, carry):
            i, z = index // 4, index % 4
            target[i, z] = (target[i, z].astype(F32) + source[i, z].astype(F32)).astype(BF16)
            return carry

        lax.fori_loop(0, m * 4, step, 0)

    def keep(self, slot, spot):
        x, y = self.place.pieces()[spot]
        source = self.part.at[:, :, x, self.place.c, :, self.cols(y)]
        return pltpu.make_async_copy(source, self.mine.at[slot], self.local.at[slot])

    def stage1(self):
        p = self.place
        spots = p.pieces()
        for slot, (here, there) in enumerate(((3, 3), (2, 1), (1, 2), (0, 0))):
            self.keep(slot, here).start()
            x, y = spots[there]
            self.copy(
                slot,
                self.part.at[:, :, x, 1 - p.c, :, self.cols(y)],
                self.from_core.at[slot],
                p.sibling(),
            )

    def joined(self, slot):
        self.keep(slot, 3 - slot).wait()
        self.arrive(slot, self.from_core.at[slot])
        self.add(self.mine.at[slot], self.from_core.at[slot])

    def stage2(self):
        p = self.place
        for slot in (0, 1):
            self.joined(slot)
            self.copy(4 + slot, self.mine.at[slot], self.from_second.at[slot], p.second())
        for slot in (2, 3):
            self.joined(slot)

    def stage3(self):
        p = self.place
        self.arrive(4, self.from_second.at[0])
        self.add(self.mine.at[2], self.from_second.at[0])
        self.copy(6, self.mine.at[2], self.from_first, p.first())
        self.arrive(5, self.from_second.at[1])
        self.add(self.mine.at[3], self.from_second.at[1])

    def stage4(self):
        self.arrive(6, self.from_first)
        self.add(self.mine.at[3], self.from_first)


class Sum:
    def __init__(self, place, source, total, box, send, recv):
        self.place, self.source, self.total = place, source, total
        self.box, self.send, self.recv = box, send, recv
        p = place
        flip = p.z + 1 - 2 * (p.z % 2)
        self.peers = (p.device(x=1 - p.x), p.across(), p.device(z=flip), p.device(z=p.turns[2]), p.sibling())

    def term(self, index):
        return self.source if index == 0 else self.total.at[index - 1]

    def exchange(self, index):
        return remote(
            self.term(index), self.box.at[index], self.send.at[index], self.recv.at[index], self.peers[index]
        )

    def hop(self, index):
        self.exchange(index).start()

    def land(self, index):
        self.exchange(index).wait()
        self.total[index] = self.term(index)[...] + self.box[index]


class PlaneSum:
    def __init__(self, place, source, middle, plane, line, send, recv):
        self.place, self.source, self.middle = place, source, middle
        self.plane, self.line, self.send, self.recv = plane, line, send, recv
        p = place
        spot = (p.x * 2 + p.y) * 2 + p.c
        self.first = [
            remote(source, plane.at[spot], send.at[k], recv.at[k], peer) for k, peer in enumerate(p.plane())
        ]
        self.second = [
            remote(middle, line.at[p.z], send.at[6 + k], recv.at[6 + k], p.z_peer(k)) for k in (1, 2, 3)
        ]
        self.spot = spot

    def start(self):
        for step in self.first:
            step.start()
        self.plane[self.spot] = self.source[...]

    def turn(self):
        for step in self.first:
            step.wait()
        total = self.plane[0]
        for k in range(1, 8):
            total = total + self.plane[k]
        self.middle[...] = total
        for step in self.second:
            step.start()
        self.line[self.place.z] = total

    def finish(self):
        for step in self.second:
            step.wait()
        total = self.line[0]
        for k in range(1, 4):
            total = total + self.line[k]
        return total


def scatter_scratch(shape):
    m, rows, w = shape
    return [
        pltpu.VMEM((4, m, 4, rows, w), BF16),
        pltpu.VMEM((4, m, 4, rows, w), BF16),
        pltpu.VMEM((2, m, 4, rows, w), BF16),
        pltpu.VMEM((m, 4, rows, w), BF16),
        pltpu.SemaphoreType.DMA((7,)),
        pltpu.SemaphoreType.DMA((7,)),
        pltpu.SemaphoreType.DMA((4,)),
    ]


def last_scratch(shape):
    return [
        pltpu.VMEM((3,) + shape, BF16),
        pltpu.SemaphoreType.DMA((3,)),
        pltpu.SemaphoreType.DMA((3,)),
    ]


def as_shards(part):
    m, rows, w = part.shape
    return part.reshape(m, 4, 2, 2, rows // GRID, w)


def scatter_kernel(subs, early, count, *refs):
    pieces, parts, smalls = refs[:early], refs[early : early + count], refs[early + count :][:2]
    input_grad, input_low = refs[early + count + 2 :][:2]
    refs = refs[early + count + 4 :]
    totals, (small_total, result, traded, trade_sems) = refs[: early + count], refs[early + count :][:4]
    refs = refs[early + count + 4 :]
    lasts, refs = refs[: 3 * (early + count)], refs[3 * (early + count) :]
    place = Place(subs)
    entry_barrier(place)
    movers = [Scatter(place, parts[i], *refs[7 * i : 7 * i + 7]) for i in range(count)]
    sources = list(pieces) + [mover.mine.at[3] for mover in movers]
    ends = [Last(place, sources[i], totals[i], *lasts[3 * i : 3 * i + 3]) for i in range(early + count)]
    small, *boxes = refs[7 * count :]
    small[...] = smalls[0][...]
    small[4:5] = smalls[1][0:1]
    small_sum = PlaneSum(place, small, *boxes)
    trade = Trade(place, input_low, traded, trade_sems)
    small_sum.start()
    for mover in movers:
        mover.stage1()
    small_sum.turn()
    for end in ends[:early]:
        end.start()
    for time in range(count + 2):
        for index in range(count):
            stage = time - index
            if 0 <= stage < 3:
                mover = movers[index]
                (mover.stage2, mover.stage3, mover.stage4)[stage]()
                if stage == 1 and index == count - 1:
                    trade.start()
                if stage == 2:
                    ends[early + index].start()
    small_total[...] = small_sum.finish()
    for end in ends[early:]:
        end.finish()
    for end in ends[:early]:
        end.finish()
    for mover in movers:
        mover.drain()
    trade.finish()
    result[...] = jnp.where(place.moved, traded[...].astype(F32), input_grad[...])


def scatter_gradients(subs, pieces, parts, smalls, input_grad, input_low):
    early, count = len(pieces), len(parts)
    shaped = [as_shards(p) for p in parts]
    shapes = [(p.shape[0],) + p.shape[2:] for p in pieces]
    whole = [(p.shape[0], p.shape[4], p.shape[5] // 2) for p in shaped]
    outs = [jax.ShapeDtypeStruct(s, F32) for s in shapes + whole]
    stack = smalls[0].shape
    outs += [jax.ShapeDtypeStruct(stack, F32), jax.ShapeDtypeStruct(input_grad.shape, F32)]
    scratch = [pltpu.VMEM(input_low.shape, BF16), pltpu.SemaphoreType.DMA((3,))]
    for s in shapes + whole:
        scratch += last_scratch(s)
    for s in whole:
        scratch += scatter_scratch(s)
    scratch += [
        pltpu.VMEM(stack, F32),
        pltpu.VMEM(stack, F32),
        pltpu.VMEM((8,) + stack, F32),
        pltpu.VMEM((4,) + stack, F32),
        pltpu.SemaphoreType.DMA((10,)),
        pltpu.SemaphoreType.DMA((10,)),
    ]
    local = pl.BlockSpec(memory_space=pltpu.VMEM)
    results = pl.pallas_call(
        functools.partial(scatter_kernel, subs, early, count),
        out_shape=outs,
        in_specs=[local] * early + [pl.BlockSpec(memory_space=pl.ANY)] * count + [local] * 4,
        out_specs=[local] * (early + count + 2),
        scratch_shapes=scratch,
        compiler_params=pltpu.CompilerParams(
            collective_id=1, has_side_effects=True, vmem_limit_bytes=VMEM_LIMIT
        ),
        name="scatter_gradients",
    )(*pieces, *shaped, *smalls, input_grad, input_low)
    return results[:-2], results[-2], results[-1]


def finish_kernel(place_of, rows, stack, biases, query, kv, up, grad, out, gains, shifts, out_bias, attn_bias, unit_bias, rms, *results):
    place = place_of()
    width = stack.shape[1]
    lines = unit_bias.shape[1] // width
    for i in range(lines):
        unit_bias[:, i * width : (i + 1) * width] = stack[pl.ds(16 + place.y * lines + i, 1), :]
    real = jnp.mean(stack[15:16], 1, keepdims=True) * (rows * width)
    lane = lax.broadcasted_iota(jnp.int32, (1, 4), 1)
    squares = jnp.zeros((1, 4), F32)
    for i in range(4):
        squares = jnp.where(lane == i, jnp.sum(stack[8 + i : 9 + i], 1, keepdims=True), squares)
    rms[...] = jnp.sqrt(squares / real)
    for i, ref in enumerate((gains, shifts, out_bias)):
        ref[0:1] = stack[i : i + 1]
        ref[1:2] = stack[12 + i : 13 + i]
    cols = attn_bias.shape[1]
    mine = pl.ds(pl.multiple_of(place.y * cols, LANES), cols)
    attn_bias[...] = biases[0:5, mine]
    for source, target in zip((query, kv, up, grad, out), results):
        target[...] = source[...]


def finish(subs, rows, stack, biases, cols, units, arrays):
    width = stack.shape[1]
    shapes = [(2, width)] * 3 + [(5, cols), (1, units), (1, 4)]
    outs = [jax.ShapeDtypeStruct(s, F32) for s in shapes] + [jax.ShapeDtypeStruct(a.shape, a.dtype) for a in arrays]
    return pl.pallas_call(
        functools.partial(finish_kernel, functools.partial(Place, subs), rows),
        out_shape=outs,
        compiler_params=pltpu.CompilerParams(vmem_limit_bytes=VMEM_LIMIT),
        name="finish",
    )(stack, biases, *arrays)


def head_lanes(half):
    lane = lax.broadcasted_iota(jnp.int32, (1, LANES), 1)
    return (lane // HEAD) == half


def dot_nt(a, b):
    return lax.dot_general(a, b, (((1,), (1,)), ((), ())), preferred_element_type=F32)


def dot_nn(a, b):
    return lax.dot_general(a, b, (((1,), (0,)), ((), ())), preferred_element_type=F32)


def forward_kernel(
    subs, both, wq, wkv, biases, facts, up_in, down_in,
    ctx, probs, word, entity, keys, values, up, down, mask, column, send, recv,
):
    place = Place(subs)
    step = pl.program_id(0)
    length, rows = mask.shape
    movers = [Gather(place, None, full, send.at[i], recv.at[i]) for i, full in enumerate((up, down))]
    own = pl.ds(pl.multiple_of(place.c * rows, LANES), rows)

    @pl.when(step == 0)
    def _():
        entry_barrier(place)
        for mover in movers:
            mover.spread()
        column[...] = facts[place.y].T
        spot = lax.broadcasted_iota(jnp.int32, (length, rows), 0)
        here = lax.broadcasted_iota(jnp.int32, (length, rows), 1) + place.c * rows
        same = column[:, 0:1] == facts[place.y, 0:1, own]
        seen = (column[:, 2:3] == 1) | (spot == here)
        mask[...] = jnp.where(same & seen, 0.0, NEG)

    @pl.when(step == 3)
    def _():
        movers[0].stage3()

    @pl.when(step == 5)
    def _():
        movers[1].stage3()

    tokens = both[...].reshape(length, both.shape[2])
    mine = both[place.c]
    bias = biases[0]
    row_ent = column[own, 1:2] == 1
    to_word = dot_nn(mine, jnp.concatenate([wq[0], wq[2]], axis=1))
    to_ent = dot_nn(mine, jnp.concatenate([wq[1], wq[3]], axis=1))
    scale = HEAD ** (-0.5)
    query_word = jnp.where(row_ent, to_word[:, LANES:] + bias[2:3], to_word[:, :LANES] + bias[0:1])
    query_ent = jnp.where(row_ent, to_ent[:, LANES:] + bias[3:4], to_ent[:, :LANES] + bias[1:2])
    word[...] = query_word.astype(BF16) * BF16(scale)
    entity[...] = query_ent.astype(BF16) * BF16(scale)
    pair = dot_nn(tokens, jnp.concatenate([wkv[0], wkv[1]], axis=1))
    key = pair[:, :LANES].astype(BF16)
    value = (pair[:, LANES:] + bias[4:5]).astype(BF16)
    keys[...] = key
    values[...] = value

    queries = jnp.concatenate([word[...], entity[...]], axis=1)
    ent = column[:, 1:2] == 1
    zero = jnp.zeros_like(key)
    turned = value.T
    for half in range(2):
        lanes = head_lanes(half)
        wide = jnp.concatenate(
            [jnp.where(lanes & ~ent, key, zero), jnp.where(lanes & ent, key, zero)], axis=1
        )
        scores = dot_nt(wide, queries) + mask[...]
        top = jnp.max(scores, axis=0, keepdims=True)
        expo = jnp.exp(scores - top)
        total = jnp.sum(expo, axis=0, keepdims=True)
        prob = (expo * (1.0 / total)).astype(BF16)
        probs[half] = prob
        ctx[half * HEAD : (half + 1) * HEAD, :] = dot_nn(
            turned[half * HEAD : (half + 1) * HEAD, :], prob
        ).astype(BF16)

    @pl.when(step == pl.num_programs(0) - 1)
    def _():
        for mover in movers:
            mover.stage4()
        for mover in movers:
            mover.stage5()


def attention_forward(subs, both, wq, wkv, biases, facts, up, down):
    _, rows, width = both.shape
    length = 2 * rows
    pairs = width // LANES
    span = biases.shape[2] // LANES
    block = lambda n: pl.BlockSpec((n, LANES), lambda i: (0, i))
    whole = lambda a: pl.BlockSpec(a.shape, lambda i: (0,) * a.ndim, pipeline_mode=pl.Buffered(1))
    cols = lambda a: pl.BlockSpec(a.shape[:2] + (LANES,), lambda i: (0, 0, i))
    anywhere = pl.BlockSpec(memory_space=pl.ANY)
    return pl.pallas_call(
        functools.partial(forward_kernel, subs),
        grid=(pairs,),
        out_shape=[
            jax.ShapeDtypeStruct((width, rows), BF16),
            jax.ShapeDtypeStruct((2 * pairs, length, rows), BF16),
            jax.ShapeDtypeStruct((rows, width), BF16),
            jax.ShapeDtypeStruct((rows, width), BF16),
            jax.ShapeDtypeStruct((length, width), BF16),
            jax.ShapeDtypeStruct((length, width), BF16),
            jax.ShapeDtypeStruct(up.shape, BF16),
            jax.ShapeDtypeStruct(down.shape, BF16),
        ],
        in_specs=[
            whole(both),
            cols(wq),
            cols(wkv),
            pl.BlockSpec((1, biases.shape[1], LANES), lambda i: (i // span, 0, i % span)),
            whole(facts),
            anywhere,
            anywhere,
        ],
        out_specs=[
            pl.BlockSpec((LANES, rows), lambda i: (i, 0)),
            pl.BlockSpec((2, length, rows), lambda i: (i, 0, 0)),
            block(rows),
            block(rows),
            block(length),
            block(length),
            anywhere,
            anywhere,
        ],
        scratch_shapes=[
            pltpu.VMEM((length, rows), F32),
            pltpu.VMEM((length, facts.shape[1]), jnp.int32),
            pltpu.SemaphoreType.DMA((2, 10)),
            pltpu.SemaphoreType.DMA((2, 10)),
        ],
        input_output_aliases={5: 6, 6: 7},
        compiler_params=pltpu.CompilerParams(
            collective_id=2, has_side_effects=True, vmem_limit_bytes=VMEM_LIMIT
        ),
        name="attention_forward",
    )(both, wq, wkv, biases, facts, up, down)


def backward_kernel(
    subs, both, facts, probs, word, entity, keys, values, ctx, dctx, wq, wkv, d_one, sums_one, sums_two, unit_sums,
    down_part, up_part, q_part, kv_part, input_grad, q_bias, v_bias, down_piece, up_piece, input_low, sums,
    column, turned_rows, pair_grad, pair_got, pair_send, pair_recv, small, running, box, sum_send, sum_recv, *scratch,
):
    place = Place(subs)
    step = pl.program_id(0)
    pairs = pl.num_programs(0) - 1
    rows = word.shape[0]
    movers = [Scatter(place, down_part, *scratch[:7]), Scatter(place, up_part, *scratch[7:])]
    small_sum = Sum(place, small, running, box, sum_send, sum_recv)
    own = pl.ds(pl.multiple_of(place.c * rows, LANES), rows)
    other = pl.ds(pl.multiple_of((1 - place.c) * rows, LANES), rows)

    @pl.when(step == 0)
    def _():
        entry_barrier(place)
        wide = small.shape[1]
        small[0:8] = sums_one[...]
        small[8:16] = sums_two[...]
        small[16:24] = jnp.zeros_like(small[16:24])
        for i in range(unit_sums.shape[1] // wide):
            small[16 + i : 17 + i] = unit_sums[:, i * wide : (i + 1) * wide]
        small_sum.hop(0)
        for mover in movers:
            mover.stage1()
        column[...] = facts[place.y].T
        turned_rows[...] = both[place.c].T
        input_grad[...] = d_one[...]

    @pl.when(step == 1)
    def _():
        small_sum.land(0)
        small_sum.hop(1)
        movers[0].stage2()

    @pl.when(step == 2)
    def _():
        small_sum.land(1)
        small_sum.hop(2)
        movers[1].stage2()

    @pl.when(step == 3)
    def _():
        small_sum.land(2)
        small_sum.hop(3)

    @pl.when(step == 4)
    def _():
        small_sum.land(3)
        small_sum.hop(4)

    @pl.when(step == 5)
    def _():
        small_sum.land(4)
        sums[...] = running[4]
        movers[0].stage3()

    @pl.when(step < pairs)
    def _():
        queries = jnp.concatenate([word[...], entity[...]], axis=1)
        value = values[...]
        turned = keys[...].T
        ent = column[:, 1:2] == 1
        ent_lane = facts[place.y, 1:2, :] == 1
        own_ent = facts[place.y, 1:2, own] == 1
        grad = dctx[...]
        zero = jnp.zeros_like(value)
        dk, dv, dw, de = [], [], [], []
        for half in range(2):
            lanes = head_lanes(half)
            here = slice(half * HEAD, (half + 1) * HEAD)
            prob = probs[half]
            delta = jnp.sum(
                ctx[here, :].astype(F32) * grad[here, :].astype(F32), axis=0, keepdims=True
            )
            dprob = dot_nn(jnp.where(lanes, value, zero), grad)
            dscore = (prob.astype(F32) * (dprob - delta)).astype(BF16)
            key_t = turned[here, :]
            none = jnp.zeros_like(key_t)
            tall = jnp.concatenate(
                [jnp.where(ent_lane, none, key_t), jnp.where(ent_lane, key_t, none)], axis=0
            )
            dq = dot_nn(tall, dscore) * (HEAD ** (-0.5))
            dw.append(dq[:HEAD])
            de.append(dq[HEAD:])
            pair = dot_nn(dscore, queries)
            dk.append(jnp.where(ent, pair[:, LANES:], pair[:, :LANES]))
            dv.append(dot_nt(prob, grad))
        first = head_lanes(0)
        pair_grad[step, :, :LANES] = jnp.where(first, dk[0], dk[1]).astype(BF16)
        pair_grad[step, :, LANES:] = jnp.where(first, dv[0], dv[1]).astype(BF16)
        remote(
            pair_grad.at[step, other], pair_got.at[step], pair_send.at[step], pair_recv.at[step], place.sibling()
        ).start()
        d_word, d_ent = jnp.concatenate(dw, axis=0), jnp.concatenate(de, axis=0)
        empty = jnp.zeros_like(d_word)
        turned_grad = jnp.concatenate(
            [
                jnp.where(own_ent, empty, d_word),
                jnp.where(own_ent, empty, d_ent),
                jnp.where(own_ent, d_word, empty),
                jnp.where(own_ent, d_ent, empty),
            ],
            axis=0,
        ).astype(BF16)
        query_grad = turned_grad.T
        weights = jnp.concatenate([wq[m] for m in range(4)], axis=1)
        input_grad[...] += dot_nt(query_grad, weights)
        part = dot_nn(turned_rows[...], query_grad).astype(BF16)
        sums = column_sum(query_grad.astype(F32))
        q_bias[...] = jnp.zeros_like(q_bias)
        for m in range(4):
            span = slice(m * LANES, (m + 1) * LANES)
            q_part[m] = part[:, span]
            q_bias[m : m + 1] = sums[:, span]

    @pl.when(step > 0)
    def _():
        before = step - 1
        remote(
            pair_got.at[before], pair_got.at[before], pair_send.at[before], pair_recv.at[before], place.sibling()
        ).wait()
        grad = (pair_grad[before, own].astype(F32) + pair_got[before].astype(F32)).astype(BF16)
        weights = jnp.concatenate([wkv[0], wkv[1]], axis=1)
        input_grad[...] += dot_nt(grad, weights)
        part = dot_nn(turned_rows[...], grad).astype(BF16)
        kv_part[0] = part[:, :LANES]
        kv_part[1] = part[:, LANES:]
        v_bias[...] = jnp.zeros_like(v_bias)
        v_bias[0:1] = column_sum(grad[:, LANES:].astype(F32))

    @pl.when(step == pairs)
    def _():
        movers[1].stage3()
        for mover in movers:
            mover.stage4()
            mover.drain()
        down_piece[...] = movers[0].mine[3]
        up_piece[...] = movers[1].mine[3]
        input_low[...] = input_grad[...].astype(BF16)


def attention_backward(
    subs, both, facts, probs, word, entity, keys, values, ctx, dctx, wq, wkv, d_one, smalls, down_part, up_part
):
    _, rows, width = both.shape
    length = 2 * rows
    pairs = width // LANES
    block = lambda n: pl.BlockSpec((n, LANES), lambda i: (0, jnp.minimum(i, pairs - 1)))
    behind = lambda n: pl.BlockSpec((n, LANES), lambda i: (0, jnp.maximum(i - 1, 0)))
    turned = pl.BlockSpec((LANES, rows), lambda i: (jnp.minimum(i, pairs - 1), 0))
    whole = lambda a: pl.BlockSpec(a.shape, lambda i: (0,) * a.ndim, pipeline_mode=pl.Buffered(1))
    q_cols = pl.BlockSpec((4, width, LANES), lambda i: (0, 0, jnp.minimum(i, pairs - 1)))
    kv_cols = pl.BlockSpec((2, width, LANES), lambda i: (0, 0, jnp.maximum(i - 1, 0)))
    anywhere = pl.BlockSpec(memory_space=pl.ANY)
    local = pl.BlockSpec(memory_space=pltpu.VMEM)
    shape = (1, down_part.shape[1] // GRID, down_part.shape[2] // 2)
    piece = jax.ShapeDtypeStruct((1, 4) + shape[1:], BF16)
    return pl.pallas_call(
        functools.partial(backward_kernel, subs),
        grid=(pairs + 1,),
        out_shape=[
            jax.ShapeDtypeStruct(wq.shape, BF16),
            jax.ShapeDtypeStruct(wkv.shape, BF16),
            jax.ShapeDtypeStruct((rows, width), F32),
            jax.ShapeDtypeStruct((8, width), F32),
            jax.ShapeDtypeStruct((8, width), F32),
            piece,
            piece,
            jax.ShapeDtypeStruct((rows, width), BF16),
            jax.ShapeDtypeStruct((24, width), F32),
        ],
        in_specs=[
            whole(both),
            whole(facts),
            pl.BlockSpec((2, length, rows), lambda i: (jnp.minimum(i, pairs - 1), 0, 0)),
            block(rows),
            block(rows),
            block(length),
            block(length),
            turned,
            turned,
            q_cols,
            kv_cols,
            whole(d_one),
        ]
        + [whole(a) for a in smalls]
        + [anywhere, anywhere],
        out_specs=[
            q_cols,
            kv_cols,
            pl.BlockSpec((rows, width), lambda i: (0, 0), pipeline_mode=pl.Buffered(1)),
            block(8),
            behind(8),
            local,
            local,
            local,
            local,
        ],
        scratch_shapes=[
            pltpu.VMEM((length, facts.shape[1]), jnp.int32),
            pltpu.VMEM((width, rows), BF16),
            pltpu.VMEM((pairs, length, 2 * LANES), BF16),
            pltpu.VMEM((pairs, rows, 2 * LANES), BF16),
            pltpu.SemaphoreType.DMA((pairs,)),
            pltpu.SemaphoreType.DMA((pairs,)),
            pltpu.VMEM((24, width), F32),
            pltpu.VMEM((5, 24, width), F32),
            pltpu.VMEM((5, 24, width), F32),
            pltpu.SemaphoreType.DMA((5,)),
            pltpu.SemaphoreType.DMA((5,)),
        ]
        + scatter_scratch(shape)
        + scatter_scratch(shape),
        compiler_params=pltpu.CompilerParams(
            collective_id=3, has_side_effects=True, vmem_limit_bytes=VMEM_LIMIT
        ),
        name="attention_backward",
    )(
        both, facts, probs, word, entity, keys, values, ctx, dctx, wq, wkv, d_one, *smalls,
        as_shards(down_part), as_shards(up_part),
    )


def ffn_forward_kernel(
    subs, both, facts, ctx, w_out, up, down, biases, out_bias, gain, shift, grad_out,
    active, slope, hidden_low, normal_one, inverse_one, output, d_two, sums, hidden, total, traded, valid, sems,
):
    step = pl.program_id(0)
    place = Place(subs)
    rows = both.shape[1]
    trade = Trade(place, grad_out, traded, sems)

    @pl.when(step == 0)
    def _():
        entry_barrier(place)
        trade.start()
        attn = dot_nt(ctx[...].T, w_out[...]) + out_bias[0:1].astype(F32)
        resid = both[place.c].astype(F32) + attn
        normal, inverse = normalize(resid)
        out = normal * gain[0:1].astype(F32) + shift[0:1].astype(F32)
        hidden[...] = out
        hidden_low[...] = out.astype(BF16)
        normal_one[...] = normal
        inverse_one[...] = inverse
        total[...] = jnp.zeros_like(total)
        own = pl.ds(pl.multiple_of(place.c * rows, LANES), rows)
        seen = facts[place.y, :, own].T[:, 2:3].astype(F32)
        valid[...] = seen
        sums[0:1] = column_sum(seen * resid * resid)
        sums[1:2] = column_sum(seen * attn * attn)

    span = biases.shape[2]
    across = pl.num_programs(0) // 2
    lines = BLOCK // span
    half = step // across
    line = 5 + lines * (step % across)
    bias = jnp.concatenate([biases[half, pl.ds(line + i, 1), :] for i in range(lines)], axis=1)
    act, rise = gelu_pair(dot_nn(hidden_low[...], up[...]) + bias)
    act = act.astype(BF16)
    active[...] = act
    slope[...] = rise.astype(BF16)
    total[...] += dot_nt(act, down[...])

    @pl.when(step == pl.num_programs(0) - 1)
    def _():
        ffn = total[...] + out_bias[1:2].astype(F32)
        resid = hidden[...] + ffn
        normal, inverse = normalize(resid)
        output[...] = (normal * gain[1:2].astype(F32) + shift[1:2].astype(F32)).astype(BF16)
        seen = valid[...]
        trade.finish()
        grad = traded[...].astype(F32)
        back = norm_backward(grad, normal, inverse, gain[1:2].astype(F32))
        d_two[...] = back
        sums[2:3] = column_sum(seen * ffn * ffn)
        sums[3:4] = column_sum(seen * resid * resid)
        sums[4:5] = column_sum(grad * normal)
        sums[5:6] = column_sum(grad)
        sums[6:7] = column_sum(back.astype(BF16).astype(F32))
        sums[7:8] = jnp.zeros_like(sums[7:8]) + jnp.sum(seen) * (1.0 / seen.shape[0])


def ffn_forward(subs, both, facts, ctx, w_out, up, down, biases, out_bias, gain, shift, grad_out):
    _, rows, width = both.shape
    units = up.shape[1]
    whole = lambda a: pl.BlockSpec(a.shape, lambda i: (0,) * a.ndim, pipeline_mode=pl.Buffered(1))
    fixed = lambda r, w: pl.BlockSpec((r, w), lambda i: (0, 0), pipeline_mode=pl.Buffered(1))
    wide = lambda r: pl.BlockSpec((r, BLOCK), lambda i: (0, i))
    return pl.pallas_call(
        functools.partial(ffn_forward_kernel, subs),
        grid=(units // BLOCK,),
        out_shape=[
            jax.ShapeDtypeStruct((rows, units), BF16),
            jax.ShapeDtypeStruct((rows, units), BF16),
            jax.ShapeDtypeStruct((rows, width), BF16),
            jax.ShapeDtypeStruct((rows, width), F32),
            jax.ShapeDtypeStruct((rows, 1), F32),
            jax.ShapeDtypeStruct((rows, width), BF16),
            jax.ShapeDtypeStruct((rows, width), F32),
            jax.ShapeDtypeStruct((8, width), F32),
        ],
        in_specs=[whole(both), whole(facts), whole(ctx), whole(w_out), wide(width), wide(width)]
        + [whole(a) for a in (biases, out_bias, gain, shift)]
        + [pl.BlockSpec(memory_space=pltpu.VMEM)],
        out_specs=[
            wide(rows),
            wide(rows),
            fixed(rows, width),
            fixed(rows, width),
            fixed(rows, 1),
            fixed(rows, width),
            fixed(rows, width),
            fixed(8, width),
        ],
        scratch_shapes=[
            pltpu.VMEM((rows, width), F32),
            pltpu.VMEM((rows, width), F32),
            pltpu.VMEM((rows, width), BF16),
            pltpu.VMEM((rows, 1), F32),
            pltpu.SemaphoreType.DMA((3,)),
        ],
        compiler_params=pltpu.CompilerParams(
            collective_id=4, has_side_effects=True, vmem_limit_bytes=VMEM_LIMIT
        ),
        cost_estimate=pl.CostEstimate(
            flops=2 * rows * width * (width + 2 * units),
            bytes_accessed=2 * width * (width + 2 * units) + 4 * rows * units,
            transcendentals=rows * units,
        ),
        name="ffn_forward",
    )(both, facts, ctx, w_out, up, down, biases, out_bias, gain, shift, grad_out)


def ffn_backward_kernel(
    subs, result, d_two, hidden_low, active, slope, up, down, ctx, w_out, gain, normal_one, inverse_one,
    up_part, down_part, bias_part, d_one, d_ctx, out_part, sums, output, d_low, d_turned, hidden_turned, total, sems,
):
    step = pl.program_id(0)
    place = Place(subs)
    trade = Trade(place, result, output, sems)

    @pl.when(step == 0)
    def _():
        entry_barrier(place)
        trade.start()
        low = d_two[...].astype(BF16)
        d_low[...] = low
        d_turned[...] = low.T
        hidden_turned[...] = hidden_low[...].T
        total[...] = d_two[...]

    d_pre = (dot_nn(d_low[...], down[...]) * slope[...].astype(F32)).astype(BF16)
    bias_part[...] = column_sum(d_pre.astype(F32))
    up_part[...] = dot_nn(hidden_turned[...], d_pre).astype(BF16)
    down_part[...] = dot_nn(d_turned[...], active[...]).astype(BF16)
    total[...] += dot_nt(d_pre, up[...])

    @pl.when(step == pl.num_programs(0) - 1)
    def _():
        grad = total[...]
        normal = normal_one[...]
        back = norm_backward(grad, normal, inverse_one[...], gain[0:1].astype(F32))
        d_one[...] = back
        low = back.astype(BF16)
        d_ctx[...] = dot_nt(w_out[...].T, low).astype(BF16)
        out_part[...] = dot_nt(low.T, ctx[...]).astype(BF16)
        sums[...] = jnp.zeros_like(sums)
        sums[0:1] = column_sum(grad * normal)
        sums[1:2] = column_sum(grad)
        sums[2:3] = column_sum(low.astype(F32))
        trade.finish()


def ffn_backward(subs, result, d_two, hidden_low, active, slope, up, down, ctx, w_out, gain, normal_one, inverse_one):
    rows, width = d_two.shape
    units = up.shape[1]
    whole = lambda a: pl.BlockSpec(a.shape, lambda i: (0,) * a.ndim, pipeline_mode=pl.Buffered(1))
    fixed = lambda r, w: pl.BlockSpec((r, w), lambda i: (0, 0), pipeline_mode=pl.Buffered(1))
    wide = lambda r: pl.BlockSpec((r, BLOCK), lambda i: (0, i))
    return pl.pallas_call(
        functools.partial(ffn_backward_kernel, subs),
        grid=(units // BLOCK,),
        out_shape=[
            jax.ShapeDtypeStruct((width, units), BF16),
            jax.ShapeDtypeStruct((width, units), BF16),
            jax.ShapeDtypeStruct((1, units), F32),
            jax.ShapeDtypeStruct((rows, width), F32),
            jax.ShapeDtypeStruct((width, rows), BF16),
            jax.ShapeDtypeStruct((width, width), BF16),
            jax.ShapeDtypeStruct((8, width), F32),
            jax.ShapeDtypeStruct((rows, width), BF16),
        ],
        in_specs=[pl.BlockSpec(memory_space=pltpu.VMEM), whole(d_two), whole(hidden_low), wide(rows), wide(rows), wide(width), wide(width)]
        + [whole(a) for a in (ctx, w_out, gain, normal_one, inverse_one)],
        out_specs=[
            wide(width),
            wide(width),
            wide(1),
            fixed(rows, width),
            fixed(width, rows),
            fixed(width, width),
            fixed(8, width),
            pl.BlockSpec(memory_space=pl.ANY),
        ],
        scratch_shapes=[
            pltpu.VMEM((rows, width), BF16),
            pltpu.VMEM((width, rows), BF16),
            pltpu.VMEM((width, rows), BF16),
            pltpu.VMEM((rows, width), F32),
            pltpu.SemaphoreType.DMA((3,)),
        ],
        compiler_params=pltpu.CompilerParams(
            collective_id=5, has_side_effects=True, vmem_limit_bytes=VMEM_LIMIT
        ),
        cost_estimate=pl.CostEstimate(
            flops=4 * rows * width * (width + 2 * units),
            bytes_accessed=2 * width * (3 * width + 4 * units) + 4 * rows * units,
            transcendentals=0,
        ),
        name="ffn_backward",
    )(result, d_two, hidden_low, active, slope, up, down, ctx, w_out, gain, normal_one, inverse_one)


def body(
    layer_input,
    grad_out,
    segment,
    entity,
    valid_mask,
    query_weight,
    key_value_weight,
    attn_bias,
    out_weight,
    out_bias,
    ln_gain,
    ln_bias,
    up_weight,
    ffn_bias,
    down_weight,
):
    rows, width = layer_input.shape
    length = segment.shape[0]
    rank = lax.axis_index("tensor")
    subs = lax.axis_size("dp") // GRID
    shards = [
        query_weight,
        key_value_weight,
        out_weight.T[None],
        up_weight[None],
        down_weight.T[None],
    ]
    groups = [[b * subs + s for s in range(subs)] for b in range(GRID)]
    if subs > 1:
        shards = [
            lax.all_gather(s, "dp", axis=1, tiled=True, axis_index_groups=groups) for s in shards
        ]
    shards = [shards[1], shards[0]] + shards[2:]
    cols = attn_bias.shape[1]
    (w_kv, w_q, w_out_t, w_up, w_down_t), (both, biases, pair_facts) = gather_weights(
        subs, shards, 3, layer_input, attn_bias, ffn_bias[None], [segment[None], entity[None], valid_mask[None]]
    )
    w_kv, w_q, w_out_t = as_matrix(w_kv), as_matrix(w_q), as_matrix(w_out_t)[0]
    context_t, probs, query_word, query_ent, keys, values, w_up, w_down_t = attention_forward(
        subs, both, w_q, w_kv, biases, pair_facts, w_up, w_down_t
    )
    w_up, w_down_t = as_matrix(w_up)[0], as_matrix(w_down_t)[0]
    active, slope, hidden_low, normal_one, inverse_one, result, d_two, sums_two = ffn_forward(
        subs, both, pair_facts, context_t, w_out_t, w_up, w_down_t, biases, out_bias, ln_gain, ln_bias, grad_out,
    )
    up_part, down_part, ffn_bias_part, d_one, d_context_t, out_part, sums_one, output = ffn_backward(
        subs, result, d_two, hidden_low, active, slope, w_up, w_down_t, context_t, w_out_t, ln_gain, normal_one, inverse_one
    )

    query_part, kv_part, input_grad, q_bias, v_bias, down_piece, up_piece, input_low, stack = attention_backward(
        subs, both, pair_facts, probs, query_word, query_ent, keys, values, context_t, d_context_t, w_q, w_kv, d_one,
        [sums_one, sums_two, ffn_bias_part], down_part[None], up_part[None],
    )
    sums, bias_sum, input_grad = scatter_gradients(
        subs,
        [down_piece, up_piece],
        [query_part, kv_part, out_part[None]],
        [q_bias, v_bias],
        input_grad,
        input_low,
    )
    if subs > 1:
        sums = [
            lax.psum_scatter(s, "dp", scatter_dimension=1, tiled=True, axis_index_groups=groups)
            for s in sums
        ]
        stack = lax.psum(stack, "dp", axis_index_groups=groups)
        bias_sum = lax.psum(bias_sum, "dp", axis_index_groups=groups)
    down_sum, up_sum, query_sum, kv_sum, out_sum = sums
    half = ffn_bias.shape[0]
    gains, shifts, out_biases, attn_biases, unit_biases, rms, query_sum, kv_sum, up_sum, input_grad, output = finish(
        subs, rows, stack, bias_sum, cols, half, [query_sum, kv_sum, up_sum, input_grad, output]
    )
    return (
        output,
        input_grad,
        rms[0],
        query_sum,
        kv_sum,
        attn_biases,
        out_sum[0].T,
        out_biases,
        gains,
        shifts,
        up_sum[0],
        unit_biases[0],
        down_sum[0].T,
    )


def solution(mesh):
    placed = (
        P(("dp", "tensor"), None),
        P(("dp", "tensor"), None),
        P("dp"),
        P("dp"),
        P("dp"),
        P(None, "dp", "tensor"),
        P(None, "dp", "tensor"),
        P(None, "tensor"),
        P("tensor", "dp"),
        P(),
        P(),
        P(),
        P("dp", "tensor"),
        P("tensor"),
        P("tensor", "dp"),
    )
    return jax.shard_map(
        body,
        mesh=mesh,
        in_specs=placed,
        out_specs=(
            P(("dp", "tensor"), None),
            P(("dp", "tensor"), None),
            P(),
            P(None, "dp", "tensor"),
            P(None, "dp", "tensor"),
            P(None, "tensor"),
            P("tensor", "dp"),
            P(),
            P(),
            P(),
            P("dp", "tensor"),
            P("tensor"),
            P("tensor", "dp"),
        ),
        check_vma=False,
    )
```

```python
import functools

import jax
import jax.numpy as jnp
from jax import lax
from jax.experimental import pallas as pl
from jax.experimental.pallas import tpu as pltpu
from jax.sharding import PartitionSpec as P

HEAD = 64
EPS = 1e-06
NEG = -1e30
GRID = 16
LANES = 128
MESH = pl.DeviceIdType.MESH
BF16 = jnp.bfloat16
F32 = jnp.float32
VMEM_LIMIT = 60 * 1024 * 1024


BLOCK = 768
TAIL = 0.34
TAIL_Q = (
    0.1918165616711201,
    0.1920366827922902,
    0.17827181747742213,
    0.1748548010854969,
    0.05944614604180367,
    0.27541659722682194,
    -0.27820700083503797,
    0.4016320911891782,
    -0.24597742961536673,
    0.050709736470982834,
)


def gelu_pair(v):
    size = jnp.abs(v)
    t = 1.0 / (1.0 + (TAIL * 0.5**0.5) * size)
    q = jnp.full_like(v, TAIL_Q[-1])
    for coefficient in TAIL_Q[-2::-1]:
        q = q * t + coefficient
    bell = jnp.exp(-0.5 * (v * v))
    tail = 0.5 * (bell * (t * q))
    cdf = jnp.where(v < 0, tail, 1.0 - tail)
    return v * cdf, cdf + v * (bell * 0.3989422804014327)


def normalize(resid):
    center = resid - jnp.mean(resid, -1, keepdims=True)
    inverse = lax.rsqrt(jnp.mean(center * center, -1, keepdims=True) + EPS)
    return center * inverse, inverse


def norm_backward(grad, normal, inverse, gain):
    scaled = grad * gain
    return inverse * (
        scaled
        - jnp.mean(scaled, -1, keepdims=True)
        - normal * jnp.mean(scaled * normal, -1, keepdims=True)
    )


def column_sum(a):
    return jnp.sum(a, 0, keepdims=True)


class Place:
    def __init__(self, subs):
        rank = lax.axis_index("dp")
        self.subs = subs
        self.sub = rank % subs
        block = rank // subs
        self.z = block // 4
        self.turns = [(self.z + step) % 4 for step in range(4)]
        self.x = (block // 2) % 2
        self.c = block % 2
        self.y = lax.axis_index("tensor")
        self.moved = self.y != self.c
        self.x1 = jnp.where(self.c == 0, 1 - self.x, self.x)
        self.y1 = jnp.where(self.c == 0, self.y, 1 - self.y)
        self.x2 = jnp.where(self.c == 0, self.x, 1 - self.x)
        self.y2 = jnp.where(self.c == 0, 1 - self.y, self.y)

    def device(self, z=None, x=None, c=None, y=None):
        z = self.z if z is None else z
        x = self.x if x is None else x
        c = self.c if c is None else c
        y = self.y if y is None else y
        return (((z * 2 + x) * 2 + c) * self.subs + self.sub, y)

    def z_peer(self, step):
        return self.device(z=(self.z + step) % 4)

    def first(self, flat=False):
        return self.across() if flat else self.device(x=self.x1, y=self.y1)

    def second(self, flat=False):
        return self.device(x=1 - self.x) if flat else self.device(x=self.x2, y=self.y2)

    def sibling(self):
        return self.device(c=1 - self.c)

    def plane(self):
        x, y, c = (self.x, 1 - self.x), (self.y, 1 - self.y), (self.c, 1 - self.c)
        return [self.device(x=x[k // 4], y=y[k // 2 % 2], c=c[k % 2]) for k in range(1, 8)]

    def across(self):
        return self.device(y=1 - self.y)

    def transposed(self):
        return self.device(c=1 - self.c, y=1 - self.y)

    def pieces(self, flat=False):
        if flat:
            return ((self.x, self.y), (self.x, 1 - self.y), (1 - self.x, self.y), (1 - self.x, 1 - self.y))
        return (
            (self.x, self.y),
            (self.x1, self.y1),
            (self.x2, self.y2),
            (1 - self.x, 1 - self.y),
        )


def entry_barrier(place):
    barrier = pltpu.get_barrier_semaphore()
    peers = [place.z_peer(step) for step in (1, 2, 3)]
    peers += place.plane()
    for peer in peers:
        pl.semaphore_signal(barrier, inc=1, device_id=peer, device_id_type=MESH)
    pl.semaphore_wait(barrier, len(peers))


def remote(src, dst, send, recv, peer):
    return pltpu.make_async_remote_copy(
        src_ref=src, dst_ref=dst, send_sem=send, recv_sem=recv, device_id=peer, device_id_type=MESH
    )


class Trade:
    def __init__(self, place, own, got, sems):
        self.moved = place.moved
        self.kept = pltpu.make_async_copy(own, got, sems.at[2])
        self.swap = remote(own, got, sems.at[0], sems.at[1], place.transposed())

    def start(self):
        @pl.when(self.moved)
        def _():
            self.swap.start()

        @pl.when(jnp.logical_not(self.moved))
        def _():
            self.kept.start()

    def finish(self):
        @pl.when(self.moved)
        def _():
            self.swap.wait()

        @pl.when(jnp.logical_not(self.moved))
        def _():
            self.kept.wait()


class Gather:
    def __init__(self, place, shard, full, send, recv, local=None, whole=True, flat=False):
        self.flat = flat
        self.place, self.shard, self.full, self.whole = place, shard, full, whole
        self.send, self.recv, self.local = send, recv, local
        self.w = full.shape[-1] // 2

    def cols(self, y):
        return pl.ds(pl.multiple_of(y * self.w, LANES), self.w)

    def piece(self, spot, c):
        x, y = spot
        return self.full.at[:, :, x, c, :, self.cols(y)]

    def copy(self, index, src, dst, peer):
        remote(src, dst, self.send.at[index], self.recv.at[index], peer).start()

    def arrive(self, index, ref):
        remote(ref, ref, self.send.at[index], self.recv.at[index], self.place.sibling()).wait_recv()

    def gone(self, index, ref):
        remote(ref, ref, self.send.at[index], self.recv.at[index], self.place.sibling()).wait_send()

    def own(self, z):
        p = self.place
        return self.full.at[:, z, p.x, p.c, :, self.cols(p.y)]

    def stage1(self):
        p = self.place
        self.kept = pltpu.make_async_copy(self.shard, self.own(p.z), self.local)
        self.kept.start()
        for step in (1, 2, 3):
            self.copy(step - 1, self.shard, self.own(p.z), p.z_peer(step))

    def land(self):
        p = self.place
        self.kept.wait()
        for step in (1, 2, 3):
            self.arrive(step - 1, self.own((p.z + 4 - step) % 4))

    def settle(self):
        self.land()
        for index in range(3):
            self.gone(index, self.shard)

    def spread(self):
        p = self.place
        mine = self.piece(p.pieces(self.flat)[0], p.c)
        self.copy(3, mine, mine, p.first(self.flat))
        self.copy(4, mine, mine, p.second(self.flat))
        self.copy(6, mine, mine, p.sibling())

    def stage2(self):
        self.land()
        self.spread()

    def stage3(self):
        p = self.place
        got = self.piece(p.pieces(self.flat)[1], p.c)
        self.arrive(3, got)
        self.copy(5, got, got, p.second(self.flat))
        self.copy(7, got, got, p.sibling())

    def stage4(self):
        p = self.place
        for index, spot in ((4, 2), (5, 3)):
            got = self.piece(p.pieces(self.flat)[spot], p.c)
            self.arrive(index, got)
            self.copy(index + 4, got, got, p.sibling())

    def stage5(self):
        p = self.place
        spots = p.pieces(self.flat)
        for index, spot in ((6, 0), (7, 1 if self.flat else 2), (8, 2 if self.flat else 1), (9, 3)):
            self.arrive(index, self.piece(spots[spot], 1 - p.c))
        for index in range(3, 10):
            self.gone(index, self.piece(spots[0], p.c))

    def last(self):
        self.stage5()
        for index in range(3):
            self.gone(index, self.shard)

    def stages(self):
        if not self.whole:
            return [self.stage1, self.settle]
        return [self.stage1, self.stage2, self.stage3, self.stage4, self.last]


def wavefront(movers):
    lists = [mover.stages() for mover in movers]
    depth = max(len(stages) for stages in lists)
    order = []
    for time in range(len(lists) + depth - 1):
        for index in range(len(lists)):
            stage = time - index
            if 0 <= stage < len(lists[index]):
                order.append(lists[index][stage])
    return order


def cuts(counts):
    return [(i, a, min(2, m)) for i, m in enumerate(counts) for a in range(0, m, 2)]


class Share:
    def __init__(self, source, pair, index, peer, sems):
        self.kept = pltpu.make_async_copy(source, pair.at[index], sems.at[2])
        self.sent = remote(source, pair.at[index], sems.at[0], sems.at[1], peer)

    def start(self):
        self.kept.start()
        self.sent.start()

    def finish(self):
        self.kept.wait()
        self.sent.wait()


class Rows:
    def __init__(self, place, rows, both, sems):
        p = place
        half = both.at[p.c]
        self.moved = p.moved
        self.kept = pltpu.make_async_copy(rows, half, sems.at[4])
        self.swap = remote(rows, both.at[p.y], sems.at[0], sems.at[1], p.transposed())
        self.swapped = remote(half, half, sems.at[0], sems.at[1], p.transposed())
        self.share = remote(rows, half, sems.at[2], sems.at[3], p.sibling())
        self.relay = remote(half, half, sems.at[2], sems.at[3], p.sibling())
        other = both.at[1 - p.c]
        self.other = remote(other, other, sems.at[2], sems.at[3], p.sibling())

    def start(self):
        @pl.when(self.moved)
        def _():
            self.swap.start()

        @pl.when(jnp.logical_not(self.moved))
        def _():
            self.kept.start()
            self.share.start()

    def forward(self):
        @pl.when(self.moved)
        def _():
            self.swapped.wait_recv()
            self.relay.start()

    def finish(self):
        @pl.when(self.moved)
        def _():
            self.swap.wait_send()
            self.relay.wait_send()

        @pl.when(jnp.logical_not(self.moved))
        def _():
            self.kept.wait()
            self.share.wait_send()

        self.other.wait_recv()


def gather_kernel(subs, count, wholes, *refs):
    shards, (rows, bias_rows, unit_bias), columns = refs[:count], refs[count : count + 3], refs[count + 3 : count + 6]
    fulls, (both, biases, pair_facts) = refs[count + 6 : 2 * count + 6], refs[2 * count + 6 : 2 * count + 9]
    send, recv, local, row_sems, share_sems, bias, facts = refs[2 * count + 9 :]
    place = Place(subs)
    entry_barrier(place)
    tokens = Rows(place, rows, both, row_sems)
    bias[...] = jnp.zeros_like(bias)
    many, span = bias_rows.shape
    bias[0:many] = bias_rows[...].astype(F32)
    for i in range(unit_bias.shape[1] // span):
        bias[many + i : many + i + 1] = unit_bias[:, i * span : (i + 1) * span].astype(F32)
    facts[...] = jnp.zeros_like(facts)
    for i in range(3):
        facts[i : i + 1] = columns[i][...]
    shares = [
        Share(facts, pair_facts, place.c, place.sibling(), share_sems.at[0]),
        Share(bias, biases, place.y, place.across(), share_sems.at[1]),
    ]
    tokens.start()
    for share in shares:
        share.start()
    movers = [
        Gather(
            place, shards[i].at[pl.ds(a, m)], fulls[i].at[pl.ds(a, m)], send.at[n], recv.at[n], local.at[n], i < wholes
        )
        for n, (i, a, m) in enumerate(cuts([shard.shape[0] for shard in shards]))
    ]
    for mover in movers[:2]:
        mover.stage1()
    steps = [s for s in wavefront(movers) if s.__func__ is not Gather.stage1]
    late = [s for s in steps if s.__func__ is Gather.settle]
    landed = 0
    for index, step in enumerate([s for s in steps if s not in late] + late):
        step()
        if index == 1:
            tokens.forward()
        if step.__func__ in (Gather.stage2, Gather.settle):
            landed += 1
            if landed + 1 < len(movers):
                movers[landed + 1].stage1()
    tokens.finish()
    for share in shares:
        share.finish()


def gather_weights(subs, shards, wholes, rows, bias_rows, unit_bias, columns):
    count = len(shards)
    outs = [
        jax.ShapeDtypeStruct((s.shape[0], 4, 2, 2, s.shape[1], 2 * s.shape[2]), BF16) for s in shards
    ]
    movers = len(cuts([s.shape[0] for s in shards]))
    bias, facts = (16, bias_rows.shape[1]), (8, columns[0].shape[1])
    outs += [
        jax.ShapeDtypeStruct((2,) + rows.shape, rows.dtype),
        jax.ShapeDtypeStruct((2,) + bias, F32),
        jax.ShapeDtypeStruct((2,) + facts, jnp.int32),
    ]
    results = pl.pallas_call(
        functools.partial(gather_kernel, subs, count, wholes),
        out_shape=outs,
        in_specs=[pl.BlockSpec(memory_space=pltpu.VMEM)] * (count + 6),
        out_specs=[pl.BlockSpec(memory_space=pl.ANY)] * (count + 3),
        scratch_shapes=[
            pltpu.SemaphoreType.DMA((movers, 10)),
            pltpu.SemaphoreType.DMA((movers, 10)),
            pltpu.SemaphoreType.DMA((movers,)),
            pltpu.SemaphoreType.DMA((5,)),
            pltpu.SemaphoreType.DMA((2, 3)),
            pltpu.VMEM(bias, F32),
            pltpu.VMEM(facts, jnp.int32),
        ],
        compiler_params=pltpu.CompilerParams(
            collective_id=0, has_side_effects=True, vmem_limit_bytes=VMEM_LIMIT
        ),
        name="gather_weights",
    )(*shards, rows, bias_rows, unit_bias, *columns)
    return results[:count], results[count:]


def as_matrix(full):
    return full.reshape(full.shape[0], GRID * full.shape[4], full.shape[5])


class Last:
    def __init__(self, place, piece, total, from_z, send, recv):
        self.place, self.piece, self.total, self.from_z = place, piece, total, from_z
        self.send, self.recv = send, recv

    def start(self):
        p = self.place
        for step in (1, 2, 3):
            remote(
                self.piece.at[:, p.turns[step]],
                self.from_z.at[step - 1],
                self.send.at[step - 1],
                self.recv.at[step - 1],
                p.z_peer(step),
            ).start()

    def finish(self):
        p = self.place
        for step in (0, 1, 2):
            slot = self.from_z.at[step]
            remote(slot, slot, self.send.at[step], self.recv.at[step], p.sibling()).wait()

        def step(i, carry):
            total = self.piece[i, p.z].astype(F32)
            for s in range(3):
                total = total + self.from_z[s, i].astype(F32)
            self.total[i] = total
            return carry

        lax.fori_loop(0, self.total.shape[0], step, 0)


class Scatter:
    def __init__(self, place, part, mine, from_core, from_second, from_first, send, recv, local):
        self.place, self.part = place, part
        self.mine, self.from_core = mine, from_core
        self.from_second, self.from_first = from_second, from_first
        self.send, self.recv, self.local = send, recv, local
        self.m, _, self.rows, self.w = from_first.shape

    def cols(self, y):
        return pl.ds(pl.multiple_of(y * self.w, LANES), self.w)

    def copy(self, index, src, dst, peer):
        remote(src, dst, self.send.at[index], self.recv.at[index], peer).start()

    def arrive(self, index, ref):
        remote(ref, ref, self.send.at[index], self.recv.at[index], self.place.sibling()).wait_recv()

    def drain(self):
        for index in range(7):
            remote(
                self.from_first, self.from_first, self.send.at[index], self.recv.at[index], self.place.sibling()
            ).wait_send()

    def add(self, target, source):
        m = self.m

        def step(index, carry):
            i, z = index // 4, index % 4
            target[i, z] = (target[i, z].astype(F32) + source[i, z].astype(F32)).astype(BF16)
            return carry

        lax.fori_loop(0, m * 4, step, 0)

    def keep(self, slot, spot):
        x, y = self.place.pieces()[spot]
        source = self.part.at[:, :, x, self.place.c, :, self.cols(y)]
        return pltpu.make_async_copy(source, self.mine.at[slot], self.local.at[slot])

    def stage1(self):
        p = self.place
        spots = p.pieces()
        for slot, (here, there) in enumerate(((3, 3), (2, 1), (1, 2), (0, 0))):
            self.keep(slot, here).start()
            x, y = spots[there]
            self.copy(
                slot,
                self.part.at[:, :, x, 1 - p.c, :, self.cols(y)],
                self.from_core.at[slot],
                p.sibling(),
            )

    def joined(self, slot):
        self.keep(slot, 3 - slot).wait()
        self.arrive(slot, self.from_core.at[slot])
        self.add(self.mine.at[slot], self.from_core.at[slot])

    def stage2(self):
        p = self.place
        for slot in (0, 1):
            self.joined(slot)
            self.copy(4 + slot, self.mine.at[slot], self.from_second.at[slot], p.second())
        for slot in (2, 3):
            self.joined(slot)

    def stage3(self):
        p = self.place
        self.arrive(4, self.from_second.at[0])
        self.add(self.mine.at[2], self.from_second.at[0])
        self.copy(6, self.mine.at[2], self.from_first, p.first())
        self.arrive(5, self.from_second.at[1])
        self.add(self.mine.at[3], self.from_second.at[1])

    def stage4(self):
        self.arrive(6, self.from_first)
        self.add(self.mine.at[3], self.from_first)


class Sum:
    def __init__(self, place, source, total, box, send, recv):
        self.place, self.source, self.total = place, source, total
        self.box, self.send, self.recv = box, send, recv
        p = place
        flip = p.z + 1 - 2 * (p.z % 2)
        self.peers = (p.device(x=1 - p.x), p.across(), p.device(z=flip), p.device(z=p.turns[2]), p.sibling())

    def term(self, index):
        return self.source if index == 0 else self.total.at[index - 1]

    def exchange(self, index):
        return remote(
            self.term(index), self.box.at[index], self.send.at[index], self.recv.at[index], self.peers[index]
        )

    def hop(self, index):
        self.exchange(index).start()

    def land(self, index):
        self.exchange(index).wait()
        self.total[index] = self.term(index)[...] + self.box[index]


class PlaneSum:
    def __init__(self, place, source, middle, plane, line, send, recv):
        self.place, self.source, self.middle = place, source, middle
        self.plane, self.line, self.send, self.recv = plane, line, send, recv
        p = place
        spot = (p.x * 2 + p.y) * 2 + p.c
        self.first = [
            remote(source, plane.at[spot], send.at[k], recv.at[k], peer) for k, peer in enumerate(p.plane())
        ]
        self.second = [
            remote(middle, line.at[p.z], send.at[6 + k], recv.at[6 + k], p.z_peer(k)) for k in (1, 2, 3)
        ]
        self.spot = spot

    def start(self):
        for step in self.first:
            step.start()
        self.plane[self.spot] = self.source[...]

    def turn(self):
        for step in self.first:
            step.wait()
        total = self.plane[0]
        for k in range(1, 8):
            total = total + self.plane[k]
        self.middle[...] = total
        for step in self.second:
            step.start()
        self.line[self.place.z] = total

    def finish(self):
        for step in self.second:
            step.wait()
        total = self.line[0]
        for k in range(1, 4):
            total = total + self.line[k]
        return total


def scatter_scratch(shape):
    m, rows, w = shape
    return [
        pltpu.VMEM((4, m, 4, rows, w), BF16),
        pltpu.VMEM((4, m, 4, rows, w), BF16),
        pltpu.VMEM((2, m, 4, rows, w), BF16),
        pltpu.VMEM((m, 4, rows, w), BF16),
        pltpu.SemaphoreType.DMA((7,)),
        pltpu.SemaphoreType.DMA((7,)),
        pltpu.SemaphoreType.DMA((4,)),
    ]


def last_scratch(shape):
    return [
        pltpu.VMEM((3,) + shape, BF16),
        pltpu.SemaphoreType.DMA((3,)),
        pltpu.SemaphoreType.DMA((3,)),
    ]


def as_shards(part):
    m, rows, w = part.shape
    return part.reshape(m, 4, 2, 2, rows // GRID, w)


def scatter_kernel(subs, early, count, *refs):
    pieces, parts, smalls = refs[:early], refs[early : early + count], refs[early + count :][:2]
    input_grad, input_low = refs[early + count + 2 :][:2]
    refs = refs[early + count + 4 :]
    totals, (small_total, result, traded, trade_sems) = refs[: early + count], refs[early + count :][:4]
    refs = refs[early + count + 4 :]
    lasts, refs = refs[: 3 * (early + count)], refs[3 * (early + count) :]
    place = Place(subs)
    entry_barrier(place)
    movers = [Scatter(place, parts[i], *refs[7 * i : 7 * i + 7]) for i in range(count)]
    sources = list(pieces) + [mover.mine.at[3] for mover in movers]
    ends = [Last(place, sources[i], totals[i], *lasts[3 * i : 3 * i + 3]) for i in range(early + count)]
    small, *boxes = refs[7 * count :]
    small[...] = smalls[0][...]
    small[4:5] = smalls[1][0:1]
    small_sum = PlaneSum(place, small, *boxes)
    trade = Trade(place, input_low, traded, trade_sems)
    small_sum.start()
    for mover in movers:
        mover.stage1()
    small_sum.turn()
    for end in ends[:early]:
        end.start()
    for time in range(count + 2):
        for index in range(count):
            stage = time - index
            if 0 <= stage < 3:
                mover = movers[index]
                (mover.stage2, mover.stage3, mover.stage4)[stage]()
                if stage == 1 and index == count - 1:
                    trade.start()
                if stage == 2:
                    ends[early + index].start()
    small_total[...] = small_sum.finish()
    for end in ends[early:]:
        end.finish()
    for end in ends[:early]:
        end.finish()
    for mover in movers:
        mover.drain()
    trade.finish()
    result[...] = jnp.where(place.moved, traded[...].astype(F32), input_grad[...])


def scatter_gradients(subs, pieces, parts, smalls, input_grad, input_low):
    early, count = len(pieces), len(parts)
    shaped = [as_shards(p) for p in parts]
    shapes = [(p.shape[0],) + p.shape[2:] for p in pieces]
    whole = [(p.shape[0], p.shape[4], p.shape[5] // 2) for p in shaped]
    outs = [jax.ShapeDtypeStruct(s, F32) for s in shapes + whole]
    stack = smalls[0].shape
    outs += [jax.ShapeDtypeStruct(stack, F32), jax.ShapeDtypeStruct(input_grad.shape, F32)]
    scratch = [pltpu.VMEM(input_low.shape, BF16), pltpu.SemaphoreType.DMA((3,))]
    for s in shapes + whole:
        scratch += last_scratch(s)
    for s in whole:
        scratch += scatter_scratch(s)
    scratch += [
        pltpu.VMEM(stack, F32),
        pltpu.VMEM(stack, F32),
        pltpu.VMEM((8,) + stack, F32),
        pltpu.VMEM((4,) + stack, F32),
        pltpu.SemaphoreType.DMA((10,)),
        pltpu.SemaphoreType.DMA((10,)),
    ]
    local = pl.BlockSpec(memory_space=pltpu.VMEM)
    results = pl.pallas_call(
        functools.partial(scatter_kernel, subs, early, count),
        out_shape=outs,
        in_specs=[local] * early + [pl.BlockSpec(memory_space=pl.ANY)] * count + [local] * 4,
        out_specs=[local] * (early + count + 2),
        scratch_shapes=scratch,
        compiler_params=pltpu.CompilerParams(
            collective_id=1, has_side_effects=True, vmem_limit_bytes=VMEM_LIMIT
        ),
        name="scatter_gradients",
    )(*pieces, *shaped, *smalls, input_grad, input_low)
    return results[:-2], results[-2], results[-1]


def finish_kernel(place_of, rows, stack, biases, query, kv, up, grad, out, gains, shifts, out_bias, attn_bias, unit_bias, rms, *results):
    place = place_of()
    width = stack.shape[1]
    lines = unit_bias.shape[1] // width
    for i in range(lines):
        unit_bias[:, i * width : (i + 1) * width] = stack[pl.ds(16 + place.y * lines + i, 1), :]
    real = jnp.mean(stack[15:16], 1, keepdims=True) * (rows * width)
    lane = lax.broadcasted_iota(jnp.int32, (1, 4), 1)
    squares = jnp.zeros((1, 4), F32)
    for i in range(4):
        squares = jnp.where(lane == i, jnp.sum(stack[8 + i : 9 + i], 1, keepdims=True), squares)
    rms[...] = jnp.sqrt(squares / real)
    for i, ref in enumerate((gains, shifts, out_bias)):
        ref[0:1] = stack[i : i + 1]
        ref[1:2] = stack[12 + i : 13 + i]
    cols = attn_bias.shape[1]
    mine = pl.ds(pl.multiple_of(place.y * cols, LANES), cols)
    attn_bias[...] = biases[0:5, mine]
    for source, target in zip((query, kv, up, grad, out), results):
        target[...] = source[...]


def finish(subs, rows, stack, biases, cols, units, arrays):
    width = stack.shape[1]
    shapes = [(2, width)] * 3 + [(5, cols), (1, units), (1, 4)]
    outs = [jax.ShapeDtypeStruct(s, F32) for s in shapes] + [jax.ShapeDtypeStruct(a.shape, a.dtype) for a in arrays]
    return pl.pallas_call(
        functools.partial(finish_kernel, functools.partial(Place, subs), rows),
        out_shape=outs,
        compiler_params=pltpu.CompilerParams(vmem_limit_bytes=VMEM_LIMIT),
        name="finish",
    )(stack, biases, *arrays)


def head_lanes(half):
    lane = lax.broadcasted_iota(jnp.int32, (1, LANES), 1)
    return (lane // HEAD) == half


def dot_nt(a, b):
    return lax.dot_general(a, b, (((1,), (1,)), ((), ())), preferred_element_type=F32)


def dot_nn(a, b):
    return lax.dot_general(a, b, (((1,), (0,)), ((), ())), preferred_element_type=F32)


def forward_kernel(
    subs, both, wq, wkv, biases, facts, up_in, down_in,
    ctx, probs, word, entity, keys, values, up, down, mask, column, send, recv,
):
    place = Place(subs)
    step = pl.program_id(0)
    length, rows = mask.shape
    movers = [Gather(place, None, full, send.at[i], recv.at[i]) for i, full in enumerate((up, down))]
    own = pl.ds(pl.multiple_of(place.c * rows, LANES), rows)

    @pl.when(step == 0)
    def _():
        entry_barrier(place)
        for mover in movers:
            mover.spread()
        column[...] = facts[place.y].T
        spot = lax.broadcasted_iota(jnp.int32, (length, rows), 0)
        here = lax.broadcasted_iota(jnp.int32, (length, rows), 1) + place.c * rows
        same = column[:, 0:1] == facts[place.y, 0:1, own]
        seen = (column[:, 2:3] == 1) | (spot == here)
        mask[...] = jnp.where(same & seen, 0.0, NEG)

    @pl.when(step == 3)
    def _():
        movers[0].stage3()

    @pl.when(step == 5)
    def _():
        movers[1].stage3()

    tokens = both[...].reshape(length, both.shape[2])
    mine = both[place.c]
    bias = biases[0]
    row_ent = column[own, 1:2] == 1
    to_word = dot_nn(mine, jnp.concatenate([wq[0], wq[2]], axis=1))
    to_ent = dot_nn(mine, jnp.concatenate([wq[1], wq[3]], axis=1))
    scale = HEAD ** (-0.5)
    query_word = jnp.where(row_ent, to_word[:, LANES:] + bias[2:3], to_word[:, :LANES] + bias[0:1])
    query_ent = jnp.where(row_ent, to_ent[:, LANES:] + bias[3:4], to_ent[:, :LANES] + bias[1:2])
    word[...] = query_word.astype(BF16) * BF16(scale)
    entity[...] = query_ent.astype(BF16) * BF16(scale)
    pair = dot_nn(tokens, jnp.concatenate([wkv[0], wkv[1]], axis=1))
    key = pair[:, :LANES].astype(BF16)
    value = (pair[:, LANES:] + bias[4:5]).astype(BF16)
    keys[...] = key
    values[...] = value

    queries = jnp.concatenate([word[...], entity[...]], axis=1)
    ent = column[:, 1:2] == 1
    zero = jnp.zeros_like(key)
    turned = value.T
    for half in range(2):
        lanes = head_lanes(half)
        wide = jnp.concatenate(
            [jnp.where(lanes & ~ent, key, zero), jnp.where(lanes & ent, key, zero)], axis=1
        )
        scores = dot_nt(wide, queries) + mask[...]
        top = jnp.max(scores, axis=0, keepdims=True)
        expo = jnp.exp(scores - top)
        total = jnp.sum(expo, axis=0, keepdims=True)
        prob = (expo * (1.0 / total)).astype(BF16)
        probs[half] = prob
        ctx[half * HEAD : (half + 1) * HEAD, :] = dot_nn(
            turned[half * HEAD : (half + 1) * HEAD, :], prob
        ).astype(BF16)

    @pl.when(step == pl.num_programs(0) - 1)
    def _():
        for mover in movers:
            mover.stage4()
        for mover in movers:
            mover.stage5()


def attention_forward(subs, both, wq, wkv, biases, facts, up, down):
    _, rows, width = both.shape
    length = 2 * rows
    pairs = width // LANES
    span = biases.shape[2] // LANES
    block = lambda n: pl.BlockSpec((n, LANES), lambda i: (0, i))
    whole = lambda a: pl.BlockSpec(a.shape, lambda i: (0,) * a.ndim, pipeline_mode=pl.Buffered(1))
    cols = lambda a: pl.BlockSpec(a.shape[:2] + (LANES,), lambda i: (0, 0, i))
    anywhere = pl.BlockSpec(memory_space=pl.ANY)
    return pl.pallas_call(
        functools.partial(forward_kernel, subs),
        grid=(pairs,),
        out_shape=[
            jax.ShapeDtypeStruct((width, rows), BF16),
            jax.ShapeDtypeStruct((2 * pairs, length, rows), BF16),
            jax.ShapeDtypeStruct((rows, width), BF16),
            jax.ShapeDtypeStruct((rows, width), BF16),
            jax.ShapeDtypeStruct((length, width), BF16),
            jax.ShapeDtypeStruct((length, width), BF16),
            jax.ShapeDtypeStruct(up.shape, BF16),
            jax.ShapeDtypeStruct(down.shape, BF16),
        ],
        in_specs=[
            whole(both),
            cols(wq),
            cols(wkv),
            pl.BlockSpec((1, biases.shape[1], LANES), lambda i: (i // span, 0, i % span)),
            whole(facts),
            anywhere,
            anywhere,
        ],
        out_specs=[
            pl.BlockSpec((LANES, rows), lambda i: (i, 0)),
            pl.BlockSpec((2, length, rows), lambda i: (i, 0, 0)),
            block(rows),
            block(rows),
            block(length),
            block(length),
            anywhere,
            anywhere,
        ],
        scratch_shapes=[
            pltpu.VMEM((length, rows), F32),
            pltpu.VMEM((length, facts.shape[1]), jnp.int32),
            pltpu.SemaphoreType.DMA((2, 10)),
            pltpu.SemaphoreType.DMA((2, 10)),
        ],
        input_output_aliases={5: 6, 6: 7},
        compiler_params=pltpu.CompilerParams(
            collective_id=2, has_side_effects=True, vmem_limit_bytes=VMEM_LIMIT
        ),
        name="attention_forward",
    )(both, wq, wkv, biases, facts, up, down)


def backward_kernel(
    subs, both, facts, probs, word, entity, keys, values, ctx, dctx, wq, wkv, d_one, sums_one, sums_two, unit_sums,
    down_part, up_part, q_part, kv_part, input_grad, q_bias, v_bias, down_piece, up_piece, input_low, sums,
    column, turned_rows, pair_grad, pair_got, pair_send, pair_recv, small, running, box, sum_send, sum_recv, *scratch,
):
    place = Place(subs)
    step = pl.program_id(0)
    pairs = pl.num_programs(0) - 1
    rows = word.shape[0]
    movers = [Scatter(place, down_part, *scratch[:7]), Scatter(place, up_part, *scratch[7:])]
    small_sum = Sum(place, small, running, box, sum_send, sum_recv)
    own = pl.ds(pl.multiple_of(place.c * rows, LANES), rows)
    other = pl.ds(pl.multiple_of((1 - place.c) * rows, LANES), rows)

    @pl.when(step == 0)
    def _():
        entry_barrier(place)
        wide = small.shape[1]
        small[0:8] = sums_one[...]
        small[8:16] = sums_two[...]
        small[16:24] = jnp.zeros_like(small[16:24])
        for i in range(unit_sums.shape[1] // wide):
            small[16 + i : 17 + i] = unit_sums[:, i * wide : (i + 1) * wide]
        small_sum.hop(0)
        for mover in movers:
            mover.stage1()
        column[...] = facts[place.y].T
        turned_rows[...] = both[place.c].T
        input_grad[...] = d_one[...]

    @pl.when(step == 1)
    def _():
        small_sum.land(0)
        small_sum.hop(1)
        movers[0].stage2()

    @pl.when(step == 2)
    def _():
        small_sum.land(1)
        small_sum.hop(2)
        movers[1].stage2()

    @pl.when(step == 3)
    def _():
        small_sum.land(2)
        small_sum.hop(3)

    @pl.when(step == 4)
    def _():
        small_sum.land(3)
        small_sum.hop(4)

    @pl.when(step == 5)
    def _():
        small_sum.land(4)
        sums[...] = running[4]
        movers[0].stage3()

    @pl.when(step < pairs)
    def _():
        queries = jnp.concatenate([word[...], entity[...]], axis=1)
        value = values[...]
        turned = keys[...].T
        ent = column[:, 1:2] == 1
        ent_lane = facts[place.y, 1:2, :] == 1
        own_ent = facts[place.y, 1:2, own] == 1
        grad = dctx[...]
        zero = jnp.zeros_like(value)
        dk, dv, dw, de = [], [], [], []
        for half in range(2):
            lanes = head_lanes(half)
            here = slice(half * HEAD, (half + 1) * HEAD)
            prob = probs[half]
            delta = jnp.sum(
                ctx[here, :].astype(F32) * grad[here, :].astype(F32), axis=0, keepdims=True
            )
            dprob = dot_nn(jnp.where(lanes, value, zero), grad)
            dscore = (prob.astype(F32) * (dprob - delta)).astype(BF16)
            key_t = turned[here, :]
            none = jnp.zeros_like(key_t)
            tall = jnp.concatenate(
                [jnp.where(ent_lane, none, key_t), jnp.where(ent_lane, key_t, none)], axis=0
            )
            dq = dot_nn(tall, dscore) * (HEAD ** (-0.5))
            dw.append(dq[:HEAD])
            de.append(dq[HEAD:])
            pair = dot_nn(dscore, queries)
            dk.append(jnp.where(ent, pair[:, LANES:], pair[:, :LANES]))
            dv.append(dot_nt(prob, grad))
        first = head_lanes(0)
        pair_grad[step, :, :LANES] = jnp.where(first, dk[0], dk[1]).astype(BF16)
        pair_grad[step, :, LANES:] = jnp.where(first, dv[0], dv[1]).astype(BF16)
        remote(
            pair_grad.at[step, other], pair_got.at[step], pair_send.at[step], pair_recv.at[step], place.sibling()
        ).start()
        d_word, d_ent = jnp.concatenate(dw, axis=0), jnp.concatenate(de, axis=0)
        empty = jnp.zeros_like(d_word)
        turned_grad = jnp.concatenate(
            [
                jnp.where(own_ent, empty, d_word),
                jnp.where(own_ent, empty, d_ent),
                jnp.where(own_ent, d_word, empty),
                jnp.where(own_ent, d_ent, empty),
            ],
            axis=0,
        ).astype(BF16)
        query_grad = turned_grad.T
        weights = jnp.concatenate([wq[m] for m in range(4)], axis=1)
        input_grad[...] += dot_nt(query_grad, weights)
        part = dot_nn(turned_rows[...], query_grad).astype(BF16)
        sums = column_sum(query_grad.astype(F32))
        q_bias[...] = jnp.zeros_like(q_bias)
        for m in range(4):
            span = slice(m * LANES, (m + 1) * LANES)
            q_part[m] = part[:, span]
            q_bias[m : m + 1] = sums[:, span]

    @pl.when(step > 0)
    def _():
        before = step - 1
        remote(
            pair_got.at[before], pair_got.at[before], pair_send.at[before], pair_recv.at[before], place.sibling()
        ).wait()
        grad = (pair_grad[before, own].astype(F32) + pair_got[before].astype(F32)).astype(BF16)
        weights = jnp.concatenate([wkv[0], wkv[1]], axis=1)
        input_grad[...] += dot_nt(grad, weights)
        part = dot_nn(turned_rows[...], grad).astype(BF16)
        kv_part[0] = part[:, :LANES]
        kv_part[1] = part[:, LANES:]
        v_bias[...] = jnp.zeros_like(v_bias)
        v_bias[0:1] = column_sum(grad[:, LANES:].astype(F32))

    @pl.when(step == pairs)
    def _():
        movers[1].stage3()
        for mover in movers:
            mover.stage4()
            mover.drain()
        down_piece[...] = movers[0].mine[3]
        up_piece[...] = movers[1].mine[3]
        input_low[...] = input_grad[...].astype(BF16)


def attention_backward(
    subs, both, facts, probs, word, entity, keys, values, ctx, dctx, wq, wkv, d_one, smalls, down_part, up_part
):
    _, rows, width = both.shape
    length = 2 * rows
    pairs = width // LANES
    block = lambda n: pl.BlockSpec((n, LANES), lambda i: (0, jnp.minimum(i, pairs - 1)))
    behind = lambda n: pl.BlockSpec((n, LANES), lambda i: (0, jnp.maximum(i - 1, 0)))
    turned = pl.BlockSpec((LANES, rows), lambda i: (jnp.minimum(i, pairs - 1), 0))
    whole = lambda a: pl.BlockSpec(a.shape, lambda i: (0,) * a.ndim, pipeline_mode=pl.Buffered(1))
    q_cols = pl.BlockSpec((4, width, LANES), lambda i: (0, 0, jnp.minimum(i, pairs - 1)))
    kv_cols = pl.BlockSpec((2, width, LANES), lambda i: (0, 0, jnp.maximum(i - 1, 0)))
    anywhere = pl.BlockSpec(memory_space=pl.ANY)
    local = pl.BlockSpec(memory_space=pltpu.VMEM)
    shape = (1, down_part.shape[1] // GRID, down_part.shape[2] // 2)
    piece = jax.ShapeDtypeStruct((1, 4) + shape[1:], BF16)
    return pl.pallas_call(
        functools.partial(backward_kernel, subs),
        grid=(pairs + 1,),
        out_shape=[
            jax.ShapeDtypeStruct(wq.shape, BF16),
            jax.ShapeDtypeStruct(wkv.shape, BF16),
            jax.ShapeDtypeStruct((rows, width), F32),
            jax.ShapeDtypeStruct((8, width), F32),
            jax.ShapeDtypeStruct((8, width), F32),
            piece,
            piece,
            jax.ShapeDtypeStruct((rows, width), BF16),
            jax.ShapeDtypeStruct((24, width), F32),
        ],
        in_specs=[
            whole(both),
            whole(facts),
            pl.BlockSpec((2, length, rows), lambda i: (jnp.minimum(i, pairs - 1), 0, 0)),
            block(rows),
            block(rows),
            block(length),
            block(length),
            turned,
            turned,
            q_cols,
            kv_cols,
            whole(d_one),
        ]
        + [whole(a) for a in smalls]
        + [anywhere, anywhere],
        out_specs=[
            q_cols,
            kv_cols,
            pl.BlockSpec((rows, width), lambda i: (0, 0), pipeline_mode=pl.Buffered(1)),
            block(8),
            behind(8),
            local,
            local,
            local,
            local,
        ],
        scratch_shapes=[
            pltpu.VMEM((length, facts.shape[1]), jnp.int32),
            pltpu.VMEM((width, rows), BF16),
            pltpu.VMEM((pairs, length, 2 * LANES), BF16),
            pltpu.VMEM((pairs, rows, 2 * LANES), BF16),
            pltpu.SemaphoreType.DMA((pairs,)),
            pltpu.SemaphoreType.DMA((pairs,)),
            pltpu.VMEM((24, width), F32),
            pltpu.VMEM((5, 24, width), F32),
            pltpu.VMEM((5, 24, width), F32),
            pltpu.SemaphoreType.DMA((5,)),
            pltpu.SemaphoreType.DMA((5,)),
        ]
        + scatter_scratch(shape)
        + scatter_scratch(shape),
        compiler_params=pltpu.CompilerParams(
            collective_id=3, has_side_effects=True, vmem_limit_bytes=VMEM_LIMIT
        ),
        name="attention_backward",
    )(
        both, facts, probs, word, entity, keys, values, ctx, dctx, wq, wkv, d_one, *smalls,
        as_shards(down_part), as_shards(up_part),
    )


def ffn_forward_kernel(
    subs, both, facts, ctx, w_out, up, down, biases, out_bias, gain, shift, grad_out,
    active, slope, hidden_low, normal_one, inverse_one, output, d_two, sums, hidden, total, traded, valid, sems,
):
    step = pl.program_id(0)
    place = Place(subs)
    rows = both.shape[1]
    trade = Trade(place, grad_out, traded, sems)

    @pl.when(step == 0)
    def _():
        entry_barrier(place)
        trade.start()
        attn = dot_nt(ctx[...].T, w_out[...]) + out_bias[0:1].astype(F32)
        resid = both[place.c].astype(F32) + attn
        normal, inverse = normalize(resid)
        out = normal * gain[0:1].astype(F32) + shift[0:1].astype(F32)
        hidden[...] = out
        hidden_low[...] = out.astype(BF16)
        normal_one[...] = normal
        inverse_one[...] = inverse
        total[...] = jnp.zeros_like(total)
        own = pl.ds(pl.multiple_of(place.c * rows, LANES), rows)
        seen = facts[place.y, :, own].T[:, 2:3].astype(F32)
        valid[...] = seen
        sums[0:1] = column_sum(seen * resid * resid)
        sums[1:2] = column_sum(seen * attn * attn)

    span = biases.shape[2]
    across = pl.num_programs(0) // 2
    lines = BLOCK // span
    half = step // across
    line = 5 + lines * (step % across)
    bias = jnp.concatenate([biases[half, pl.ds(line + i, 1), :] for i in range(lines)], axis=1)
    act, rise = gelu_pair(dot_nn(hidden_low[...], up[...]) + bias)
    act = act.astype(BF16)
    active[...] = act
    slope[...] = rise.astype(BF16)
    total[...] += dot_nt(act, down[...])

    @pl.when(step == pl.num_programs(0) - 1)
    def _():
        ffn = total[...] + out_bias[1:2].astype(F32)
        resid = hidden[...] + ffn
        normal, inverse = normalize(resid)
        output[...] = (normal * gain[1:2].astype(F32) + shift[1:2].astype(F32)).astype(BF16)
        seen = valid[...]
        trade.finish()
        grad = traded[...].astype(F32)
        back = norm_backward(grad, normal, inverse, gain[1:2].astype(F32))
        d_two[...] = back
        sums[2:3] = column_sum(seen * ffn * ffn)
        sums[3:4] = column_sum(seen * resid * resid)
        sums[4:5] = column_sum(grad * normal)
        sums[5:6] = column_sum(grad)
        sums[6:7] = column_sum(back.astype(BF16).astype(F32))
        sums[7:8] = jnp.zeros_like(sums[7:8]) + jnp.sum(seen) * (1.0 / seen.shape[0])


def ffn_forward(subs, both, facts, ctx, w_out, up, down, biases, out_bias, gain, shift, grad_out):
    _, rows, width = both.shape
    units = up.shape[1]
    whole = lambda a: pl.BlockSpec(a.shape, lambda i: (0,) * a.ndim, pipeline_mode=pl.Buffered(1))
    fixed = lambda r, w: pl.BlockSpec((r, w), lambda i: (0, 0), pipeline_mode=pl.Buffered(1))
    wide = lambda r: pl.BlockSpec((r, BLOCK), lambda i: (0, i))
    return pl.pallas_call(
        functools.partial(ffn_forward_kernel, subs),
        grid=(units // BLOCK,),
        out_shape=[
            jax.ShapeDtypeStruct((rows, units), BF16),
            jax.ShapeDtypeStruct((rows, units), BF16),
            jax.ShapeDtypeStruct((rows, width), BF16),
            jax.ShapeDtypeStruct((rows, width), F32),
            jax.ShapeDtypeStruct((rows, 1), F32),
            jax.ShapeDtypeStruct((rows, width), BF16),
            jax.ShapeDtypeStruct((rows, width), F32),
            jax.ShapeDtypeStruct((8, width), F32),
        ],
        in_specs=[whole(both), whole(facts), whole(ctx), whole(w_out), wide(width), wide(width)]
        + [whole(a) for a in (biases, out_bias, gain, shift)]
        + [pl.BlockSpec(memory_space=pltpu.VMEM)],
        out_specs=[
            wide(rows),
            wide(rows),
            fixed(rows, width),
            fixed(rows, width),
            fixed(rows, 1),
            fixed(rows, width),
            fixed(rows, width),
            fixed(8, width),
        ],
        scratch_shapes=[
            pltpu.VMEM((rows, width), F32),
            pltpu.VMEM((rows, width), F32),
            pltpu.VMEM((rows, width), BF16),
            pltpu.VMEM((rows, 1), F32),
            pltpu.SemaphoreType.DMA((3,)),
        ],
        compiler_params=pltpu.CompilerParams(
            collective_id=4, has_side_effects=True, vmem_limit_bytes=VMEM_LIMIT
        ),
        cost_estimate=pl.CostEstimate(
            flops=2 * rows * width * (width + 2 * units),
            bytes_accessed=2 * width * (width + 2 * units) + 4 * rows * units,
            transcendentals=rows * units,
        ),
        name="ffn_forward",
    )(both, facts, ctx, w_out, up, down, biases, out_bias, gain, shift, grad_out)


def ffn_backward_kernel(
    subs, result, d_two, hidden_low, active, slope, up, down, ctx, w_out, gain, normal_one, inverse_one,
    up_part, down_part, bias_part, d_one, d_ctx, out_part, sums, output, d_low, d_turned, hidden_turned, total, sems,
):
    step = pl.program_id(0)
    place = Place(subs)
    trade = Trade(place, result, output, sems)

    @pl.when(step == 0)
    def _():
        entry_barrier(place)
        trade.start()
        low = d_two[...].astype(BF16)
        d_low[...] = low
        d_turned[...] = low.T
        hidden_turned[...] = hidden_low[...].T
        total[...] = d_two[...]

    d_pre = (dot_nn(d_low[...], down[...]) * slope[...].astype(F32)).astype(BF16)
    bias_part[...] = column_sum(d_pre.astype(F32))
    up_part[...] = dot_nn(hidden_turned[...], d_pre).astype(BF16)
    down_part[...] = dot_nn(d_turned[...], active[...]).astype(BF16)
    total[...] += dot_nt(d_pre, up[...])

    @pl.when(step == pl.num_programs(0) - 1)
    def _():
        grad = total[...]
        normal = normal_one[...]
        back = norm_backward(grad, normal, inverse_one[...], gain[0:1].astype(F32))
        d_one[...] = back
        low = back.astype(BF16)
        d_ctx[...] = dot_nt(w_out[...].T, low).astype(BF16)
        out_part[...] = dot_nt(low.T, ctx[...]).astype(BF16)
        sums[...] = jnp.zeros_like(sums)
        sums[0:1] = column_sum(grad * normal)
        sums[1:2] = column_sum(grad)
        sums[2:3] = column_sum(low.astype(F32))
        trade.finish()


def ffn_backward(subs, result, d_two, hidden_low, active, slope, up, down, ctx, w_out, gain, normal_one, inverse_one):
    rows, width = d_two.shape
    units = up.shape[1]
    whole = lambda a: pl.BlockSpec(a.shape, lambda i: (0,) * a.ndim, pipeline_mode=pl.Buffered(1))
    fixed = lambda r, w: pl.BlockSpec((r, w), lambda i: (0, 0), pipeline_mode=pl.Buffered(1))
    wide = lambda r: pl.BlockSpec((r, BLOCK), lambda i: (0, i))
    return pl.pallas_call(
        functools.partial(ffn_backward_kernel, subs),
        grid=(units // BLOCK,),
        out_shape=[
            jax.ShapeDtypeStruct((width, units), BF16),
            jax.ShapeDtypeStruct((width, units), BF16),
            jax.ShapeDtypeStruct((1, units), F32),
            jax.ShapeDtypeStruct((rows, width), F32),
            jax.ShapeDtypeStruct((width, rows), BF16),
            jax.ShapeDtypeStruct((width, width), BF16),
            jax.ShapeDtypeStruct((8, width), F32),
            jax.ShapeDtypeStruct((rows, width), BF16),
        ],
        in_specs=[pl.BlockSpec(memory_space=pltpu.VMEM), whole(d_two), whole(hidden_low), wide(rows), wide(rows), wide(width), wide(width)]
        + [whole(a) for a in (ctx, w_out, gain, normal_one, inverse_one)],
        out_specs=[
            wide(width),
            wide(width),
            wide(1),
            fixed(rows, width),
            fixed(width, rows),
            fixed(width, width),
            fixed(8, width),
            pl.BlockSpec(memory_space=pl.ANY),
        ],
        scratch_shapes=[
            pltpu.VMEM((rows, width), BF16),
            pltpu.VMEM((width, rows), BF16),
            pltpu.VMEM((width, rows), BF16),
            pltpu.VMEM((rows, width), F32),
            pltpu.SemaphoreType.DMA((3,)),
        ],
        compiler_params=pltpu.CompilerParams(
            collective_id=5, has_side_effects=True, vmem_limit_bytes=VMEM_LIMIT
        ),
        cost_estimate=pl.CostEstimate(
            flops=4 * rows * width * (width + 2 * units),
            bytes_accessed=2 * width * (3 * width + 4 * units) + 4 * rows * units,
            transcendentals=0,
        ),
        name="ffn_backward",
    )(result, d_two, hidden_low, active, slope, up, down, ctx, w_out, gain, normal_one, inverse_one)


def body(
    layer_input,
    grad_out,
    segment,
    entity,
    valid_mask,
    query_weight,
    key_value_weight,
    attn_bias,
    out_weight,
    out_bias,
    ln_gain,
    ln_bias,
    up_weight,
    ffn_bias,
    down_weight,
):
    rows, width = layer_input.shape
    length = segment.shape[0]
    rank = lax.axis_index("tensor")
    subs = lax.axis_size("dp") // GRID
    shards = [
        query_weight,
        key_value_weight,
        out_weight.T[None],
        up_weight[None],
        down_weight.T[None],
    ]
    groups = [[b * subs + s for s in range(subs)] for b in range(GRID)]
    if subs > 1:
        shards = [
            lax.all_gather(s, "dp", axis=1, tiled=True, axis_index_groups=groups) for s in shards
        ]
    shards = [shards[1], shards[0]] + shards[2:]
    cols = attn_bias.shape[1]
    (w_kv, w_q, w_out_t, w_up, w_down_t), (both, biases, pair_facts) = gather_weights(
        subs, shards, 3, layer_input, attn_bias, ffn_bias[None], [segment[None], entity[None], valid_mask[None]]
    )
    w_kv, w_q, w_out_t = as_matrix(w_kv), as_matrix(w_q), as_matrix(w_out_t)[0]
    context_t, probs, query_word, query_ent, keys, values, w_up, w_down_t = attention_forward(
        subs, both, w_q, w_kv, biases, pair_facts, w_up, w_down_t
    )
    w_up, w_down_t = as_matrix(w_up)[0], as_matrix(w_down_t)[0]
    active, slope, hidden_low, normal_one, inverse_one, result, d_two, sums_two = ffn_forward(
        subs, both, pair_facts, context_t, w_out_t, w_up, w_down_t, biases, out_bias, ln_gain, ln_bias, grad_out,
    )
    up_part, down_part, ffn_bias_part, d_one, d_context_t, out_part, sums_one, output = ffn_backward(
        subs, result, d_two, hidden_low, active, slope, w_up, w_down_t, context_t, w_out_t, ln_gain, normal_one, inverse_one
    )

    query_part, kv_part, input_grad, q_bias, v_bias, down_piece, up_piece, input_low, stack = attention_backward(
        subs, both, pair_facts, probs, query_word, query_ent, keys, values, context_t, d_context_t, w_q, w_kv, d_one,
        [sums_one, sums_two, ffn_bias_part], down_part[None], up_part[None],
    )
    sums, bias_sum, input_grad = scatter_gradients(
        subs,
        [down_piece, up_piece],
        [query_part, kv_part, out_part[None]],
        [q_bias, v_bias],
        input_grad,
        input_low,
    )
    if subs > 1:
        sums = [
            lax.psum_scatter(s, "dp", scatter_dimension=1, tiled=True, axis_index_groups=groups)
            for s in sums
        ]
        stack = lax.psum(stack, "dp", axis_index_groups=groups)
        bias_sum = lax.psum(bias_sum, "dp", axis_index_groups=groups)
    down_sum, up_sum, query_sum, kv_sum, out_sum = sums
    half = ffn_bias.shape[0]
    gains, shifts, out_biases, attn_biases, unit_biases, rms, query_sum, kv_sum, up_sum, input_grad, output = finish(
        subs, rows, stack, bias_sum, cols, half, [query_sum, kv_sum, up_sum, input_grad, output]
    )
    return (
        output,
        input_grad,
        rms[0],
        query_sum,
        kv_sum,
        attn_biases,
        out_sum[0].T,
        out_biases,
        gains,
        shifts,
        up_sum[0],
        unit_biases[0],
        down_sum[0].T,
    )


def solution(mesh):
    placed = (
        P(("dp", "tensor"), None),
        P(("dp", "tensor"), None),
        P("dp"),
        P("dp"),
        P("dp"),
        P(None, "dp", "tensor"),
        P(None, "dp", "tensor"),
        P(None, "tensor"),
        P("tensor", "dp"),
        P(),
        P(),
        P(),
        P("dp", "tensor"),
        P("tensor"),
        P("tensor", "dp"),
    )
    return jax.shard_map(
        body,
        mesh=mesh,
        in_specs=placed,
        out_specs=(
            P(("dp", "tensor"), None),
            P(("dp", "tensor"), None),
            P(),
            P(None, "dp", "tensor"),
            P(None, "dp", "tensor"),
            P(None, "tensor"),
            P("tensor", "dp"),
            P(),
            P(),
            P(),
            P("dp", "tensor"),
            P("tensor"),
            P("tensor", "dp"),
        ),
        check_vma=False,
    )
```

```python
import functools

import jax
import jax.numpy as jnp
from jax import lax
from jax.experimental import pallas as pl
from jax.experimental.pallas import tpu as pltpu
from jax.sharding import PartitionSpec as P

HEAD = 64
EPS = 1e-06
NEG = -1e30
GRID = 16
LANES = 128
MESH = pl.DeviceIdType.MESH
BF16 = jnp.bfloat16
F32 = jnp.float32
VMEM_LIMIT = 60 * 1024 * 1024


BLOCK = 768
TAIL = 0.34
TAIL_Q = (
    0.1918165616711201,
    0.1920366827922902,
    0.17827181747742213,
    0.1748548010854969,
    0.05944614604180367,
    0.27541659722682194,
    -0.27820700083503797,
    0.4016320911891782,
    -0.24597742961536673,
    0.050709736470982834,
)


def gelu_pair(v):
    size = jnp.abs(v)
    t = 1.0 / (1.0 + (TAIL * 0.5**0.5) * size)
    q = jnp.full_like(v, TAIL_Q[-1])
    for coefficient in TAIL_Q[-2::-1]:
        q = q * t + coefficient
    bell = jnp.exp(-0.5 * (v * v))
    tail = 0.5 * (bell * (t * q))
    cdf = jnp.where(v < 0, tail, 1.0 - tail)
    return v * cdf, cdf + v * (bell * 0.3989422804014327)


def normalize(resid):
    center = resid - jnp.mean(resid, -1, keepdims=True)
    inverse = lax.rsqrt(jnp.mean(center * center, -1, keepdims=True) + EPS)
    return center * inverse, inverse


def norm_backward(grad, normal, inverse, gain):
    scaled = grad * gain
    return inverse * (
        scaled
        - jnp.mean(scaled, -1, keepdims=True)
        - normal * jnp.mean(scaled * normal, -1, keepdims=True)
    )


def column_sum(a):
    return jnp.sum(a, 0, keepdims=True)


class Place:
    def __init__(self, subs):
        rank = lax.axis_index("dp")
        self.subs = subs
        self.sub = rank % subs
        block = rank // subs
        self.z = block // 4
        self.turns = [(self.z + step) % 4 for step in range(4)]
        self.x = (block // 2) % 2
        self.c = block % 2
        self.y = lax.axis_index("tensor")
        self.moved = self.y != self.c
        self.x1 = jnp.where(self.c == 0, 1 - self.x, self.x)
        self.y1 = jnp.where(self.c == 0, self.y, 1 - self.y)
        self.x2 = jnp.where(self.c == 0, self.x, 1 - self.x)
        self.y2 = jnp.where(self.c == 0, 1 - self.y, self.y)

    def device(self, z=None, x=None, c=None, y=None):
        z = self.z if z is None else z
        x = self.x if x is None else x
        c = self.c if c is None else c
        y = self.y if y is None else y
        return (((z * 2 + x) * 2 + c) * self.subs + self.sub, y)

    def z_peer(self, step):
        return self.device(z=(self.z + step) % 4)

    def first(self, flat=False):
        return self.across() if flat else self.device(x=self.x1, y=self.y1)

    def second(self, flat=False):
        return self.device(x=1 - self.x) if flat else self.device(x=self.x2, y=self.y2)

    def sibling(self):
        return self.device(c=1 - self.c)

    def plane(self):
        x, y, c = (self.x, 1 - self.x), (self.y, 1 - self.y), (self.c, 1 - self.c)
        return [self.device(x=x[k // 4], y=y[k // 2 % 2], c=c[k % 2]) for k in range(1, 8)]

    def across(self):
        return self.device(y=1 - self.y)

    def transposed(self):
        return self.device(c=1 - self.c, y=1 - self.y)

    def pieces(self, flat=False):
        if flat:
            return ((self.x, self.y), (self.x, 1 - self.y), (1 - self.x, self.y), (1 - self.x, 1 - self.y))
        return (
            (self.x, self.y),
            (self.x1, self.y1),
            (self.x2, self.y2),
            (1 - self.x, 1 - self.y),
        )


def entry_barrier(place):
    barrier = pltpu.get_barrier_semaphore()
    peers = [place.z_peer(step) for step in (1, 2, 3)]
    peers += place.plane()
    for peer in peers:
        pl.semaphore_signal(barrier, inc=1, device_id=peer, device_id_type=MESH)
    pl.semaphore_wait(barrier, len(peers))


def remote(src, dst, send, recv, peer):
    return pltpu.make_async_remote_copy(
        src_ref=src, dst_ref=dst, send_sem=send, recv_sem=recv, device_id=peer, device_id_type=MESH
    )


class Trade:
    def __init__(self, place, own, got, sems):
        self.moved = place.moved
        self.kept = pltpu.make_async_copy(own, got, sems.at[2])
        self.swap = remote(own, got, sems.at[0], sems.at[1], place.transposed())

    def start(self):
        @pl.when(self.moved)
        def _():
            self.swap.start()

        @pl.when(jnp.logical_not(self.moved))
        def _():
            self.kept.start()

    def finish(self):
        @pl.when(self.moved)
        def _():
            self.swap.wait()

        @pl.when(jnp.logical_not(self.moved))
        def _():
            self.kept.wait()


class Gather:
    def __init__(self, place, shard, full, send, recv, local=None, whole=True, flat=False):
        self.flat = flat
        self.place, self.shard, self.full, self.whole = place, shard, full, whole
        self.send, self.recv, self.local = send, recv, local
        self.w = full.shape[-1] // 2

    def cols(self, y):
        return pl.ds(pl.multiple_of(y * self.w, LANES), self.w)

    def piece(self, spot, c):
        x, y = spot
        return self.full.at[:, :, x, c, :, self.cols(y)]

    def copy(self, index, src, dst, peer):
        remote(src, dst, self.send.at[index], self.recv.at[index], peer).start()

    def arrive(self, index, ref):
        remote(ref, ref, self.send.at[index], self.recv.at[index], self.place.sibling()).wait_recv()

    def gone(self, index, ref):
        remote(ref, ref, self.send.at[index], self.recv.at[index], self.place.sibling()).wait_send()

    def own(self, z):
        p = self.place
        return self.full.at[:, z, p.x, p.c, :, self.cols(p.y)]

    def stage1(self):
        p = self.place
        self.kept = pltpu.make_async_copy(self.shard, self.own(p.z), self.local)
        self.kept.start()
        for step in (1, 2, 3):
            self.copy(step - 1, self.shard, self.own(p.z), p.z_peer(step))

    def land(self):
        p = self.place
        self.kept.wait()
        for step in (1, 2, 3):
            self.arrive(step - 1, self.own((p.z + 4 - step) % 4))

    def settle(self):
        self.land()
        for index in range(3):
            self.gone(index, self.shard)

    def spread(self):
        p = self.place
        mine = self.piece(p.pieces(self.flat)[0], p.c)
        self.copy(3, mine, mine, p.first(self.flat))
        self.copy(4, mine, mine, p.second(self.flat))
        self.copy(6, mine, mine, p.sibling())

    def stage2(self):
        self.land()
        self.spread()

    def stage3(self):
        p = self.place
        got = self.piece(p.pieces(self.flat)[1], p.c)
        self.arrive(3, got)
        self.copy(5, got, got, p.second(self.flat))
        self.copy(7, got, got, p.sibling())

    def stage4(self):
        p = self.place
        for index, spot in ((4, 2), (5, 3)):
            got = self.piece(p.pieces(self.flat)[spot], p.c)
            self.arrive(index, got)
            self.copy(index + 4, got, got, p.sibling())

    def stage5(self):
        p = self.place
        spots = p.pieces(self.flat)
        for index, spot in ((6, 0), (7, 1 if self.flat else 2), (8, 2 if self.flat else 1), (9, 3)):
            self.arrive(index, self.piece(spots[spot], 1 - p.c))
        for index in range(3, 10):
            self.gone(index, self.piece(spots[0], p.c))

    def last(self):
        self.stage5()
        for index in range(3):
            self.gone(index, self.shard)

    def stages(self):
        if not self.whole:
            return [self.stage1, self.settle]
        return [self.stage1, self.stage2, self.stage3, self.stage4, self.last]


def wavefront(movers):
    lists = [mover.stages() for mover in movers]
    depth = max(len(stages) for stages in lists)
    order = []
    for time in range(len(lists) + depth - 1):
        for index in range(len(lists)):
            stage = time - index
            if 0 <= stage < len(lists[index]):
                order.append(lists[index][stage])
    return order


def cuts(counts):
    return [(i, a, min(2, m)) for i, m in enumerate(counts) for a in range(0, m, 2)]


class Share:
    def __init__(self, source, pair, index, peer, sems):
        self.kept = pltpu.make_async_copy(source, pair.at[index], sems.at[2])
        self.sent = remote(source, pair.at[index], sems.at[0], sems.at[1], peer)

    def start(self):
        self.kept.start()
        self.sent.start()

    def finish(self):
        self.kept.wait()
        self.sent.wait()


class Rows:
    def __init__(self, place, rows, both, sems):
        p = place
        half = both.at[p.c]
        self.moved = p.moved
        self.kept = pltpu.make_async_copy(rows, half, sems.at[4])
        self.swap = remote(rows, both.at[p.y], sems.at[0], sems.at[1], p.transposed())
        self.swapped = remote(half, half, sems.at[0], sems.at[1], p.transposed())
        self.share = remote(rows, half, sems.at[2], sems.at[3], p.sibling())
        self.relay = remote(half, half, sems.at[2], sems.at[3], p.sibling())
        other = both.at[1 - p.c]
        self.other = remote(other, other, sems.at[2], sems.at[3], p.sibling())

    def start(self):
        @pl.when(self.moved)
        def _():
            self.swap.start()

        @pl.when(jnp.logical_not(self.moved))
        def _():
            self.kept.start()
            self.share.start()

    def forward(self):
        @pl.when(self.moved)
        def _():
            self.swapped.wait_recv()
            self.relay.start()

    def finish(self):
        @pl.when(self.moved)
        def _():
            self.swap.wait_send()
            self.relay.wait_send()

        @pl.when(jnp.logical_not(self.moved))
        def _():
            self.kept.wait()
            self.share.wait_send()

        self.other.wait_recv()


def gather_kernel(subs, count, wholes, *refs):
    shards, (rows, bias_rows, unit_bias), columns = refs[:count], refs[count : count + 3], refs[count + 3 : count + 6]
    fulls, (both, biases, pair_facts) = refs[count + 6 : 2 * count + 6], refs[2 * count + 6 : 2 * count + 9]
    send, recv, local, row_sems, share_sems, bias, facts = refs[2 * count + 9 :]
    place = Place(subs)
    entry_barrier(place)
    tokens = Rows(place, rows, both, row_sems)
    bias[...] = jnp.zeros_like(bias)
    many, span = bias_rows.shape
    bias[0:many] = bias_rows[...].astype(F32)
    for i in range(unit_bias.shape[1] // span):
        bias[many + i : many + i + 1] = unit_bias[:, i * span : (i + 1) * span].astype(F32)
    facts[...] = jnp.zeros_like(facts)
    for i in range(3):
        facts[i : i + 1] = columns[i][...]
    shares = [
        Share(facts, pair_facts, place.c, place.sibling(), share_sems.at[0]),
        Share(bias, biases, place.y, place.across(), share_sems.at[1]),
    ]
    tokens.start()
    for share in shares:
        share.start()
    movers = [
        Gather(
            place, shards[i].at[pl.ds(a, m)], fulls[i].at[pl.ds(a, m)], send.at[n], recv.at[n], local.at[n], i < wholes
        )
        for n, (i, a, m) in enumerate(cuts([shard.shape[0] for shard in shards]))
    ]
    for mover in movers[:2]:
        mover.stage1()
    steps = [s for s in wavefront(movers) if s.__func__ is not Gather.stage1]
    late = [s for s in steps if s.__func__ is Gather.settle]
    landed = 0
    for index, step in enumerate([s for s in steps if s not in late] + late):
        step()
        if index == 1:
            tokens.forward()
        if step.__func__ in (Gather.stage2, Gather.settle):
            landed += 1
            if landed + 1 < len(movers):
                movers[landed + 1].stage1()
    tokens.finish()
    for share in shares:
        share.finish()


def gather_weights(subs, shards, wholes, rows, bias_rows, unit_bias, columns):
    count = len(shards)
    outs = [
        jax.ShapeDtypeStruct((s.shape[0], 4, 2, 2, s.shape[1], 2 * s.shape[2]), BF16) for s in shards
    ]
    movers = len(cuts([s.shape[0] for s in shards]))
    bias, facts = (16, bias_rows.shape[1]), (8, columns[0].shape[1])
    outs += [
        jax.ShapeDtypeStruct((2,) + rows.shape, rows.dtype),
        jax.ShapeDtypeStruct((2,) + bias, F32),
        jax.ShapeDtypeStruct((2,) + facts, jnp.int32),
    ]
    results = pl.pallas_call(
        functools.partial(gather_kernel, subs, count, wholes),
        out_shape=outs,
        in_specs=[pl.BlockSpec(memory_space=pltpu.VMEM)] * (count + 6),
        out_specs=[pl.BlockSpec(memory_space=pl.ANY)] * (count + 3),
        scratch_shapes=[
            pltpu.SemaphoreType.DMA((movers, 10)),
            pltpu.SemaphoreType.DMA((movers, 10)),
            pltpu.SemaphoreType.DMA((movers,)),
            pltpu.SemaphoreType.DMA((5,)),
            pltpu.SemaphoreType.DMA((2, 3)),
            pltpu.VMEM(bias, F32),
            pltpu.VMEM(facts, jnp.int32),
        ],
        compiler_params=pltpu.CompilerParams(
            collective_id=0, has_side_effects=True, vmem_limit_bytes=VMEM_LIMIT
        ),
        name="gather_weights",
    )(*shards, rows, bias_rows, unit_bias, *columns)
    return results[:count], results[count:]


def as_matrix(full):
    return full.reshape(full.shape[0], GRID * full.shape[4], full.shape[5])


class Last:
    def __init__(self, place, piece, total, from_z, send, recv):
        self.place, self.piece, self.total, self.from_z = place, piece, total, from_z
        self.send, self.recv = send, recv

    def start(self):
        p = self.place
        for step in (1, 2, 3):
            remote(
                self.piece.at[:, p.turns[step]],
                self.from_z.at[step - 1],
                self.send.at[step - 1],
                self.recv.at[step - 1],
                p.z_peer(step),
            ).start()

    def finish(self):
        p = self.place
        for step in (0, 1, 2):
            slot = self.from_z.at[step]
            remote(slot, slot, self.send.at[step], self.recv.at[step], p.sibling()).wait()

        def step(i, carry):
            total = self.piece[i, p.z].astype(F32)
            for s in range(3):
                total = total + self.from_z[s, i].astype(F32)
            self.total[i] = total
            return carry

        lax.fori_loop(0, self.total.shape[0], step, 0)


class Scatter:
    def __init__(self, place, part, mine, from_core, from_second, from_first, send, recv, local):
        self.place, self.part = place, part
        self.mine, self.from_core = mine, from_core
        self.from_second, self.from_first = from_second, from_first
        self.send, self.recv, self.local = send, recv, local
        self.m, _, self.rows, self.w = from_first.shape

    def cols(self, y):
        return pl.ds(pl.multiple_of(y * self.w, LANES), self.w)

    def copy(self, index, src, dst, peer):
        remote(src, dst, self.send.at[index], self.recv.at[index], peer).start()

    def arrive(self, index, ref):
        remote(ref, ref, self.send.at[index], self.recv.at[index], self.place.sibling()).wait_recv()

    def drain(self):
        for index in range(7):
            remote(
                self.from_first, self.from_first, self.send.at[index], self.recv.at[index], self.place.sibling()
            ).wait_send()

    def add(self, target, source):
        m = self.m

        def step(index, carry):
            i, z = index // 4, index % 4
            target[i, z] = (target[i, z].astype(F32) + source[i, z].astype(F32)).astype(BF16)
            return carry

        lax.fori_loop(0, m * 4, step, 0)

    def keep(self, slot, spot):
        x, y = self.place.pieces()[spot]
        source = self.part.at[:, :, x, self.place.c, :, self.cols(y)]
        return pltpu.make_async_copy(source, self.mine.at[slot], self.local.at[slot])

    def stage1(self):
        p = self.place
        spots = p.pieces()
        for slot, (here, there) in enumerate(((3, 3), (2, 1), (1, 2), (0, 0))):
            self.keep(slot, here).start()
            x, y = spots[there]
            self.copy(
                slot,
                self.part.at[:, :, x, 1 - p.c, :, self.cols(y)],
                self.from_core.at[slot],
                p.sibling(),
            )

    def joined(self, slot):
        self.keep(slot, 3 - slot).wait()
        self.arrive(slot, self.from_core.at[slot])
        self.add(self.mine.at[slot], self.from_core.at[slot])

    def stage2(self):
        p = self.place
        for slot in (0, 1):
            self.joined(slot)
            self.copy(4 + slot, self.mine.at[slot], self.from_second.at[slot], p.second())
        for slot in (2, 3):
            self.joined(slot)

    def stage3(self):
        p = self.place
        self.arrive(4, self.from_second.at[0])
        self.add(self.mine.at[2], self.from_second.at[0])
        self.copy(6, self.mine.at[2], self.from_first, p.first())
        self.arrive(5, self.from_second.at[1])
        self.add(self.mine.at[3], self.from_second.at[1])

    def stage4(self):
        self.arrive(6, self.from_first)
        self.add(self.mine.at[3], self.from_first)


class Sum:
    def __init__(self, place, source, total, box, send, recv):
        self.place, self.source, self.total = place, source, total
        self.box, self.send, self.recv = box, send, recv
        p = place
        flip = p.z + 1 - 2 * (p.z % 2)
        self.peers = (p.device(x=1 - p.x), p.across(), p.device(z=flip), p.device(z=p.turns[2]), p.sibling())

    def term(self, index):
        return self.source if index == 0 else self.total.at[index - 1]

    def exchange(self, index):
        return remote(
            self.term(index), self.box.at[index], self.send.at[index], self.recv.at[index], self.peers[index]
        )

    def hop(self, index):
        self.exchange(index).start()

    def land(self, index):
        self.exchange(index).wait()
        self.total[index] = self.term(index)[...] + self.box[index]


class PlaneSum:
    def __init__(self, place, source, middle, plane, line, send, recv):
        self.place, self.source, self.middle = place, source, middle
        self.plane, self.line, self.send, self.recv = plane, line, send, recv
        p = place
        spot = (p.x * 2 + p.y) * 2 + p.c
        self.first = [
            remote(source, plane.at[spot], send.at[k], recv.at[k], peer) for k, peer in enumerate(p.plane())
        ]
        self.second = [
            remote(middle, line.at[p.z], send.at[6 + k], recv.at[6 + k], p.z_peer(k)) for k in (1, 2, 3)
        ]
        self.spot = spot

    def start(self):
        for step in self.first:
            step.start()
        self.plane[self.spot] = self.source[...]

    def turn(self):
        for step in self.first:
            step.wait()
        total = self.plane[0]
        for k in range(1, 8):
            total = total + self.plane[k]
        self.middle[...] = total
        for step in self.second:
            step.start()
        self.line[self.place.z] = total

    def finish(self):
        for step in self.second:
            step.wait()
        total = self.line[0]
        for k in range(1, 4):
            total = total + self.line[k]
        return total


def scatter_scratch(shape):
    m, rows, w = shape
    return [
        pltpu.VMEM((4, m, 4, rows, w), BF16),
        pltpu.VMEM((4, m, 4, rows, w), BF16),
        pltpu.VMEM((2, m, 4, rows, w), BF16),
        pltpu.VMEM((m, 4, rows, w), BF16),
        pltpu.SemaphoreType.DMA((7,)),
        pltpu.SemaphoreType.DMA((7,)),
        pltpu.SemaphoreType.DMA((4,)),
    ]


def last_scratch(shape):
    return [
        pltpu.VMEM((3,) + shape, BF16),
        pltpu.SemaphoreType.DMA((3,)),
        pltpu.SemaphoreType.DMA((3,)),
    ]


def as_shards(part):
    m, rows, w = part.shape
    return part.reshape(m, 4, 2, 2, rows // GRID, w)


def scatter_kernel(subs, early, count, *refs):
    pieces, parts, smalls = refs[:early], refs[early : early + count], refs[early + count :][:2]
    input_grad, input_low = refs[early + count + 2 :][:2]
    refs = refs[early + count + 4 :]
    totals, (small_total, result, traded, trade_sems) = refs[: early + count], refs[early + count :][:4]
    refs = refs[early + count + 4 :]
    lasts, refs = refs[: 3 * (early + count)], refs[3 * (early + count) :]
    place = Place(subs)
    entry_barrier(place)
    movers = [Scatter(place, parts[i], *refs[7 * i : 7 * i + 7]) for i in range(count)]
    sources = list(pieces) + [mover.mine.at[3] for mover in movers]
    ends = [Last(place, sources[i], totals[i], *lasts[3 * i : 3 * i + 3]) for i in range(early + count)]
    small, *boxes = refs[7 * count :]
    small[...] = smalls[0][...]
    small[4:5] = smalls[1][0:1]
    small_sum = PlaneSum(place, small, *boxes)
    trade = Trade(place, input_low, traded, trade_sems)
    small_sum.start()
    for mover in movers:
        mover.stage1()
    small_sum.turn()
    for end in ends[:early]:
        end.start()
    for time in range(count + 2):
        for index in range(count):
            stage = time - index
            if 0 <= stage < 3:
                mover = movers[index]
                (mover.stage2, mover.stage3, mover.stage4)[stage]()
                if stage == 1 and index == count - 1:
                    trade.start()
                if stage == 2:
                    ends[early + index].start()
    small_total[...] = small_sum.finish()
    for end in ends[early:]:
        end.finish()
    for end in ends[:early]:
        end.finish()
    for mover in movers:
        mover.drain()
    trade.finish()
    result[...] = jnp.where(place.moved, traded[...].astype(F32), input_grad[...])


def scatter_gradients(subs, pieces, parts, smalls, input_grad, input_low):
    early, count = len(pieces), len(parts)
    shaped = [as_shards(p) for p in parts]
    shapes = [(p.shape[0],) + p.shape[2:] for p in pieces]
    whole = [(p.shape[0], p.shape[4], p.shape[5] // 2) for p in shaped]
    outs = [jax.ShapeDtypeStruct(s, F32) for s in shapes + whole]
    stack = smalls[0].shape
    outs += [jax.ShapeDtypeStruct(stack, F32), jax.ShapeDtypeStruct(input_grad.shape, F32)]
    scratch = [pltpu.VMEM(input_low.shape, BF16), pltpu.SemaphoreType.DMA((3,))]
    for s in shapes + whole:
        scratch += last_scratch(s)
    for s in whole:
        scratch += scatter_scratch(s)
    scratch += [
        pltpu.VMEM(stack, F32),
        pltpu.VMEM(stack, F32),
        pltpu.VMEM((8,) + stack, F32),
        pltpu.VMEM((4,) + stack, F32),
        pltpu.SemaphoreType.DMA((10,)),
        pltpu.SemaphoreType.DMA((10,)),
    ]
    local = pl.BlockSpec(memory_space=pltpu.VMEM)
    results = pl.pallas_call(
        functools.partial(scatter_kernel, subs, early, count),
        out_shape=outs,
        in_specs=[local] * early + [pl.BlockSpec(memory_space=pl.ANY)] * count + [local] * 4,
        out_specs=[local] * (early + count + 2),
        scratch_shapes=scratch,
        compiler_params=pltpu.CompilerParams(
            collective_id=1, has_side_effects=True, vmem_limit_bytes=VMEM_LIMIT
        ),
        name="scatter_gradients",
    )(*pieces, *shaped, *smalls, input_grad, input_low)
    return results[:-2], results[-2], results[-1]


def finish_kernel(place_of, rows, stack, biases, query, kv, up, grad, out, gains, shifts, out_bias, attn_bias, unit_bias, rms, *results):
    place = place_of()
    width = stack.shape[1]
    lines = unit_bias.shape[1] // width
    for i in range(lines):
        unit_bias[:, i * width : (i + 1) * width] = stack[pl.ds(16 + place.y * lines + i, 1), :]
    real = jnp.mean(stack[15:16], 1, keepdims=True) * (rows * width)
    lane = lax.broadcasted_iota(jnp.int32, (1, 4), 1)
    squares = jnp.zeros((1, 4), F32)
    for i in range(4):
        squares = jnp.where(lane == i, jnp.sum(stack[8 + i : 9 + i], 1, keepdims=True), squares)
    rms[...] = jnp.sqrt(squares / real)
    for i, ref in enumerate((gains, shifts, out_bias)):
        ref[0:1] = stack[i : i + 1]
        ref[1:2] = stack[12 + i : 13 + i]
    cols = attn_bias.shape[1]
    mine = pl.ds(pl.multiple_of(place.y * cols, LANES), cols)
    attn_bias[...] = biases[0:5, mine]
    for source, target in zip((query, kv, up, grad, out), results):
        target[...] = source[...]


def finish(subs, rows, stack, biases, cols, units, arrays):
    width = stack.shape[1]
    shapes = [(2, width)] * 3 + [(5, cols), (1, units), (1, 4)]
    outs = [jax.ShapeDtypeStruct(s, F32) for s in shapes] + [jax.ShapeDtypeStruct(a.shape, a.dtype) for a in arrays]
    return pl.pallas_call(
        functools.partial(finish_kernel, functools.partial(Place, subs), rows),
        out_shape=outs,
        compiler_params=pltpu.CompilerParams(vmem_limit_bytes=VMEM_LIMIT),
        name="finish",
    )(stack, biases, *arrays)


def head_lanes(half):
    lane = lax.broadcasted_iota(jnp.int32, (1, LANES), 1)
    return (lane // HEAD) == half


def dot_nt(a, b):
    return lax.dot_general(a, b, (((1,), (1,)), ((), ())), preferred_element_type=F32)


def dot_nn(a, b):
    return lax.dot_general(a, b, (((1,), (0,)), ((), ())), preferred_element_type=F32)


def forward_kernel(
    subs, both, wq, wkv, biases, facts, up_in, down_in,
    ctx, probs, word, entity, keys, values, up, down, mask, column, send, recv,
):
    place = Place(subs)
    step = pl.program_id(0)
    length, rows = mask.shape
    movers = [Gather(place, None, full, send.at[i], recv.at[i]) for i, full in enumerate((up, down))]
    own = pl.ds(pl.multiple_of(place.c * rows, LANES), rows)

    @pl.when(step == 0)
    def _():
        entry_barrier(place)
        for mover in movers:
            mover.spread()
        column[...] = facts[place.y].T
        spot = lax.broadcasted_iota(jnp.int32, (length, rows), 0)
        here = lax.broadcasted_iota(jnp.int32, (length, rows), 1) + place.c * rows
        same = column[:, 0:1] == facts[place.y, 0:1, own]
        seen = (column[:, 2:3] == 1) | (spot == here)
        mask[...] = jnp.where(same & seen, 0.0, NEG)

    @pl.when(step == 3)
    def _():
        movers[0].stage3()

    @pl.when(step == 5)
    def _():
        movers[1].stage3()
        movers[0].stage4()

    tokens = both[...].reshape(length, both.shape[2])
    mine = both[place.c]
    bias = biases[0]
    row_ent = column[own, 1:2] == 1
    to_word = dot_nn(mine, jnp.concatenate([wq[0], wq[2]], axis=1))
    to_ent = dot_nn(mine, jnp.concatenate([wq[1], wq[3]], axis=1))
    scale = HEAD ** (-0.5)
    query_word = jnp.where(row_ent, to_word[:, LANES:] + bias[2:3], to_word[:, :LANES] + bias[0:1])
    query_ent = jnp.where(row_ent, to_ent[:, LANES:] + bias[3:4], to_ent[:, :LANES] + bias[1:2])
    word[...] = query_word.astype(BF16) * BF16(scale)
    entity[...] = query_ent.astype(BF16) * BF16(scale)
    pair = dot_nn(tokens, jnp.concatenate([wkv[0], wkv[1]], axis=1))
    key = pair[:, :LANES].astype(BF16)
    value = (pair[:, LANES:] + bias[4:5]).astype(BF16)
    keys[...] = key
    values[...] = value

    queries = jnp.concatenate([word[...], entity[...]], axis=1)
    ent = column[:, 1:2] == 1
    zero = jnp.zeros_like(key)
    turned = value.T
    for half in range(2):
        lanes = head_lanes(half)
        wide = jnp.concatenate(
            [jnp.where(lanes & ~ent, key, zero), jnp.where(lanes & ent, key, zero)], axis=1
        )
        scores = dot_nt(wide, queries) + mask[...]
        top = jnp.max(scores, axis=0, keepdims=True)
        expo = jnp.exp(scores - top)
        total = jnp.sum(expo, axis=0, keepdims=True)
        prob = (expo * (1.0 / total)).astype(BF16)
        probs[half] = prob
        ctx[half * HEAD : (half + 1) * HEAD, :] = dot_nn(
            turned[half * HEAD : (half + 1) * HEAD, :], prob
        ).astype(BF16)

    @pl.when(step == pl.num_programs(0) - 1)
    def _():
        movers[1].stage4()
        for mover in movers:
            mover.stage5()


def attention_forward(subs, both, wq, wkv, biases, facts, up, down):
    _, rows, width = both.shape
    length = 2 * rows
    pairs = width // LANES
    span = biases.shape[2] // LANES
    block = lambda n: pl.BlockSpec((n, LANES), lambda i: (0, i))
    whole = lambda a: pl.BlockSpec(a.shape, lambda i: (0,) * a.ndim, pipeline_mode=pl.Buffered(1))
    cols = lambda a: pl.BlockSpec(a.shape[:2] + (LANES,), lambda i: (0, 0, i))
    anywhere = pl.BlockSpec(memory_space=pl.ANY)
    return pl.pallas_call(
        functools.partial(forward_kernel, subs),
        grid=(pairs,),
        out_shape=[
            jax.ShapeDtypeStruct((width, rows), BF16),
            jax.ShapeDtypeStruct((2 * pairs, length, rows), BF16),
            jax.ShapeDtypeStruct((rows, width), BF16),
            jax.ShapeDtypeStruct((rows, width), BF16),
            jax.ShapeDtypeStruct((length, width), BF16),
            jax.ShapeDtypeStruct((length, width), BF16),
            jax.ShapeDtypeStruct(up.shape, BF16),
            jax.ShapeDtypeStruct(down.shape, BF16),
        ],
        in_specs=[
            whole(both),
            cols(wq),
            cols(wkv),
            pl.BlockSpec((1, biases.shape[1], LANES), lambda i: (i // span, 0, i % span)),
            whole(facts),
            anywhere,
            anywhere,
        ],
        out_specs=[
            pl.BlockSpec((LANES, rows), lambda i: (i, 0)),
            pl.BlockSpec((2, length, rows), lambda i: (i, 0, 0)),
            block(rows),
            block(rows),
            block(length),
            block(length),
            anywhere,
            anywhere,
        ],
        scratch_shapes=[
            pltpu.VMEM((length, rows), F32),
            pltpu.VMEM((length, facts.shape[1]), jnp.int32),
            pltpu.SemaphoreType.DMA((2, 10)),
            pltpu.SemaphoreType.DMA((2, 10)),
        ],
        input_output_aliases={5: 6, 6: 7},
        compiler_params=pltpu.CompilerParams(
            collective_id=2, has_side_effects=True, vmem_limit_bytes=VMEM_LIMIT
        ),
        name="attention_forward",
    )(both, wq, wkv, biases, facts, up, down)


def backward_kernel(
    subs, both, facts, probs, word, entity, keys, values, ctx, dctx, wq, wkv, d_one, sums_one, sums_two, unit_sums,
    down_part, up_part, q_part, kv_part, input_grad, q_bias, v_bias, down_piece, up_piece, input_low, sums,
    column, turned_rows, pair_grad, pair_got, pair_send, pair_recv, small, running, box, sum_send, sum_recv, *scratch,
):
    place = Place(subs)
    step = pl.program_id(0)
    pairs = pl.num_programs(0) - 1
    rows = word.shape[0]
    movers = [Scatter(place, down_part, *scratch[:7]), Scatter(place, up_part, *scratch[7:])]
    small_sum = Sum(place, small, running, box, sum_send, sum_recv)
    own = pl.ds(pl.multiple_of(place.c * rows, LANES), rows)
    other = pl.ds(pl.multiple_of((1 - place.c) * rows, LANES), rows)

    @pl.when(step == 0)
    def _():
        entry_barrier(place)
        wide = small.shape[1]
        small[0:8] = sums_one[...]
        small[8:16] = sums_two[...]
        small[16:24] = jnp.zeros_like(small[16:24])
        for i in range(unit_sums.shape[1] // wide):
            small[16 + i : 17 + i] = unit_sums[:, i * wide : (i + 1) * wide]
        small_sum.hop(0)
        for mover in movers:
            mover.stage1()
        column[...] = facts[place.y].T
        turned_rows[...] = both[place.c].T
        input_grad[...] = d_one[...]

    @pl.when(step == 1)
    def _():
        small_sum.land(0)
        small_sum.hop(1)
        movers[0].stage2()

    @pl.when(step == 2)
    def _():
        small_sum.land(1)
        small_sum.hop(2)
        movers[1].stage2()

    @pl.when(step == 3)
    def _():
        small_sum.land(2)
        small_sum.hop(3)

    @pl.when(step == 4)
    def _():
        small_sum.land(3)
        small_sum.hop(4)
        movers[0].stage3()

    @pl.when(step == 5)
    def _():
        small_sum.land(4)
        sums[...] = running[4]

    @pl.when(step < pairs)
    def _():
        queries = jnp.concatenate([word[...], entity[...]], axis=1)
        value = values[...]
        turned = keys[...].T
        ent = column[:, 1:2] == 1
        ent_lane = facts[place.y, 1:2, :] == 1
        own_ent = facts[place.y, 1:2, own] == 1
        grad = dctx[...]
        zero = jnp.zeros_like(value)
        dk, dv, dw, de = [], [], [], []
        for half in range(2):
            lanes = head_lanes(half)
            here = slice(half * HEAD, (half + 1) * HEAD)
            prob = probs[half]
            delta = jnp.sum(
                ctx[here, :].astype(F32) * grad[here, :].astype(F32), axis=0, keepdims=True
            )
            dprob = dot_nn(jnp.where(lanes, value, zero), grad)
            dscore = (prob.astype(F32) * (dprob - delta)).astype(BF16)
            key_t = turned[here, :]
            none = jnp.zeros_like(key_t)
            tall = jnp.concatenate(
                [jnp.where(ent_lane, none, key_t), jnp.where(ent_lane, key_t, none)], axis=0
            )
            dq = dot_nn(tall, dscore) * (HEAD ** (-0.5))
            dw.append(dq[:HEAD])
            de.append(dq[HEAD:])
            pair = dot_nn(dscore, queries)
            dk.append(jnp.where(ent, pair[:, LANES:], pair[:, :LANES]))
            dv.append(dot_nt(prob, grad))
        first = head_lanes(0)
        pair_grad[step, :, :LANES] = jnp.where(first, dk[0], dk[1]).astype(BF16)
        pair_grad[step, :, LANES:] = jnp.where(first, dv[0], dv[1]).astype(BF16)
        remote(
            pair_grad.at[step, other], pair_got.at[step], pair_send.at[step], pair_recv.at[step], place.sibling()
        ).start()
        d_word, d_ent = jnp.concatenate(dw, axis=0), jnp.concatenate(de, axis=0)
        empty = jnp.zeros_like(d_word)
        turned_grad = jnp.concatenate(
            [
                jnp.where(own_ent, empty, d_word),
                jnp.where(own_ent, empty, d_ent),
                jnp.where(own_ent, d_word, empty),
                jnp.where(own_ent, d_ent, empty),
            ],
            axis=0,
        ).astype(BF16)
        query_grad = turned_grad.T
        weights = jnp.concatenate([wq[m] for m in range(4)], axis=1)
        input_grad[...] += dot_nt(query_grad, weights)
        part = dot_nn(turned_rows[...], query_grad).astype(BF16)
        sums = column_sum(query_grad.astype(F32))
        q_bias[...] = jnp.zeros_like(q_bias)
        for m in range(4):
            span = slice(m * LANES, (m + 1) * LANES)
            q_part[m] = part[:, span]
            q_bias[m : m + 1] = sums[:, span]

    @pl.when(step > 0)
    def _():
        before = step - 1
        remote(
            pair_got.at[before], pair_got.at[before], pair_send.at[before], pair_recv.at[before], place.sibling()
        ).wait()
        grad = (pair_grad[before, own].astype(F32) + pair_got[before].astype(F32)).astype(BF16)
        weights = jnp.concatenate([wkv[0], wkv[1]], axis=1)
        input_grad[...] += dot_nt(grad, weights)
        part = dot_nn(turned_rows[...], grad).astype(BF16)
        kv_part[0] = part[:, :LANES]
        kv_part[1] = part[:, LANES:]
        v_bias[...] = jnp.zeros_like(v_bias)
        v_bias[0:1] = column_sum(grad[:, LANES:].astype(F32))

    @pl.when(step == pairs)
    def _():
        movers[1].stage3()
        for mover in movers:
            mover.stage4()
            mover.drain()
        down_piece[...] = movers[0].mine[3]
        up_piece[...] = movers[1].mine[3]
        input_low[...] = input_grad[...].astype(BF16)


def attention_backward(
    subs, both, facts, probs, word, entity, keys, values, ctx, dctx, wq, wkv, d_one, smalls, down_part, up_part
):
    _, rows, width = both.shape
    length = 2 * rows
    pairs = width // LANES
    block = lambda n: pl.BlockSpec((n, LANES), lambda i: (0, jnp.minimum(i, pairs - 1)))
    behind = lambda n: pl.BlockSpec((n, LANES), lambda i: (0, jnp.maximum(i - 1, 0)))
    turned = pl.BlockSpec((LANES, rows), lambda i: (jnp.minimum(i, pairs - 1), 0))
    whole = lambda a: pl.BlockSpec(a.shape, lambda i: (0,) * a.ndim, pipeline_mode=pl.Buffered(1))
    q_cols = pl.BlockSpec((4, width, LANES), lambda i: (0, 0, jnp.minimum(i, pairs - 1)))
    kv_cols = pl.BlockSpec((2, width, LANES), lambda i: (0, 0, jnp.maximum(i - 1, 0)))
    anywhere = pl.BlockSpec(memory_space=pl.ANY)
    local = pl.BlockSpec(memory_space=pltpu.VMEM)
    shape = (1, down_part.shape[1] // GRID, down_part.shape[2] // 2)
    piece = jax.ShapeDtypeStruct((1, 4) + shape[1:], BF16)
    return pl.pallas_call(
        functools.partial(backward_kernel, subs),
        grid=(pairs + 1,),
        out_shape=[
            jax.ShapeDtypeStruct(wq.shape, BF16),
            jax.ShapeDtypeStruct(wkv.shape, BF16),
            jax.ShapeDtypeStruct((rows, width), F32),
            jax.ShapeDtypeStruct((8, width), F32),
            jax.ShapeDtypeStruct((8, width), F32),
            piece,
            piece,
            jax.ShapeDtypeStruct((rows, width), BF16),
            jax.ShapeDtypeStruct((24, width), F32),
        ],
        in_specs=[
            whole(both),
            whole(facts),
            pl.BlockSpec((2, length, rows), lambda i: (jnp.minimum(i, pairs - 1), 0, 0)),
            block(rows),
            block(rows),
            block(length),
            block(length),
            turned,
            turned,
            q_cols,
            kv_cols,
            whole(d_one),
        ]
        + [whole(a) for a in smalls]
        + [anywhere, anywhere],
        out_specs=[
            q_cols,
            kv_cols,
            pl.BlockSpec((rows, width), lambda i: (0, 0), pipeline_mode=pl.Buffered(1)),
            block(8),
            behind(8),
            local,
            local,
            local,
            local,
        ],
        scratch_shapes=[
            pltpu.VMEM((length, facts.shape[1]), jnp.int32),
            pltpu.VMEM((width, rows), BF16),
            pltpu.VMEM((pairs, length, 2 * LANES), BF16),
            pltpu.VMEM((pairs, rows, 2 * LANES), BF16),
            pltpu.SemaphoreType.DMA((pairs,)),
            pltpu.SemaphoreType.DMA((pairs,)),
            pltpu.VMEM((24, width), F32),
            pltpu.VMEM((5, 24, width), F32),
            pltpu.VMEM((5, 24, width), F32),
            pltpu.SemaphoreType.DMA((5,)),
            pltpu.SemaphoreType.DMA((5,)),
        ]
        + scatter_scratch(shape)
        + scatter_scratch(shape),
        compiler_params=pltpu.CompilerParams(
            collective_id=3, has_side_effects=True, vmem_limit_bytes=VMEM_LIMIT
        ),
        name="attention_backward",
    )(
        both, facts, probs, word, entity, keys, values, ctx, dctx, wq, wkv, d_one, *smalls,
        as_shards(down_part), as_shards(up_part),
    )


def ffn_forward_kernel(
    subs, both, facts, ctx, w_out, up, down, biases, out_bias, gain, shift, grad_out,
    active, slope, hidden_low, normal_one, inverse_one, output, d_two, sums, hidden, total, traded, valid, sems,
):
    step = pl.program_id(0)
    place = Place(subs)
    rows = both.shape[1]
    trade = Trade(place, grad_out, traded, sems)

    @pl.when(step == 0)
    def _():
        entry_barrier(place)
        trade.start()
        attn = dot_nt(ctx[...].T, w_out[...]) + out_bias[0:1].astype(F32)
        resid = both[place.c].astype(F32) + attn
        normal, inverse = normalize(resid)
        out = normal * gain[0:1].astype(F32) + shift[0:1].astype(F32)
        hidden[...] = out
        hidden_low[...] = out.astype(BF16)
        normal_one[...] = normal
        inverse_one[...] = inverse
        total[...] = jnp.zeros_like(total)
        own = pl.ds(pl.multiple_of(place.c * rows, LANES), rows)
        seen = facts[place.y, :, own].T[:, 2:3].astype(F32)
        valid[...] = seen
        sums[0:1] = column_sum(seen * resid * resid)
        sums[1:2] = column_sum(seen * attn * attn)

    span = biases.shape[2]
    across = pl.num_programs(0) // 2
    lines = BLOCK // span
    half = step // across
    line = 5 + lines * (step % across)
    bias = jnp.concatenate([biases[half, pl.ds(line + i, 1), :] for i in range(lines)], axis=1)
    act, rise = gelu_pair(dot_nn(hidden_low[...], up[...]) + bias)
    act = act.astype(BF16)
    active[...] = act
    slope[...] = rise.astype(BF16)
    total[...] += dot_nt(act, down[...])

    @pl.when(step == pl.num_programs(0) - 1)
    def _():
        ffn = total[...] + out_bias[1:2].astype(F32)
        resid = hidden[...] + ffn
        normal, inverse = normalize(resid)
        output[...] = (normal * gain[1:2].astype(F32) + shift[1:2].astype(F32)).astype(BF16)
        seen = valid[...]
        trade.finish()
        grad = traded[...].astype(F32)
        back = norm_backward(grad, normal, inverse, gain[1:2].astype(F32))
        d_two[...] = back
        sums[2:3] = column_sum(seen * ffn * ffn)
        sums[3:4] = column_sum(seen * resid * resid)
        sums[4:5] = column_sum(grad * normal)
        sums[5:6] = column_sum(grad)
        sums[6:7] = column_sum(back.astype(BF16).astype(F32))
        sums[7:8] = jnp.zeros_like(sums[7:8]) + jnp.sum(seen) * (1.0 / seen.shape[0])


def ffn_forward(subs, both, facts, ctx, w_out, up, down, biases, out_bias, gain, shift, grad_out):
    _, rows, width = both.shape
    units = up.shape[1]
    whole = lambda a: pl.BlockSpec(a.shape, lambda i: (0,) * a.ndim, pipeline_mode=pl.Buffered(1))
    fixed = lambda r, w: pl.BlockSpec((r, w), lambda i: (0, 0), pipeline_mode=pl.Buffered(1))
    wide = lambda r: pl.BlockSpec((r, BLOCK), lambda i: (0, i))
    return pl.pallas_call(
        functools.partial(ffn_forward_kernel, subs),
        grid=(units // BLOCK,),
        out_shape=[
            jax.ShapeDtypeStruct((rows, units), BF16),
            jax.ShapeDtypeStruct((rows, units), BF16),
            jax.ShapeDtypeStruct((rows, width), BF16),
            jax.ShapeDtypeStruct((rows, width), F32),
            jax.ShapeDtypeStruct((rows, 1), F32),
            jax.ShapeDtypeStruct((rows, width), BF16),
            jax.ShapeDtypeStruct((rows, width), F32),
            jax.ShapeDtypeStruct((8, width), F32),
        ],
        in_specs=[whole(both), whole(facts), whole(ctx), whole(w_out), wide(width), wide(width)]
        + [whole(a) for a in (biases, out_bias, gain, shift)]
        + [pl.BlockSpec(memory_space=pltpu.VMEM)],
        out_specs=[
            wide(rows),
            wide(rows),
            fixed(rows, width),
            fixed(rows, width),
            fixed(rows, 1),
            fixed(rows, width),
            fixed(rows, width),
            fixed(8, width),
        ],
        scratch_shapes=[
            pltpu.VMEM((rows, width), F32),
            pltpu.VMEM((rows, width), F32),
            pltpu.VMEM((rows, width), BF16),
            pltpu.VMEM((rows, 1), F32),
            pltpu.SemaphoreType.DMA((3,)),
        ],
        compiler_params=pltpu.CompilerParams(
            collective_id=4, has_side_effects=True, vmem_limit_bytes=VMEM_LIMIT
        ),
        cost_estimate=pl.CostEstimate(
            flops=2 * rows * width * (width + 2 * units),
            bytes_accessed=2 * width * (width + 2 * units) + 4 * rows * units,
            transcendentals=rows * units,
        ),
        name="ffn_forward",
    )(both, facts, ctx, w_out, up, down, biases, out_bias, gain, shift, grad_out)


def ffn_backward_kernel(
    subs, result, d_two, hidden_low, active, slope, up, down, ctx, w_out, gain, normal_one, inverse_one,
    up_part, down_part, bias_part, d_one, d_ctx, out_part, sums, output, d_low, d_turned, hidden_turned, total, sems,
):
    step = pl.program_id(0)
    place = Place(subs)
    trade = Trade(place, result, output, sems)

    @pl.when(step == 0)
    def _():
        entry_barrier(place)
        trade.start()
        low = d_two[...].astype(BF16)
        d_low[...] = low
        d_turned[...] = low.T
        hidden_turned[...] = hidden_low[...].T
        total[...] = d_two[...]

    d_pre = (dot_nn(d_low[...], down[...]) * slope[...].astype(F32)).astype(BF16)
    bias_part[...] = column_sum(d_pre.astype(F32))
    up_part[...] = dot_nn(hidden_turned[...], d_pre).astype(BF16)
    down_part[...] = dot_nn(d_turned[...], active[...]).astype(BF16)
    total[...] += dot_nt(d_pre, up[...])

    @pl.when(step == pl.num_programs(0) - 1)
    def _():
        grad = total[...]
        normal = normal_one[...]
        back = norm_backward(grad, normal, inverse_one[...], gain[0:1].astype(F32))
        d_one[...] = back
        low = back.astype(BF16)
        d_ctx[...] = dot_nt(w_out[...].T, low).astype(BF16)
        out_part[...] = dot_nt(low.T, ctx[...]).astype(BF16)
        sums[...] = jnp.zeros_like(sums)
        sums[0:1] = column_sum(grad * normal)
        sums[1:2] = column_sum(grad)
        sums[2:3] = column_sum(low.astype(F32))
        trade.finish()


def ffn_backward(subs, result, d_two, hidden_low, active, slope, up, down, ctx, w_out, gain, normal_one, inverse_one):
    rows, width = d_two.shape
    units = up.shape[1]
    whole = lambda a: pl.BlockSpec(a.shape, lambda i: (0,) * a.ndim, pipeline_mode=pl.Buffered(1))
    fixed = lambda r, w: pl.BlockSpec((r, w), lambda i: (0, 0), pipeline_mode=pl.Buffered(1))
    wide = lambda r: pl.BlockSpec((r, BLOCK), lambda i: (0, i))
    return pl.pallas_call(
        functools.partial(ffn_backward_kernel, subs),
        grid=(units // BLOCK,),
        out_shape=[
            jax.ShapeDtypeStruct((width, units), BF16),
            jax.ShapeDtypeStruct((width, units), BF16),
            jax.ShapeDtypeStruct((1, units), F32),
            jax.ShapeDtypeStruct((rows, width), F32),
            jax.ShapeDtypeStruct((width, rows), BF16),
            jax.ShapeDtypeStruct((width, width), BF16),
            jax.ShapeDtypeStruct((8, width), F32),
            jax.ShapeDtypeStruct((rows, width), BF16),
        ],
        in_specs=[pl.BlockSpec(memory_space=pltpu.VMEM), whole(d_two), whole(hidden_low), wide(rows), wide(rows), wide(width), wide(width)]
        + [whole(a) for a in (ctx, w_out, gain, normal_one, inverse_one)],
        out_specs=[
            wide(width),
            wide(width),
            wide(1),
            fixed(rows, width),
            fixed(width, rows),
            fixed(width, width),
            fixed(8, width),
            pl.BlockSpec(memory_space=pl.ANY),
        ],
        scratch_shapes=[
            pltpu.VMEM((rows, width), BF16),
            pltpu.VMEM((width, rows), BF16),
            pltpu.VMEM((width, rows), BF16),
            pltpu.VMEM((rows, width), F32),
            pltpu.SemaphoreType.DMA((3,)),
        ],
        compiler_params=pltpu.CompilerParams(
            collective_id=5, has_side_effects=True, vmem_limit_bytes=VMEM_LIMIT
        ),
        cost_estimate=pl.CostEstimate(
            flops=4 * rows * width * (width + 2 * units),
            bytes_accessed=2 * width * (3 * width + 4 * units) + 4 * rows * units,
            transcendentals=0,
        ),
        name="ffn_backward",
    )(result, d_two, hidden_low, active, slope, up, down, ctx, w_out, gain, normal_one, inverse_one)


def body(
    layer_input,
    grad_out,
    segment,
    entity,
    valid_mask,
    query_weight,
    key_value_weight,
    attn_bias,
    out_weight,
    out_bias,
    ln_gain,
    ln_bias,
    up_weight,
    ffn_bias,
    down_weight,
):
    rows, width = layer_input.shape
    length = segment.shape[0]
    rank = lax.axis_index("tensor")
    subs = lax.axis_size("dp") // GRID
    shards = [
        query_weight,
        key_value_weight,
        out_weight.T[None],
        up_weight[None],
        down_weight.T[None],
    ]
    groups = [[b * subs + s for s in range(subs)] for b in range(GRID)]
    if subs > 1:
        shards = [
            lax.all_gather(s, "dp", axis=1, tiled=True, axis_index_groups=groups) for s in shards
        ]
    shards = [shards[1], shards[0]] + shards[2:]
    cols = attn_bias.shape[1]
    (w_kv, w_q, w_out_t, w_up, w_down_t), (both, biases, pair_facts) = gather_weights(
        subs, shards, 3, layer_input, attn_bias, ffn_bias[None], [segment[None], entity[None], valid_mask[None]]
    )
    w_kv, w_q, w_out_t = as_matrix(w_kv), as_matrix(w_q), as_matrix(w_out_t)[0]
    context_t, probs, query_word, query_ent, keys, values, w_up, w_down_t = attention_forward(
        subs, both, w_q, w_kv, biases, pair_facts, w_up, w_down_t
    )
    w_up, w_down_t = as_matrix(w_up)[0], as_matrix(w_down_t)[0]
    active, slope, hidden_low, normal_one, inverse_one, result, d_two, sums_two = ffn_forward(
        subs, both, pair_facts, context_t, w_out_t, w_up, w_down_t, biases, out_bias, ln_gain, ln_bias, grad_out,
    )
    up_part, down_part, ffn_bias_part, d_one, d_context_t, out_part, sums_one, output = ffn_backward(
        subs, result, d_two, hidden_low, active, slope, w_up, w_down_t, context_t, w_out_t, ln_gain, normal_one, inverse_one
    )

    query_part, kv_part, input_grad, q_bias, v_bias, down_piece, up_piece, input_low, stack = attention_backward(
        subs, both, pair_facts, probs, query_word, query_ent, keys, values, context_t, d_context_t, w_q, w_kv, d_one,
        [sums_one, sums_two, ffn_bias_part], down_part[None], up_part[None],
    )
    sums, bias_sum, input_grad = scatter_gradients(
        subs,
        [down_piece, up_piece],
        [kv_part, query_part, out_part[None]],
        [q_bias, v_bias],
        input_grad,
        input_low,
    )
    if subs > 1:
        sums = [
            lax.psum_scatter(s, "dp", scatter_dimension=1, tiled=True, axis_index_groups=groups)
            for s in sums
        ]
        stack = lax.psum(stack, "dp", axis_index_groups=groups)
        bias_sum = lax.psum(bias_sum, "dp", axis_index_groups=groups)
    down_sum, up_sum, kv_sum, query_sum, out_sum = sums
    half = ffn_bias.shape[0]
    gains, shifts, out_biases, attn_biases, unit_biases, rms, query_sum, kv_sum, up_sum, input_grad, output = finish(
        subs, rows, stack, bias_sum, cols, half, [query_sum, kv_sum, up_sum, input_grad, output]
    )
    return (
        output,
        input_grad,
        rms[0],
        query_sum,
        kv_sum,
        attn_biases,
        out_sum[0].T,
        out_biases,
        gains,
        shifts,
        up_sum[0],
        unit_biases[0],
        down_sum[0].T,
    )


def solution(mesh):
    placed = (
        P(("dp", "tensor"), None),
        P(("dp", "tensor"), None),
        P("dp"),
        P("dp"),
        P("dp"),
        P(None, "dp", "tensor"),
        P(None, "dp", "tensor"),
        P(None, "tensor"),
        P("tensor", "dp"),
        P(),
        P(),
        P(),
        P("dp", "tensor"),
        P("tensor"),
        P("tensor", "dp"),
    )
    return jax.shard_map(
        body,
        mesh=mesh,
        in_specs=placed,
        out_specs=(
            P(("dp", "tensor"), None),
            P(("dp", "tensor"), None),
            P(),
            P(None, "dp", "tensor"),
            P(None, "dp", "tensor"),
            P(None, "tensor"),
            P("tensor", "dp"),
            P(),
            P(),
            P(),
            P("dp", "tensor"),
            P("tensor"),
            P("tensor", "dp"),
        ),
        check_vma=False,
    )
```
